32 devices in a mesh: user: 4 (over x, core), heads: 2 (over y), ctx: 4 (over z).
Axes of the slice: x: 2, y: 2, z: 4, core: 2. Of those that a mesh axis runs over, the one named last changes fastest.
Arguments:
- keys: bfloat16 [65536, 512], P(('user', 'ctx'), 'heads'), parts along dimension 0, may hold values from -6 to 6
- values: bfloat16 [65536, 512], P(('user', 'ctx'), 'heads'), parts along dimension 0, may hold values from -6 to 6
- queries: bfloat16 [4, 12288, 128], P('heads', ('user', 'ctx')), parts along dimension 1, may hold values from -240 to 240
- positions: int32 [12288], P(('user', 'ctx')), parts along dimension 0, may hold values from 0 to 16383
Outputs:
- attended: bfloat16 [4, 12288, 128], P('heads', ('user', 'ctx')), parts along dimension 1
The draws below stay inside these ranges and needn't reach their ends.
There are 4 independent parts, one for each index of `user`. The reference program is written for one: setup_inputs(seed, part) draws one part's arguments, and reference() takes and returns one part's arrays. A program takes and returns all parts, laid end to end along the dimension named above; each array names one. Nothing has to cross between parts.
All inputs are finite; a program needn't handle non-finite values.
Results may differ from the reference program's by a relative error of at most 0.008.
The reference program's roundings to bfloat16 on the way count: a program that leaves them out, or rounds other values in their place, can miss the bound.
Values may be sent and summed in bfloat16 or wider, within the bound.
A program may use at most 128 MiB of HBM per device.

```python
import math
import jax
import jax.numpy as jnp
from jax import lax

WINDOW = 16384
KV_HEADS = 4
HEAD_DIM = 128
QUERY_DEV = 768
QUERIES = 3072


def draw_queries(key, part):
    first_key = jax.random.fold_in(jax.random.fold_in(key, 11), 0)
    base = jax.random.truncated_normal(first_key, -4.0, 4.0, (KV_HEADS, QUERIES, HEAD_DIM), jnp.float32)
    return base.astype(jnp.bfloat16)


def set_ends(drawn, key, low, largest):
    spot = [jax.random.randint(jax.random.fold_in(key, axis), (), 0, length) for axis, length in enumerate(drawn.shape)]
    main_axis = drawn.shape.index(max(drawn.shape))
    next_to = spot[:main_axis] + [(spot[main_axis] + 1) % drawn.shape[main_axis]] + spot[main_axis + 1:]
    return drawn.at[tuple(spot)].set(low).at[tuple(next_to)].set(largest)


def steps_of(own_key, extent, shards, smallest, high):
    loudness = 1.0
    for axis_at, parts in shards:
        heights = jax.random.uniform(jax.random.fold_in(jax.random.fold_in(own_key, 6), axis_at), (parts,), jnp.float32, smallest / len(shards), high / len(shards))
        loudness = loudness * jnp.repeat(jnp.exp(heights), extent[axis_at] // parts).reshape((-1,) + (1,) * (len(extent) - 1 - axis_at))
    return loudness


def normal_values(stream_key, extent, deviation, most, cuts=(), kind=jnp.bfloat16):
    entries = deviation * jax.random.normal(stream_key, extent, jnp.float32)
    if cuts:
        entries = entries * steps_of(stream_key, extent, cuts, -0.22, 0.18)
    return jnp.clip(entries, -most, most).astype(kind)


def setup_inputs(seed: int = 0, part: int = 0) -> dict:
    seeds = jax.random.split(jax.random.key(seed), 5)
    part_keys = jax.random.split(jax.random.fold_in(seeds[4], part), 5)
    keys = normal_values(part_keys[0], (WINDOW, KV_HEADS * HEAD_DIM), 1.0, 6.0, ((0, 4), (1, 2)))
    values = normal_values(part_keys[1], (WINDOW, KV_HEADS * HEAD_DIM), 1.0, 6.0, ((0, 4), (1, 2)))
    queries = draw_queries(jax.random.fold_in(jax.random.fold_in(seeds[4], part), 71), part)
    positions = set_ends(jax.random.randint(part_keys[3], (QUERIES,), 0, WINDOW), jax.random.fold_in(part_keys[3], 1), 0, WINDOW - 1).astype(jnp.int32)
    return {"keys": keys, "values": values, "queries": queries, "positions": positions}


def compress(signal):
    length = signal.shape[0]
    reordered = jnp.concatenate([signal[0::2], signal[1::2][::-1]], axis=0)
    spectrum = jnp.fft.fft(reordered, axis=0)
    index = jnp.arange(length // 2).astype(jnp.float32)[:, None]
    kept = spectrum[:length // 2]
    coeffs = jnp.real(kept) * jnp.cos(math.pi * index / (2 * length)) + jnp.imag(kept) * jnp.sin(math.pi * index / (2 * length))
    weight = jnp.where(index == 0.0, 1.0 / length, 2.0 / length)
    scaled = coeffs * weight
    twisted = lax.complex(scaled * jnp.cos(math.pi * index / length), scaled * jnp.sin(math.pi * index / length))
    padded = jnp.concatenate([twisted, jnp.zeros_like(twisted)], axis=0)
    return jnp.real(jnp.fft.ifft(padded, axis=0))[:length // 2] * length

def inverse_freq(width):
    return jnp.exp(jnp.arange(width // 2).astype(jnp.float32) * (-2.0 * math.log(500000.0) / width))

def rotate_rows(block, places):
    width = block.shape[-1]
    half = width // 2
    angles = places[:, None] * inverse_freq(width)[None, :]
    cosine = jnp.cos(angles)
    sine = jnp.sin(angles)
    first = block[..., :half]
    second = block[..., half:]
    return jnp.concatenate([first * cosine - second * sine, second * cosine + first * sine], axis=-1)

def reference(keys, values, queries, positions):
    key_small = compress(keys.astype(jnp.float32)).astype(jnp.bfloat16)
    value_small = compress(values.astype(jnp.float32)).astype(jnp.bfloat16)
    kept_len = key_small.shape[0]
    places = jnp.arange(kept_len).astype(jnp.float32)
    query_places = positions.astype(jnp.float32)
    scaling = 1.0 / math.sqrt(HEAD_DIM)
    results = []
    for head_index in range(KV_HEADS):
        low = head_index * HEAD_DIM
        key_head = rotate_rows(key_small[:, low:low + HEAD_DIM].astype(jnp.float32), places).astype(jnp.bfloat16)
        value_head = value_small[:, low:low + HEAD_DIM]
        query_head = rotate_rows(queries[head_index].astype(jnp.float32), query_places).astype(jnp.bfloat16)
        blocks = query_head.reshape(QUERIES // QUERY_DEV, QUERY_DEV, HEAD_DIM)

        def attend_block(query_block):
            scores = jnp.dot(query_block, key_head.T, preferred_element_type=jnp.float32) * scaling
            top = lax.optimization_barrier(jnp.max(scores, axis=1, keepdims=True))
            expo = jnp.exp(scores - top)
            denom = lax.optimization_barrier(jnp.sum(expo, axis=1, keepdims=True))
            summed = jnp.dot(expo.astype(jnp.bfloat16), value_head, preferred_element_type=jnp.float32)
            return (summed / denom).astype(jnp.bfloat16)
        results.append(lax.map(attend_block, blocks).reshape(QUERIES, HEAD_DIM))
    return jnp.stack(results)
```

```python
import functools
import math

import jax
import jax.numpy as jnp
import numpy as np
from jax import lax
from jax.experimental import pallas as pl
from jax.experimental.pallas import tpu as pltpu
from jax.sharding import PartitionSpec as P

OUTER = 128
PARTS = 4
ORDER = 64
BLOCK = 256
MESH = pl.DeviceIdType.MESH


def split_two(matrix):
    high = matrix.astype(jnp.bfloat16)
    low = (matrix - np.asarray(high).astype(np.float64)).astype(jnp.bfloat16)
    return high, low


@functools.lru_cache(maxsize=None)
def stages(length):
    outer = OUTER
    inner = length // outer
    step = inner // 2
    a = np.arange(outer)
    c = np.arange(outer)
    turn = 2 * outer
    angle = np.pi / outer * ((c[:, None] * a[None, :]) % turn)
    alternate = np.where(a % 2 == 0, 1.0, -1.0)
    first = np.stack([np.cos(angle), -np.sin(angle)], axis=1)
    first[0, 1] = alternate
    d = np.arange(length // 2 // turn)
    k = np.concatenate([c[:, None] + turn * d, (turn - c[:, None]) % turn + turn * d], axis=1)
    k[0, d.size :] = outer + turn * d
    sign = np.concatenate([np.ones(d.size), -np.ones(d.size)])
    b = np.arange(inner)
    q = np.arange(step)
    theta = np.pi / (2 * length) * ((k[:, :, None] * (2 * b + 1)) % (4 * length))
    phi = np.pi / length * ((k[:, None, :] * (2 * q + 1)[:, None]) % (2 * length))
    forward = np.stack([np.cos(theta), np.sin(theta) * sign[None, :, None]], axis=2)
    weight = np.where(k == 0, 1.0, 2.0) / length
    back = np.stack([np.cos(phi), np.sin(phi) * sign], axis=1) * weight[:, None, None, :]
    half = d.size
    forward[0, :half, 1] = 0.0
    forward[0, half:, 1] = np.cos(theta[0, half:])
    forward[0, half:, 0] = 0.0
    back[0, 1, :, :half] = 0.0
    back[0, 1, :, half:] = np.cos(phi[0, :, half:]) * weight[0, half:]
    back[0, 0, :, half:] = 0.0
    middle = back.reshape(outer, 2 * step, 2 * half) @ forward.reshape(outer, 2 * half, 2 * inner)
    last = first.transpose(2, 0, 1).reshape(outer, 2 * outer)
    return first.reshape(2 * outer, outer), middle, last


def compress(signal):
    length, columns = signal.shape
    outer, inner = OUTER, length // OUTER
    first, middle, last = stages(length)
    first_high, first_low = split_two(first)
    flat = signal.reshape(outer, inner * columns)
    one = jnp.dot(first_high, flat, preferred_element_type=jnp.float32) + jnp.dot(
        first_low, flat, preferred_element_type=jnp.float32
    )
    one = one.reshape(outer, 2 * inner, columns)
    two = jnp.einsum(
        "cob,cbl->col", jnp.asarray(middle.astype(np.float32)), one, precision=lax.Precision.HIGH
    )
    three = jnp.dot(
        jnp.asarray(last.astype(np.float32)),
        two.reshape(2 * outer, inner // 2 * columns),
        precision=lax.Precision.HIGH,
    )
    return three.reshape(length // 2, columns).astype(jnp.bfloat16)

def strict_dot(left, right):
    rows, columns = left.shape[0] // 2, right.shape[1]
    high = right.astype(jnp.bfloat16)
    low = (right - high.astype(jnp.float32)).astype(jnp.bfloat16)
    both = jnp.dot(
        left, jnp.concatenate([high, low], axis=1), preferred_element_type=jnp.float32
    )
    return both[:rows, :columns] + (both[:rows, columns:] + both[rows:, :columns])


def inverse_freq(width):
    return jnp.exp(jnp.arange(width // 2).astype(jnp.float32) * (-2.0 * math.log(500000.0) / width))


def rotate_rows(block, places):
    width = block.shape[-1]
    half = width // 2
    angles = places[:, None] * inverse_freq(width)[None, :]
    cosine = jnp.cos(angles)
    sine = jnp.sin(angles)
    first = block[..., :half]
    second = block[..., half:]
    return jnp.concatenate(
        [first * cosine - second * sine, second * cosine + first * sine], axis=-1
    )


def attend_kernel(chunk, scale, resume, finish, swap_ref, q_ref, k_ref, v_ref, *refs):
    q = q_ref[0]
    swap = swap_ref[0] == 1
    rows, width = q.shape
    factor = scale * math.log2(math.e)
    if resume:
        accum = refs[0][0]
        best = refs[1][0][:, :1]
        total = refs[2][0][:, :1]
        refs = refs[3:]
    else:
        best = jnp.full((rows, 1), -jnp.inf, jnp.float32)
        total = jnp.zeros((rows, 1), jnp.float32)
        accum = jnp.zeros((rows, width), jnp.float32)
    tokens = k_ref.shape[1]
    for start in range(0, tokens, chunk):
        one = k_ref[0, start : start + chunk, :]
        two = v_ref[0, start : start + chunk, :]
        k, v = jnp.where(swap, two, one), jnp.where(swap, one, two)
        scores = lax.dot_general(
            q, k, (((1,), (1,)), ((), ())), preferred_element_type=jnp.float32
        )
        fresh = jnp.maximum(best, jnp.max(scores, axis=1, keepdims=True))
        expo = jnp.exp2((scores - fresh) * factor)
        shrink = jnp.exp2((best - fresh) * factor)
        total = total * shrink + jnp.sum(expo, axis=1, keepdims=True)
        accum = accum * shrink + jnp.dot(
            expo.astype(jnp.bfloat16), v, preferred_element_type=jnp.float32
        )
        best = fresh
    if finish:
        refs[0][0] = (accum / total).astype(refs[0].dtype)
        refs[1][0] = jnp.broadcast_to(best * factor + jnp.log2(total), (rows, 8))
    else:
        refs[0][0] = accum
        refs[1][0] = jnp.broadcast_to(best, (rows, 8))
        refs[2][0] = jnp.broadcast_to(total, (rows, 8))


def attend(queries, keys, values, swap, part=0, parts=1, state=None):
    groups, rows, width = queries.shape
    heads, tokens, _ = values.shape
    per_head = groups // heads
    block = math.gcd(rows, 768)
    chunk = math.gcd(tokens, 1024)
    scale = 1.0 / math.sqrt(width)
    finish = part == parts - 1
    wide = pl.BlockSpec((1, block, width), lambda g, i: (g, i, 0))
    thin = pl.BlockSpec((1, block, 8), lambda g, i: (g, i, 0))
    thin_shape = jax.ShapeDtypeStruct((groups, rows, 8), jnp.float32)
    state = () if state is None else tuple(state)
    wide_type = jnp.bfloat16 if finish else jnp.float32
    return pl.pallas_call(
        functools.partial(attend_kernel, chunk, scale, bool(state), finish),
        grid=(groups, rows // block),
        in_specs=[
            pl.BlockSpec(memory_space=pltpu.SMEM),
            wide,
            pl.BlockSpec((1, tokens, width), lambda g, i: (g // per_head, part, 0)),
            pl.BlockSpec((1, tokens, width), lambda g, i: (g // per_head, 0, 0)),
        ]
        + ([wide, thin, thin] if state else []),
        out_specs=[wide, thin] if finish else [wide, thin, thin],
        out_shape=[jax.ShapeDtypeStruct((groups, rows, width), wide_type), thin_shape]
        + ([] if finish else [thin_shape]),
        cost_estimate=pl.CostEstimate(
            flops=8 * groups * rows * tokens * width,
            bytes_accessed=4 * groups * rows * width * 2,
            transcendentals=groups * rows * tokens,
        ),
    )(swap.reshape(1), queries, keys, values, *state)


def nodes(count, order, pad):
    half = np.log((count - 1 + pad) / pad)
    e = np.exp(half * np.cos(np.pi * (2 * np.arange(order) + 1) / (2 * order)))
    return ((count - 1 + pad) * e - pad) / (1 + e)


def cardinals(places, count, order, pad):
    half = np.log((count - 1 + pad) / pad)
    at = np.arccos(np.clip(np.log((places + pad) / (count - 1 + pad - places)) / half, -1.0, 1.0))
    own = np.pi * (2 * np.arange(order) + 1) / (2 * order)
    total = np.zeros((places.size, order))
    for k in range(order):
        total += (1.0 if k == 0 else 2.0) / order * np.cos(k * at)[:, None] * np.cos(k * own)[None, :]
    return total


@functools.lru_cache(maxsize=None)
def fields(length, devices):
    parts, order = PARTS, ORDER
    scale = math.sqrt(0.5) / (2 * length)

    def cot(m):
        return 1.0 / np.tan(np.pi * m / (4 * length))

    n_dev = length // devices
    n_part, t_dev = n_dev // parts, n_dev // 2
    t_part = n_part // 2
    n, t = np.arange(n_part), np.arange(t_part)
    sign_n = np.array([1.0, -1.0, -1.0, 1.0])[n % 4]
    sign_t = np.where(t % 2 == 0, 1.0, -1.0)
    near = sign_t[:, None] * sign_n * scale * cot(4 * t[:, None] - 2 * n + 1.0)
    down = cardinals(n, n_part, order, 1.5).T * sign_n
    up = sign_t[:, None] * cardinals(t, t_part, order, 0.75)
    part = np.arange(parts)[:, None]
    source = (part * n_part + nodes(n_part, order, 1.5)).reshape(-1)
    target = (part * t_part + nodes(t_part, order, 0.75)).reshape(-1)
    merge = cardinals(source, n_dev, order, 1.5).T
    own = np.arange(parts * order) // order
    same = own[:, None] == own[None, :]
    local = np.where(same, 0.0, scale * cot(np.where(same, 1.0, 4 * target[:, None] - 2 * source + 1)))
    whole = nodes(n_dev, order, 1.5)
    cross = np.zeros((devices, parts * order, devices, order))
    for r in range(devices):
        for d in range(devices):
            a = 4 * (target + r * t_dev)[:, None]
            b = 2 * (whole + (r - d) % devices * n_dev)
            cross[r, :, d] = scale * cot(a + b + 3)
            if d:
                cross[r, :, d] += scale * cot(a - b + 1)
    return near, down, up, local, merge, cross.reshape(devices, parts * order, devices * order)


def spins(places, width):
    freq = 500000.0 ** (-2.0 * np.arange(width // 2) / width)
    angles = places[:, None] * freq
    cosine, sine = np.cos(angles), np.sin(angles)
    return np.stack(
        [np.concatenate([cosine, cosine], axis=1), np.concatenate([-sine, sine], axis=1)]
    ).astype(np.float32)


def fused_kernel(
    count,
    factor,
    keys_ref,
    values_ref,
    asked_ref,
    near_ref,
    down_ref,
    up_ref,
    local_ref,
    merge_ref,
    cross_hbm,
    coarse_ref,
    fine_ref,
    out_ref,
    cross_ref,
    parts_ref,
    whole_ref,
    others_ref,
    close_ref,
    field_ref,
    k_ref,
    v_ref,
    scores_ref,
    asks_ref,
    sent_ref,
    sent_log_ref,
    got_ref,
    got_log_ref,
    cross_sem,
    field_send,
    field_recv,
    ask_send,
    ask_recv,
    part_send,
    part_recv,
    log_send,
    log_recv,
):
    me = lax.axis_index("ctx")
    heads, width, rows = asked_ref.shape
    order = whole_ref.shape[0]
    n_part = near_ref.shape[1]
    t_part = n_part // 2
    half_columns = keys_ref.shape[1]
    tokens = k_ref.shape[1]

    def copy(src, dst, send, recv, step):
        return pltpu.make_async_remote_copy(
            src_ref=src,
            dst_ref=dst,
            send_sem=send,
            recv_sem=recv,
            device_id={"ctx": lax.rem(me + step, count)},
            device_id_type=MESH,
        )

    fetch = pltpu.make_async_copy(cross_hbm.at[me], cross_ref, cross_sem)
    fetch.start()
    barrier = pltpu.get_barrier_semaphore()
    for step in range(1, count):
        pl.semaphore_signal(
            barrier, inc=1, device_id={"ctx": lax.rem(me + step, count)}, device_id_type=MESH
        )
    pl.semaphore_wait(barrier, count - 1)

    for p in range(PARTS):
        for side, x_ref in enumerate((keys_ref, values_ref)):
            z = jnp.dot(
                down_ref[...], x_ref[p * n_part : (p + 1) * n_part, :], preferred_element_type=jnp.float32
            )
            parts_ref[
                p * order : (p + 1) * order, side * half_columns : (side + 1) * half_columns
            ] = z[:order] + z[order:]
    whole_ref[...] = strict_dot(merge_ref[...], parts_ref[...])
    field_copies = [
        copy(whole_ref, others_ref.at[step - 1], field_send.at[step - 1], field_recv.at[step - 1], step)
        for step in range(1, count)
    ]
    for each in field_copies:
        each.start()
    ask_copies = [
        copy(asked_ref, asks_ref.at[step - 1], ask_send.at[step - 1], ask_recv.at[step - 1], step)
        for step in range(1, count)
    ]
    for each in ask_copies:
        each.start()

    def close(p, carry):
        start = pl.multiple_of(p * n_part, n_part)
        for side, x_ref in enumerate((keys_ref, values_ref)):
            z = jnp.dot(near_ref[...], x_ref[pl.ds(start, n_part), :], preferred_element_type=jnp.float32)
            close_ref[p, :, side * half_columns : (side + 1) * half_columns] = z[:t_part] + z[t_part:]
        return carry

    lax.fori_loop(0, PARTS, close, 0)
    asks_ref[count - 1] = asked_ref[...]
    field_ref[...] = strict_dot(local_ref[...], parts_ref[...])
    fetch.wait()
    for each in field_copies:
        each.wait_recv()
    field_ref[...] += strict_dot(
        cross_ref[...],
        jnp.concatenate([whole_ref[...]] + [others_ref[i] for i in range(count - 1)], axis=0),
    )

    def finish(p, carry):
        f = field_ref[pl.ds(pl.multiple_of(p * order, order), order), :]
        high = f.astype(jnp.bfloat16)
        low = (f - high.astype(jnp.float32)).astype(jnp.bfloat16)
        y = close_ref[p] + jnp.dot(
            up_ref[...], jnp.concatenate([high, low, high], axis=0), preferred_element_type=jnp.float32
        )
        y = y.astype(jnp.bfloat16).astype(jnp.float32)
        begin = pl.multiple_of(p * t_part, t_part)
        place = me * PARTS + p
        cos_p, sin_p = coarse_ref[0, pl.ds(place, 1), :], coarse_ref[1, pl.ds(place, 1), :]
        cosine = cos_p * fine_ref[0] - sin_p * fine_ref[1]
        sine = sin_p * fine_ref[0] + cos_p * fine_ref[1]
        for head in range(heads):
            k = y[:, head * width : (head + 1) * width]
            turned = k * cosine + pltpu.roll(k, width // 2, 1) * sine
            k_ref[head, pl.ds(begin, t_part), :] = turned.astype(jnp.bfloat16)
            v = y[:, half_columns + head * width : half_columns + (head + 1) * width]
            v_ref[head, :, pl.ds(begin, t_part)] = v.T.astype(jnp.bfloat16)
        return carry

    lax.fori_loop(0, PARTS, finish, 0)

    def attend_one(slot, head):
        chunk = 512
        for block in range(rows // BLOCK):
            lanes = slice(block * BLOCK, (block + 1) * BLOCK)
            keep = scores_ref.at[block % 2]
            q = asks_ref[slot, head, :, lanes]
            best = None
            for c in range(0, tokens, chunk):
                s = jnp.dot(k_ref[head, c : c + chunk, :], q, preferred_element_type=jnp.float32)
                keep[c : c + chunk, :] = s
                top = jnp.max(s, axis=0, keepdims=True)
                best = top if best is None else jnp.maximum(best, top)
            total = jnp.zeros((1, BLOCK), jnp.float32)
            accum = jnp.zeros((width, BLOCK), jnp.float32)
            for c in range(0, tokens, chunk):
                e = jnp.exp2((keep[c : c + chunk, :] - best) * factor)
                total += jnp.sum(e, axis=0, keepdims=True)
                accum += jnp.dot(
                    v_ref[head, :, c : c + chunk], e.astype(jnp.bfloat16), preferred_element_type=jnp.float32
                )
            sent_ref[slot, head, :, lanes] = (accum / total).astype(jnp.bfloat16)
            sent_log_ref[slot, head, :, lanes] = jnp.broadcast_to(best * factor + jnp.log2(total), (8, BLOCK))

    def part_copy(slot, head):
        return copy(
            sent_ref.at[slot, head],
            got_ref.at[slot, head],
            part_send.at[slot, head],
            part_recv.at[slot, head],
            count - 1 - slot,
        )

    def log_copy(slot, head):
        return copy(
            sent_log_ref.at[slot, head],
            got_log_ref.at[slot, head],
            log_send.at[slot, head],
            log_recv.at[slot, head],
            count - 1 - slot,
        )

    def serve(i, carry):
        slot, head = i // heads, lax.rem(i, heads)

        @pl.when(jnp.logical_and(head == 0, slot < count - 1))
        def _():
            copy(asked_ref, asks_ref.at[slot], ask_send.at[slot], ask_recv.at[slot], slot + 1).wait_recv()

        attend_one(slot, head)

        @pl.when(slot < count - 1)
        def _():
            part_copy(slot, head).start()
            log_copy(slot, head).start()

        return carry

    lax.fori_loop(0, count * heads, serve, 0)

    for each in field_copies + ask_copies:
        each.wait_send()
    for slot in range(count - 1):
        for head in range(heads):
            part_copy(slot, head).wait()
            log_copy(slot, head).wait()
    for head in range(heads):
        logs = [got_log_ref[i, head, :1, :] for i in range(count - 1)] + [sent_log_ref[count - 1, head, :1, :]]
        best = functools.reduce(jnp.maximum, logs)
        shares = [jnp.exp2(log - best) for log in logs]
        total = functools.reduce(jnp.add, shares)
        parts = [got_ref[i, head] for i in range(count - 1)] + [sent_ref[count - 1, head]]
        mixed = functools.reduce(
            jnp.add, [part.astype(jnp.float32) * (share / total) for part, share in zip(parts, shares)]
        )
        out_ref[head] = mixed.T.astype(out_ref.dtype)


def by_tokens(keys, values, queries, positions, count):
    heads, rows, width = queries.shape
    n_dev, columns = keys.shape
    length = n_dev * count
    near, down, up, local, merge, cross = fields(length, count)

    def tall(matrix):
        return np.concatenate(split_two(matrix), axis=-2)

    up_high, up_low = split_two(up)
    t_part = near.shape[0]
    rotated = rotate_rows(queries.astype(jnp.float32), positions.astype(jnp.float32)).astype(
        jnp.bfloat16
    )
    asked = rotated.swapaxes(1, 2)
    tokens = n_dev // 2
    coarse = spins(np.arange(count * PARTS) * float(t_part), width)
    fine = spins(np.arange(t_part) * 1.0, width)
    vmem = pl.BlockSpec(memory_space=pltpu.VMEM)
    dma = pltpu.SemaphoreType.DMA
    return pl.pallas_call(
        functools.partial(fused_kernel, count, math.log2(math.e) / math.sqrt(width)),
        in_specs=[vmem] * 8 + [pl.BlockSpec(memory_space=pl.ANY)] + [vmem] * 2,
        out_specs=vmem,
        out_shape=jax.ShapeDtypeStruct(queries.shape, jnp.bfloat16),
        scratch_shapes=[
            pltpu.VMEM((2 * PARTS * ORDER, count * ORDER), jnp.bfloat16),
            pltpu.VMEM((PARTS * ORDER, 2 * columns), jnp.float32),
            pltpu.VMEM((ORDER, 2 * columns), jnp.float32),
            pltpu.VMEM((count - 1, ORDER, 2 * columns), jnp.float32),
            pltpu.VMEM((PARTS, t_part, 2 * columns), jnp.float32),
            pltpu.VMEM((PARTS * ORDER, 2 * columns), jnp.float32),
            pltpu.VMEM((heads, tokens, width), jnp.bfloat16),
            pltpu.VMEM((heads, width, tokens), jnp.bfloat16),
            pltpu.VMEM((2, tokens, BLOCK), jnp.float32),
            pltpu.VMEM((count, heads, width, rows), jnp.bfloat16),
            pltpu.VMEM((count, heads, width, rows), jnp.bfloat16),
            pltpu.VMEM((count, heads, 8, rows), jnp.float32),
            pltpu.VMEM((count - 1, heads, width, rows), jnp.bfloat16),
            pltpu.VMEM((count - 1, heads, 8, rows), jnp.float32),
            dma,
            dma((count - 1,)),
            dma((count - 1,)),
            dma((count - 1,)),
            dma((count - 1,)),
            dma((count - 1, heads)),
            dma((count - 1, heads)),
            dma((count - 1, heads)),
            dma((count - 1, heads)),
        ],
        compiler_params=pltpu.CompilerParams(
            collective_id=0, has_side_effects=True, vmem_limit_bytes=60 * 1024 * 1024
        ),
    )(
        keys,
        values,
        asked,
        tall(near),
        tall(down),
        np.concatenate([up_high, up_high, up_low], axis=1),
        tall(local),
        tall(merge),
        tall(cross),
        coarse,
        fine,
    )


def by_columns(keys, values, queries, positions):
    key_parts = lax.all_to_all(keys, "ctx", split_axis=1, concat_axis=0, tiled=True)
    value_parts = lax.all_to_all(values, "ctx", split_axis=1, concat_axis=0, tiled=True)
    heads, rows, width = queries.shape
    per_device = key_parts.shape[1]
    compact = compress(jnp.concatenate([key_parts, value_parts], axis=1))
    rotated = rotate_rows(queries.astype(jnp.float32), positions.astype(jnp.float32)).astype(
        jnp.bfloat16
    )
    whole = lax.all_gather(compact.T, "ctx", axis=0, tiled=True)
    tokens = whole.shape[1]
    shaped = whole.reshape(-1, 2, per_device, tokens)
    key_rows = shaped[:, 0].reshape(heads, width, tokens).swapaxes(1, 2)
    value_rows = shaped[:, 1].reshape(heads, width, tokens).swapaxes(1, 2)
    places = jnp.arange(tokens).astype(jnp.float32)
    ready = rotate_rows(key_rows.astype(jnp.float32), places).astype(jnp.bfloat16)
    return attend(rotated, ready, value_rows, jnp.zeros((), jnp.int32))[0]


def solution(mesh):
    count = mesh.shape["ctx"]

    def on_device(keys, values, queries, positions):
        heads, rows, width = queries.shape
        if count <= 2 * heads and keys.shape[0] % (PARTS * 512) == 0 and rows % BLOCK == 0:
            return by_tokens(keys, values, queries, positions, count)
        return by_columns(keys, values, queries, positions)

    return jax.shard_map(
        on_device,
        mesh=mesh,
        in_specs=(
            P(("user", "ctx"), "heads"),
            P(("user", "ctx"), "heads"),
            P("heads", ("user", "ctx"), None),
            P(("user", "ctx")),
        ),
        out_specs=P("heads", ("user", "ctx"), None),
        check_vma=False,
    )
```

```python
import functools
import math

import jax
import jax.numpy as jnp
import numpy as np
from jax import lax
from jax.experimental import pallas as pl
from jax.experimental.pallas import tpu as pltpu
from jax.sharding import PartitionSpec as P

OUTER = 128
PARTS = 4
ORDER = 64
FAR = 16
BLOCK = 256
MESH = pl.DeviceIdType.MESH


def split_two(matrix):
    high = matrix.astype(jnp.bfloat16)
    low = (matrix - np.asarray(high).astype(np.float64)).astype(jnp.bfloat16)
    return high, low


@functools.lru_cache(maxsize=None)
def stages(length):
    outer = OUTER
    inner = length // outer
    step = inner // 2
    a = np.arange(outer)
    c = np.arange(outer)
    turn = 2 * outer
    angle = np.pi / outer * ((c[:, None] * a[None, :]) % turn)
    alternate = np.where(a % 2 == 0, 1.0, -1.0)
    first = np.stack([np.cos(angle), -np.sin(angle)], axis=1)
    first[0, 1] = alternate
    d = np.arange(length // 2 // turn)
    k = np.concatenate([c[:, None] + turn * d, (turn - c[:, None]) % turn + turn * d], axis=1)
    k[0, d.size :] = outer + turn * d
    sign = np.concatenate([np.ones(d.size), -np.ones(d.size)])
    b = np.arange(inner)
    q = np.arange(step)
    theta = np.pi / (2 * length) * ((k[:, :, None] * (2 * b + 1)) % (4 * length))
    phi = np.pi / length * ((k[:, None, :] * (2 * q + 1)[:, None]) % (2 * length))
    forward = np.stack([np.cos(theta), np.sin(theta) * sign[None, :, None]], axis=2)
    weight = np.where(k == 0, 1.0, 2.0) / length
    back = np.stack([np.cos(phi), np.sin(phi) * sign], axis=1) * weight[:, None, None, :]
    half = d.size
    forward[0, :half, 1] = 0.0
    forward[0, half:, 1] = np.cos(theta[0, half:])
    forward[0, half:, 0] = 0.0
    back[0, 1, :, :half] = 0.0
    back[0, 1, :, half:] = np.cos(phi[0, :, half:]) * weight[0, half:]
    back[0, 0, :, half:] = 0.0
    middle = back.reshape(outer, 2 * step, 2 * half) @ forward.reshape(outer, 2 * half, 2 * inner)
    last = first.transpose(2, 0, 1).reshape(outer, 2 * outer)
    return first.reshape(2 * outer, outer), middle, last


def compress(signal):
    length, columns = signal.shape
    outer, inner = OUTER, length // OUTER
    first, middle, last = stages(length)
    first_high, first_low = split_two(first)
    flat = signal.reshape(outer, inner * columns)
    one = jnp.dot(first_high, flat, preferred_element_type=jnp.float32) + jnp.dot(
        first_low, flat, preferred_element_type=jnp.float32
    )
    one = one.reshape(outer, 2 * inner, columns)
    two = jnp.einsum(
        "cob,cbl->col", jnp.asarray(middle.astype(np.float32)), one, precision=lax.Precision.HIGH
    )
    three = jnp.dot(
        jnp.asarray(last.astype(np.float32)),
        two.reshape(2 * outer, inner // 2 * columns),
        precision=lax.Precision.HIGH,
    )
    return three.reshape(length // 2, columns).astype(jnp.bfloat16)

def strict_dot(left, right):
    rows, columns = left.shape[0] // 2, right.shape[1]
    high = right.astype(jnp.bfloat16)
    low = (right - high.astype(jnp.float32)).astype(jnp.bfloat16)
    both = jnp.dot(
        left, jnp.concatenate([high, low], axis=1), preferred_element_type=jnp.float32
    )
    return both[:rows, :columns] + (both[:rows, columns:] + both[rows:, :columns])


def inverse_freq(width):
    return jnp.exp(jnp.arange(width // 2).astype(jnp.float32) * (-2.0 * math.log(500000.0) / width))


def rotate_rows(block, places):
    width = block.shape[-1]
    half = width // 2
    angles = places[:, None] * inverse_freq(width)[None, :]
    cosine = jnp.cos(angles)
    sine = jnp.sin(angles)
    first = block[..., :half]
    second = block[..., half:]
    return jnp.concatenate(
        [first * cosine - second * sine, second * cosine + first * sine], axis=-1
    )


def attend_kernel(chunk, scale, resume, finish, swap_ref, q_ref, k_ref, v_ref, *refs):
    q = q_ref[0]
    swap = swap_ref[0] == 1
    rows, width = q.shape
    factor = scale * math.log2(math.e)
    if resume:
        accum = refs[0][0]
        best = refs[1][0][:, :1]
        total = refs[2][0][:, :1]
        refs = refs[3:]
    else:
        best = jnp.full((rows, 1), -jnp.inf, jnp.float32)
        total = jnp.zeros((rows, 1), jnp.float32)
        accum = jnp.zeros((rows, width), jnp.float32)
    tokens = k_ref.shape[1]
    for start in range(0, tokens, chunk):
        one = k_ref[0, start : start + chunk, :]
        two = v_ref[0, start : start + chunk, :]
        k, v = jnp.where(swap, two, one), jnp.where(swap, one, two)
        scores = lax.dot_general(
            q, k, (((1,), (1,)), ((), ())), preferred_element_type=jnp.float32
        )
        fresh = jnp.maximum(best, jnp.max(scores, axis=1, keepdims=True))
        expo = jnp.exp2((scores - fresh) * factor)
        shrink = jnp.exp2((best - fresh) * factor)
        total = total * shrink + jnp.sum(expo, axis=1, keepdims=True)
        accum = accum * shrink + jnp.dot(
            expo.astype(jnp.bfloat16), v, preferred_element_type=jnp.float32
        )
        best = fresh
    if finish:
        refs[0][0] = (accum / total).astype(refs[0].dtype)
        refs[1][0] = jnp.broadcast_to(best * factor + jnp.log2(total), (rows, 8))
    else:
        refs[0][0] = accum
        refs[1][0] = jnp.broadcast_to(best, (rows, 8))
        refs[2][0] = jnp.broadcast_to(total, (rows, 8))


def attend(queries, keys, values, swap, part=0, parts=1, state=None):
    groups, rows, width = queries.shape
    heads, tokens, _ = values.shape
    per_head = groups // heads
    block = math.gcd(rows, 768)
    chunk = math.gcd(tokens, 1024)
    scale = 1.0 / math.sqrt(width)
    finish = part == parts - 1
    wide = pl.BlockSpec((1, block, width), lambda g, i: (g, i, 0))
    thin = pl.BlockSpec((1, block, 8), lambda g, i: (g, i, 0))
    thin_shape = jax.ShapeDtypeStruct((groups, rows, 8), jnp.float32)
    state = () if state is None else tuple(state)
    wide_type = jnp.bfloat16 if finish else jnp.float32
    return pl.pallas_call(
        functools.partial(attend_kernel, chunk, scale, bool(state), finish),
        grid=(groups, rows // block),
        in_specs=[
            pl.BlockSpec(memory_space=pltpu.SMEM),
            wide,
            pl.BlockSpec((1, tokens, width), lambda g, i: (g // per_head, part, 0)),
            pl.BlockSpec((1, tokens, width), lambda g, i: (g // per_head, 0, 0)),
        ]
        + ([wide, thin, thin] if state else []),
        out_specs=[wide, thin] if finish else [wide, thin, thin],
        out_shape=[jax.ShapeDtypeStruct((groups, rows, width), wide_type), thin_shape]
        + ([] if finish else [thin_shape]),
        cost_estimate=pl.CostEstimate(
            flops=8 * groups * rows * tokens * width,
            bytes_accessed=4 * groups * rows * width * 2,
            transcendentals=groups * rows * tokens,
        ),
    )(swap.reshape(1), queries, keys, values, *state)


def nodes(count, order, pad):
    half = np.log((count - 1 + pad) / pad)
    e = np.exp(half * np.cos(np.pi * (2 * np.arange(order) + 1) / (2 * order)))
    return ((count - 1 + pad) * e - pad) / (1 + e)


def cardinals(places, count, order, pad):
    half = np.log((count - 1 + pad) / pad)
    at = np.arccos(np.clip(np.log((places + pad) / (count - 1 + pad - places)) / half, -1.0, 1.0))
    own = np.pi * (2 * np.arange(order) + 1) / (2 * order)
    total = np.zeros((places.size, order))
    for k in range(order):
        total += (1.0 if k == 0 else 2.0) / order * np.cos(k * at)[:, None] * np.cos(k * own)[None, :]
    return total


@functools.lru_cache(maxsize=None)
def fields(length, devices):
    parts, order = PARTS, ORDER
    scale = math.sqrt(0.5) / (2 * length)

    def cot(m):
        return 1.0 / np.tan(np.pi * m / (4 * length))

    n_dev = length // devices
    n_part, t_dev = n_dev // parts, n_dev // 2
    t_part = n_part // 2
    n, t = np.arange(n_part), np.arange(t_part)
    sign_n = np.array([1.0, -1.0, -1.0, 1.0])[n % 4]
    sign_t = np.where(t % 2 == 0, 1.0, -1.0)
    near = sign_t[:, None] * sign_n * scale * cot(4 * t[:, None] - 2 * n + 1.0)
    down = cardinals(n, n_part, order, 1.5).T * sign_n
    up = sign_t[:, None] * cardinals(t, t_part, order, 0.75)
    part = np.arange(parts)[:, None]
    source = (part * n_part + nodes(n_part, order, 1.5)).reshape(-1)
    target = (part * t_part + nodes(t_part, order, 0.75)).reshape(-1)
    bend = np.pi * (2 * np.arange(FAR) + 1) / (2 * FAR)
    spot = np.arccos(np.clip(2.0 * source / (n_dev - 1) - 1.0, -1.0, 1.0))
    plain = sum(
        (1.0 if k == 0 else 2.0) / FAR * np.cos(k * bend)[:, None] * np.cos(k * spot)[None, :]
        for k in range(FAR)
    )
    merge = np.concatenate([cardinals(source, n_dev, order, 1.5).T, plain])
    own = np.arange(parts * order) // order
    same = own[:, None] == own[None, :]
    local = np.where(same, 0.0, scale * cot(np.where(same, 1.0, 4 * target[:, None] - 2 * source + 1)))
    whole = nodes(n_dev, order, 1.5)
    sparse = (np.cos(bend) + 1.0) * (n_dev - 1) / 2
    cross = np.zeros((devices, parts * order, 3 * order + devices * FAR))
    for r in range(devices):
        a = 4 * (target + r * t_dev)[:, None]
        for s in range(devices):
            b = 2 * ((sparse if abs(r - s) > 1 else whole) + s * n_dev)
            block = scale * cot(a + b + 3)
            if r != s:
                block = block + scale * cot(a - b + 1)
            if abs(r - s) > 1:
                start = 3 * order + s * FAR
            else:
                start = {0: 0, 1: order, -1: 2 * order}[r - s]
            cross[r, :, start : start + block.shape[1]] = block
    return near, down, up, local, merge, cross


def spins(places, width):
    freq = 500000.0 ** (-2.0 * np.arange(width // 2) / width)
    angles = places[:, None] * freq
    cosine, sine = np.cos(angles), np.sin(angles)
    return np.stack(
        [np.concatenate([cosine, cosine], axis=1), np.concatenate([-sine, sine], axis=1)]
    ).astype(np.float32)


def fused_kernel(
    count,
    factor,
    keys_ref,
    values_ref,
    asked_ref,
    near_ref,
    down_ref,
    up_ref,
    local_ref,
    merge_ref,
    cross_hbm,
    coarse_ref,
    fine_ref,
    out_ref,
    cross_ref,
    parts_ref,
    whole_ref,
    others_ref,
    close_ref,
    field_ref,
    k_ref,
    v_ref,
    scores_ref,
    asks_ref,
    own_ref,
    own_log_ref,
    half_ref,
    half_log_ref,
    merged_ref,
    merged_log_ref,
    over_ref,
    over_log_ref,
    mate_ref,
    mate_log_ref,
    cross_sem,
    field_send,
    field_recv,
    ask_send,
    ask_recv,
    half_send,
    half_recv,
    over_send,
    over_recv,
    mate_send,
    mate_recv,
):
    me = lax.axis_index("ctx")
    heads, width, rows = asked_ref.shape
    order = ORDER
    n_part = near_ref.shape[1]
    t_part = n_part // 2
    half_columns = keys_ref.shape[1]
    tokens = k_ref.shape[1]
    mate = me + 1 - 2 * lax.rem(me, 2)
    mine = lax.rem(me, heads)

    def copy(src, dst, send, recv, other):
        return pltpu.make_async_remote_copy(
            src_ref=src,
            dst_ref=dst,
            send_sem=send,
            recv_sem=recv,
            device_id={"ctx": other},
            device_id_type=MESH,
        )

    fetch = pltpu.make_async_copy(cross_hbm.at[me], cross_ref, cross_sem)
    fetch.start()
    others_ref[...] = jnp.zeros_like(others_ref)
    asks_ref[me] = asked_ref[...]
    barrier = pltpu.get_barrier_semaphore()
    for step in range(1, count):
        pl.semaphore_signal(
            barrier, inc=1, device_id={"ctx": lax.rem(me + step, count)}, device_id_type=MESH
        )
    pl.semaphore_wait(barrier, count - 1)

    has_left, has_right = me > 0, me < count - 1

    def ask_copy(source, side):
        return copy(
            asks_ref.at[source],
            asks_ref.at[source],
            ask_send.at[source, side],
            ask_recv.at[source],
            me + 2 * side - 1,
        )

    def first_copy(side):
        return copy(
            asked_ref, asks_ref.at[me], ask_send.at[me, side], ask_recv.at[me], me + 2 * side - 1
        )

    @pl.when(has_left)
    def _():
        first_copy(0).start()

    @pl.when(has_right)
    def _():
        first_copy(1).start()

    for p in range(PARTS):
        for side, x_ref in enumerate((keys_ref, values_ref)):
            z = jnp.dot(
                down_ref[...], x_ref[p * n_part : (p + 1) * n_part, :], preferred_element_type=jnp.float32
            )
            parts_ref[
                p * order : (p + 1) * order, side * half_columns : (side + 1) * half_columns
            ] = z[:order] + z[order:]
    whole_ref[...] = strict_dot(merge_ref[...], parts_ref[...])
    others_ref[:order] = whole_ref[:order]

    def near_copy(side):
        start = order * (2 - side)
        return copy(
            whole_ref.at[pl.ds(0, order)],
            others_ref.at[pl.ds(start, order)],
            field_send.at[me + 2 * side - 1],
            field_recv.at[me],
            me + 2 * side - 1,
        )

    def far_copy(other):
        return copy(
            whole_ref.at[pl.ds(order, FAR)],
            others_ref.at[pl.ds(pl.multiple_of(3 * order + me * FAR, FAR), FAR)],
            field_send.at[other],
            field_recv.at[me],
            other,
        )

    def near_wait(side):
        start = order * (1 + side)
        source = me + 2 * side - 1
        copy(
            whole_ref.at[pl.ds(0, order)],
            others_ref.at[pl.ds(start, order)],
            field_send.at[source],
            field_recv.at[source],
            source,
        ).wait_recv()

    def far_wait(source):
        copy(
            whole_ref.at[pl.ds(order, FAR)],
            others_ref.at[pl.ds(3 * order + source * FAR, FAR)],
            field_send.at[source],
            field_recv.at[source],
            source,
        ).wait_recv()

    def far_from(other):
        return jnp.logical_or(other - me > 1, me - other > 1)

    for side, there in enumerate((has_left, has_right)):

        @pl.when(there)
        def _():
            near_copy(side).start()

    for other in range(count):

        @pl.when(far_from(other))
        def _():
            far_copy(other).start()

    def close(p, carry):
        start = pl.multiple_of(p * n_part, n_part)
        for side, x_ref in enumerate((keys_ref, values_ref)):
            z = jnp.dot(near_ref[...], x_ref[pl.ds(start, n_part), :], preferred_element_type=jnp.float32)
            close_ref[p, :, side * half_columns : (side + 1) * half_columns] = z[:t_part] + z[t_part:]
        return carry

    lax.fori_loop(0, PARTS, close, 0)
    field_ref[...] = strict_dot(local_ref[...], parts_ref[...])

    @pl.when(has_left)
    def _():
        ask_copy(me - 1, 1).wait_recv()

    @pl.when(has_right)
    def _():
        ask_copy(me + 1, 0).wait_recv()

    inside = jnp.logical_and(has_left, has_right)

    @pl.when(inside)
    def _():
        ask_copy(me - 1, 1).start()
        ask_copy(me + 1, 0).start()

    fetch.wait()
    for side, there in enumerate((has_left, has_right)):

        @pl.when(there)
        def _():
            near_wait(side)

    for other in range(count):

        @pl.when(far_from(other))
        def _():
            far_wait(other)

    field_ref[...] += strict_dot(cross_ref[...], others_ref[...])

    def finish(p, carry):
        f = field_ref[pl.ds(pl.multiple_of(p * order, order), order), :]
        high = f.astype(jnp.bfloat16)
        low = (f - high.astype(jnp.float32)).astype(jnp.bfloat16)
        y = close_ref[p] + jnp.dot(
            up_ref[...], jnp.concatenate([high, low, high], axis=0), preferred_element_type=jnp.float32
        )
        y = y.astype(jnp.bfloat16).astype(jnp.float32)
        begin = pl.multiple_of(p * t_part, t_part)
        place = me * PARTS + p
        cos_p, sin_p = coarse_ref[0, pl.ds(place, 1), :], coarse_ref[1, pl.ds(place, 1), :]
        cosine = cos_p * fine_ref[0] - sin_p * fine_ref[1]
        sine = sin_p * fine_ref[0] + cos_p * fine_ref[1]
        for head in range(heads):
            k = y[:, head * width : (head + 1) * width]
            turned = k * cosine + pltpu.roll(k, width // 2, 1) * sine
            k_ref[head, pl.ds(begin, t_part), :] = turned.astype(jnp.bfloat16)
            v = y[:, half_columns + head * width : half_columns + (head + 1) * width]
            v_ref[head, :, pl.ds(begin, t_part)] = v.T.astype(jnp.bfloat16)
        return carry

    lax.fori_loop(0, PARTS, finish, 0)

    lower = me < count // 2
    far_end = jnp.where(lower, count - 1, 0)
    near_over = jnp.where(lower, count // 2, count // 2 - 1)
    out_side = jnp.where(lower, 0, 1)

    @pl.when(inside)
    def _():
        handed = ask_copy(far_end, out_side)
        handed.wait_recv()
        handed.start()

    def attend_one(slot, source, head):
        chunk = 512
        for block in range(rows // BLOCK):
            lanes = slice(block * BLOCK, (block + 1) * BLOCK)
            keep = scores_ref.at[block % 2]
            q = asks_ref[source, head, :, lanes]
            best = None
            for c in range(0, tokens, chunk):
                s = jnp.dot(k_ref[head, c : c + chunk, :], q, preferred_element_type=jnp.float32)
                keep[c : c + chunk, :] = s
                top = jnp.max(s, axis=0, keepdims=True)
                best = top if best is None else jnp.maximum(best, top)
            total = jnp.zeros((1, BLOCK), jnp.float32)
            accum = jnp.zeros((width, BLOCK), jnp.float32)
            for c in range(0, tokens, chunk):
                e = jnp.exp2((keep[c : c + chunk, :] - best) * factor)
                total += jnp.sum(e, axis=0, keepdims=True)
                accum += jnp.dot(
                    v_ref[head, :, c : c + chunk], e.astype(jnp.bfloat16), preferred_element_type=jnp.float32
                )
            own_ref[slot, head, :, lanes] = (accum / total).astype(jnp.bfloat16)
            own_log_ref[slot, head, :, lanes] = best * factor + jnp.log2(total)

    def both(src, src_log, dst, dst_log, send, recv, other):
        return (
            copy(src, dst, send.at[0], recv.at[0], other),
            copy(src_log, dst_log, send.at[1], recv.at[1], other),
        )

    def half_copy(j):
        return both(
            own_ref.at[j + 1, 1 - mine],
            own_log_ref.at[j + 1, 1 - mine],
            half_ref.at[j],
            half_log_ref.at[j],
            half_send.at[j],
            half_recv.at[j],
            mate,
        )

    def over_copy(j):
        return both(
            merged_ref.at[j],
            merged_log_ref.at[j],
            over_ref.at[mine],
            over_log_ref.at[mine],
            over_send.at[j],
            over_recv.at[mine],
            near_over if j == 0 else far_end,
        )

    def mate_copy(head):
        return both(
            own_ref.at[3, head],
            own_log_ref.at[3, head],
            mate_ref.at[head],
            mate_log_ref.at[head],
            mate_send.at[head],
            mate_recv.at[head],
            mate,
        )

    def blend(parts, logs):
        best = functools.reduce(jnp.maximum, logs)
        shares = [jnp.exp2(log - best) for log in logs]
        total = functools.reduce(jnp.add, shares)
        mixed = functools.reduce(
            jnp.add, [part.astype(jnp.float32) * (share / total) for part, share in zip(parts, shares)]
        )
        return mixed, best + jnp.log2(total)

    def merge_half(j):
        for each in half_copy(j):
            each.wait_recv()
        mixed, log = blend(
            [own_ref[j + 1, mine], half_ref[j]], [own_log_ref[j + 1, mine], half_log_ref[j]]
        )
        merged_ref[j] = mixed.astype(jnp.bfloat16)
        merged_log_ref[j] = log
        for each in over_copy(j):
            each.start()

    def serve(u, carry):
        slot = u // heads
        second = lax.rem(u, heads)
        head = jnp.where(second == 0, 1 - mine, mine)
        source = jnp.where(
            slot == 0, me, jnp.where(slot == 1, near_over, jnp.where(slot == 2, far_end, mate))
        )

        @pl.when(
            jnp.logical_and(
                jnp.logical_and(second == 0, jnp.logical_not(inside)),
                jnp.logical_or(slot == 1, slot == 2),
            )
        )
        def _():
            ask_copy(source, 1 - out_side).wait_recv()

        attend_one(slot, source, head)
        for j in range(2):

            @pl.when(u == (j + 1) * heads)
            def _():
                for each in half_copy(j):
                    each.start()

            @pl.when(u == (j + 2) * heads)
            def _():
                merge_half(j)

        @pl.when(slot == 3)
        def _():
            for each in mate_copy(head):
                each.start()

        return carry

    lax.fori_loop(0, 4 * heads, serve, 0)

    for head in range(heads):
        for each in both(
            merged_ref.at[0],
            merged_log_ref.at[0],
            over_ref.at[head],
            over_log_ref.at[head],
            over_send.at[0],
            over_recv.at[head],
            near_over,
        ):
            each.wait_recv()
    for head in range(heads):
        for each in mate_copy(head):
            each.wait_recv()
    for head in range(heads):
        mixed, _ = blend(
            [own_ref[0, head], over_ref[head], mate_ref[head]],
            [own_log_ref[0, head], over_log_ref[head], mate_log_ref[head]],
        )
        out_ref[head] = mixed.T.astype(out_ref.dtype)

    for side, there in enumerate((has_left, has_right)):

        @pl.when(there)
        def _():
            first_copy(side).wait_send()
            near_copy(side).wait_send()

    for other in range(count):

        @pl.when(far_from(other))
        def _():
            far_copy(other).wait_send()

    @pl.when(inside)
    def _():
        ask_copy(me - 1, 1).wait_send()
        ask_copy(me + 1, 0).wait_send()
        ask_copy(far_end, out_side).wait_send()

    for j in range(2):
        for each in half_copy(j) + over_copy(j):
            each.wait_send()
    for head in range(heads):
        for each in mate_copy(head):
            each.wait_send()


def by_tokens(keys, values, queries, positions, count):
    heads, rows, width = queries.shape
    n_dev, columns = keys.shape
    length = n_dev * count
    near, down, up, local, merge, cross = fields(length, count)

    def tall(matrix):
        return np.concatenate(split_two(matrix), axis=-2)

    up_high, up_low = split_two(up)
    t_part = near.shape[0]
    rotated = rotate_rows(queries.astype(jnp.float32), positions.astype(jnp.float32)).astype(
        jnp.bfloat16
    )
    asked = rotated.swapaxes(1, 2)
    tokens = n_dev // 2
    coarse = spins(np.arange(count * PARTS) * float(t_part), width)
    fine = spins(np.arange(t_part) * 1.0, width)
    vmem = pl.BlockSpec(memory_space=pltpu.VMEM)
    dma = pltpu.SemaphoreType.DMA
    return pl.pallas_call(
        functools.partial(fused_kernel, count, math.log2(math.e) / math.sqrt(width)),
        in_specs=[vmem] * 8 + [pl.BlockSpec(memory_space=pl.ANY)] + [vmem] * 2,
        out_specs=vmem,
        out_shape=jax.ShapeDtypeStruct(queries.shape, jnp.bfloat16),
        scratch_shapes=[
            pltpu.VMEM((2 * cross.shape[1], cross.shape[2]), jnp.bfloat16),
            pltpu.VMEM((PARTS * ORDER, 2 * columns), jnp.float32),
            pltpu.VMEM((ORDER + FAR, 2 * columns), jnp.float32),
            pltpu.VMEM((cross.shape[2], 2 * columns), jnp.float32),
            pltpu.VMEM((PARTS, t_part, 2 * columns), jnp.float32),
            pltpu.VMEM((PARTS * ORDER, 2 * columns), jnp.float32),
            pltpu.VMEM((heads, tokens, width), jnp.bfloat16),
            pltpu.VMEM((heads, width, tokens), jnp.bfloat16),
            pltpu.VMEM((2, tokens, BLOCK), jnp.float32),
            pltpu.VMEM((count, heads, width, rows), jnp.bfloat16),
            pltpu.VMEM((4, heads, width, rows), jnp.bfloat16),
            pltpu.VMEM((4, heads, 1, rows), jnp.float32),
            pltpu.VMEM((2, width, rows), jnp.bfloat16),
            pltpu.VMEM((2, 1, rows), jnp.float32),
            pltpu.VMEM((2, width, rows), jnp.bfloat16),
            pltpu.VMEM((2, 1, rows), jnp.float32),
            pltpu.VMEM((heads, width, rows), jnp.bfloat16),
            pltpu.VMEM((heads, 1, rows), jnp.float32),
            pltpu.VMEM((heads, width, rows), jnp.bfloat16),
            pltpu.VMEM((heads, 1, rows), jnp.float32),
            dma,
            dma((count,)),
            dma((count,)),
            dma((count, 2)),
            dma((count,)),
            dma((2, 2)),
            dma((2, 2)),
            dma((2, 2)),
            dma((heads, 2)),
            dma((heads, 2)),
            dma((heads, 2)),
        ],
        compiler_params=pltpu.CompilerParams(
            collective_id=0, has_side_effects=True, vmem_limit_bytes=60 * 1024 * 1024
        ),
    )(
        keys,
        values,
        asked,
        tall(near),
        tall(down),
        np.concatenate([up_high, up_high, up_low], axis=1),
        tall(local),
        tall(merge),
        tall(cross),
        coarse,
        fine,
    )


def by_columns(keys, values, queries, positions):
    key_parts = lax.all_to_all(keys, "ctx", split_axis=1, concat_axis=0, tiled=True)
    value_parts = lax.all_to_all(values, "ctx", split_axis=1, concat_axis=0, tiled=True)
    heads, rows, width = queries.shape
    per_device = key_parts.shape[1]
    compact = compress(jnp.concatenate([key_parts, value_parts], axis=1))
    rotated = rotate_rows(queries.astype(jnp.float32), positions.astype(jnp.float32)).astype(
        jnp.bfloat16
    )
    whole = lax.all_gather(compact.T, "ctx", axis=0, tiled=True)
    tokens = whole.shape[1]
    shaped = whole.reshape(-1, 2, per_device, tokens)
    key_rows = shaped[:, 0].reshape(heads, width, tokens).swapaxes(1, 2)
    value_rows = shaped[:, 1].reshape(heads, width, tokens).swapaxes(1, 2)
    places = jnp.arange(tokens).astype(jnp.float32)
    ready = rotate_rows(key_rows.astype(jnp.float32), places).astype(jnp.bfloat16)
    return attend(rotated, ready, value_rows, jnp.zeros((), jnp.int32))[0]


def solution(mesh):
    count = mesh.shape["ctx"]

    def on_device(keys, values, queries, positions):
        heads, rows, width = queries.shape
        if count == 4 and heads == 2 and keys.shape[0] % (PARTS * 512) == 0 and rows % BLOCK == 0:
            return by_tokens(keys, values, queries, positions, count)
        return by_columns(keys, values, queries, positions)

    return jax.shard_map(
        on_device,
        mesh=mesh,
        in_specs=(
            P(("user", "ctx"), "heads"),
            P(("user", "ctx"), "heads"),
            P("heads", ("user", "ctx"), None),
            P(("user", "ctx")),
        ),
        out_specs=P("heads", ("user", "ctx"), None),
        check_vma=False,
    )
```

```python
import functools
import math

import jax
import jax.numpy as jnp
import numpy as np
from jax import lax
from jax.experimental import pallas as pl
from jax.experimental.pallas import tpu as pltpu
from jax.sharding import PartitionSpec as P

OUTER = 128
PARTS = 4
ORDER = 64
FAR = 16
BLOCK = 256
MESH = pl.DeviceIdType.MESH


def split_two(matrix):
    high = matrix.astype(jnp.bfloat16)
    low = (matrix - np.asarray(high).astype(np.float64)).astype(jnp.bfloat16)
    return high, low


@functools.lru_cache(maxsize=None)
def stages(length):
    outer = OUTER
    inner = length // outer
    step = inner // 2
    a = np.arange(outer)
    c = np.arange(outer)
    turn = 2 * outer
    angle = np.pi / outer * ((c[:, None] * a[None, :]) % turn)
    alternate = np.where(a % 2 == 0, 1.0, -1.0)
    first = np.stack([np.cos(angle), -np.sin(angle)], axis=1)
    first[0, 1] = alternate
    d = np.arange(length // 2 // turn)
    k = np.concatenate([c[:, None] + turn * d, (turn - c[:, None]) % turn + turn * d], axis=1)
    k[0, d.size :] = outer + turn * d
    sign = np.concatenate([np.ones(d.size), -np.ones(d.size)])
    b = np.arange(inner)
    q = np.arange(step)
    theta = np.pi / (2 * length) * ((k[:, :, None] * (2 * b + 1)) % (4 * length))
    phi = np.pi / length * ((k[:, None, :] * (2 * q + 1)[:, None]) % (2 * length))
    forward = np.stack([np.cos(theta), np.sin(theta) * sign[None, :, None]], axis=2)
    weight = np.where(k == 0, 1.0, 2.0) / length
    back = np.stack([np.cos(phi), np.sin(phi) * sign], axis=1) * weight[:, None, None, :]
    half = d.size
    forward[0, :half, 1] = 0.0
    forward[0, half:, 1] = np.cos(theta[0, half:])
    forward[0, half:, 0] = 0.0
    back[0, 1, :, :half] = 0.0
    back[0, 1, :, half:] = np.cos(phi[0, :, half:]) * weight[0, half:]
    back[0, 0, :, half:] = 0.0
    middle = back.reshape(outer, 2 * step, 2 * half) @ forward.reshape(outer, 2 * half, 2 * inner)
    last = first.transpose(2, 0, 1).reshape(outer, 2 * outer)
    return first.reshape(2 * outer, outer), middle, last


def compress(signal):
    length, columns = signal.shape
    outer, inner = OUTER, length // OUTER
    first, middle, last = stages(length)
    first_high, first_low = split_two(first)
    flat = signal.reshape(outer, inner * columns)
    one = jnp.dot(first_high, flat, preferred_element_type=jnp.float32) + jnp.dot(
        first_low, flat, preferred_element_type=jnp.float32
    )
    one = one.reshape(outer, 2 * inner, columns)
    two = jnp.einsum(
        "cob,cbl->col", jnp.asarray(middle.astype(np.float32)), one, precision=lax.Precision.HIGH
    )
    three = jnp.dot(
        jnp.asarray(last.astype(np.float32)),
        two.reshape(2 * outer, inner // 2 * columns),
        precision=lax.Precision.HIGH,
    )
    return three.reshape(length // 2, columns).astype(jnp.bfloat16)

def strict_dot(left, right):
    rows, columns = left.shape[0] // 2, right.shape[1]
    high = right.astype(jnp.bfloat16)
    low = (right - high.astype(jnp.float32)).astype(jnp.bfloat16)
    both = jnp.dot(
        left, jnp.concatenate([high, low], axis=1), preferred_element_type=jnp.float32
    )
    return both[:rows, :columns] + (both[:rows, columns:] + both[rows:, :columns])


def inverse_freq(width):
    return jnp.exp(jnp.arange(width // 2).astype(jnp.float32) * (-2.0 * math.log(500000.0) / width))


def rotate_rows(block, places):
    width = block.shape[-1]
    half = width // 2
    angles = places[:, None] * inverse_freq(width)[None, :]
    cosine = jnp.cos(angles)
    sine = jnp.sin(angles)
    first = block[..., :half]
    second = block[..., half:]
    return jnp.concatenate(
        [first * cosine - second * sine, second * cosine + first * sine], axis=-1
    )


def attend_kernel(chunk, scale, resume, finish, swap_ref, q_ref, k_ref, v_ref, *refs):
    q = q_ref[0]
    swap = swap_ref[0] == 1
    rows, width = q.shape
    factor = scale * math.log2(math.e)
    if resume:
        accum = refs[0][0]
        best = refs[1][0][:, :1]
        total = refs[2][0][:, :1]
        refs = refs[3:]
    else:
        best = jnp.full((rows, 1), -jnp.inf, jnp.float32)
        total = jnp.zeros((rows, 1), jnp.float32)
        accum = jnp.zeros((rows, width), jnp.float32)
    tokens = k_ref.shape[1]
    for start in range(0, tokens, chunk):
        one = k_ref[0, start : start + chunk, :]
        two = v_ref[0, start : start + chunk, :]
        k, v = jnp.where(swap, two, one), jnp.where(swap, one, two)
        scores = lax.dot_general(
            q, k, (((1,), (1,)), ((), ())), preferred_element_type=jnp.float32
        )
        fresh = jnp.maximum(best, jnp.max(scores, axis=1, keepdims=True))
        expo = jnp.exp2((scores - fresh) * factor)
        shrink = jnp.exp2((best - fresh) * factor)
        total = total * shrink + jnp.sum(expo, axis=1, keepdims=True)
        accum = accum * shrink + jnp.dot(
            expo.astype(jnp.bfloat16), v, preferred_element_type=jnp.float32
        )
        best = fresh
    if finish:
        refs[0][0] = (accum / total).astype(refs[0].dtype)
        refs[1][0] = jnp.broadcast_to(best * factor + jnp.log2(total), (rows, 8))
    else:
        refs[0][0] = accum
        refs[1][0] = jnp.broadcast_to(best, (rows, 8))
        refs[2][0] = jnp.broadcast_to(total, (rows, 8))


def attend(queries, keys, values, swap, part=0, parts=1, state=None):
    groups, rows, width = queries.shape
    heads, tokens, _ = values.shape
    per_head = groups // heads
    block = math.gcd(rows, 768)
    chunk = math.gcd(tokens, 1024)
    scale = 1.0 / math.sqrt(width)
    finish = part == parts - 1
    wide = pl.BlockSpec((1, block, width), lambda g, i: (g, i, 0))
    thin = pl.BlockSpec((1, block, 8), lambda g, i: (g, i, 0))
    thin_shape = jax.ShapeDtypeStruct((groups, rows, 8), jnp.float32)
    state = () if state is None else tuple(state)
    wide_type = jnp.bfloat16 if finish else jnp.float32
    return pl.pallas_call(
        functools.partial(attend_kernel, chunk, scale, bool(state), finish),
        grid=(groups, rows // block),
        in_specs=[
            pl.BlockSpec(memory_space=pltpu.SMEM),
            wide,
            pl.BlockSpec((1, tokens, width), lambda g, i: (g // per_head, part, 0)),
            pl.BlockSpec((1, tokens, width), lambda g, i: (g // per_head, 0, 0)),
        ]
        + ([wide, thin, thin] if state else []),
        out_specs=[wide, thin] if finish else [wide, thin, thin],
        out_shape=[jax.ShapeDtypeStruct((groups, rows, width), wide_type), thin_shape]
        + ([] if finish else [thin_shape]),
        cost_estimate=pl.CostEstimate(
            flops=8 * groups * rows * tokens * width,
            bytes_accessed=4 * groups * rows * width * 2,
            transcendentals=groups * rows * tokens,
        ),
    )(swap.reshape(1), queries, keys, values, *state)


def nodes(count, order, pad):
    half = np.log((count - 1 + pad) / pad)
    e = np.exp(half * np.cos(np.pi * (2 * np.arange(order) + 1) / (2 * order)))
    return ((count - 1 + pad) * e - pad) / (1 + e)


def cardinals(places, count, order, pad):
    half = np.log((count - 1 + pad) / pad)
    at = np.arccos(np.clip(np.log((places + pad) / (count - 1 + pad - places)) / half, -1.0, 1.0))
    own = np.pi * (2 * np.arange(order) + 1) / (2 * order)
    total = np.zeros((places.size, order))
    for k in range(order):
        total += (1.0 if k == 0 else 2.0) / order * np.cos(k * at)[:, None] * np.cos(k * own)[None, :]
    return total


@functools.lru_cache(maxsize=None)
def fields(length, devices):
    parts, order = PARTS, ORDER
    scale = math.sqrt(0.5) / (2 * length)

    def cot(m):
        return 1.0 / np.tan(np.pi * m / (4 * length))

    n_dev = length // devices
    n_part, t_dev = n_dev // parts, n_dev // 2
    t_part = n_part // 2
    n, t = np.arange(n_part), np.arange(t_part)
    sign_n = np.array([1.0, -1.0, -1.0, 1.0])[n % 4]
    sign_t = np.where(t % 2 == 0, 1.0, -1.0)
    near = sign_t[:, None] * sign_n * scale * cot(4 * t[:, None] - 2 * n + 1.0)
    down = cardinals(n, n_part, order, 1.5).T * sign_n
    up = sign_t[:, None] * cardinals(t, t_part, order, 0.75)
    part = np.arange(parts)[:, None]
    source = (part * n_part + nodes(n_part, order, 1.5)).reshape(-1)
    target = (part * t_part + nodes(t_part, order, 0.75)).reshape(-1)
    bend = np.pi * (2 * np.arange(FAR) + 1) / (2 * FAR)
    spot = np.arccos(np.clip(2.0 * source / (n_dev - 1) - 1.0, -1.0, 1.0))
    plain = sum(
        (1.0 if k == 0 else 2.0) / FAR * np.cos(k * bend)[:, None] * np.cos(k * spot)[None, :]
        for k in range(FAR)
    )
    merge = np.concatenate([cardinals(source, n_dev, order, 1.5).T, plain])
    own = np.arange(parts * order) // order
    same = own[:, None] == own[None, :]
    local = np.where(same, 0.0, scale * cot(np.where(same, 1.0, 4 * target[:, None] - 2 * source + 1)))
    whole = nodes(n_dev, order, 1.5)
    sparse = (np.cos(bend) + 1.0) * (n_dev - 1) / 2
    cross = np.zeros((devices, parts * order, 3 * order + devices * FAR))
    for r in range(devices):
        a = 4 * (target + r * t_dev)[:, None]
        for s in range(devices):
            b = 2 * ((sparse if abs(r - s) > 1 else whole) + s * n_dev)
            block = scale * cot(a + b + 3)
            if r != s:
                block = block + scale * cot(a - b + 1)
            if abs(r - s) > 1:
                start = 3 * order + s * FAR
            else:
                start = {0: 0, 1: order, -1: 2 * order}[r - s]
            cross[r, :, start : start + block.shape[1]] = block
    return near, down, up, local, merge, cross


def spins(places, width):
    freq = 500000.0 ** (-2.0 * np.arange(width // 2) / width)
    angles = places[:, None] * freq
    cosine, sine = np.cos(angles), np.sin(angles)
    return np.stack(
        [np.concatenate([cosine, cosine], axis=1), np.concatenate([-sine, sine], axis=1)]
    ).astype(np.float32)


def fused_kernel(
    count,
    factor,
    keys_hbm,
    values_hbm,
    queries_hbm,
    places_hbm,
    high_hbm,
    low_hbm,
    near_hbm,
    down_hbm,
    up_hbm,
    local_hbm,
    merge_hbm,
    cross_hbm,
    coarse_hbm,
    fine_hbm,
    out_ref,
    keys_ref,
    values_ref,
    queries_ref,
    places_ref,
    high_ref,
    low_ref,
    near_ref,
    down_ref,
    up_ref,
    local_ref,
    merge_ref,
    cross_ref,
    coarse_ref,
    fine_ref,
    parts_ref,
    whole_ref,
    others_ref,
    close_ref,
    field_ref,
    k_ref,
    v_ref,
    even_ref,
    odd_ref,
    even_top_ref,
    odd_top_ref,
    asks_ref,
    own_ref,
    own_log_ref,
    half_ref,
    half_log_ref,
    merged_ref,
    merged_log_ref,
    over_ref,
    over_log_ref,
    ready_ref,
    ready_log_ref,
    last_ref,
    last_log_ref,
    load_sem,
    token_sem,
    field_send,
    field_recv,
    ask_send,
    ask_recv,
    half_send,
    half_recv,
    over_send,
    over_recv,
    last_send,
    last_recv,
):
    me = lax.axis_index("ctx")
    heads, rows, width = queries_ref.shape
    order = ORDER
    blocks = rows // BLOCK
    n_part = near_ref.shape[1]
    t_part = n_part // 2
    half_columns = keys_ref.shape[1]
    tokens = k_ref.shape[1]
    has_left, has_right = me > 0, me < count - 1
    inside = jnp.logical_and(has_left, has_right)
    lower = me < count // 2
    mate = me + 1 - 2 * lax.rem(me, 2)
    far_end = jnp.where(lower, count - 1, 0)
    near_over = jnp.where(lower, count // 2, count // 2 - 1)
    outward = jnp.where(lower, 0, 1)

    def copy(src, dst, send, recv, other):
        return pltpu.make_async_remote_copy(
            src_ref=src,
            dst_ref=dst,
            send_sem=send,
            recv_sem=recv,
            device_id={"ctx": other},
            device_id_type=MESH,
        )

    others_ref[...] = jnp.zeros_like(others_ref)
    barrier = pltpu.get_barrier_semaphore()
    for step in range(1, count):
        pl.semaphore_signal(
            barrier, inc=1, device_id={"ctx": lax.rem(me + step, count)}, device_id_type=MESH
        )
    pairs = (
        (places_hbm, places_ref),
        (queries_hbm, queries_ref),
        (high_hbm, high_ref),
        (low_hbm, low_ref),
        (down_hbm, down_ref),
        (merge_hbm, merge_ref),
        (near_hbm, near_ref),
        (local_hbm, local_ref),
        (cross_hbm.at[me], cross_ref),
        (up_hbm, up_ref),
        (coarse_hbm, coarse_ref),
        (fine_hbm, fine_ref),
    )
    loads = [pltpu.make_async_copy(src, dst, load_sem.at[i]) for i, (src, dst) in enumerate(pairs)]
    sides = ((keys_hbm, keys_ref), (values_hbm, values_ref))
    token_loads = [
        [
            pltpu.make_async_copy(
                src.at[pl.ds(p * n_part, n_part)], dst.at[pl.ds(p * n_part, n_part)], token_sem.at[p, side]
            )
            for side, (src, dst) in enumerate(sides)
        ]
        for p in range(PARTS)
    ]
    for each in loads[:6]:
        each.start()
    for p in range(PARTS):
        for each in token_loads[p]:
            each.start()
    for each in loads[6:]:
        each.start()
    for each in loads[:4]:
        each.wait()

    split = low_ref.shape[0] // 2
    for i in range(rows // split):
        here = slice(i * split, (i + 1) * split)
        place = jnp.broadcast_to(places_ref[:, here].astype(jnp.float32), (split, split)).T.astype(jnp.int32)
        spun = []
        for value, table_ref in ((place // split, high_ref), (lax.rem(place, split), low_ref)):
            size = table_ref.shape[0] // 2
            value = value if size == split else value[:, :1]
            picked = value == lax.broadcasted_iota(jnp.int32, (split, size), 1)
            picked = jnp.where(picked, 1.0, 0.0).astype(jnp.bfloat16)
            got = jnp.dot(
                jnp.concatenate([picked, picked], axis=1), table_ref[...], preferred_element_type=jnp.float32
            )
            spun.append((got[:, :width], got[:, width:]))
        (cos_a, sin_a), (cos_b, sin_b) = spun
        cosine, sine = cos_a * cos_b - sin_a * sin_b, sin_a * cos_b + cos_a * sin_b
        for head in range(heads):
            x = queries_ref[head, here, :].astype(jnp.float32)
            asks_ref[me, head, here, :] = (x * cosine + pltpu.roll(x, width // 2, 1) * sine).astype(jnp.bfloat16)

    def ask_copy(source, head, side):
        return copy(
            asks_ref.at[source, head],
            asks_ref.at[source, head],
            ask_send.at[source, head, side],
            ask_recv.at[source, head],
            me + 2 * side - 1,
        )

    def for_sides(action):
        for side, there in enumerate((has_left, has_right)):

            @pl.when(there)
            def _():
                action(side)

    pl.semaphore_wait(barrier, count - 1)
    for_sides(lambda side: ask_copy(me, 0, side).start())

    for each in loads[4:6]:
        each.wait()
    for p in range(PARTS):
        for side, (_, x_ref) in enumerate(sides):
            token_loads[p][side].wait()
            z = jnp.dot(
                down_ref[...], x_ref[p * n_part : (p + 1) * n_part, :], preferred_element_type=jnp.float32
            )
            parts_ref[
                p * order : (p + 1) * order, side * half_columns : (side + 1) * half_columns
            ] = z[:order] + z[order:]
    whole_ref[...] = strict_dot(merge_ref[...], parts_ref[...])
    others_ref[:order] = whole_ref[:order]

    def near_copy(side):
        start = order * (2 - side)
        other = me + 2 * side - 1
        return copy(
            whole_ref.at[pl.ds(0, order)],
            others_ref.at[pl.ds(start, order)],
            field_send.at[other],
            field_recv.at[me],
            other,
        )

    def far_copy(other):
        return copy(
            whole_ref.at[pl.ds(order, FAR)],
            others_ref.at[pl.ds(pl.multiple_of(3 * order + me * FAR, FAR), FAR)],
            field_send.at[other],
            field_recv.at[me],
            other,
        )

    def near_wait(side):
        source = me + 2 * side - 1
        copy(
            whole_ref.at[pl.ds(0, order)],
            others_ref.at[pl.ds(order * (1 + side), order)],
            field_send.at[source],
            field_recv.at[source],
            source,
        ).wait_recv()

    def far_wait(source):
        copy(
            whole_ref.at[pl.ds(order, FAR)],
            others_ref.at[pl.ds(3 * order + source * FAR, FAR)],
            field_send.at[source],
            field_recv.at[source],
            source,
        ).wait_recv()

    def for_far(action):
        for other in range(count):

            @pl.when(jnp.logical_or(other - me > 1, me - other > 1))
            def _():
                action(other)

    for_sides(lambda side: near_copy(side).start())
    for_far(lambda other: far_copy(other).start())
    for_sides(lambda side: ask_copy(me, 1, side).start())

    loads[6].wait()

    def close(p, carry):
        start = pl.multiple_of(p * n_part, n_part)
        for side, (_, x_ref) in enumerate(sides):
            z = jnp.dot(near_ref[...], x_ref[pl.ds(start, n_part), :], preferred_element_type=jnp.float32)
            close_ref[p, :, side * half_columns : (side + 1) * half_columns] = z[:t_part] + z[t_part:]
        return carry

    lax.fori_loop(0, PARTS, close, 0)
    for each in loads[7:]:
        each.wait()
    field_ref[...] = strict_dot(local_ref[...], parts_ref[...])

    def hand_on(head):
        for_sides(lambda side: ask_copy(me + 2 * side - 1, head, 1 - side).wait_recv())

        @pl.when(inside)
        def _():
            ask_copy(me - 1, head, 1).start()
            ask_copy(me + 1, head, 0).start()

    def hand_far(head):
        handed = ask_copy(far_end, head, outward)
        handed.wait_recv()
        handed.start()

    hand_on(0)
    for_sides(near_wait)
    for_far(far_wait)
    field_ref[...] += strict_dot(cross_ref[...], others_ref[...])

    def finish(p, carry):
        f = field_ref[pl.ds(pl.multiple_of(p * order, order), order), :]
        high = f.astype(jnp.bfloat16)
        low = (f - high.astype(jnp.float32)).astype(jnp.bfloat16)
        y = close_ref[p] + jnp.dot(
            up_ref[...], jnp.concatenate([high, low, high], axis=0), preferred_element_type=jnp.float32
        )
        y = y.astype(jnp.bfloat16).astype(jnp.float32)
        begin = pl.multiple_of(p * t_part, t_part)
        place = me * PARTS + p
        cos_p, sin_p = coarse_ref[0, pl.ds(place, 1), :], coarse_ref[1, pl.ds(place, 1), :]
        cosine = cos_p * fine_ref[0] - sin_p * fine_ref[1]
        sine = sin_p * fine_ref[0] + cos_p * fine_ref[1]
        for head in range(heads):
            k = y[:, head * width : (head + 1) * width]
            turned = k * cosine + pltpu.roll(k, width // 2, 1) * sine
            k_ref[head, pl.ds(begin, t_part), :] = turned.astype(jnp.bfloat16)
            v = y[:, half_columns + head * width : half_columns + (head + 1) * width]
            v_ref[head, :, pl.ds(begin, t_part)] = v.T.astype(jnp.bfloat16)
        return carry

    lax.fori_loop(0, PARTS, finish, 0)

    def decode(u):
        group = u // blocks
        own = jnp.logical_or(group == 4, group == 7)
        kind = jnp.where(own, 3, jnp.where(group < 2, 0, jnp.where(group < 4, 1, 2)))
        head = jnp.where(group < 4, lax.rem(group, 2), jnp.where(own, (group - 4) // 3, group - 5))
        source = jnp.where(
            kind == 0, mate, jnp.where(kind == 1, near_over, jnp.where(kind == 2, far_end, me))
        )
        return kind, head, lax.rem(u, blocks), source

    chunk = 512

    def score(u, keep_ref, top_ref):
        _, head, block, source = decode(u)
        q = asks_ref[source, head, pl.ds(pl.multiple_of(block * BLOCK, BLOCK), BLOCK), :]
        best = None
        for c in range(0, tokens, chunk):
            s = lax.dot_general(
                k_ref[head, c : c + chunk, :],
                q,
                (((1,), (1,)), ((), ())),
                preferred_element_type=jnp.float32,
            )
            keep_ref[c : c + chunk, :] = s
            top = jnp.max(s, axis=0, keepdims=True)
            best = top if best is None else jnp.maximum(best, top)
        top_ref[...] = best

    def weigh(u, keep_ref, top_ref):
        kind, head, block, _ = decode(u)
        best = top_ref[...]
        total = jnp.zeros((1, BLOCK), jnp.float32)
        accum = jnp.zeros((width, BLOCK), jnp.float32)
        for c in range(0, tokens, chunk):
            e = jnp.exp2((keep_ref[c : c + chunk, :] - best) * factor)
            total += jnp.sum(e, axis=0, keepdims=True)
            accum += jnp.dot(
                v_ref[head, :, c : c + chunk], e.astype(jnp.bfloat16), preferred_element_type=jnp.float32
            )
        own_ref[kind, head, block] = (accum / total).astype(jnp.bfloat16)
        own_log_ref[kind, head, block] = best * factor + jnp.log2(total)

    def both(src, src_log, dst, dst_log, send, recv, other):
        return (
            copy(src, dst, send.at[0], recv.at[0], other),
            copy(src_log, dst_log, send.at[1], recv.at[1], other),
        )

    def half_copy(kind, head, block):
        at = (kind, head, block)
        return both(
            own_ref.at[at],
            own_log_ref.at[at],
            half_ref.at[at],
            half_log_ref.at[at],
            half_send.at[at],
            half_recv.at[at],
            mate,
        )

    def over_copy(j, head, block):
        at = (j, head, block)
        return both(
            merged_ref.at[at],
            merged_log_ref.at[at],
            over_ref.at[at],
            over_log_ref.at[at],
            over_send.at[at],
            over_recv.at[at],
            near_over,
        )

    def last_copy(head, block):
        at = (head, block)
        return both(
            ready_ref.at[at],
            ready_log_ref.at[at],
            last_ref.at[at],
            last_log_ref.at[at],
            last_send.at[at],
            last_recv.at[at],
            mate,
        )

    def blend(parts, logs):
        best = functools.reduce(jnp.maximum, logs)
        shares = [jnp.exp2(log - best) for log in logs]
        total = functools.reduce(jnp.add, shares)
        mixed = functools.reduce(
            jnp.add, [part.astype(jnp.float32) * (share / total) for part, share in zip(parts, shares)]
        )
        return mixed, best + jnp.log2(total)

    def merge_half(kind, head, block):
        for each in half_copy(kind, head, block):
            each.wait_recv()
        at = (kind - 1, head, block)
        mixed, log = blend(
            [own_ref[kind, head, block], half_ref[kind, head, block]],
            [own_log_ref[kind, head, block], half_log_ref[kind, head, block]],
        )
        merged_ref[at] = mixed.astype(jnp.bfloat16)
        merged_log_ref[at] = log
        for each in over_copy(*at):
            each.start()

    group_size = heads * blocks
    lag = 5

    def await_ask(u):
        kind, head, block, source = decode(u)
        fresh = jnp.logical_and(block == 0, jnp.logical_or(kind == 1, kind == 2))

        @pl.when(jnp.logical_and(fresh, jnp.logical_not(inside)))
        def _():
            ask_copy(source, head, 1 - outward).wait_recv()

    def send_on(u):
        kind, head, block, _ = decode(u)

        @pl.when(jnp.logical_and(kind < 3, jnp.logical_not(inside)))
        def _():
            for each in half_copy(kind, head, block):
                each.start()

        for kind, first in ((1, group_size), (2, group_size + group_size + blocks)):
            k = u - first - lag

            @pl.when(jnp.logical_and(inside, jnp.logical_and(k >= 0, k < group_size)))
            def _():
                merge_half(kind, k // blocks, lax.rem(k, blocks))

    score(0, even_ref, even_top_ref)
    units = 4 * group_size

    def serve(i, carry):
        u = 2 * i

        @pl.when(i == 0)
        def _():
            hand_on(1)

        @pl.when(jnp.logical_and(inside, i == group_size // 2))
        def _():
            hand_far(0)

        @pl.when(jnp.logical_and(inside, i == group_size - 1))
        def _():
            hand_far(1)

        await_ask(u + 1)
        score(u + 1, odd_ref, odd_top_ref)
        weigh(u, even_ref, even_top_ref)
        send_on(u)
        ahead = jnp.minimum(u + 2, units - 1)
        await_ask(ahead)
        score(ahead, even_ref, even_top_ref)
        weigh(u + 1, odd_ref, odd_top_ref)
        send_on(u + 1)
        return carry

    lax.fori_loop(0, units // 2, serve, 0)

    @pl.when(inside)
    def _():
        for k in range(units - (2 * group_size + blocks + lag), group_size):
            merge_half(2, k // blocks, k % blocks)
        for head in range(heads):
            for block in range(blocks):
                for each in over_copy(1, head, block):
                    each.wait_recv()
                mixed, log = blend(
                    [own_ref[0, head, block], over_ref[1, head, block]],
                    [own_log_ref[0, head, block], over_log_ref[1, head, block]],
                )
                ready_ref[head, block] = mixed.astype(jnp.bfloat16)
                ready_log_ref[head, block] = log
                for each in last_copy(head, block):
                    each.start()
        for head in range(heads):
            for block in range(blocks):
                for each in half_copy(0, head, block) + over_copy(0, head, block):
                    each.wait_recv()
                mixed, _ = blend(
                    [own_ref[3, head, block], half_ref[0, head, block], over_ref[0, head, block]],
                    [own_log_ref[3, head, block], half_log_ref[0, head, block], over_log_ref[0, head, block]],
                )
                out_ref[head, block * BLOCK : (block + 1) * BLOCK, :] = mixed.T.astype(out_ref.dtype)
        for head in range(heads):
            ask_copy(me - 1, head, 1).wait_send()
            ask_copy(me + 1, head, 0).wait_send()
            ask_copy(far_end, head, outward).wait_send()
            for block in range(blocks):
                for each in over_copy(0, head, block) + over_copy(1, head, block) + last_copy(head, block):
                    each.wait_send()

    @pl.when(jnp.logical_not(inside))
    def _():
        for head in range(heads):
            for block in range(blocks):
                for each in last_copy(head, block):
                    each.wait_recv()
                mixed, _ = blend(
                    [own_ref[3, head, block], last_ref[head, block]],
                    [own_log_ref[3, head, block], last_log_ref[head, block]],
                )
                out_ref[head, block * BLOCK : (block + 1) * BLOCK, :] = mixed.T.astype(out_ref.dtype)
        for kind in range(3):
            for head in range(heads):
                for block in range(blocks):
                    for each in half_copy(kind, head, block):
                        each.wait_send()

    for head in range(heads):
        for_sides(lambda side: ask_copy(me, head, side).wait_send())
    for_sides(lambda side: near_copy(side).wait_send())
    for_far(lambda other: far_copy(other).wait_send())


def by_tokens(keys, values, queries, positions, count):
    heads, rows, width = queries.shape
    n_dev, columns = keys.shape
    length = n_dev * count
    near, down, up, local, merge, cross = fields(length, count)

    def tall(matrix):
        return np.concatenate(split_two(matrix), axis=-2)

    def table(places):
        return tall(np.concatenate(spins(places, width).astype(np.float64), axis=1))

    up_high, up_low = split_two(up)
    t_part = near.shape[0]
    tokens = n_dev // 2
    blocks = rows // BLOCK
    split = 128
    operands = (
        table(np.arange(length // split) * float(split)),
        table(np.arange(split) * 1.0),
        tall(near),
        tall(down),
        np.concatenate([up_high, up_high, up_low], axis=1),
        tall(local),
        tall(merge),
        tall(cross),
        spins(np.arange(count * PARTS) * float(t_part), width),
        spins(np.arange(t_part) * 1.0, width),
    )
    held = [jax.ShapeDtypeStruct(o.shape[1:] if o.ndim == 3 and o.shape[0] == count else o.shape, o.dtype) for o in operands]
    dma = pltpu.SemaphoreType.DMA

    def parts(*lead):
        return [
            pltpu.VMEM(lead + (heads, blocks, width, BLOCK), jnp.bfloat16),
            pltpu.VMEM(lead + (heads, blocks, 1, BLOCK), jnp.float32),
        ]

    return pl.pallas_call(
        functools.partial(fused_kernel, count, math.log2(math.e) / math.sqrt(width)),
        in_specs=[pl.BlockSpec(memory_space=pl.ANY)] * 14,
        out_specs=pl.BlockSpec(memory_space=pltpu.VMEM),
        out_shape=jax.ShapeDtypeStruct(queries.shape, jnp.bfloat16),
        scratch_shapes=[
            pltpu.VMEM(keys.shape, keys.dtype),
            pltpu.VMEM(values.shape, values.dtype),
            pltpu.VMEM(queries.shape, queries.dtype),
            pltpu.VMEM((1, rows), jnp.int32),
        ]
        + [pltpu.VMEM(h.shape, h.dtype) for h in held]
        + [
            pltpu.VMEM((PARTS * ORDER, 2 * columns), jnp.float32),
            pltpu.VMEM((ORDER + FAR, 2 * columns), jnp.float32),
            pltpu.VMEM((cross.shape[2], 2 * columns), jnp.float32),
            pltpu.VMEM((PARTS, t_part, 2 * columns), jnp.float32),
            pltpu.VMEM((PARTS * ORDER, 2 * columns), jnp.float32),
            pltpu.VMEM((heads, tokens, width), jnp.bfloat16),
            pltpu.VMEM((heads, width, tokens), jnp.bfloat16),
            pltpu.VMEM((tokens, BLOCK), jnp.float32),
            pltpu.VMEM((tokens, BLOCK), jnp.float32),
            pltpu.VMEM((1, BLOCK), jnp.float32),
            pltpu.VMEM((1, BLOCK), jnp.float32),
            pltpu.VMEM((count, heads, rows, width), jnp.bfloat16),
        ]
        + parts(4)
        + parts(3)
        + parts(2)
        + parts(2)
        + parts()
        + parts()
        + [
            dma((12,)),
            dma((PARTS, 2)),
            dma((count,)),
            dma((count,)),
            dma((count, heads, 2)),
            dma((count, heads)),
            dma((3, heads, blocks, 2)),
            dma((3, heads, blocks, 2)),
            dma((2, heads, blocks, 2)),
            dma((2, heads, blocks, 2)),
            dma((heads, blocks, 2)),
            dma((heads, blocks, 2)),
        ],
        compiler_params=pltpu.CompilerParams(
            collective_id=0, has_side_effects=True, vmem_limit_bytes=60 * 1024 * 1024
        ),
    )(keys, values, queries, positions.reshape(1, rows), *operands)


def by_columns(keys, values, queries, positions):
    key_parts = lax.all_to_all(keys, "ctx", split_axis=1, concat_axis=0, tiled=True)
    value_parts = lax.all_to_all(values, "ctx", split_axis=1, concat_axis=0, tiled=True)
    heads, rows, width = queries.shape
    per_device = key_parts.shape[1]
    compact = compress(jnp.concatenate([key_parts, value_parts], axis=1))
    rotated = rotate_rows(queries.astype(jnp.float32), positions.astype(jnp.float32)).astype(
        jnp.bfloat16
    )
    whole = lax.all_gather(compact.T, "ctx", axis=0, tiled=True)
    tokens = whole.shape[1]
    shaped = whole.reshape(-1, 2, per_device, tokens)
    key_rows = shaped[:, 0].reshape(heads, width, tokens).swapaxes(1, 2)
    value_rows = shaped[:, 1].reshape(heads, width, tokens).swapaxes(1, 2)
    places = jnp.arange(tokens).astype(jnp.float32)
    ready = rotate_rows(key_rows.astype(jnp.float32), places).astype(jnp.bfloat16)
    return attend(rotated, ready, value_rows, jnp.zeros((), jnp.int32))[0]


def solution(mesh):
    count = mesh.shape["ctx"]

    def on_device(keys, values, queries, positions):
        heads, rows, width = queries.shape
        if count == 4 and heads == 2 and keys.shape[0] % (PARTS * 512) == 0 and rows % BLOCK == 0 and width == 128:
            return by_tokens(keys, values, queries, positions, count)
        return by_columns(keys, values, queries, positions)

    return jax.shard_map(
        on_device,
        mesh=mesh,
        in_specs=(
            P(("user", "ctx"), "heads"),
            P(("user", "ctx"), "heads"),
            P("heads", ("user", "ctx"), None),
            P(("user", "ctx")),
        ),
        out_specs=P("heads", ("user", "ctx"), None),
        check_vma=False,
    )
```

```python
import functools
import math

import jax
import jax.numpy as jnp
import numpy as np
from jax import lax
from jax.experimental import pallas as pl
from jax.experimental.pallas import tpu as pltpu
from jax.sharding import PartitionSpec as P

OUTER = 128
PARTS = 4
ORDER = 64
FAR = 16
BLOCK = 256
MESH = pl.DeviceIdType.MESH


def split_two(matrix):
    high = matrix.astype(jnp.bfloat16)
    low = (matrix - np.asarray(high).astype(np.float64)).astype(jnp.bfloat16)
    return high, low


@functools.lru_cache(maxsize=None)
def stages(length):
    outer = OUTER
    inner = length // outer
    step = inner // 2
    a = np.arange(outer)
    c = np.arange(outer)
    turn = 2 * outer
    angle = np.pi / outer * ((c[:, None] * a[None, :]) % turn)
    alternate = np.where(a % 2 == 0, 1.0, -1.0)
    first = np.stack([np.cos(angle), -np.sin(angle)], axis=1)
    first[0, 1] = alternate
    d = np.arange(length // 2 // turn)
    k = np.concatenate([c[:, None] + turn * d, (turn - c[:, None]) % turn + turn * d], axis=1)
    k[0, d.size :] = outer + turn * d
    sign = np.concatenate([np.ones(d.size), -np.ones(d.size)])
    b = np.arange(inner)
    q = np.arange(step)
    theta = np.pi / (2 * length) * ((k[:, :, None] * (2 * b + 1)) % (4 * length))
    phi = np.pi / length * ((k[:, None, :] * (2 * q + 1)[:, None]) % (2 * length))
    forward = np.stack([np.cos(theta), np.sin(theta) * sign[None, :, None]], axis=2)
    weight = np.where(k == 0, 1.0, 2.0) / length
    back = np.stack([np.cos(phi), np.sin(phi) * sign], axis=1) * weight[:, None, None, :]
    half = d.size
    forward[0, :half, 1] = 0.0
    forward[0, half:, 1] = np.cos(theta[0, half:])
    forward[0, half:, 0] = 0.0
    back[0, 1, :, :half] = 0.0
    back[0, 1, :, half:] = np.cos(phi[0, :, half:]) * weight[0, half:]
    back[0, 0, :, half:] = 0.0
    middle = back.reshape(outer, 2 * step, 2 * half) @ forward.reshape(outer, 2 * half, 2 * inner)
    last = first.transpose(2, 0, 1).reshape(outer, 2 * outer)
    return first.reshape(2 * outer, outer), middle, last


def compress(signal):
    length, columns = signal.shape
    outer, inner = OUTER, length // OUTER
    first, middle, last = stages(length)
    first_high, first_low = split_two(first)
    flat = signal.reshape(outer, inner * columns)
    one = jnp.dot(first_high, flat, preferred_element_type=jnp.float32) + jnp.dot(
        first_low, flat, preferred_element_type=jnp.float32
    )
    one = one.reshape(outer, 2 * inner, columns)
    two = jnp.einsum(
        "cob,cbl->col", jnp.asarray(middle.astype(np.float32)), one, precision=lax.Precision.HIGH
    )
    three = jnp.dot(
        jnp.asarray(last.astype(np.float32)),
        two.reshape(2 * outer, inner // 2 * columns),
        precision=lax.Precision.HIGH,
    )
    return three.reshape(length // 2, columns).astype(jnp.bfloat16)

def strict_dot(left, right):
    rows, columns = left.shape[0] // 2, right.shape[1]
    high = right.astype(jnp.bfloat16)
    low = (right - high.astype(jnp.float32)).astype(jnp.bfloat16)
    both = jnp.dot(
        left, jnp.concatenate([high, low], axis=1), preferred_element_type=jnp.float32
    )
    return both[:rows, :columns] + (both[:rows, columns:] + both[rows:, :columns])


def inverse_freq(width):
    return jnp.exp(jnp.arange(width // 2).astype(jnp.float32) * (-2.0 * math.log(500000.0) / width))


def rotate_rows(block, places):
    width = block.shape[-1]
    half = width // 2
    angles = places[:, None] * inverse_freq(width)[None, :]
    cosine = jnp.cos(angles)
    sine = jnp.sin(angles)
    first = block[..., :half]
    second = block[..., half:]
    return jnp.concatenate(
        [first * cosine - second * sine, second * cosine + first * sine], axis=-1
    )


def attend_kernel(chunk, scale, resume, finish, swap_ref, q_ref, k_ref, v_ref, *refs):
    q = q_ref[0]
    swap = swap_ref[0] == 1
    rows, width = q.shape
    factor = scale * math.log2(math.e)
    if resume:
        accum = refs[0][0]
        best = refs[1][0][:, :1]
        total = refs[2][0][:, :1]
        refs = refs[3:]
    else:
        best = jnp.full((rows, 1), -jnp.inf, jnp.float32)
        total = jnp.zeros((rows, 1), jnp.float32)
        accum = jnp.zeros((rows, width), jnp.float32)
    tokens = k_ref.shape[1]
    for start in range(0, tokens, chunk):
        one = k_ref[0, start : start + chunk, :]
        two = v_ref[0, start : start + chunk, :]
        k, v = jnp.where(swap, two, one), jnp.where(swap, one, two)
        scores = lax.dot_general(
            q, k, (((1,), (1,)), ((), ())), preferred_element_type=jnp.float32
        )
        fresh = jnp.maximum(best, jnp.max(scores, axis=1, keepdims=True))
        expo = jnp.exp2((scores - fresh) * factor)
        shrink = jnp.exp2((best - fresh) * factor)
        total = total * shrink + jnp.sum(expo, axis=1, keepdims=True)
        accum = accum * shrink + jnp.dot(
            expo.astype(jnp.bfloat16), v, preferred_element_type=jnp.float32
        )
        best = fresh
    if finish:
        refs[0][0] = (accum / total).astype(refs[0].dtype)
        refs[1][0] = jnp.broadcast_to(best * factor + jnp.log2(total), (rows, 8))
    else:
        refs[0][0] = accum
        refs[1][0] = jnp.broadcast_to(best, (rows, 8))
        refs[2][0] = jnp.broadcast_to(total, (rows, 8))


def attend(queries, keys, values, swap, part=0, parts=1, state=None):
    groups, rows, width = queries.shape
    heads, tokens, _ = values.shape
    per_head = groups // heads
    block = math.gcd(rows, 768)
    chunk = math.gcd(tokens, 1024)
    scale = 1.0 / math.sqrt(width)
    finish = part == parts - 1
    wide = pl.BlockSpec((1, block, width), lambda g, i: (g, i, 0))
    thin = pl.BlockSpec((1, block, 8), lambda g, i: (g, i, 0))
    thin_shape = jax.ShapeDtypeStruct((groups, rows, 8), jnp.float32)
    state = () if state is None else tuple(state)
    wide_type = jnp.bfloat16 if finish else jnp.float32
    return pl.pallas_call(
        functools.partial(attend_kernel, chunk, scale, bool(state), finish),
        grid=(groups, rows // block),
        in_specs=[
            pl.BlockSpec(memory_space=pltpu.SMEM),
            wide,
            pl.BlockSpec((1, tokens, width), lambda g, i: (g // per_head, part, 0)),
            pl.BlockSpec((1, tokens, width), lambda g, i: (g // per_head, 0, 0)),
        ]
        + ([wide, thin, thin] if state else []),
        out_specs=[wide, thin] if finish else [wide, thin, thin],
        out_shape=[jax.ShapeDtypeStruct((groups, rows, width), wide_type), thin_shape]
        + ([] if finish else [thin_shape]),
        cost_estimate=pl.CostEstimate(
            flops=8 * groups * rows * tokens * width,
            bytes_accessed=4 * groups * rows * width * 2,
            transcendentals=groups * rows * tokens,
        ),
    )(swap.reshape(1), queries, keys, values, *state)


def nodes(count, order, pad):
    half = np.log((count - 1 + pad) / pad)
    e = np.exp(half * np.cos(np.pi * (2 * np.arange(order) + 1) / (2 * order)))
    return ((count - 1 + pad) * e - pad) / (1 + e)


def cardinals(places, count, order, pad):
    half = np.log((count - 1 + pad) / pad)
    at = np.arccos(np.clip(np.log((places + pad) / (count - 1 + pad - places)) / half, -1.0, 1.0))
    own = np.pi * (2 * np.arange(order) + 1) / (2 * order)
    total = np.zeros((places.size, order))
    for k in range(order):
        total += (1.0 if k == 0 else 2.0) / order * np.cos(k * at)[:, None] * np.cos(k * own)[None, :]
    return total


@functools.lru_cache(maxsize=None)
def fields(length, devices):
    parts, order = PARTS, ORDER
    scale = math.sqrt(0.5) / (2 * length)

    def cot(m):
        return 1.0 / np.tan(np.pi * m / (4 * length))

    n_dev = length // devices
    n_part, t_dev = n_dev // parts, n_dev // 2
    t_part = n_part // 2
    n, t = np.arange(n_part), np.arange(t_part)
    sign_n = np.array([1.0, -1.0, -1.0, 1.0])[n % 4]
    sign_t = np.where(t % 2 == 0, 1.0, -1.0)
    near = sign_t[:, None] * sign_n * scale * cot(4 * t[:, None] - 2 * n + 1.0)
    down = cardinals(n, n_part, order, 1.5).T * sign_n
    up = sign_t[:, None] * cardinals(t, t_part, order, 0.75)
    part = np.arange(parts)[:, None]
    source = (part * n_part + nodes(n_part, order, 1.5)).reshape(-1)
    target = (part * t_part + nodes(t_part, order, 0.75)).reshape(-1)
    bend = np.pi * (2 * np.arange(FAR) + 1) / (2 * FAR)
    spot = np.arccos(np.clip(2.0 * source / (n_dev - 1) - 1.0, -1.0, 1.0))
    plain = sum(
        (1.0 if k == 0 else 2.0) / FAR * np.cos(k * bend)[:, None] * np.cos(k * spot)[None, :]
        for k in range(FAR)
    )
    merge = np.concatenate([cardinals(source, n_dev, order, 1.5).T, plain])
    own = np.arange(parts * order) // order
    same = own[:, None] == own[None, :]
    local = np.where(same, 0.0, scale * cot(np.where(same, 1.0, 4 * target[:, None] - 2 * source + 1)))
    whole = nodes(n_dev, order, 1.5)
    sparse = (np.cos(bend) + 1.0) * (n_dev - 1) / 2
    cross = np.zeros((devices, parts * order, 3 * order + devices * FAR))
    for r in range(devices):
        a = 4 * (target + r * t_dev)[:, None]
        for s in range(devices):
            b = 2 * ((sparse if abs(r - s) > 1 else whole) + s * n_dev)
            block = scale * cot(a + b + 3)
            if r != s:
                block = block + scale * cot(a - b + 1)
            if abs(r - s) > 1:
                start = 3 * order + s * FAR
            else:
                start = {0: 0, 1: order, -1: 2 * order}[r - s]
            cross[r, :, start : start + block.shape[1]] = block
    return near, down, up, local, merge, cross


def spins(places, width):
    freq = 500000.0 ** (-2.0 * np.arange(width // 2) / width)
    angles = places[:, None] * freq
    cosine, sine = np.cos(angles), np.sin(angles)
    return np.stack(
        [np.concatenate([cosine, cosine], axis=1), np.concatenate([-sine, sine], axis=1)]
    ).astype(np.float32)


def fused_kernel(
    count,
    factor,
    keys_hbm,
    values_hbm,
    queries_hbm,
    places_hbm,
    high_hbm,
    low_hbm,
    near_hbm,
    down_hbm,
    up_hbm,
    local_hbm,
    merge_hbm,
    cross_hbm,
    coarse_hbm,
    fine_hbm,
    out_ref,
    keys_ref,
    values_ref,
    queries_ref,
    places_ref,
    high_ref,
    low_ref,
    near_ref,
    down_ref,
    up_ref,
    local_ref,
    merge_ref,
    cross_ref,
    coarse_ref,
    fine_ref,
    parts_ref,
    whole_ref,
    others_ref,
    close_ref,
    field_ref,
    k_ref,
    v_ref,
    even_ref,
    odd_ref,
    even_top_ref,
    odd_top_ref,
    asks_ref,
    own_ref,
    own_log_ref,
    half_ref,
    half_log_ref,
    merged_ref,
    merged_log_ref,
    over_ref,
    over_log_ref,
    ready_ref,
    ready_log_ref,
    last_ref,
    last_log_ref,
    load_sem,
    token_sem,
    field_send,
    field_recv,
    ask_send,
    ask_recv,
    half_send,
    half_recv,
    over_send,
    over_recv,
    last_send,
    last_recv,
):
    me = lax.axis_index("ctx")
    heads, rows, width = queries_ref.shape
    order = ORDER
    blocks = rows // BLOCK
    n_part = near_ref.shape[1]
    t_part = n_part // 2
    half_columns = keys_ref.shape[1]
    tokens = k_ref.shape[1]
    has_left, has_right = me > 0, me < count - 1
    inside = jnp.logical_and(has_left, has_right)
    lower = me < count // 2
    mate = me + 1 - 2 * lax.rem(me, 2)
    far_end = jnp.where(lower, count - 1, 0)
    near_over = jnp.where(lower, count // 2, count // 2 - 1)
    outward = jnp.where(lower, 0, 1)

    def copy(src, dst, send, recv, other):
        return pltpu.make_async_remote_copy(
            src_ref=src,
            dst_ref=dst,
            send_sem=send,
            recv_sem=recv,
            device_id={"ctx": other},
            device_id_type=MESH,
        )

    others_ref[...] = jnp.zeros_like(others_ref)
    barrier = pltpu.get_barrier_semaphore()
    for step in range(1, count):
        pl.semaphore_signal(
            barrier, inc=1, device_id={"ctx": lax.rem(me + step, count)}, device_id_type=MESH
        )
    pairs = (
        (places_hbm, places_ref),
        (queries_hbm, queries_ref),
        (high_hbm, high_ref),
        (low_hbm, low_ref),
        (down_hbm, down_ref),
        (merge_hbm, merge_ref),
        (near_hbm, near_ref),
        (local_hbm, local_ref),
        (cross_hbm.at[me], cross_ref),
        (up_hbm, up_ref),
        (coarse_hbm, coarse_ref),
        (fine_hbm, fine_ref),
    )
    loads = [pltpu.make_async_copy(src, dst, load_sem.at[i]) for i, (src, dst) in enumerate(pairs)]
    sides = ((keys_hbm, keys_ref), (values_hbm, values_ref))
    token_loads = [
        [
            pltpu.make_async_copy(
                src.at[pl.ds(p * n_part, n_part)], dst.at[pl.ds(p * n_part, n_part)], token_sem.at[p, side]
            )
            for side, (src, dst) in enumerate(sides)
        ]
        for p in range(PARTS)
    ]
    for each in loads[:6]:
        each.start()
    for p in range(PARTS):
        for each in token_loads[p]:
            each.start()
    for each in loads[6:]:
        each.start()
    for each in loads[:4]:
        each.wait()

    split = low_ref.shape[0] // 2
    for i in range(rows // split):
        here = slice(i * split, (i + 1) * split)
        place = jnp.broadcast_to(places_ref[here].astype(jnp.float32)[None], (split, split)).T.astype(jnp.int32)
        spun = []
        for value, table_ref in ((place // split, high_ref), (lax.rem(place, split), low_ref)):
            size = table_ref.shape[0] // 2
            value = value if size == split else value[:, :1]
            picked = value == lax.broadcasted_iota(jnp.int32, (split, size), 1)
            picked = jnp.where(picked, 1.0, 0.0).astype(jnp.bfloat16)
            got = jnp.dot(
                jnp.concatenate([picked, picked], axis=1), table_ref[...], preferred_element_type=jnp.float32
            )
            spun.append((got[:, :width], got[:, width:]))
        (cos_a, sin_a), (cos_b, sin_b) = spun
        cosine, sine = cos_a * cos_b - sin_a * sin_b, sin_a * cos_b + cos_a * sin_b
        for head in range(heads):
            x = queries_ref[head, here, :].astype(jnp.float32)
            asks_ref[me, head, here, :] = (x * cosine + pltpu.roll(x, width // 2, 1) * sine).astype(jnp.bfloat16)

    def ask_copy(source, head, side):
        return copy(
            asks_ref.at[source, head],
            asks_ref.at[source, head],
            ask_send.at[source, head, side],
            ask_recv.at[source, head],
            me + 2 * side - 1,
        )

    def for_sides(action):
        for side, there in enumerate((has_left, has_right)):

            @pl.when(there)
            def _():
                action(side)

    pl.semaphore_wait(barrier, count - 1)
    for_sides(lambda side: ask_copy(me, 0, side).start())

    for each in loads[4:6]:
        each.wait()
    for p in range(PARTS):
        for side, (_, x_ref) in enumerate(sides):
            token_loads[p][side].wait()
            z = jnp.dot(
                down_ref[...], x_ref[p * n_part : (p + 1) * n_part, :], preferred_element_type=jnp.float32
            )
            parts_ref[
                p * order : (p + 1) * order, side * half_columns : (side + 1) * half_columns
            ] = z[:order] + z[order:]
    whole_ref[...] = strict_dot(merge_ref[...], parts_ref[...])
    others_ref[:order] = whole_ref[:order]

    def near_copy(side):
        start = order * (2 - side)
        other = me + 2 * side - 1
        return copy(
            whole_ref.at[pl.ds(0, order)],
            others_ref.at[pl.ds(start, order)],
            field_send.at[other],
            field_recv.at[me],
            other,
        )

    def far_copy(other):
        return copy(
            whole_ref.at[pl.ds(order, FAR)],
            others_ref.at[pl.ds(pl.multiple_of(3 * order + me * FAR, FAR), FAR)],
            field_send.at[other],
            field_recv.at[me],
            other,
        )

    def near_wait(side):
        source = me + 2 * side - 1
        copy(
            whole_ref.at[pl.ds(0, order)],
            others_ref.at[pl.ds(order * (1 + side), order)],
            field_send.at[source],
            field_recv.at[source],
            source,
        ).wait_recv()

    def far_wait(source):
        copy(
            whole_ref.at[pl.ds(order, FAR)],
            others_ref.at[pl.ds(3 * order + source * FAR, FAR)],
            field_send.at[source],
            field_recv.at[source],
            source,
        ).wait_recv()

    def for_far(action):
        for other in range(count):

            @pl.when(jnp.logical_or(other - me > 1, me - other > 1))
            def _():
                action(other)

    for_sides(lambda side: near_copy(side).start())
    for_far(lambda other: far_copy(other).start())

    @pl.when(jnp.logical_not(inside))
    def _():
        ask_copy(me, 1, 1 - outward).start()

    loads[6].wait()

    def close(p, carry):
        start = p * n_part if isinstance(p, int) else pl.multiple_of(p * n_part, n_part)
        for side, (_, x_ref) in enumerate(sides):
            z = jnp.dot(near_ref[...], x_ref[pl.ds(start, n_part), :], preferred_element_type=jnp.float32)
            close_ref[p, :, side * half_columns : (side + 1) * half_columns] = z[:t_part] + z[t_part:]
        return carry

    close(0, 0)

    @pl.when(inside)
    def _():
        for side in range(2):
            ask_copy(me + 2 * side - 1, 0, 1 - side).wait_recv()
            ask_copy(me + 2 * side - 1, 0, 1 - side).start()
        ask_copy(me, 1, outward).start()

    lax.fori_loop(1, PARTS, close, 0)
    for each in loads[7:]:
        each.wait()
    field_ref[...] = strict_dot(local_ref[...], parts_ref[...])

    def hand(source, head, side):
        handed = ask_copy(source, head, side)
        handed.wait_recv()
        handed.start()

    for_sides(near_wait)
    for_far(far_wait)
    field_ref[...] += strict_dot(cross_ref[...], others_ref[...])

    def finish(p, carry):
        f = field_ref[pl.ds(pl.multiple_of(p * order, order), order), :]
        high = f.astype(jnp.bfloat16)
        low = (f - high.astype(jnp.float32)).astype(jnp.bfloat16)
        y = close_ref[p] + jnp.dot(
            up_ref[...], jnp.concatenate([high, low, high], axis=0), preferred_element_type=jnp.float32
        )
        y = y.astype(jnp.bfloat16).astype(jnp.float32)
        begin = pl.multiple_of(p * t_part, t_part)
        place = me * PARTS + p
        cos_p, sin_p = coarse_ref[0, pl.ds(place, 1), :], coarse_ref[1, pl.ds(place, 1), :]
        cosine = cos_p * fine_ref[0] - sin_p * fine_ref[1]
        sine = sin_p * fine_ref[0] + cos_p * fine_ref[1]
        for head in range(heads):
            k = y[:, head * width : (head + 1) * width]
            turned = k * cosine + pltpu.roll(k, width // 2, 1) * sine
            k_ref[head, pl.ds(begin, t_part), :] = turned.astype(jnp.bfloat16)
            v = y[:, half_columns + head * width : half_columns + (head + 1) * width]
            v_ref[head, :, pl.ds(begin, t_part)] = v.T.astype(jnp.bfloat16)
        return carry

    lax.fori_loop(0, PARTS, finish, 0)

    @pl.when(inside)
    def _():
        hand(mate, 1, 1 - outward)
        ask_copy(me, 1, 1 - outward).start()

    runs = [
        (0, 0, 0, blocks),
        (1, 0, 0, blocks),
        (0, 1, 0, blocks),
        (3, 0, 0, blocks),
        (2, 0, 0, blocks),
        (3, 1, 0, blocks - 1),
        (2, 1, 0, blocks),
        (3, 1, blocks - 1, 1),
        (1, 1, 0, blocks),
    ]
    begins = [sum(run[3] for run in runs[:i]) for i in range(len(runs))]
    units = begins[-1] + blocks

    def decode(u):
        kind, head, block = runs[0][0], runs[0][1], u
        for begin, run in zip(begins[1:], runs[1:]):
            late = u >= begin
            kind = jnp.where(late, run[0], kind)
            head = jnp.where(late, run[1], head)
            block = jnp.where(late, u - begin + run[2], block)
        source = jnp.where(
            kind == 0, mate, jnp.where(kind == 1, near_over, jnp.where(kind == 2, far_end, me))
        )
        return kind, head, block, source

    chunk = 512

    def score(u, keep_ref, top_ref):
        _, head, block, source = decode(u)
        q = asks_ref[source, head, pl.ds(pl.multiple_of(block * BLOCK, BLOCK), BLOCK), :]
        best = None
        for c in range(0, tokens, chunk):
            s = lax.dot_general(
                k_ref[head, c : c + chunk, :],
                q,
                (((1,), (1,)), ((), ())),
                preferred_element_type=jnp.float32,
            )
            keep_ref[c : c + chunk, :] = s
            top = jnp.max(s, axis=0, keepdims=True)
            best = top if best is None else jnp.maximum(best, top)
        top_ref[...] = best

    def weigh(u, keep_ref, top_ref):
        kind, head, block, _ = decode(u)
        best = top_ref[...]
        total = jnp.zeros((1, BLOCK), jnp.float32)
        accum = jnp.zeros((width, BLOCK), jnp.float32)
        for c in range(0, tokens, chunk):
            e = jnp.exp2((keep_ref[c : c + chunk, :] - best) * factor)
            total += jnp.sum(e, axis=0, keepdims=True)
            accum += jnp.dot(
                v_ref[head, :, c : c + chunk], e.astype(jnp.bfloat16), preferred_element_type=jnp.float32
            )
        own_ref[kind, head, block] = (accum / total).astype(jnp.bfloat16)
        own_log_ref[kind, head, block] = best * factor + jnp.log2(total)

    def both(src, src_log, dst, dst_log, send, recv, other):
        return (
            copy(src, dst, send.at[0], recv.at[0], other),
            copy(src_log, dst_log, send.at[1], recv.at[1], other),
        )

    def half_copy(kind, head, block):
        at = (kind, head, block)
        return both(
            own_ref.at[at],
            own_log_ref.at[at],
            half_ref.at[at],
            half_log_ref.at[at],
            half_send.at[at],
            half_recv.at[at],
            mate,
        )

    def over_copy(j, head, block):
        at = (j, head, block)
        return both(
            merged_ref.at[at],
            merged_log_ref.at[at],
            over_ref.at[at],
            over_log_ref.at[at],
            over_send.at[at],
            over_recv.at[at],
            near_over,
        )

    def last_copy(head, block):
        at = (head, block)
        return both(
            ready_ref.at[at],
            ready_log_ref.at[at],
            last_ref.at[at],
            last_log_ref.at[at],
            last_send.at[at],
            last_recv.at[at],
            mate,
        )

    def blend(parts, logs):
        best = functools.reduce(jnp.maximum, logs)
        shares = [jnp.exp2(log - best) for log in logs]
        total = functools.reduce(jnp.add, shares)
        mixed = functools.reduce(
            jnp.add, [part.astype(jnp.float32) * (share / total) for part, share in zip(parts, shares)]
        )
        return mixed, best + jnp.log2(total)

    def merge_half(kind, head, block):
        for each in half_copy(kind, head, block):
            each.wait_recv()
        at = (kind - 1, head, block)
        mixed, log = blend(
            [own_ref[kind, head, block], half_ref[kind, head, block]],
            [own_log_ref[kind, head, block], half_log_ref[kind, head, block]],
        )
        merged_ref[at] = mixed.astype(jnp.bfloat16)
        merged_log_ref[at] = log
        for each in over_copy(*at):
            each.start()

    def await_ask(u):
        kind, head, block, source = decode(u)

        @pl.when(jnp.logical_and(jnp.logical_and(block == 0, kind < 3), jnp.logical_not(inside)))
        def _():
            ask_copy(source, head, 1 - outward).wait_recv()

    lag = 6

    def send_on(u):
        kind, head, block, _ = decode(u)

        @pl.when(jnp.logical_and(kind < 3, jnp.logical_not(inside)))
        def _():
            for each in half_copy(kind, head, block):
                each.start()

        for kind, first in ((1, begins[1]), (2, begins[4])):
            k = u - first - lag

            @pl.when(jnp.logical_and(inside, jnp.logical_and(k >= 0, k < blocks)))
            def _():
                merge_half(kind, 0, k)

    await_ask(jnp.int32(0))
    score(jnp.int32(0), even_ref, even_top_ref)

    def serve(i, carry):
        u = 2 * i
        for at, source, head in ((1, far_end, 0), (4, far_end, 1), (7, near_over, 1)):

            @pl.when(jnp.logical_and(inside, i == at))
            def _():
                hand(source, head, outward)

        await_ask(u + 1)
        score(u + 1, odd_ref, odd_top_ref)
        weigh(u, even_ref, even_top_ref)
        send_on(u)
        ahead = jnp.minimum(u + 2, units - 1)

        @pl.when(u + 2 < units)
        def _():
            await_ask(ahead)

        score(ahead, even_ref, even_top_ref)
        weigh(u + 1, odd_ref, odd_top_ref)
        send_on(u + 1)
        return carry

    lax.fori_loop(0, units // 2, serve, 0)

    def pass_on(head, block):
        for each in over_copy(1, head, block):
            each.wait_recv()
        mixed, log = blend(
            [own_ref[0, head, block], over_ref[1, head, block]],
            [own_log_ref[0, head, block], over_log_ref[1, head, block]],
        )
        ready_ref[head, block] = mixed.astype(jnp.bfloat16)
        ready_log_ref[head, block] = log
        for each in last_copy(head, block):
            each.start()

    @pl.when(inside)
    def _():
        for block in range(blocks):
            merge_half(2, 1, block)
            pass_on(0, block)
        for block in range(blocks):
            pass_on(1, block)
            merge_half(1, 1, block)
        for head in range(heads):
            for block in range(blocks):
                for each in half_copy(0, head, block) + over_copy(0, head, block):
                    each.wait_recv()
                mixed, _ = blend(
                    [own_ref[3, head, block], half_ref[0, head, block], over_ref[0, head, block]],
                    [own_log_ref[3, head, block], half_log_ref[0, head, block], over_log_ref[0, head, block]],
                )
                out_ref[head, block * BLOCK : (block + 1) * BLOCK, :] = mixed.T.astype(out_ref.dtype)
        for head in range(heads):
            ask_copy(me - 1, head, 1).wait_send()
            ask_copy(me + 1, head, 0).wait_send()
            ask_copy(far_end, head, outward).wait_send()
            for block in range(blocks):
                for each in over_copy(0, head, block) + over_copy(1, head, block) + last_copy(head, block):
                    each.wait_send()

    @pl.when(jnp.logical_not(inside))
    def _():
        for head in range(heads):
            for block in range(blocks):
                for each in last_copy(head, block):
                    each.wait_recv()
                mixed, _ = blend(
                    [own_ref[3, head, block], last_ref[head, block]],
                    [own_log_ref[3, head, block], last_log_ref[head, block]],
                )
                out_ref[head, block * BLOCK : (block + 1) * BLOCK, :] = mixed.T.astype(out_ref.dtype)
        for kind in range(3):
            for head in range(heads):
                for block in range(blocks):
                    for each in half_copy(kind, head, block):
                        each.wait_send()

    for head in range(heads):
        for_sides(lambda side: ask_copy(me, head, side).wait_send())
    for_sides(lambda side: near_copy(side).wait_send())
    for_far(lambda other: far_copy(other).wait_send())


def by_tokens(keys, values, queries, positions, count):
    heads, rows, width = queries.shape
    n_dev, columns = keys.shape
    length = n_dev * count
    near, down, up, local, merge, cross = fields(length, count)

    def tall(matrix):
        return np.concatenate(split_two(matrix), axis=-2)

    def table(places):
        return tall(np.concatenate(spins(places, width).astype(np.float64), axis=1))

    up_high, up_low = split_two(up)
    t_part = near.shape[0]
    tokens = n_dev // 2
    blocks = rows // BLOCK
    split = 128
    operands = (
        table(np.arange(length // split) * float(split)),
        table(np.arange(split) * 1.0),
        tall(near),
        tall(down),
        np.concatenate([up_high, up_high, up_low], axis=1),
        tall(local),
        tall(merge),
        tall(cross),
        spins(np.arange(count * PARTS) * float(t_part), width),
        spins(np.arange(t_part) * 1.0, width),
    )
    held = [jax.ShapeDtypeStruct(o.shape[1:] if o.ndim == 3 and o.shape[0] == count else o.shape, o.dtype) for o in operands]
    dma = pltpu.SemaphoreType.DMA

    def parts(*lead):
        return [
            pltpu.VMEM(lead + (heads, blocks, width, BLOCK), jnp.bfloat16),
            pltpu.VMEM(lead + (heads, blocks, 1, BLOCK), jnp.float32),
        ]

    return pl.pallas_call(
        functools.partial(fused_kernel, count, math.log2(math.e) / math.sqrt(width)),
        in_specs=[pl.BlockSpec(memory_space=pl.ANY)] * 14,
        out_specs=pl.BlockSpec(memory_space=pltpu.VMEM),
        out_shape=jax.ShapeDtypeStruct(queries.shape, jnp.bfloat16),
        scratch_shapes=[
            pltpu.VMEM(keys.shape, keys.dtype),
            pltpu.VMEM(values.shape, values.dtype),
            pltpu.VMEM(queries.shape, queries.dtype),
            pltpu.VMEM((rows,), jnp.int32),
        ]
        + [pltpu.VMEM(h.shape, h.dtype) for h in held]
        + [
            pltpu.VMEM((PARTS * ORDER, 2 * columns), jnp.float32),
            pltpu.VMEM((ORDER + FAR, 2 * columns), jnp.float32),
            pltpu.VMEM((cross.shape[2], 2 * columns), jnp.float32),
            pltpu.VMEM((PARTS, t_part, 2 * columns), jnp.float32),
            pltpu.VMEM((PARTS * ORDER, 2 * columns), jnp.float32),
            pltpu.VMEM((heads, tokens, width), jnp.bfloat16),
            pltpu.VMEM((heads, width, tokens), jnp.bfloat16),
            pltpu.VMEM((tokens, BLOCK), jnp.float32),
            pltpu.VMEM((tokens, BLOCK), jnp.float32),
            pltpu.VMEM((1, BLOCK), jnp.float32),
            pltpu.VMEM((1, BLOCK), jnp.float32),
            pltpu.VMEM((count, heads, rows, width), jnp.bfloat16),
        ]
        + parts(4)
        + parts(3)
        + parts(2)
        + parts(2)
        + parts()
        + parts()
        + [
            dma((12,)),
            dma((PARTS, 2)),
            dma((count,)),
            dma((count,)),
            dma((count, heads, 2)),
            dma((count, heads)),
            dma((3, heads, blocks, 2)),
            dma((3, heads, blocks, 2)),
            dma((2, heads, blocks, 2)),
            dma((2, heads, blocks, 2)),
            dma((heads, blocks, 2)),
            dma((heads, blocks, 2)),
        ],
        compiler_params=pltpu.CompilerParams(
            collective_id=0, has_side_effects=True, vmem_limit_bytes=60 * 1024 * 1024
        ),
    )(keys, values, queries, positions, *operands)


def by_columns(keys, values, queries, positions):
    key_parts = lax.all_to_all(keys, "ctx", split_axis=1, concat_axis=0, tiled=True)
    value_parts = lax.all_to_all(values, "ctx", split_axis=1, concat_axis=0, tiled=True)
    heads, rows, width = queries.shape
    per_device = key_parts.shape[1]
    compact = compress(jnp.concatenate([key_parts, value_parts], axis=1))
    rotated = rotate_rows(queries.astype(jnp.float32), positions.astype(jnp.float32)).astype(
        jnp.bfloat16
    )
    whole = lax.all_gather(compact.T, "ctx", axis=0, tiled=True)
    tokens = whole.shape[1]
    shaped = whole.reshape(-1, 2, per_device, tokens)
    key_rows = shaped[:, 0].reshape(heads, width, tokens).swapaxes(1, 2)
    value_rows = shaped[:, 1].reshape(heads, width, tokens).swapaxes(1, 2)
    places = jnp.arange(tokens).astype(jnp.float32)
    ready = rotate_rows(key_rows.astype(jnp.float32), places).astype(jnp.bfloat16)
    return attend(rotated, ready, value_rows, jnp.zeros((), jnp.int32))[0]


def solution(mesh):
    count = mesh.shape["ctx"]

    def on_device(keys, values, queries, positions):
        heads, rows, width = queries.shape
        if count == 4 and heads == 2 and keys.shape[0] % (PARTS * 512) == 0 and rows % BLOCK == 0 and width == 128:
            return by_tokens(keys, values, queries, positions, count)
        return by_columns(keys, values, queries, positions)

    return jax.shard_map(
        on_device,
        mesh=mesh,
        in_specs=(
            P(("user", "ctx"), "heads"),
            P(("user", "ctx"), "heads"),
            P("heads", ("user", "ctx"), None),
            P(("user", "ctx")),
        ),
        out_specs=P("heads", ("user", "ctx"), None),
        check_vma=False,
    )
```

```python
import functools
import math

import jax
import jax.numpy as jnp
import numpy as np
from jax import lax
from jax.experimental import pallas as pl
from jax.experimental.pallas import tpu as pltpu
from jax.sharding import PartitionSpec as P

OUTER = 128
PARTS = 4
ORDER = 64
EDGE = 32
FAR = 16
BLOCK = 256
MESH = pl.DeviceIdType.MESH


def split_two(matrix):
    high = matrix.astype(jnp.bfloat16)
    low = (matrix - np.asarray(high).astype(np.float64)).astype(jnp.bfloat16)
    return high, low


@functools.lru_cache(maxsize=None)
def stages(length):
    outer = OUTER
    inner = length // outer
    step = inner // 2
    a = np.arange(outer)
    c = np.arange(outer)
    turn = 2 * outer
    angle = np.pi / outer * ((c[:, None] * a[None, :]) % turn)
    alternate = np.where(a % 2 == 0, 1.0, -1.0)
    first = np.stack([np.cos(angle), -np.sin(angle)], axis=1)
    first[0, 1] = alternate
    d = np.arange(length // 2 // turn)
    k = np.concatenate([c[:, None] + turn * d, (turn - c[:, None]) % turn + turn * d], axis=1)
    k[0, d.size :] = outer + turn * d
    sign = np.concatenate([np.ones(d.size), -np.ones(d.size)])
    b = np.arange(inner)
    q = np.arange(step)
    theta = np.pi / (2 * length) * ((k[:, :, None] * (2 * b + 1)) % (4 * length))
    phi = np.pi / length * ((k[:, None, :] * (2 * q + 1)[:, None]) % (2 * length))
    forward = np.stack([np.cos(theta), np.sin(theta) * sign[None, :, None]], axis=2)
    weight = np.where(k == 0, 1.0, 2.0) / length
    back = np.stack([np.cos(phi), np.sin(phi) * sign], axis=1) * weight[:, None, None, :]
    half = d.size
    forward[0, :half, 1] = 0.0
    forward[0, half:, 1] = np.cos(theta[0, half:])
    forward[0, half:, 0] = 0.0
    back[0, 1, :, :half] = 0.0
    back[0, 1, :, half:] = np.cos(phi[0, :, half:]) * weight[0, half:]
    back[0, 0, :, half:] = 0.0
    middle = back.reshape(outer, 2 * step, 2 * half) @ forward.reshape(outer, 2 * half, 2 * inner)
    last = first.transpose(2, 0, 1).reshape(outer, 2 * outer)
    return first.reshape(2 * outer, outer), middle, last


def compress(signal):
    length, columns = signal.shape
    outer, inner = OUTER, length // OUTER
    first, middle, last = stages(length)
    first_high, first_low = split_two(first)
    flat = signal.reshape(outer, inner * columns)
    one = jnp.dot(first_high, flat, preferred_element_type=jnp.float32) + jnp.dot(
        first_low, flat, preferred_element_type=jnp.float32
    )
    one = one.reshape(outer, 2 * inner, columns)
    two = jnp.einsum(
        "cob,cbl->col", jnp.asarray(middle.astype(np.float32)), one, precision=lax.Precision.HIGH
    )
    three = jnp.dot(
        jnp.asarray(last.astype(np.float32)),
        two.reshape(2 * outer, inner // 2 * columns),
        precision=lax.Precision.HIGH,
    )
    return three.reshape(length // 2, columns).astype(jnp.bfloat16)

def strict_dot(left, right):
    rows, columns = left.shape[0] // 2, right.shape[1]
    high = right.astype(jnp.bfloat16)
    low = (right - high.astype(jnp.float32)).astype(jnp.bfloat16)
    both = jnp.dot(
        left, jnp.concatenate([high, low], axis=1), preferred_element_type=jnp.float32
    )
    return both[:rows, :columns] + (both[:rows, columns:] + both[rows:, :columns])


def inverse_freq(width):
    return jnp.exp(jnp.arange(width // 2).astype(jnp.float32) * (-2.0 * math.log(500000.0) / width))


def rotate_rows(block, places):
    width = block.shape[-1]
    half = width // 2
    angles = places[:, None] * inverse_freq(width)[None, :]
    cosine = jnp.cos(angles)
    sine = jnp.sin(angles)
    first = block[..., :half]
    second = block[..., half:]
    return jnp.concatenate(
        [first * cosine - second * sine, second * cosine + first * sine], axis=-1
    )


def attend_kernel(chunk, scale, resume, finish, swap_ref, q_ref, k_ref, v_ref, *refs):
    q = q_ref[0]
    swap = swap_ref[0] == 1
    rows, width = q.shape
    factor = scale * math.log2(math.e)
    if resume:
        accum = refs[0][0]
        best = refs[1][0][:, :1]
        total = refs[2][0][:, :1]
        refs = refs[3:]
    else:
        best = jnp.full((rows, 1), -jnp.inf, jnp.float32)
        total = jnp.zeros((rows, 1), jnp.float32)
        accum = jnp.zeros((rows, width), jnp.float32)
    tokens = k_ref.shape[1]
    for start in range(0, tokens, chunk):
        one = k_ref[0, start : start + chunk, :]
        two = v_ref[0, start : start + chunk, :]
        k, v = jnp.where(swap, two, one), jnp.where(swap, one, two)
        scores = lax.dot_general(
            q, k, (((1,), (1,)), ((), ())), preferred_element_type=jnp.float32
        )
        fresh = jnp.maximum(best, jnp.max(scores, axis=1, keepdims=True))
        expo = jnp.exp2((scores - fresh) * factor)
        shrink = jnp.exp2((best - fresh) * factor)
        total = total * shrink + jnp.sum(expo, axis=1, keepdims=True)
        accum = accum * shrink + jnp.dot(
            expo.astype(jnp.bfloat16), v, preferred_element_type=jnp.float32
        )
        best = fresh
    if finish:
        refs[0][0] = (accum / total).astype(refs[0].dtype)
        refs[1][0] = jnp.broadcast_to(best * factor + jnp.log2(total), (rows, 8))
    else:
        refs[0][0] = accum
        refs[1][0] = jnp.broadcast_to(best, (rows, 8))
        refs[2][0] = jnp.broadcast_to(total, (rows, 8))


def attend(queries, keys, values, swap, part=0, parts=1, state=None):
    groups, rows, width = queries.shape
    heads, tokens, _ = values.shape
    per_head = groups // heads
    block = math.gcd(rows, 768)
    chunk = math.gcd(tokens, 1024)
    scale = 1.0 / math.sqrt(width)
    finish = part == parts - 1
    wide = pl.BlockSpec((1, block, width), lambda g, i: (g, i, 0))
    thin = pl.BlockSpec((1, block, 8), lambda g, i: (g, i, 0))
    thin_shape = jax.ShapeDtypeStruct((groups, rows, 8), jnp.float32)
    state = () if state is None else tuple(state)
    wide_type = jnp.bfloat16 if finish else jnp.float32
    return pl.pallas_call(
        functools.partial(attend_kernel, chunk, scale, bool(state), finish),
        grid=(groups, rows // block),
        in_specs=[
            pl.BlockSpec(memory_space=pltpu.SMEM),
            wide,
            pl.BlockSpec((1, tokens, width), lambda g, i: (g // per_head, part, 0)),
            pl.BlockSpec((1, tokens, width), lambda g, i: (g // per_head, 0, 0)),
        ]
        + ([wide, thin, thin] if state else []),
        out_specs=[wide, thin] if finish else [wide, thin, thin],
        out_shape=[jax.ShapeDtypeStruct((groups, rows, width), wide_type), thin_shape]
        + ([] if finish else [thin_shape]),
        cost_estimate=pl.CostEstimate(
            flops=8 * groups * rows * tokens * width,
            bytes_accessed=4 * groups * rows * width * 2,
            transcendentals=groups * rows * tokens,
        ),
    )(swap.reshape(1), queries, keys, values, *state)


def bounds(count, left, right):
    return np.log(left / (count - 1 + right)), np.log((count - 1 + left) / right)


def nodes(count, order, left, right):
    low, top = bounds(count, left, right)
    e = np.exp((top - low) / 2 * np.cos(np.pi * (2 * np.arange(order) + 1) / (2 * order)) + (top + low) / 2)
    return ((count - 1 + right) * e - left) / (1 + e)


def cardinals(places, count, order, left, right):
    low, top = bounds(count, left, right)
    at = (2 * np.log((places + left) / (count - 1 + right - places)) - top - low) / (top - low)
    at = np.arccos(np.clip(at, -1.0, 1.0))
    own = np.pi * (2 * np.arange(order) + 1) / (2 * order)
    total = np.zeros((places.size, order))
    for k in range(order):
        total += (1.0 if k == 0 else 2.0) / order * np.cos(k * at)[:, None] * np.cos(k * own)[None, :]
    return total


@functools.lru_cache(maxsize=None)
def fields(length, devices):
    parts, order = PARTS, ORDER
    scale = math.sqrt(0.5) / (2 * length)

    def cot(m):
        return 1.0 / np.tan(np.pi * m / (4 * length))

    n_dev = length // devices
    n_part, t_dev = n_dev // parts, n_dev // 2
    t_part = n_part // 2
    n, t = np.arange(n_part), np.arange(t_part)
    sign_n = np.array([1.0, -1.0, -1.0, 1.0])[n % 4]
    sign_t = np.where(t % 2 == 0, 1.0, -1.0)
    near = sign_t[:, None] * sign_n * scale * cot(4 * t[:, None] - 2 * n + 1.0)
    down = cardinals(n, n_part, order, 1.5, 1.5).T * sign_n
    up = sign_t[:, None] * cardinals(t, t_part, order, 0.75, 0.75)
    part = np.arange(parts)[:, None]
    source = (part * n_part + nodes(n_part, order, 1.5, 1.5)).reshape(-1)
    target = (part * t_part + nodes(t_part, order, 0.75, 0.75)).reshape(-1)
    own = np.arange(parts * order) // order
    same = own[:, None] == own[None, :]
    local = np.where(same, 0.0, scale * cot(np.where(same, 1.0, 4 * target[:, None] - 2 * source + 1)))
    last = n_dev - 1
    wide = float(n_dev)
    merge = np.concatenate(
        [
            cardinals(source, n_dev, EDGE, 1.5, wide).T,
            cardinals(last - source, n_dev, EDGE, 1.5, wide).T,
            cardinals(source, n_dev, FAR, 2 * wide, 2 * wide).T,
        ]
    )
    to_left = nodes(n_dev, EDGE, 1.5, wide)
    sparse = nodes(n_dev, FAR, 2 * wide, 2 * wide)
    size = 3 * EDGE + devices * FAR
    cross = np.zeros((devices, parts * order, size + -size % 128))
    for r in range(devices):
        a = 4 * (target + r * t_dev)[:, None]
        for s in range(devices):
            if abs(r - s) > 1:
                spots, start = sparse, 3 * EDGE + s * FAR
            elif s < r or (s == r and 2 * r >= devices):
                spots, start = last - to_left, EDGE * (r - s)
            else:
                spots, start = to_left, 2 * EDGE * (s - r)
            b = 2 * (spots + s * n_dev)
            block = scale * cot(a + b + 3)
            if r != s:
                block = block + scale * cot(a - b + 1)
            cross[r, :, start : start + block.shape[1]] = block
    return near, down, up, local, merge, cross


def spins(places, width):
    freq = 500000.0 ** (-2.0 * np.arange(width // 2) / width)
    angles = places[:, None] * freq
    cosine, sine = np.cos(angles), np.sin(angles)
    return np.stack(
        [np.concatenate([cosine, cosine], axis=1), np.concatenate([-sine, sine], axis=1)]
    ).astype(np.float32)


def fused_kernel(
    count,
    factor,
    keys_hbm,
    values_hbm,
    queries_hbm,
    places_hbm,
    high_hbm,
    low_hbm,
    near_hbm,
    down_hbm,
    up_hbm,
    local_hbm,
    merge_hbm,
    cross_hbm,
    coarse_hbm,
    fine_hbm,
    out_ref,
    keys_ref,
    values_ref,
    queries_ref,
    places_ref,
    high_ref,
    low_ref,
    near_ref,
    down_ref,
    up_ref,
    local_ref,
    merge_ref,
    cross_ref,
    coarse_ref,
    fine_ref,
    parts_ref,
    whole_ref,
    others_ref,
    close_ref,
    field_ref,
    k_ref,
    v_ref,
    even_ref,
    odd_ref,
    even_top_ref,
    odd_top_ref,
    asks_ref,
    own_ref,
    own_log_ref,
    half_ref,
    half_log_ref,
    merged_ref,
    merged_log_ref,
    over_ref,
    over_log_ref,
    ready_ref,
    ready_log_ref,
    last_ref,
    last_log_ref,
    load_sem,
    token_sem,
    behind_sem,
    end_sem,
    field_send,
    field_recv,
    ask_send,
    ask_recv,
    half_send,
    half_recv,
    over_send,
    over_recv,
    last_send,
    last_recv,
):
    me = lax.axis_index("ctx")
    heads, rows, width = queries_ref.shape
    order = ORDER
    blocks = rows // BLOCK
    n_part = near_ref.shape[1]
    t_part = n_part // 2
    half_columns = keys_ref.shape[1]
    tokens = k_ref.shape[1]
    has_left, has_right = me > 0, me < count - 1
    inside = jnp.logical_and(has_left, has_right)
    lower = me < count // 2
    mate = me + 1 - 2 * lax.rem(me, 2)
    far_end = jnp.where(lower, count - 1, 0)
    near_over = jnp.where(lower, count // 2, count // 2 - 1)
    outward = jnp.where(lower, 0, 1)

    def copy(src, dst, send, recv, other):
        return pltpu.make_async_remote_copy(
            src_ref=src,
            dst_ref=dst,
            send_sem=send,
            recv_sem=recv,
            device_id={"ctx": other},
            device_id_type=MESH,
        )

    def for_sides(action):
        for side, there in enumerate((has_left, has_right)):

            @pl.when(there)
            def _():
                action(side)

    def greet(sem, other):
        pl.semaphore_signal(sem, inc=1, device_id={"ctx": other}, device_id_type=MESH)

    others_ref[...] = jnp.zeros_like(others_ref)
    barrier = pltpu.get_barrier_semaphore()
    for_sides(lambda side: greet(barrier, me + 2 * side - 1))
    pairs = (
        (places_hbm, places_ref),
        (queries_hbm, queries_ref),
        (high_hbm, high_ref),
        (low_hbm, low_ref),
        (down_hbm, down_ref),
        (merge_hbm, merge_ref),
        (near_hbm, near_ref),
        (local_hbm, local_ref),
        (cross_hbm.at[me], cross_ref),
        (up_hbm, up_ref),
        (coarse_hbm, coarse_ref),
        (fine_hbm, fine_ref),
    )
    loads = [pltpu.make_async_copy(src, dst, load_sem.at[i]) for i, (src, dst) in enumerate(pairs)]
    sides = ((keys_hbm, keys_ref), (values_hbm, values_ref))
    token_loads = [
        [
            pltpu.make_async_copy(
                src.at[pl.ds(p * n_part, n_part)], dst.at[pl.ds(p * n_part, n_part)], token_sem.at[p, side]
            )
            for side, (src, dst) in enumerate(sides)
        ]
        for p in range(PARTS)
    ]
    for each in loads[:6]:
        each.start()
    for p in range(PARTS):
        for each in token_loads[p]:
            each.start()
    for each in loads[6:]:
        each.start()
    for each in loads[:4]:
        each.wait()

    split = low_ref.shape[0] // 2
    for i in range(rows // split):
        here = slice(i * split, (i + 1) * split)
        place = jnp.broadcast_to(places_ref[here].astype(jnp.float32)[None], (split, split)).T.astype(jnp.int32)
        spun = []
        for value, table_ref in ((place // split, high_ref), (lax.rem(place, split), low_ref)):
            size = table_ref.shape[0] // 2
            value = value if size == split else value[:, :1]
            picked = value == lax.broadcasted_iota(jnp.int32, (split, size), 1)
            picked = jnp.where(picked, 1.0, 0.0).astype(jnp.bfloat16)
            got = jnp.dot(
                jnp.concatenate([picked, picked], axis=1), table_ref[...], preferred_element_type=jnp.float32
            )
            spun.append((got[:, :width], got[:, width:]))
        (cos_a, sin_a), (cos_b, sin_b) = spun
        cosine, sine = cos_a * cos_b - sin_a * sin_b, sin_a * cos_b + cos_a * sin_b
        for head in range(heads):
            x = queries_ref[head, here, :].astype(jnp.float32)
            asks_ref[me, head, here, :] = (x * cosine + pltpu.roll(x, width // 2, 1) * sine).astype(jnp.bfloat16)

    def ask_copy(source, head, block, side):
        here = pl.ds(block * BLOCK if isinstance(block, int) else pl.multiple_of(block * BLOCK, BLOCK), BLOCK)
        return copy(
            asks_ref.at[source, head, here],
            asks_ref.at[source, head, here],
            ask_send.at[source, head, block, side],
            ask_recv.at[source, head, block],
            me + 2 * side - 1,
        )

    pl.semaphore_wait(barrier, jnp.where(inside, 2, 1))
    for block in range(blocks):
        for_sides(lambda side: ask_copy(me, 0, block, side).start())
    for_sides(lambda side: greet(behind_sem.at[1 - side], me + 2 * side - 1))
    for_sides(lambda side: pl.semaphore_wait(behind_sem.at[side], 1))

    @pl.when(inside)
    def _():
        greet(end_sem, mate)

    for each in loads[4:6]:
        each.wait()
    for p in range(PARTS):
        for side, (_, x_ref) in enumerate(sides):
            token_loads[p][side].wait()
            z = jnp.dot(
                down_ref[...], x_ref[p * n_part : (p + 1) * n_part, :], preferred_element_type=jnp.float32
            )
            parts_ref[
                p * order : (p + 1) * order, side * half_columns : (side + 1) * half_columns
            ] = z[:order] + z[order:]
    whole_ref[...] = strict_dot(merge_ref[...], parts_ref[...])
    others_ref[:EDGE] = whole_ref[pl.ds(pl.multiple_of(jnp.where(lower, 0, EDGE), EDGE), EDGE), :]

    def near_copy(side):
        other = me + 2 * side - 1
        return copy(
            whole_ref.at[pl.ds(side * EDGE, EDGE)],
            others_ref.at[pl.ds(EDGE * (2 - side), EDGE)],
            field_send.at[other],
            field_recv.at[me],
            other,
        )

    def far_copy(other):
        return copy(
            whole_ref.at[pl.ds(2 * EDGE, FAR)],
            others_ref.at[pl.ds(pl.multiple_of(3 * EDGE + me * FAR, FAR), FAR)],
            field_send.at[other],
            field_recv.at[me],
            other,
        )

    def near_wait(side):
        source = me + 2 * side - 1
        copy(
            whole_ref.at[pl.ds(0, EDGE)],
            others_ref.at[pl.ds(EDGE * (1 + side), EDGE)],
            field_send.at[source],
            field_recv.at[source],
            source,
        ).wait_recv()

    def far_wait(source):
        copy(
            whole_ref.at[pl.ds(2 * EDGE, FAR)],
            others_ref.at[pl.ds(3 * EDGE + source * FAR, FAR)],
            field_send.at[source],
            field_recv.at[source],
            source,
        ).wait_recv()

    def for_far(action):
        for other in range(count):

            @pl.when(jnp.logical_or(other - me > 1, me - other > 1))
            def _():
                action(other)

    for_sides(lambda side: near_copy(side).start())

    @pl.when(jnp.logical_not(inside))
    def _():
        pl.semaphore_wait(end_sem, 1)

    for_far(lambda other: far_copy(other).start())

    @pl.when(jnp.logical_not(inside))
    def _():
        for block in range(blocks):
            ask_copy(me, 1, block, 1 - outward).start()

    loads[6].wait()

    def close(p, carry):
        start = p * n_part if isinstance(p, int) else pl.multiple_of(p * n_part, n_part)
        for side, (_, x_ref) in enumerate(sides):
            z = jnp.dot(near_ref[...], x_ref[pl.ds(start, n_part), :], preferred_element_type=jnp.float32)
            close_ref[p, :, side * half_columns : (side + 1) * half_columns] = z[:t_part] + z[t_part:]
        return carry

    close(0, 0)

    @pl.when(inside)
    def _():
        for block in range(blocks):
            for side in range(2):
                handed = ask_copy(me + 2 * side - 1, 0, block, 1 - side)
                handed.wait_recv()
                handed.start()
        for block in range(blocks):
            ask_copy(me, 1, block, outward).start()

    lax.fori_loop(1, PARTS, close, 0)
    for each in loads[7:]:
        each.wait()
    field_ref[...] = strict_dot(local_ref[...], parts_ref[...])

    def hand(source, head, side):
        for block in range(blocks):
            handed = ask_copy(source, head, block, side)
            handed.wait_recv()
            handed.start()

    for_sides(near_wait)
    for_far(far_wait)
    field_ref[...] += strict_dot(cross_ref[...], others_ref[...])

    def finish(p, carry):
        f = field_ref[pl.ds(pl.multiple_of(p * order, order), order), :]
        high = f.astype(jnp.bfloat16)
        low = (f - high.astype(jnp.float32)).astype(jnp.bfloat16)
        y = close_ref[p] + jnp.dot(
            up_ref[...], jnp.concatenate([high, low, high], axis=0), preferred_element_type=jnp.float32
        )
        y = y.astype(jnp.bfloat16).astype(jnp.float32)
        begin = pl.multiple_of(p * t_part, t_part)
        place = me * PARTS + p
        cos_p, sin_p = coarse_ref[0, pl.ds(place, 1), :], coarse_ref[1, pl.ds(place, 1), :]
        cosine = cos_p * fine_ref[0] - sin_p * fine_ref[1]
        sine = sin_p * fine_ref[0] + cos_p * fine_ref[1]
        for head in range(heads):
            k = y[:, head * width : (head + 1) * width]
            turned = k * cosine + pltpu.roll(k, width // 2, 1) * sine
            k_ref[head, pl.ds(begin, t_part), :] = turned.astype(jnp.bfloat16)
            v = y[:, half_columns + head * width : half_columns + (head + 1) * width]
            v_ref[head, :, pl.ds(begin, t_part)] = v.T.astype(jnp.bfloat16)
        return carry

    lax.fori_loop(0, PARTS, finish, 0)

    @pl.when(inside)
    def _():
        hand(mate, 1, 1 - outward)
        for block in range(blocks):
            ask_copy(me, 1, block, 1 - outward).start()

    runs = [
        (0, 0, 0, blocks),
        (1, 0, 0, blocks),
        (0, 1, 0, blocks),
        (3, 0, 0, blocks),
        (2, 0, 0, blocks),
        (3, 1, 0, blocks - 1),
        (2, 1, 0, blocks),
        (3, 1, blocks - 1, 1),
        (1, 1, 0, blocks),
    ]
    begins = [sum(run[3] for run in runs[:i]) for i in range(len(runs))]
    units = begins[-1] + blocks

    def decode(u):
        kind, head, block = runs[0][0], runs[0][1], u
        for begin, run in zip(begins[1:], runs[1:]):
            late = u >= begin
            kind = jnp.where(late, run[0], kind)
            head = jnp.where(late, run[1], head)
            block = jnp.where(late, u - begin + run[2], block)
        source = jnp.where(
            kind == 0, mate, jnp.where(kind == 1, near_over, jnp.where(kind == 2, far_end, me))
        )
        return kind, head, block, source

    chunk = 512

    def score(u, keep_ref, top_ref):
        _, head, block, source = decode(u)
        q = asks_ref[source, head, pl.ds(pl.multiple_of(block * BLOCK, BLOCK), BLOCK), :]
        best = None
        for c in range(0, tokens, chunk):
            s = lax.dot_general(
                k_ref[head, c : c + chunk, :],
                q,
                (((1,), (1,)), ((), ())),
                preferred_element_type=jnp.float32,
            )
            keep_ref[c : c + chunk, :] = s
            top = jnp.max(s, axis=0, keepdims=True)
            best = top if best is None else jnp.maximum(best, top)
        top_ref[...] = best

    def weigh(u, keep_ref, top_ref):
        kind, head, block, _ = decode(u)
        best = top_ref[...]
        total = jnp.zeros((1, BLOCK), jnp.float32)
        accum = jnp.zeros((width, BLOCK), jnp.float32)
        for c in range(0, tokens, chunk):
            e = jnp.exp2((keep_ref[c : c + chunk, :] - best) * factor)
            total += jnp.sum(e, axis=0, keepdims=True)
            accum += jnp.dot(
                v_ref[head, :, c : c + chunk], e.astype(jnp.bfloat16), preferred_element_type=jnp.float32
            )
        own_ref[kind, head, block] = (accum / total).astype(jnp.bfloat16)
        own_log_ref[kind, head, block] = best * factor + jnp.log2(total)

    def both(src, src_log, dst, dst_log, send, recv, other):
        return (
            copy(src, dst, send.at[0], recv.at[0], other),
            copy(src_log, dst_log, send.at[1], recv.at[1], other),
        )

    def half_copy(kind, head, block):
        at = (kind, head, block)
        return both(
            own_ref.at[at],
            own_log_ref.at[at],
            half_ref.at[at],
            half_log_ref.at[at],
            half_send.at[at],
            half_recv.at[at],
            mate,
        )

    def over_copy(j, head, block):
        at = (j, head, block)
        return both(
            merged_ref.at[at],
            merged_log_ref.at[at],
            over_ref.at[at],
            over_log_ref.at[at],
            over_send.at[at],
            over_recv.at[at],
            near_over,
        )

    def last_copy(head, block):
        at = (head, block)
        return both(
            ready_ref.at[at],
            ready_log_ref.at[at],
            last_ref.at[at],
            last_log_ref.at[at],
            last_send.at[at],
            last_recv.at[at],
            mate,
        )

    def blend(parts, logs):
        best = functools.reduce(jnp.maximum, logs)
        shares = [jnp.exp2(log - best) for log in logs]
        total = functools.reduce(jnp.add, shares)
        mixed = functools.reduce(
            jnp.add, [part.astype(jnp.float32) * (share / total) for part, share in zip(parts, shares)]
        )
        return mixed, best + jnp.log2(total)

    def merge_half(kind, head, block):
        for each in half_copy(kind, head, block):
            each.wait_recv()
        at = (kind - 1, head, block)
        mixed, log = blend(
            [own_ref[kind, head, block], half_ref[kind, head, block]],
            [own_log_ref[kind, head, block], half_log_ref[kind, head, block]],
        )
        merged_ref[at] = mixed.astype(jnp.bfloat16)
        merged_log_ref[at] = log
        for each in over_copy(*at):
            each.start()

    def await_ask(u):
        kind, head, block, source = decode(u)

        @pl.when(jnp.logical_and(kind < 3, jnp.logical_not(inside)))
        def _():
            ask_copy(source, head, block, 1 - outward).wait_recv()

    lag = 6

    def send_on(u):
        kind, head, block, _ = decode(u)

        @pl.when(jnp.logical_and(kind < 3, jnp.logical_not(inside)))
        def _():
            for each in half_copy(kind, head, block):
                each.start()

        for kind, first in ((1, begins[1]), (2, begins[4])):
            k = u - first - lag

            @pl.when(jnp.logical_and(inside, jnp.logical_and(k >= 0, k < blocks)))
            def _():
                merge_half(kind, 0, k)

    await_ask(jnp.int32(0))
    score(jnp.int32(0), even_ref, even_top_ref)

    def serve(i, carry):
        u = 2 * i
        for at, source, head in ((1, far_end, 0), (4, far_end, 1), (7, near_over, 1)):

            @pl.when(jnp.logical_and(inside, i == at))
            def _():
                hand(source, head, outward)

        await_ask(u + 1)
        score(u + 1, odd_ref, odd_top_ref)
        weigh(u, even_ref, even_top_ref)
        send_on(u)
        ahead = jnp.minimum(u + 2, units - 1)

        @pl.when(u + 2 < units)
        def _():
            await_ask(ahead)

        score(ahead, even_ref, even_top_ref)
        weigh(u + 1, odd_ref, odd_top_ref)
        send_on(u + 1)
        return carry

    lax.fori_loop(0, units // 2, serve, 0)

    def settle(head, block):
        for each in half_copy(0, head, block) + over_copy(0, head, block):
            each.wait_recv()
        mixed, _ = blend(
            [own_ref[3, head, block], half_ref[0, head, block], over_ref[0, head, block]],
            [own_log_ref[3, head, block], half_log_ref[0, head, block], over_log_ref[0, head, block]],
        )
        out_ref[head, block * BLOCK : (block + 1) * BLOCK, :] = mixed.T.astype(out_ref.dtype)

    def pass_on(head, block):
        for each in over_copy(1, head, block):
            each.wait_recv()
        mixed, log = blend(
            [own_ref[0, head, block], over_ref[1, head, block]],
            [own_log_ref[0, head, block], over_log_ref[1, head, block]],
        )
        ready_ref[head, block] = mixed.astype(jnp.bfloat16)
        ready_log_ref[head, block] = log
        for each in last_copy(head, block):
            each.start()

    @pl.when(inside)
    def _():
        for block in range(blocks):
            merge_half(2, 1, block)
            pass_on(0, block)
        for block in range(blocks):
            settle(0, block)
        for block in range(blocks):
            pass_on(1, block)
            merge_half(1, 1, block)
        for block in range(blocks):
            settle(1, block)
        for head in range(heads):
            for block in range(blocks):
                ask_copy(me - 1, head, block, 1).wait_send()
                ask_copy(me + 1, head, block, 0).wait_send()
                ask_copy(far_end, head, block, outward).wait_send()
                for each in over_copy(0, head, block) + over_copy(1, head, block) + last_copy(head, block):
                    each.wait_send()

    @pl.when(jnp.logical_not(inside))
    def _():
        for head in range(heads):
            for block in range(blocks):
                for each in last_copy(head, block):
                    each.wait_recv()
                mixed, _ = blend(
                    [own_ref[3, head, block], last_ref[head, block]],
                    [own_log_ref[3, head, block], last_log_ref[head, block]],
                )
                out_ref[head, block * BLOCK : (block + 1) * BLOCK, :] = mixed.T.astype(out_ref.dtype)
        for kind in range(3):
            for head in range(heads):
                for block in range(blocks):
                    for each in half_copy(kind, head, block):
                        each.wait_send()

    for head in range(heads):
        for block in range(blocks):
            for_sides(lambda side: ask_copy(me, head, block, side).wait_send())
    for_sides(lambda side: near_copy(side).wait_send())
    for_far(lambda other: far_copy(other).wait_send())


def by_tokens(keys, values, queries, positions, count):
    heads, rows, width = queries.shape
    n_dev, columns = keys.shape
    length = n_dev * count
    near, down, up, local, merge, cross = fields(length, count)

    def tall(matrix):
        return np.concatenate(split_two(matrix), axis=-2)

    def table(places):
        return tall(np.concatenate(spins(places, width).astype(np.float64), axis=1))

    up_high, up_low = split_two(up)
    t_part = near.shape[0]
    tokens = n_dev // 2
    blocks = rows // BLOCK
    split = 128
    operands = (
        table(np.arange(length // split) * float(split)),
        table(np.arange(split) * 1.0),
        tall(near),
        tall(down),
        np.concatenate([up_high, up_high, up_low], axis=1),
        tall(local),
        tall(merge),
        tall(cross),
        spins(np.arange(count * PARTS) * float(t_part), width),
        spins(np.arange(t_part) * 1.0, width),
    )
    held = [jax.ShapeDtypeStruct(o.shape[1:] if o.ndim == 3 and o.shape[0] == count else o.shape, o.dtype) for o in operands]
    dma = pltpu.SemaphoreType.DMA

    def parts(*lead):
        return [
            pltpu.VMEM(lead + (heads, blocks, width, BLOCK), jnp.bfloat16),
            pltpu.VMEM(lead + (heads, blocks, 1, BLOCK), jnp.float32),
        ]

    return pl.pallas_call(
        functools.partial(fused_kernel, count, math.log2(math.e) / math.sqrt(width)),
        in_specs=[pl.BlockSpec(memory_space=pl.ANY)] * 14,
        out_specs=pl.BlockSpec(memory_space=pltpu.VMEM),
        out_shape=jax.ShapeDtypeStruct(queries.shape, jnp.bfloat16),
        scratch_shapes=[
            pltpu.VMEM(keys.shape, keys.dtype),
            pltpu.VMEM(values.shape, values.dtype),
            pltpu.VMEM(queries.shape, queries.dtype),
            pltpu.VMEM((rows,), jnp.int32),
        ]
        + [pltpu.VMEM(h.shape, h.dtype) for h in held]
        + [
            pltpu.VMEM((PARTS * ORDER, 2 * columns), jnp.float32),
            pltpu.VMEM((2 * EDGE + FAR, 2 * columns), jnp.float32),
            pltpu.VMEM((cross.shape[2], 2 * columns), jnp.float32),
            pltpu.VMEM((PARTS, t_part, 2 * columns), jnp.float32),
            pltpu.VMEM((PARTS * ORDER, 2 * columns), jnp.float32),
            pltpu.VMEM((heads, tokens, width), jnp.bfloat16),
            pltpu.VMEM((heads, width, tokens), jnp.bfloat16),
            pltpu.VMEM((tokens, BLOCK), jnp.float32),
            pltpu.VMEM((tokens, BLOCK), jnp.float32),
            pltpu.VMEM((1, BLOCK), jnp.float32),
            pltpu.VMEM((1, BLOCK), jnp.float32),
            pltpu.VMEM((count, heads, rows, width), jnp.bfloat16),
        ]
        + parts(4)
        + parts(3)
        + parts(2)
        + parts(2)
        + parts()
        + parts()
        + [
            dma((12,)),
            dma((PARTS, 2)),
            pltpu.SemaphoreType.REGULAR((2,)),
            pltpu.SemaphoreType.REGULAR,
            dma((count,)),
            dma((count,)),
            dma((count, heads, blocks, 2)),
            dma((count, heads, blocks)),
            dma((3, heads, blocks, 2)),
            dma((3, heads, blocks, 2)),
            dma((2, heads, blocks, 2)),
            dma((2, heads, blocks, 2)),
            dma((heads, blocks, 2)),
            dma((heads, blocks, 2)),
        ],
        compiler_params=pltpu.CompilerParams(
            collective_id=0, has_side_effects=True, vmem_limit_bytes=60 * 1024 * 1024
        ),
    )(keys, values, queries, positions, *operands)


def by_columns(keys, values, queries, positions):
    key_parts = lax.all_to_all(keys, "ctx", split_axis=1, concat_axis=0, tiled=True)
    value_parts = lax.all_to_all(values, "ctx", split_axis=1, concat_axis=0, tiled=True)
    heads, rows, width = queries.shape
    per_device = key_parts.shape[1]
    compact = compress(jnp.concatenate([key_parts, value_parts], axis=1))
    rotated = rotate_rows(queries.astype(jnp.float32), positions.astype(jnp.float32)).astype(
        jnp.bfloat16
    )
    whole = lax.all_gather(compact.T, "ctx", axis=0, tiled=True)
    tokens = whole.shape[1]
    shaped = whole.reshape(-1, 2, per_device, tokens)
    key_rows = shaped[:, 0].reshape(heads, width, tokens).swapaxes(1, 2)
    value_rows = shaped[:, 1].reshape(heads, width, tokens).swapaxes(1, 2)
    places = jnp.arange(tokens).astype(jnp.float32)
    ready = rotate_rows(key_rows.astype(jnp.float32), places).astype(jnp.bfloat16)
    return attend(rotated, ready, value_rows, jnp.zeros((), jnp.int32))[0]


def solution(mesh):
    count = mesh.shape["ctx"]

    def on_device(keys, values, queries, positions):
        heads, rows, width = queries.shape
        if count == 4 and heads == 2 and keys.shape[0] % (PARTS * 512) == 0 and rows % BLOCK == 0 and width == 128:
            return by_tokens(keys, values, queries, positions, count)
        return by_columns(keys, values, queries, positions)

    return jax.shard_map(
        on_device,
        mesh=mesh,
        in_specs=(
            P(("user", "ctx"), "heads"),
            P(("user", "ctx"), "heads"),
            P("heads", ("user", "ctx"), None),
            P(("user", "ctx")),
        ),
        out_specs=P("heads", ("user", "ctx"), None),
        check_vma=False,
    )
```

```python
import functools
import math

import jax
import jax.numpy as jnp
import numpy as np
from jax import lax
from jax.experimental import pallas as pl
from jax.experimental.pallas import tpu as pltpu
from jax.sharding import PartitionSpec as P

OUTER = 128
PARTS = 4
ORDER = 64
EDGE = 32
FAR = 16
BLOCK = 256
MESH = pl.DeviceIdType.MESH


def split_two(matrix):
    high = matrix.astype(jnp.bfloat16)
    low = (matrix - np.asarray(high).astype(np.float64)).astype(jnp.bfloat16)
    return high, low


@functools.lru_cache(maxsize=None)
def stages(length):
    outer = OUTER
    inner = length // outer
    step = inner // 2
    a = np.arange(outer)
    c = np.arange(outer)
    turn = 2 * outer
    angle = np.pi / outer * ((c[:, None] * a[None, :]) % turn)
    alternate = np.where(a % 2 == 0, 1.0, -1.0)
    first = np.stack([np.cos(angle), -np.sin(angle)], axis=1)
    first[0, 1] = alternate
    d = np.arange(length // 2 // turn)
    k = np.concatenate([c[:, None] + turn * d, (turn - c[:, None]) % turn + turn * d], axis=1)
    k[0, d.size :] = outer + turn * d
    sign = np.concatenate([np.ones(d.size), -np.ones(d.size)])
    b = np.arange(inner)
    q = np.arange(step)
    theta = np.pi / (2 * length) * ((k[:, :, None] * (2 * b + 1)) % (4 * length))
    phi = np.pi / length * ((k[:, None, :] * (2 * q + 1)[:, None]) % (2 * length))
    forward = np.stack([np.cos(theta), np.sin(theta) * sign[None, :, None]], axis=2)
    weight = np.where(k == 0, 1.0, 2.0) / length
    back = np.stack([np.cos(phi), np.sin(phi) * sign], axis=1) * weight[:, None, None, :]
    half = d.size
    forward[0, :half, 1] = 0.0
    forward[0, half:, 1] = np.cos(theta[0, half:])
    forward[0, half:, 0] = 0.0
    back[0, 1, :, :half] = 0.0
    back[0, 1, :, half:] = np.cos(phi[0, :, half:]) * weight[0, half:]
    back[0, 0, :, half:] = 0.0
    middle = back.reshape(outer, 2 * step, 2 * half) @ forward.reshape(outer, 2 * half, 2 * inner)
    last = first.transpose(2, 0, 1).reshape(outer, 2 * outer)
    return first.reshape(2 * outer, outer), middle, last


def compress(signal):
    length, columns = signal.shape
    outer, inner = OUTER, length // OUTER
    first, middle, last = stages(length)
    first_high, first_low = split_two(first)
    flat = signal.reshape(outer, inner * columns)
    one = jnp.dot(first_high, flat, preferred_element_type=jnp.float32) + jnp.dot(
        first_low, flat, preferred_element_type=jnp.float32
    )
    one = one.reshape(outer, 2 * inner, columns)
    two = jnp.einsum(
        "cob,cbl->col", jnp.asarray(middle.astype(np.float32)), one, precision=lax.Precision.HIGH
    )
    three = jnp.dot(
        jnp.asarray(last.astype(np.float32)),
        two.reshape(2 * outer, inner // 2 * columns),
        precision=lax.Precision.HIGH,
    )
    return three.reshape(length // 2, columns).astype(jnp.bfloat16)

def strict_dot(left, right):
    rows, columns = left.shape[0] // 2, right.shape[1]
    high = right.astype(jnp.bfloat16)
    low = (right - high.astype(jnp.float32)).astype(jnp.bfloat16)
    both = jnp.dot(
        left, jnp.concatenate([high, low], axis=1), preferred_element_type=jnp.float32
    )
    return both[:rows, :columns] + (both[:rows, columns:] + both[rows:, :columns])


def inverse_freq(width):
    return jnp.exp(jnp.arange(width // 2).astype(jnp.float32) * (-2.0 * math.log(500000.0) / width))


def rotate_rows(block, places):
    width = block.shape[-1]
    half = width // 2
    angles = places[:, None] * inverse_freq(width)[None, :]
    cosine = jnp.cos(angles)
    sine = jnp.sin(angles)
    first = block[..., :half]
    second = block[..., half:]
    return jnp.concatenate(
        [first * cosine - second * sine, second * cosine + first * sine], axis=-1
    )


def attend_kernel(chunk, scale, resume, finish, swap_ref, q_ref, k_ref, v_ref, *refs):
    q = q_ref[0]
    swap = swap_ref[0] == 1
    rows, width = q.shape
    factor = scale * math.log2(math.e)
    if resume:
        accum = refs[0][0]
        best = refs[1][0][:, :1]
        total = refs[2][0][:, :1]
        refs = refs[3:]
    else:
        best = jnp.full((rows, 1), -jnp.inf, jnp.float32)
        total = jnp.zeros((rows, 1), jnp.float32)
        accum = jnp.zeros((rows, width), jnp.float32)
    tokens = k_ref.shape[1]
    for start in range(0, tokens, chunk):
        one = k_ref[0, start : start + chunk, :]
        two = v_ref[0, start : start + chunk, :]
        k, v = jnp.where(swap, two, one), jnp.where(swap, one, two)
        scores = lax.dot_general(
            q, k, (((1,), (1,)), ((), ())), preferred_element_type=jnp.float32
        )
        fresh = jnp.maximum(best, jnp.max(scores, axis=1, keepdims=True))
        expo = jnp.exp2((scores - fresh) * factor)
        shrink = jnp.exp2((best - fresh) * factor)
        total = total * shrink + jnp.sum(expo, axis=1, keepdims=True)
        accum = accum * shrink + jnp.dot(
            expo.astype(jnp.bfloat16), v, preferred_element_type=jnp.float32
        )
        best = fresh
    if finish:
        refs[0][0] = (accum / total).astype(refs[0].dtype)
        refs[1][0] = jnp.broadcast_to(best * factor + jnp.log2(total), (rows, 8))
    else:
        refs[0][0] = accum
        refs[1][0] = jnp.broadcast_to(best, (rows, 8))
        refs[2][0] = jnp.broadcast_to(total, (rows, 8))


def attend(queries, keys, values, swap, part=0, parts=1, state=None):
    groups, rows, width = queries.shape
    heads, tokens, _ = values.shape
    per_head = groups // heads
    block = math.gcd(rows, 768)
    chunk = math.gcd(tokens, 1024)
    scale = 1.0 / math.sqrt(width)
    finish = part == parts - 1
    wide = pl.BlockSpec((1, block, width), lambda g, i: (g, i, 0))
    thin = pl.BlockSpec((1, block, 8), lambda g, i: (g, i, 0))
    thin_shape = jax.ShapeDtypeStruct((groups, rows, 8), jnp.float32)
    state = () if state is None else tuple(state)
    wide_type = jnp.bfloat16 if finish else jnp.float32
    return pl.pallas_call(
        functools.partial(attend_kernel, chunk, scale, bool(state), finish),
        grid=(groups, rows // block),
        in_specs=[
            pl.BlockSpec(memory_space=pltpu.SMEM),
            wide,
            pl.BlockSpec((1, tokens, width), lambda g, i: (g // per_head, part, 0)),
            pl.BlockSpec((1, tokens, width), lambda g, i: (g // per_head, 0, 0)),
        ]
        + ([wide, thin, thin] if state else []),
        out_specs=[wide, thin] if finish else [wide, thin, thin],
        out_shape=[jax.ShapeDtypeStruct((groups, rows, width), wide_type), thin_shape]
        + ([] if finish else [thin_shape]),
        cost_estimate=pl.CostEstimate(
            flops=8 * groups * rows * tokens * width,
            bytes_accessed=4 * groups * rows * width * 2,
            transcendentals=groups * rows * tokens,
        ),
    )(swap.reshape(1), queries, keys, values, *state)


def bounds(count, left, right):
    return np.log(left / (count - 1 + right)), np.log((count - 1 + left) / right)


def nodes(count, order, left, right):
    low, top = bounds(count, left, right)
    e = np.exp((top - low) / 2 * np.cos(np.pi * (2 * np.arange(order) + 1) / (2 * order)) + (top + low) / 2)
    return ((count - 1 + right) * e - left) / (1 + e)


def cardinals(places, count, order, left, right):
    low, top = bounds(count, left, right)
    at = (2 * np.log((places + left) / (count - 1 + right - places)) - top - low) / (top - low)
    at = np.arccos(np.clip(at, -1.0, 1.0))
    own = np.pi * (2 * np.arange(order) + 1) / (2 * order)
    total = np.zeros((places.size, order))
    for k in range(order):
        total += (1.0 if k == 0 else 2.0) / order * np.cos(k * at)[:, None] * np.cos(k * own)[None, :]
    return total


@functools.lru_cache(maxsize=None)
def fields(length, devices):
    parts, order = PARTS, ORDER
    scale = math.sqrt(0.5) / (2 * length)

    def cot(m):
        return 1.0 / np.tan(np.pi * m / (4 * length))

    n_dev = length // devices
    n_part, t_dev = n_dev // parts, n_dev // 2
    t_part = n_part // 2
    n, t = np.arange(n_part), np.arange(t_part)
    sign_n = np.array([1.0, -1.0, -1.0, 1.0])[n % 4]
    sign_t = np.where(t % 2 == 0, 1.0, -1.0)
    near = sign_t[:, None] * sign_n * scale * cot(4 * t[:, None] - 2 * n + 1.0)
    down = cardinals(n, n_part, order, 1.5, 1.5).T * sign_n
    up = sign_t[:, None] * cardinals(t, t_part, order, 0.75, 0.75)
    part = np.arange(parts)[:, None]
    source = (part * n_part + nodes(n_part, order, 1.5, 1.5)).reshape(-1)
    target = (part * t_part + nodes(t_part, order, 0.75, 0.75)).reshape(-1)
    own = np.arange(parts * order) // order
    same = own[:, None] == own[None, :]
    local = np.where(same, 0.0, scale * cot(np.where(same, 1.0, 4 * target[:, None] - 2 * source + 1)))
    last = n_dev - 1
    wide = float(n_dev)
    merge = np.concatenate(
        [
            cardinals(source, n_dev, EDGE, 1.5, wide).T,
            cardinals(last - source, n_dev, EDGE, 1.5, wide).T,
            cardinals(source, n_dev, FAR, 2 * wide, 2 * wide).T,
        ]
    )
    to_left = nodes(n_dev, EDGE, 1.5, wide)
    sparse = nodes(n_dev, FAR, 2 * wide, 2 * wide)
    size = 3 * EDGE + devices * FAR
    cross = np.zeros((devices, parts * order, size + -size % 128))
    for r in range(devices):
        a = 4 * (target + r * t_dev)[:, None]
        for s in range(devices):
            if abs(r - s) > 1:
                spots, start = sparse, 3 * EDGE + s * FAR
            elif s < r or (s == r and 2 * r >= devices):
                spots, start = last - to_left, EDGE * (r - s)
            else:
                spots, start = to_left, 2 * EDGE * (s - r)
            b = 2 * (spots + s * n_dev)
            block = scale * cot(a + b + 3)
            if r != s:
                block = block + scale * cot(a - b + 1)
            cross[r, :, start : start + block.shape[1]] = block
    return near, down, up, local, merge, cross


def spins(places, width):
    freq = 500000.0 ** (-2.0 * np.arange(width // 2) / width)
    angles = places[:, None] * freq
    cosine, sine = np.cos(angles), np.sin(angles)
    return np.stack(
        [np.concatenate([cosine, cosine], axis=1), np.concatenate([-sine, sine], axis=1)]
    ).astype(np.float32)


def fused_kernel(
    count,
    factor,
    keys_hbm,
    values_hbm,
    queries_hbm,
    places_hbm,
    high_hbm,
    low_hbm,
    near_hbm,
    down_hbm,
    up_hbm,
    local_hbm,
    merge_hbm,
    cross_hbm,
    coarse_hbm,
    fine_hbm,
    out_ref,
    keys_ref,
    values_ref,
    queries_ref,
    places_ref,
    high_ref,
    low_ref,
    near_ref,
    down_ref,
    up_ref,
    local_ref,
    merge_ref,
    cross_ref,
    coarse_ref,
    fine_ref,
    parts_ref,
    whole_ref,
    others_ref,
    close_ref,
    field_ref,
    k_ref,
    v_ref,
    even_ref,
    odd_ref,
    even_top_ref,
    odd_top_ref,
    asks_ref,
    own_ref,
    own_log_ref,
    half_ref,
    half_log_ref,
    merged_ref,
    merged_log_ref,
    over_ref,
    over_log_ref,
    ready_ref,
    ready_log_ref,
    last_ref,
    last_log_ref,
    load_sem,
    token_sem,
    behind_sem,
    end_sem,
    field_send,
    field_recv,
    ask_send,
    ask_recv,
    half_send,
    half_recv,
    over_send,
    over_recv,
    last_send,
    last_recv,
):
    me = lax.axis_index("ctx")
    heads, rows, width = queries_ref.shape
    order = ORDER
    blocks = rows // BLOCK
    n_part = near_ref.shape[1]
    t_part = n_part // 2
    half_columns = keys_ref.shape[1]
    tokens = k_ref.shape[1]
    has_left, has_right = me > 0, me < count - 1
    inside = jnp.logical_and(has_left, has_right)
    lower = me < count // 2
    mate = me + 1 - 2 * lax.rem(me, 2)
    far_end = jnp.where(lower, count - 1, 0)
    near_over = jnp.where(lower, count // 2, count // 2 - 1)
    outward = jnp.where(lower, 0, 1)

    def copy(src, dst, send, recv, other):
        return pltpu.make_async_remote_copy(
            src_ref=src,
            dst_ref=dst,
            send_sem=send,
            recv_sem=recv,
            device_id={"ctx": other},
            device_id_type=MESH,
        )

    def for_sides(action):
        for side, there in enumerate((has_left, has_right)):

            @pl.when(there)
            def _():
                action(side)

    def greet(sem, other):
        pl.semaphore_signal(sem, inc=1, device_id={"ctx": other}, device_id_type=MESH)

    others_ref[...] = jnp.zeros_like(others_ref)
    barrier = pltpu.get_barrier_semaphore()
    for_sides(lambda side: greet(barrier, me + 2 * side - 1))
    pairs = (
        (places_hbm, places_ref),
        (queries_hbm, queries_ref),
        (high_hbm, high_ref),
        (low_hbm, low_ref),
        (down_hbm, down_ref),
        (merge_hbm, merge_ref),
        (near_hbm, near_ref),
        (local_hbm, local_ref),
        (cross_hbm.at[me], cross_ref),
        (up_hbm, up_ref),
        (coarse_hbm, coarse_ref),
        (fine_hbm, fine_ref),
    )
    loads = [pltpu.make_async_copy(src, dst, load_sem.at[i]) for i, (src, dst) in enumerate(pairs)]
    sides = ((keys_hbm, keys_ref), (values_hbm, values_ref))
    token_loads = [
        [
            pltpu.make_async_copy(
                src.at[pl.ds(p * n_part, n_part)], dst.at[pl.ds(p * n_part, n_part)], token_sem.at[p, side]
            )
            for side, (src, dst) in enumerate(sides)
        ]
        for p in range(PARTS)
    ]
    for each in loads[:6]:
        each.start()
    for p in range(PARTS):
        for each in token_loads[p]:
            each.start()
    for each in loads[6:]:
        each.start()
    for each in loads[:4]:
        each.wait()

    split = low_ref.shape[0] // 2
    for i in range(rows // split):
        here = slice(i * split, (i + 1) * split)
        place = jnp.broadcast_to(places_ref[here].astype(jnp.float32)[None], (split, split)).T.astype(jnp.int32)
        spun = []
        for value, table_ref in ((place // split, high_ref), (lax.rem(place, split), low_ref)):
            size = table_ref.shape[0] // 2
            value = value if size == split else value[:, :1]
            picked = value == lax.broadcasted_iota(jnp.int32, (split, size), 1)
            picked = jnp.where(picked, 1.0, 0.0).astype(jnp.bfloat16)
            got = jnp.dot(
                jnp.concatenate([picked, picked], axis=1), table_ref[...], preferred_element_type=jnp.float32
            )
            spun.append((got[:, :width], got[:, width:]))
        (cos_a, sin_a), (cos_b, sin_b) = spun
        cosine, sine = cos_a * cos_b - sin_a * sin_b, sin_a * cos_b + cos_a * sin_b
        for head in range(heads):
            x = queries_ref[head, here, :].astype(jnp.float32)
            asks_ref[me, head, here, :] = (x * cosine + pltpu.roll(x, width // 2, 1) * sine).astype(jnp.bfloat16)

    def ask_copy(source, head, block, side):
        here = pl.ds(block * BLOCK if isinstance(block, int) else pl.multiple_of(block * BLOCK, BLOCK), BLOCK)
        return copy(
            asks_ref.at[source, head, here],
            asks_ref.at[source, head, here],
            ask_send.at[source, head, block, side],
            ask_recv.at[source, head, block],
            me + 2 * side - 1,
        )

    pl.semaphore_wait(barrier, jnp.where(inside, 2, 1))
    for block in range(blocks):
        for_sides(lambda side: ask_copy(me, 0, block, side).start())
    for_sides(lambda side: greet(behind_sem.at[1 - side], me + 2 * side - 1))
    for_sides(lambda side: pl.semaphore_wait(behind_sem.at[side], 1))

    @pl.when(inside)
    def _():
        greet(end_sem, mate)

    for each in loads[4:6]:
        each.wait()
    for p in range(PARTS):
        for side, (_, x_ref) in enumerate(sides):
            token_loads[p][side].wait()
            z = jnp.dot(
                down_ref[...], x_ref[p * n_part : (p + 1) * n_part, :], preferred_element_type=jnp.float32
            )
            parts_ref[
                p * order : (p + 1) * order, side * half_columns : (side + 1) * half_columns
            ] = z[:order] + z[order:]
    whole_ref[...] = strict_dot(merge_ref[...], parts_ref[...])
    others_ref[:EDGE] = whole_ref[pl.ds(pl.multiple_of(jnp.where(lower, 0, EDGE), EDGE), EDGE), :]

    def near_copy(side):
        other = me + 2 * side - 1
        return copy(
            whole_ref.at[pl.ds(side * EDGE, EDGE)],
            others_ref.at[pl.ds(EDGE * (2 - side), EDGE)],
            field_send.at[other],
            field_recv.at[me],
            other,
        )

    def far_copy(other):
        return copy(
            whole_ref.at[pl.ds(2 * EDGE, FAR)],
            others_ref.at[pl.ds(pl.multiple_of(3 * EDGE + me * FAR, FAR), FAR)],
            field_send.at[other],
            field_recv.at[me],
            other,
        )

    def near_wait(side):
        source = me + 2 * side - 1
        copy(
            whole_ref.at[pl.ds(0, EDGE)],
            others_ref.at[pl.ds(EDGE * (1 + side), EDGE)],
            field_send.at[source],
            field_recv.at[source],
            source,
        ).wait_recv()

    def far_wait(source):
        copy(
            whole_ref.at[pl.ds(2 * EDGE, FAR)],
            others_ref.at[pl.ds(3 * EDGE + source * FAR, FAR)],
            field_send.at[source],
            field_recv.at[source],
            source,
        ).wait_recv()

    def for_far(action):
        for other in range(count):

            @pl.when(jnp.logical_or(other - me > 1, me - other > 1))
            def _():
                action(other)

    for_sides(lambda side: near_copy(side).start())

    @pl.when(jnp.logical_not(inside))
    def _():
        pl.semaphore_wait(end_sem, 1)

    for_far(lambda other: far_copy(other).start())

    @pl.when(jnp.logical_not(inside))
    def _():
        for block in range(blocks):
            ask_copy(me, 1, block, 1 - outward).start()

    loads[6].wait()

    def close(p, carry):
        start = p * n_part if isinstance(p, int) else pl.multiple_of(p * n_part, n_part)
        for side, (_, x_ref) in enumerate(sides):
            z = jnp.dot(near_ref[...], x_ref[pl.ds(start, n_part), :], preferred_element_type=jnp.float32)
            close_ref[p, :, side * half_columns : (side + 1) * half_columns] = z[:t_part] + z[t_part:]
        return carry

    close(0, 0)

    @pl.when(inside)
    def _():
        for block in range(blocks):
            for side in range(2):
                handed = ask_copy(me + 2 * side - 1, 0, block, 1 - side)
                handed.wait_recv()
                handed.start()

    lax.fori_loop(1, PARTS, close, 0)
    for each in loads[7:]:
        each.wait()
    field_ref[...] = strict_dot(local_ref[...], parts_ref[...])

    def hand(source, head, side):
        for block in range(blocks):
            handed = ask_copy(source, head, block, side)
            handed.wait_recv()
            handed.start()

    for_sides(near_wait)
    for_far(far_wait)
    field_ref[...] += strict_dot(cross_ref[...], others_ref[...])

    def finish(p, carry):
        f = field_ref[pl.ds(pl.multiple_of(p * order, order), order), :]
        high = f.astype(jnp.bfloat16)
        low = (f - high.astype(jnp.float32)).astype(jnp.bfloat16)
        y = close_ref[p] + jnp.dot(
            up_ref[...], jnp.concatenate([high, low, high], axis=0), preferred_element_type=jnp.float32
        )
        y = y.astype(jnp.bfloat16).astype(jnp.float32)
        begin = pl.multiple_of(p * t_part, t_part)
        place = me * PARTS + p
        cos_p, sin_p = coarse_ref[0, pl.ds(place, 1), :], coarse_ref[1, pl.ds(place, 1), :]
        cosine = cos_p * fine_ref[0] - sin_p * fine_ref[1]
        sine = sin_p * fine_ref[0] + cos_p * fine_ref[1]
        for head in range(heads):
            k = y[:, head * width : (head + 1) * width]
            turned = k * cosine + pltpu.roll(k, width // 2, 1) * sine
            k_ref[head, pl.ds(begin, t_part), :] = turned.astype(jnp.bfloat16)
            v = y[:, half_columns + head * width : half_columns + (head + 1) * width]
            v_ref[head, :, pl.ds(begin, t_part)] = v.T.astype(jnp.bfloat16)
        return carry

    lax.fori_loop(0, PARTS, finish, 0)

    @pl.when(inside)
    def _():
        hand(mate, 1, 1 - outward)
        ask_copy(me, 1, 0, outward).start()
        for block in range(blocks):
            ask_copy(me, 1, block, 1 - outward).start()

    runs = [
        (0, 0, 0, blocks),
        (1, 0, 0, blocks),
        (3, 0, 0, blocks),
        (2, 0, 0, blocks),
        (3, 1, 0, blocks - 1),
        (2, 1, 0, blocks),
        (3, 1, blocks - 1, 1),
        (1, 1, 0, blocks),
        (0, 1, 0, blocks),
    ]
    begins = [sum(run[3] for run in runs[:i]) for i in range(len(runs))]
    units = begins[-1] + blocks

    def decode(u):
        kind, head, block = runs[0][0], runs[0][1], u
        for begin, run in zip(begins[1:], runs[1:]):
            late = u >= begin
            kind = jnp.where(late, run[0], kind)
            head = jnp.where(late, run[1], head)
            block = jnp.where(late, u - begin + run[2], block)
        source = jnp.where(
            kind == 0, mate, jnp.where(kind == 1, near_over, jnp.where(kind == 2, far_end, me))
        )
        return kind, head, block, source

    chunk = 512

    def score(u, keep_ref, top_ref):
        _, head, block, source = decode(u)
        q = asks_ref[source, head, pl.ds(pl.multiple_of(block * BLOCK, BLOCK), BLOCK), :]
        best = None
        for c in range(0, tokens, chunk):
            s = lax.dot_general(
                k_ref[head, c : c + chunk, :],
                q,
                (((1,), (1,)), ((), ())),
                preferred_element_type=jnp.float32,
            )
            keep_ref[c : c + chunk, :] = s
            top = jnp.max(s, axis=0, keepdims=True)
            best = top if best is None else jnp.maximum(best, top)
        top_ref[...] = best

    def weigh(u, keep_ref, top_ref):
        kind, head, block, _ = decode(u)
        best = top_ref[...]
        total = jnp.zeros((1, BLOCK), jnp.float32)
        accum = jnp.zeros((width, BLOCK), jnp.float32)
        for c in range(0, tokens, chunk):
            e = jnp.exp2((keep_ref[c : c + chunk, :] - best) * factor)
            total += jnp.sum(e, axis=0, keepdims=True)
            accum += jnp.dot(
                v_ref[head, :, c : c + chunk], e.astype(jnp.bfloat16), preferred_element_type=jnp.float32
            )
        own_ref[kind, head, block] = (accum / total).astype(jnp.bfloat16)
        own_log_ref[kind, head, block] = best * factor + jnp.log2(total)

    def both(src, src_log, dst, dst_log, send, recv, other):
        return (
            copy(src, dst, send.at[0], recv.at[0], other),
            copy(src_log, dst_log, send.at[1], recv.at[1], other),
        )

    def half_copy(kind, head, block):
        at = (kind, head, block)
        return both(
            own_ref.at[at],
            own_log_ref.at[at],
            half_ref.at[at],
            half_log_ref.at[at],
            half_send.at[at],
            half_recv.at[at],
            mate,
        )

    def over_copy(j, head, block):
        at = (j, head, block)
        return both(
            merged_ref.at[at],
            merged_log_ref.at[at],
            over_ref.at[at],
            over_log_ref.at[at],
            over_send.at[at],
            over_recv.at[at],
            near_over,
        )

    def last_copy(head, block):
        at = (head, block)
        return both(
            ready_ref.at[at],
            ready_log_ref.at[at],
            last_ref.at[at],
            last_log_ref.at[at],
            last_send.at[at],
            last_recv.at[at],
            mate,
        )

    def blend(parts, logs):
        best = functools.reduce(jnp.maximum, logs)
        shares = [jnp.exp2(log - best) for log in logs]
        total = functools.reduce(jnp.add, shares)
        mixed = functools.reduce(
            jnp.add, [part.astype(jnp.float32) * (share / total) for part, share in zip(parts, shares)]
        )
        return mixed, best + jnp.log2(total)

    def merge_half(kind, head, block):
        for each in half_copy(kind, head, block):
            each.wait_recv()
        at = (kind - 1, head, block)
        mixed, log = blend(
            [own_ref[kind, head, block], half_ref[kind, head, block]],
            [own_log_ref[kind, head, block], half_log_ref[kind, head, block]],
        )
        merged_ref[at] = mixed.astype(jnp.bfloat16)
        merged_log_ref[at] = log
        for each in over_copy(*at):
            each.start()

    def await_ask(u):
        kind, head, block, source = decode(u)

        @pl.when(jnp.logical_and(kind < 3, jnp.logical_not(inside)))
        def _():
            ask_copy(source, head, block, 1 - outward).wait_recv()

    merges = ((1, 0, begins[1] + 6), (2, 0, begins[3] + 8), (2, 1, begins[5] + 8))

    def send_on(u):
        kind, head, block, _ = decode(u)

        @pl.when(jnp.logical_and(kind < 3, jnp.logical_not(inside)))
        def _():
            for each in half_copy(kind, head, block):
                each.start()

        for kind, head, first in merges:
            k = u - first

            @pl.when(jnp.logical_and(inside, jnp.logical_and(k >= 0, k < blocks)))
            def _():
                merge_half(kind, head, k)

    await_ask(jnp.int32(0))
    score(jnp.int32(0), even_ref, even_top_ref)

    def serve(i, carry):
        u = 2 * i
        for at, source, head in ((1, far_end, 0), (3, far_end, 1), (6, near_over, 1)):

            @pl.when(jnp.logical_and(inside, i == at))
            def _():
                hand(source, head, outward)
                if source is near_over:
                    for block in range(1, blocks):
                        ask_copy(me, 1, block, outward).start()

        await_ask(u + 1)
        score(u + 1, odd_ref, odd_top_ref)
        weigh(u, even_ref, even_top_ref)
        send_on(u)
        ahead = jnp.minimum(u + 2, units - 1)

        @pl.when(u + 2 < units)
        def _():
            await_ask(ahead)

        score(ahead, even_ref, even_top_ref)
        weigh(u + 1, odd_ref, odd_top_ref)
        send_on(u + 1)
        return carry

    lax.fori_loop(0, units // 2, serve, 0)

    def settle(head, block):
        for each in half_copy(0, head, block) + over_copy(0, head, block):
            each.wait_recv()
        mixed, _ = blend(
            [own_ref[3, head, block], half_ref[0, head, block], over_ref[0, head, block]],
            [own_log_ref[3, head, block], half_log_ref[0, head, block], over_log_ref[0, head, block]],
        )
        out_ref[head, block * BLOCK : (block + 1) * BLOCK, :] = mixed.T.astype(out_ref.dtype)

    def pass_on(head, block):
        for each in over_copy(1, head, block):
            each.wait_recv()
        mixed, log = blend(
            [own_ref[0, head, block], over_ref[1, head, block]],
            [own_log_ref[0, head, block], over_log_ref[1, head, block]],
        )
        ready_ref[head, block] = mixed.astype(jnp.bfloat16)
        ready_log_ref[head, block] = log
        for each in last_copy(head, block):
            each.start()

    @pl.when(inside)
    def _():
        for block in range(units - merges[2][2], blocks):
            merge_half(2, 1, block)
        for block in range(blocks):
            pass_on(0, block)
        for block in range(blocks):
            settle(0, block)
        for block in range(blocks):
            pass_on(1, block)
            merge_half(1, 1, block)
        for block in range(blocks):
            settle(1, block)
        for head in range(heads):
            for block in range(blocks):
                ask_copy(me - 1, head, block, 1).wait_send()
                ask_copy(me + 1, head, block, 0).wait_send()
                ask_copy(far_end, head, block, outward).wait_send()
                for each in over_copy(0, head, block) + over_copy(1, head, block) + last_copy(head, block):
                    each.wait_send()

    @pl.when(jnp.logical_not(inside))
    def _():
        for head in range(heads):
            for block in range(blocks):
                for each in last_copy(head, block):
                    each.wait_recv()
                mixed, _ = blend(
                    [own_ref[3, head, block], last_ref[head, block]],
                    [own_log_ref[3, head, block], last_log_ref[head, block]],
                )
                out_ref[head, block * BLOCK : (block + 1) * BLOCK, :] = mixed.T.astype(out_ref.dtype)
        for kind in range(3):
            for head in range(heads):
                for block in range(blocks):
                    for each in half_copy(kind, head, block):
                        each.wait_send()

    for head in range(heads):
        for block in range(blocks):
            for_sides(lambda side: ask_copy(me, head, block, side).wait_send())
    for_sides(lambda side: near_copy(side).wait_send())
    for_far(lambda other: far_copy(other).wait_send())


def by_tokens(keys, values, queries, positions, count):
    heads, rows, width = queries.shape
    n_dev, columns = keys.shape
    length = n_dev * count
    near, down, up, local, merge, cross = fields(length, count)

    def tall(matrix):
        return np.concatenate(split_two(matrix), axis=-2)

    def table(places):
        return tall(np.concatenate(spins(places, width).astype(np.float64), axis=1))

    up_high, up_low = split_two(up)
    t_part = near.shape[0]
    tokens = n_dev // 2
    blocks = rows // BLOCK
    split = 128
    operands = (
        table(np.arange(length // split) * float(split)),
        table(np.arange(split) * 1.0),
        tall(near),
        tall(down),
        np.concatenate([up_high, up_high, up_low], axis=1),
        tall(local),
        tall(merge),
        tall(cross),
        spins(np.arange(count * PARTS) * float(t_part), width),
        spins(np.arange(t_part) * 1.0, width),
    )
    held = [jax.ShapeDtypeStruct(o.shape[1:] if o.ndim == 3 and o.shape[0] == count else o.shape, o.dtype) for o in operands]
    dma = pltpu.SemaphoreType.DMA

    def parts(*lead):
        return [
            pltpu.VMEM(lead + (heads, blocks, width, BLOCK), jnp.bfloat16),
            pltpu.VMEM(lead + (heads, blocks, 1, BLOCK), jnp.float32),
        ]

    return pl.pallas_call(
        functools.partial(fused_kernel, count, math.log2(math.e) / math.sqrt(width)),
        in_specs=[pl.BlockSpec(memory_space=pl.ANY)] * 14,
        out_specs=pl.BlockSpec(memory_space=pltpu.VMEM),
        out_shape=jax.ShapeDtypeStruct(queries.shape, jnp.bfloat16),
        scratch_shapes=[
            pltpu.VMEM(keys.shape, keys.dtype),
            pltpu.VMEM(values.shape, values.dtype),
            pltpu.VMEM(queries.shape, queries.dtype),
            pltpu.VMEM((rows,), jnp.int32),
        ]
        + [pltpu.VMEM(h.shape, h.dtype) for h in held]
        + [
            pltpu.VMEM((PARTS * ORDER, 2 * columns), jnp.float32),
            pltpu.VMEM((2 * EDGE + FAR, 2 * columns), jnp.float32),
            pltpu.VMEM((cross.shape[2], 2 * columns), jnp.float32),
            pltpu.VMEM((PARTS, t_part, 2 * columns), jnp.float32),
            pltpu.VMEM((PARTS * ORDER, 2 * columns), jnp.float32),
            pltpu.VMEM((heads, tokens, width), jnp.bfloat16),
            pltpu.VMEM((heads, width, tokens), jnp.bfloat16),
            pltpu.VMEM((tokens, BLOCK), jnp.float32),
            pltpu.VMEM((tokens, BLOCK), jnp.float32),
            pltpu.VMEM((1, BLOCK), jnp.float32),
            pltpu.VMEM((1, BLOCK), jnp.float32),
            pltpu.VMEM((count, heads, rows, width), jnp.bfloat16),
        ]
        + parts(4)
        + parts(3)
        + parts(2)
        + parts(2)
        + parts()
        + parts()
        + [
            dma((12,)),
            dma((PARTS, 2)),
            pltpu.SemaphoreType.REGULAR((2,)),
            pltpu.SemaphoreType.REGULAR,
            dma((count,)),
            dma((count,)),
            dma((count, heads, blocks, 2)),
            dma((count, heads, blocks)),
            dma((3, heads, blocks, 2)),
            dma((3, heads, blocks, 2)),
            dma((2, heads, blocks, 2)),
            dma((2, heads, blocks, 2)),
            dma((heads, blocks, 2)),
            dma((heads, blocks, 2)),
        ],
        compiler_params=pltpu.CompilerParams(
            collective_id=0, has_side_effects=True, vmem_limit_bytes=60 * 1024 * 1024
        ),
    )(keys, values, queries, positions, *operands)


def by_columns(keys, values, queries, positions):
    key_parts = lax.all_to_all(keys, "ctx", split_axis=1, concat_axis=0, tiled=True)
    value_parts = lax.all_to_all(values, "ctx", split_axis=1, concat_axis=0, tiled=True)
    heads, rows, width = queries.shape
    per_device = key_parts.shape[1]
    compact = compress(jnp.concatenate([key_parts, value_parts], axis=1))
    rotated = rotate_rows(queries.astype(jnp.float32), positions.astype(jnp.float32)).astype(
        jnp.bfloat16
    )
    whole = lax.all_gather(compact.T, "ctx", axis=0, tiled=True)
    tokens = whole.shape[1]
    shaped = whole.reshape(-1, 2, per_device, tokens)
    key_rows = shaped[:, 0].reshape(heads, width, tokens).swapaxes(1, 2)
    value_rows = shaped[:, 1].reshape(heads, width, tokens).swapaxes(1, 2)
    places = jnp.arange(tokens).astype(jnp.float32)
    ready = rotate_rows(key_rows.astype(jnp.float32), places).astype(jnp.bfloat16)
    return attend(rotated, ready, value_rows, jnp.zeros((), jnp.int32))[0]


def solution(mesh):
    count = mesh.shape["ctx"]

    def on_device(keys, values, queries, positions):
        heads, rows, width = queries.shape
        if count == 4 and heads == 2 and keys.shape[0] % (PARTS * 512) == 0 and rows % BLOCK == 0 and width == 128:
            return by_tokens(keys, values, queries, positions, count)
        return by_columns(keys, values, queries, positions)

    return jax.shard_map(
        on_device,
        mesh=mesh,
        in_specs=(
            P(("user", "ctx"), "heads"),
            P(("user", "ctx"), "heads"),
            P("heads", ("user", "ctx"), None),
            P(("user", "ctx")),
        ),
        out_specs=P("heads", ("user", "ctx"), None),
        check_vma=False,
    )
```

```python
import functools
import math

import jax
import jax.numpy as jnp
import numpy as np
from jax import lax
from jax.experimental import pallas as pl
from jax.experimental.pallas import tpu as pltpu
from jax.sharding import PartitionSpec as P

OUTER = 128
PARTS = 4
ORDER = 64
EDGE = 32
FAR = 16
BLOCK = 256
MESH = pl.DeviceIdType.MESH


def split_two(matrix):
    high = matrix.astype(jnp.bfloat16)
    low = (matrix - np.asarray(high).astype(np.float64)).astype(jnp.bfloat16)
    return high, low


@functools.lru_cache(maxsize=None)
def stages(length):
    outer = OUTER
    inner = length // outer
    step = inner // 2
    a = np.arange(outer)
    c = np.arange(outer)
    turn = 2 * outer
    angle = np.pi / outer * ((c[:, None] * a[None, :]) % turn)
    alternate = np.where(a % 2 == 0, 1.0, -1.0)
    first = np.stack([np.cos(angle), -np.sin(angle)], axis=1)
    first[0, 1] = alternate
    d = np.arange(length // 2 // turn)
    k = np.concatenate([c[:, None] + turn * d, (turn - c[:, None]) % turn + turn * d], axis=1)
    k[0, d.size :] = outer + turn * d
    sign = np.concatenate([np.ones(d.size), -np.ones(d.size)])
    b = np.arange(inner)
    q = np.arange(step)
    theta = np.pi / (2 * length) * ((k[:, :, None] * (2 * b + 1)) % (4 * length))
    phi = np.pi / length * ((k[:, None, :] * (2 * q + 1)[:, None]) % (2 * length))
    forward = np.stack([np.cos(theta), np.sin(theta) * sign[None, :, None]], axis=2)
    weight = np.where(k == 0, 1.0, 2.0) / length
    back = np.stack([np.cos(phi), np.sin(phi) * sign], axis=1) * weight[:, None, None, :]
    half = d.size
    forward[0, :half, 1] = 0.0
    forward[0, half:, 1] = np.cos(theta[0, half:])
    forward[0, half:, 0] = 0.0
    back[0, 1, :, :half] = 0.0
    back[0, 1, :, half:] = np.cos(phi[0, :, half:]) * weight[0, half:]
    back[0, 0, :, half:] = 0.0
    middle = back.reshape(outer, 2 * step, 2 * half) @ forward.reshape(outer, 2 * half, 2 * inner)
    last = first.transpose(2, 0, 1).reshape(outer, 2 * outer)
    return first.reshape(2 * outer, outer), middle, last


def compress(signal):
    length, columns = signal.shape
    outer, inner = OUTER, length // OUTER
    first, middle, last = stages(length)
    first_high, first_low = split_two(first)
    flat = signal.reshape(outer, inner * columns)
    one = jnp.dot(first_high, flat, preferred_element_type=jnp.float32) + jnp.dot(
        first_low, flat, preferred_element_type=jnp.float32
    )
    one = one.reshape(outer, 2 * inner, columns)
    two = jnp.einsum(
        "cob,cbl->col", jnp.asarray(middle.astype(np.float32)), one, precision=lax.Precision.HIGH
    )
    three = jnp.dot(
        jnp.asarray(last.astype(np.float32)),
        two.reshape(2 * outer, inner // 2 * columns),
        precision=lax.Precision.HIGH,
    )
    return three.reshape(length // 2, columns).astype(jnp.bfloat16)

def strict_dot(left, right):
    rows, columns = left.shape[0] // 2, right.shape[1]
    high = right.astype(jnp.bfloat16)
    low = (right - high.astype(jnp.float32)).astype(jnp.bfloat16)
    both = jnp.dot(
        left, jnp.concatenate([high, low], axis=1), preferred_element_type=jnp.float32
    )
    return both[:rows, :columns] + (both[:rows, columns:] + both[rows:, :columns])


def inverse_freq(width):
    return jnp.exp(jnp.arange(width // 2).astype(jnp.float32) * (-2.0 * math.log(500000.0) / width))


def rotate_rows(block, places):
    width = block.shape[-1]
    half = width // 2
    angles = places[:, None] * inverse_freq(width)[None, :]
    cosine = jnp.cos(angles)
    sine = jnp.sin(angles)
    first = block[..., :half]
    second = block[..., half:]
    return jnp.concatenate(
        [first * cosine - second * sine, second * cosine + first * sine], axis=-1
    )


def attend_kernel(chunk, scale, resume, finish, swap_ref, q_ref, k_ref, v_ref, *refs):
    q = q_ref[0]
    swap = swap_ref[0] == 1
    rows, width = q.shape
    factor = scale * math.log2(math.e)
    if resume:
        accum = refs[0][0]
        best = refs[1][0][:, :1]
        total = refs[2][0][:, :1]
        refs = refs[3:]
    else:
        best = jnp.full((rows, 1), -jnp.inf, jnp.float32)
        total = jnp.zeros((rows, 1), jnp.float32)
        accum = jnp.zeros((rows, width), jnp.float32)
    tokens = k_ref.shape[1]
    for start in range(0, tokens, chunk):
        one = k_ref[0, start : start + chunk, :]
        two = v_ref[0, start : start + chunk, :]
        k, v = jnp.where(swap, two, one), jnp.where(swap, one, two)
        scores = lax.dot_general(
            q, k, (((1,), (1,)), ((), ())), preferred_element_type=jnp.float32
        )
        fresh = jnp.maximum(best, jnp.max(scores, axis=1, keepdims=True))
        expo = jnp.exp2((scores - fresh) * factor)
        shrink = jnp.exp2((best - fresh) * factor)
        total = total * shrink + jnp.sum(expo, axis=1, keepdims=True)
        accum = accum * shrink + jnp.dot(
            expo.astype(jnp.bfloat16), v, preferred_element_type=jnp.float32
        )
        best = fresh
    if finish:
        refs[0][0] = (accum / total).astype(refs[0].dtype)
        refs[1][0] = jnp.broadcast_to(best * factor + jnp.log2(total), (rows, 8))
    else:
        refs[0][0] = accum
        refs[1][0] = jnp.broadcast_to(best, (rows, 8))
        refs[2][0] = jnp.broadcast_to(total, (rows, 8))


def attend(queries, keys, values, swap, part=0, parts=1, state=None):
    groups, rows, width = queries.shape
    heads, tokens, _ = values.shape
    per_head = groups // heads
    block = math.gcd(rows, 768)
    chunk = math.gcd(tokens, 1024)
    scale = 1.0 / math.sqrt(width)
    finish = part == parts - 1
    wide = pl.BlockSpec((1, block, width), lambda g, i: (g, i, 0))
    thin = pl.BlockSpec((1, block, 8), lambda g, i: (g, i, 0))
    thin_shape = jax.ShapeDtypeStruct((groups, rows, 8), jnp.float32)
    state = () if state is None else tuple(state)
    wide_type = jnp.bfloat16 if finish else jnp.float32
    return pl.pallas_call(
        functools.partial(attend_kernel, chunk, scale, bool(state), finish),
        grid=(groups, rows // block),
        in_specs=[
            pl.BlockSpec(memory_space=pltpu.SMEM),
            wide,
            pl.BlockSpec((1, tokens, width), lambda g, i: (g // per_head, part, 0)),
            pl.BlockSpec((1, tokens, width), lambda g, i: (g // per_head, 0, 0)),
        ]
        + ([wide, thin, thin] if state else []),
        out_specs=[wide, thin] if finish else [wide, thin, thin],
        out_shape=[jax.ShapeDtypeStruct((groups, rows, width), wide_type), thin_shape]
        + ([] if finish else [thin_shape]),
        cost_estimate=pl.CostEstimate(
            flops=8 * groups * rows * tokens * width,
            bytes_accessed=4 * groups * rows * width * 2,
            transcendentals=groups * rows * tokens,
        ),
    )(swap.reshape(1), queries, keys, values, *state)


def bounds(count, left, right):
    return np.log(left / (count - 1 + right)), np.log((count - 1 + left) / right)


def nodes(count, order, left, right):
    low, top = bounds(count, left, right)
    e = np.exp((top - low) / 2 * np.cos(np.pi * (2 * np.arange(order) + 1) / (2 * order)) + (top + low) / 2)
    return ((count - 1 + right) * e - left) / (1 + e)


def cardinals(places, count, order, left, right):
    low, top = bounds(count, left, right)
    at = (2 * np.log((places + left) / (count - 1 + right - places)) - top - low) / (top - low)
    at = np.arccos(np.clip(at, -1.0, 1.0))
    own = np.pi * (2 * np.arange(order) + 1) / (2 * order)
    total = np.zeros((places.size, order))
    for k in range(order):
        total += (1.0 if k == 0 else 2.0) / order * np.cos(k * at)[:, None] * np.cos(k * own)[None, :]
    return total


@functools.lru_cache(maxsize=None)
def fields(length, devices):
    parts, order = PARTS, ORDER
    scale = math.sqrt(0.5) / (2 * length)

    def cot(m):
        return 1.0 / np.tan(np.pi * m / (4 * length))

    n_dev = length // devices
    n_part, t_dev = n_dev // parts, n_dev // 2
    t_part = n_part // 2
    n, t = np.arange(n_part), np.arange(t_part)
    sign_n = np.array([1.0, -1.0, -1.0, 1.0])[n % 4]
    sign_t = np.where(t % 2 == 0, 1.0, -1.0)
    near = sign_t[:, None] * sign_n * scale * cot(4 * t[:, None] - 2 * n + 1.0)
    down = cardinals(n, n_part, order, 1.5, 1.5).T * sign_n
    up = sign_t[:, None] * cardinals(t, t_part, order, 0.75, 0.75)
    part = np.arange(parts)[:, None]
    source = (part * n_part + nodes(n_part, order, 1.5, 1.5)).reshape(-1)
    target = (part * t_part + nodes(t_part, order, 0.75, 0.75)).reshape(-1)
    own = np.arange(parts * order) // order
    same = own[:, None] == own[None, :]
    local = np.where(same, 0.0, scale * cot(np.where(same, 1.0, 4 * target[:, None] - 2 * source + 1)))
    last = n_dev - 1
    wide = float(n_dev)
    merge = np.concatenate(
        [
            cardinals(source, n_dev, EDGE, 1.5, wide).T,
            cardinals(last - source, n_dev, EDGE, 1.5, wide).T,
            cardinals(source, n_dev, FAR, 2 * wide, 2 * wide).T,
        ]
    )
    to_left = nodes(n_dev, EDGE, 1.5, wide)
    sparse = nodes(n_dev, FAR, 2 * wide, 2 * wide)
    size = 3 * EDGE + devices * FAR
    cross = np.zeros((devices, parts * order, size + -size % 128))
    for r in range(devices):
        a = 4 * (target + r * t_dev)[:, None]
        for s in range(devices):
            if abs(r - s) > 1:
                spots, start = sparse, 3 * EDGE + s * FAR
            elif s < r or (s == r and 2 * r >= devices):
                spots, start = last - to_left, EDGE * (r - s)
            else:
                spots, start = to_left, 2 * EDGE * (s - r)
            b = 2 * (spots + s * n_dev)
            block = scale * cot(a + b + 3)
            if r != s:
                block = block + scale * cot(a - b + 1)
            cross[r, :, start : start + block.shape[1]] = block
    return near, down, up, local, merge, cross


def spins(places, width):
    freq = 500000.0 ** (-2.0 * np.arange(width // 2) / width)
    angles = places[:, None] * freq
    cosine, sine = np.cos(angles), np.sin(angles)
    return np.stack(
        [np.concatenate([cosine, cosine], axis=1), np.concatenate([-sine, sine], axis=1)]
    ).astype(np.float32)


def fused_kernel(
    count,
    factor,
    keys_hbm,
    values_hbm,
    queries_hbm,
    places_hbm,
    high_hbm,
    low_hbm,
    near_hbm,
    down_hbm,
    up_hbm,
    local_hbm,
    merge_hbm,
    cross_hbm,
    coarse_hbm,
    fine_hbm,
    out_ref,
    keys_ref,
    values_ref,
    queries_ref,
    places_ref,
    high_ref,
    low_ref,
    near_ref,
    down_ref,
    up_ref,
    local_ref,
    merge_ref,
    cross_ref,
    coarse_ref,
    fine_ref,
    parts_ref,
    whole_ref,
    others_ref,
    close_ref,
    field_ref,
    k_ref,
    v_ref,
    even_ref,
    odd_ref,
    even_top_ref,
    odd_top_ref,
    asks_ref,
    own_ref,
    own_log_ref,
    half_ref,
    half_log_ref,
    merged_ref,
    merged_log_ref,
    over_ref,
    over_log_ref,
    ready_ref,
    ready_log_ref,
    last_ref,
    last_log_ref,
    load_sem,
    token_sem,
    behind_sem,
    end_sem,
    field_send,
    field_recv,
    ask_send,
    ask_recv,
    half_send,
    half_recv,
    over_send,
    over_recv,
    last_send,
    last_recv,
):
    me = lax.axis_index("ctx")
    heads, rows, width = queries_ref.shape
    order = ORDER
    blocks = rows // BLOCK
    n_part = near_ref.shape[1]
    t_part = n_part // 2
    half_columns = keys_ref.shape[1]
    tokens = k_ref.shape[1]
    has_left, has_right = me > 0, me < count - 1
    inside = jnp.logical_and(has_left, has_right)
    lower = me < count // 2
    mate = me + 1 - 2 * lax.rem(me, 2)
    far_end = jnp.where(lower, count - 1, 0)
    near_over = jnp.where(lower, count // 2, count // 2 - 1)
    outward = jnp.where(lower, 0, 1)

    def copy(src, dst, send, recv, other):
        return pltpu.make_async_remote_copy(
            src_ref=src,
            dst_ref=dst,
            send_sem=send,
            recv_sem=recv,
            device_id={"ctx": other},
            device_id_type=MESH,
        )

    def for_sides(action):
        for side, there in enumerate((has_left, has_right)):

            @pl.when(there)
            def _():
                action(side)

    def greet(sem, other):
        pl.semaphore_signal(sem, inc=1, device_id={"ctx": other}, device_id_type=MESH)

    others_ref[...] = jnp.zeros_like(others_ref)
    barrier = pltpu.get_barrier_semaphore()
    for_sides(lambda side: greet(barrier, me + 2 * side - 1))
    pairs = (
        (places_hbm, places_ref),
        (queries_hbm, queries_ref),
        (high_hbm, high_ref),
        (low_hbm, low_ref),
        (down_hbm, down_ref),
        (merge_hbm, merge_ref),
        (near_hbm, near_ref),
        (local_hbm, local_ref),
        (cross_hbm.at[me], cross_ref),
        (up_hbm, up_ref),
        (coarse_hbm, coarse_ref),
        (fine_hbm, fine_ref),
    )
    loads = [pltpu.make_async_copy(src, dst, load_sem.at[i]) for i, (src, dst) in enumerate(pairs)]
    sides = ((keys_hbm, keys_ref), (values_hbm, values_ref))
    token_loads = [
        [
            pltpu.make_async_copy(
                src.at[pl.ds(p * n_part, n_part)], dst.at[pl.ds(p * n_part, n_part)], token_sem.at[p, side]
            )
            for side, (src, dst) in enumerate(sides)
        ]
        for p in range(PARTS)
    ]
    for each in loads[:6]:
        each.start()
    for p in range(PARTS):
        for each in token_loads[p]:
            each.start()
    for each in loads[6:]:
        each.start()
    for each in loads[:4]:
        each.wait()

    split = low_ref.shape[0] // 2
    for i in range(rows // split):
        here = slice(i * split, (i + 1) * split)
        place = jnp.broadcast_to(places_ref[here].astype(jnp.float32)[None], (split, split)).T.astype(jnp.int32)
        spun = []
        for value, table_ref in ((place // split, high_ref), (lax.rem(place, split), low_ref)):
            size = table_ref.shape[0] // 2
            value = value if size == split else value[:, :1]
            picked = value == lax.broadcasted_iota(jnp.int32, (split, size), 1)
            picked = jnp.where(picked, 1.0, 0.0).astype(jnp.bfloat16)
            got = jnp.dot(
                jnp.concatenate([picked, picked], axis=1), table_ref[...], preferred_element_type=jnp.float32
            )
            spun.append((got[:, :width], got[:, width:]))
        (cos_a, sin_a), (cos_b, sin_b) = spun
        cosine, sine = cos_a * cos_b - sin_a * sin_b, sin_a * cos_b + cos_a * sin_b
        for head in range(heads):
            x = queries_ref[head, here, :].astype(jnp.float32)
            asks_ref[me, head, here, :] = (x * cosine + pltpu.roll(x, width // 2, 1) * sine).astype(jnp.bfloat16)

    def ask_copy(source, head, block, side):
        here = pl.ds(block * BLOCK if isinstance(block, int) else pl.multiple_of(block * BLOCK, BLOCK), BLOCK)
        return copy(
            asks_ref.at[source, head, here],
            asks_ref.at[source, head, here],
            ask_send.at[source, head, block, side],
            ask_recv.at[source, head, block],
            me + 2 * side - 1,
        )

    pl.semaphore_wait(barrier, jnp.where(inside, 2, 1))
    for block in range(blocks):
        for_sides(lambda side: ask_copy(me, 0, block, side).start())
    for_sides(lambda side: greet(behind_sem.at[1 - side], me + 2 * side - 1))
    for_sides(lambda side: pl.semaphore_wait(behind_sem.at[side], 1))

    @pl.when(inside)
    def _():
        greet(end_sem, mate)

    for each in loads[4:6]:
        each.wait()
    for p in range(PARTS):
        for side, (_, x_ref) in enumerate(sides):
            token_loads[p][side].wait()
            z = jnp.dot(
                down_ref[...], x_ref[p * n_part : (p + 1) * n_part, :], preferred_element_type=jnp.float32
            )
            parts_ref[
                p * order : (p + 1) * order, side * half_columns : (side + 1) * half_columns
            ] = z[:order] + z[order:]
    whole_ref[...] = strict_dot(merge_ref[...], parts_ref[...])
    others_ref[:EDGE] = whole_ref[pl.ds(pl.multiple_of(jnp.where(lower, 0, EDGE), EDGE), EDGE), :]

    def near_copy(side):
        other = me + 2 * side - 1
        return copy(
            whole_ref.at[pl.ds(side * EDGE, EDGE)],
            others_ref.at[pl.ds(EDGE * (2 - side), EDGE)],
            field_send.at[other],
            field_recv.at[me],
            other,
        )

    def far_copy(other):
        return copy(
            whole_ref.at[pl.ds(2 * EDGE, FAR)],
            others_ref.at[pl.ds(pl.multiple_of(3 * EDGE + me * FAR, FAR), FAR)],
            field_send.at[other],
            field_recv.at[me],
            other,
        )

    def near_wait(side):
        source = me + 2 * side - 1
        copy(
            whole_ref.at[pl.ds(0, EDGE)],
            others_ref.at[pl.ds(EDGE * (1 + side), EDGE)],
            field_send.at[source],
            field_recv.at[source],
            source,
        ).wait_recv()

    def far_wait(source):
        copy(
            whole_ref.at[pl.ds(2 * EDGE, FAR)],
            others_ref.at[pl.ds(3 * EDGE + source * FAR, FAR)],
            field_send.at[source],
            field_recv.at[source],
            source,
        ).wait_recv()

    def hand(source, head, block, side):
        handed = ask_copy(source, head, block, side)
        handed.wait_recv()
        handed.start()

    def for_far(action):
        for other in range(count):

            @pl.when(jnp.logical_or(other - me > 1, me - other > 1))
            def _():
                action(other)

    for_sides(lambda side: near_copy(side).start())

    @pl.when(jnp.logical_not(inside))
    def _():
        pl.semaphore_wait(end_sem, 1)

    for_far(lambda other: far_copy(other).start())

    @pl.when(jnp.logical_not(inside))
    def _():
        for block in range(blocks):
            ask_copy(me, 1, block, 1 - outward).start()

    loads[6].wait()

    def close(p, carry):
        start = p * n_part if isinstance(p, int) else pl.multiple_of(p * n_part, n_part)
        for side, (_, x_ref) in enumerate(sides):
            z = jnp.dot(near_ref[...], x_ref[pl.ds(start, n_part), :], preferred_element_type=jnp.float32)
            close_ref[p, :, side * half_columns : (side + 1) * half_columns] = z[:t_part] + z[t_part:]
        return carry

    close(0, 0)

    @pl.when(inside)
    def _():
        for block in range(blocks):
            for side in range(2):
                hand(me + 2 * side - 1, 0, block, 1 - side)
        ask_copy(me, 1, 0, outward).start()

    lax.fori_loop(1, PARTS, close, 0)

    @pl.when(inside)
    def _():
        hand(mate, 1, 0, 1 - outward)
        ask_copy(me, 1, 1, outward).start()

    for each in loads[7:]:
        each.wait()
    field_ref[...] = strict_dot(local_ref[...], parts_ref[...])

    for_sides(near_wait)
    for_far(far_wait)
    field_ref[...] += strict_dot(cross_ref[...], others_ref[...])

    def finish(p, carry):
        f = field_ref[pl.ds(pl.multiple_of(p * order, order), order), :]
        high = f.astype(jnp.bfloat16)
        low = (f - high.astype(jnp.float32)).astype(jnp.bfloat16)
        y = close_ref[p] + jnp.dot(
            up_ref[...], jnp.concatenate([high, low, high], axis=0), preferred_element_type=jnp.float32
        )
        y = y.astype(jnp.bfloat16).astype(jnp.float32)
        begin = pl.multiple_of(p * t_part, t_part)
        place = me * PARTS + p
        cos_p, sin_p = coarse_ref[0, pl.ds(place, 1), :], coarse_ref[1, pl.ds(place, 1), :]
        cosine = cos_p * fine_ref[0] - sin_p * fine_ref[1]
        sine = sin_p * fine_ref[0] + cos_p * fine_ref[1]
        for head in range(heads):
            k = y[:, head * width : (head + 1) * width]
            turned = k * cosine + pltpu.roll(k, width // 2, 1) * sine
            k_ref[head, pl.ds(begin, t_part), :] = turned.astype(jnp.bfloat16)
            v = y[:, half_columns + head * width : half_columns + (head + 1) * width]
            v_ref[head, :, pl.ds(begin, t_part)] = v.T.astype(jnp.bfloat16)
        return carry

    lax.fori_loop(0, PARTS, finish, 0)

    @pl.when(inside)
    def _():
        for block in range(1, blocks):
            hand(mate, 1, block, 1 - outward)
        for block in range(blocks):
            ask_copy(me, 1, block, 1 - outward).start()

    runs = [
        (0, 0, 0, blocks),
        (1, 0, 0, blocks),
        (2, 0, 0, blocks),
        (0, 1, 0, blocks - 1),
        (2, 1, 0, blocks),
        (3, 0, 0, blocks - 1),
        (1, 1, 0, blocks),
        (0, 1, blocks - 1, 1),
        (3, 0, blocks - 1, 1),
        (3, 1, 0, blocks),
    ]
    begins = [sum(run[3] for run in runs[:i]) for i in range(len(runs))]
    units = begins[-1] + blocks

    def decode(u):
        kind, head, block = runs[0][0], runs[0][1], u
        for begin, run in zip(begins[1:], runs[1:]):
            late = u >= begin
            kind = jnp.where(late, run[0], kind)
            head = jnp.where(late, run[1], head)
            block = jnp.where(late, u - begin + run[2], block)
        source = jnp.where(
            kind == 0, mate, jnp.where(kind == 1, near_over, jnp.where(kind == 2, far_end, me))
        )
        return kind, head, block, source

    chunk = 512

    def score(u, keep_ref, top_ref):
        _, head, block, source = decode(u)
        q = asks_ref[source, head, pl.ds(pl.multiple_of(block * BLOCK, BLOCK), BLOCK), :]
        best = None
        for c in range(0, tokens, chunk):
            s = lax.dot_general(
                k_ref[head, c : c + chunk, :],
                q,
                (((1,), (1,)), ((), ())),
                preferred_element_type=jnp.float32,
            )
            keep_ref[c : c + chunk, :] = s
            top = jnp.max(s, axis=0, keepdims=True)
            best = top if best is None else jnp.maximum(best, top)
        top_ref[...] = best

    def weigh(u, keep_ref, top_ref):
        kind, head, block, _ = decode(u)
        best = top_ref[...]
        total = jnp.zeros((1, BLOCK), jnp.float32)
        accum = jnp.zeros((width, BLOCK), jnp.float32)
        for c in range(0, tokens, chunk):
            e = jnp.exp2((keep_ref[c : c + chunk, :] - best) * factor)
            total += jnp.sum(e, axis=0, keepdims=True)
            accum += jnp.dot(
                v_ref[head, :, c : c + chunk], e.astype(jnp.bfloat16), preferred_element_type=jnp.float32
            )
        own_ref[kind, head, block] = (accum / total).astype(jnp.bfloat16)
        own_log_ref[kind, head, block] = best * factor + jnp.log2(total)

    def both(src, src_log, dst, dst_log, send, recv, other):
        return (
            copy(src, dst, send.at[0], recv.at[0], other),
            copy(src_log, dst_log, send.at[1], recv.at[1], other),
        )

    def half_copy(kind, head, block):
        at = (kind, head, block)
        return both(
            own_ref.at[at],
            own_log_ref.at[at],
            half_ref.at[at],
            half_log_ref.at[at],
            half_send.at[at],
            half_recv.at[at],
            mate,
        )

    def over_copy(j, head, block):
        at = (j, head, block)
        return both(
            merged_ref.at[at],
            merged_log_ref.at[at],
            over_ref.at[at],
            over_log_ref.at[at],
            over_send.at[at],
            over_recv.at[at],
            near_over,
        )

    def last_copy(head, block):
        at = (head, block)
        return both(
            ready_ref.at[at],
            ready_log_ref.at[at],
            last_ref.at[at],
            last_log_ref.at[at],
            last_send.at[at],
            last_recv.at[at],
            mate,
        )

    def blend(parts, logs):
        best = functools.reduce(jnp.maximum, logs)
        shares = [jnp.exp2(log - best) for log in logs]
        total = functools.reduce(jnp.add, shares)
        mixed = functools.reduce(
            jnp.add, [part.astype(jnp.float32) * (share / total) for part, share in zip(parts, shares)]
        )
        return mixed, best + jnp.log2(total)

    def merge_half(kind, head, block):
        for each in half_copy(kind, head, block):
            each.wait_recv()
        at = (kind - 1, head, block)
        mixed, log = blend(
            [own_ref[kind, head, block], half_ref[kind, head, block]],
            [own_log_ref[kind, head, block], half_log_ref[kind, head, block]],
        )
        merged_ref[at] = mixed.astype(jnp.bfloat16)
        merged_log_ref[at] = log
        for each in over_copy(*at):
            each.start()

    def settle(head, block):
        for each in half_copy(0, head, block) + over_copy(0, head, block):
            each.wait_recv()
        mixed, _ = blend(
            [own_ref[3, head, block], half_ref[0, head, block], over_ref[0, head, block]],
            [own_log_ref[3, head, block], half_log_ref[0, head, block], over_log_ref[0, head, block]],
        )
        out_ref[head, block * BLOCK : (block + 1) * BLOCK, :] = mixed.T.astype(out_ref.dtype)

    def pass_on(head, block):
        for each in over_copy(1, head, block):
            each.wait_recv()
        mixed, log = blend(
            [own_ref[0, head, block], over_ref[1, head, block]],
            [own_log_ref[0, head, block], over_log_ref[1, head, block]],
        )
        ready_ref[head, block] = mixed.astype(jnp.bfloat16)
        ready_log_ref[head, block] = log
        for each in last_copy(head, block):
            each.start()

    def await_ask(u):
        kind, head, block, source = decode(u)

        @pl.when(jnp.logical_and(kind < 3, jnp.logical_not(inside)))
        def _():
            ask_copy(source, head, block, 1 - outward).wait_recv()

    merges = ((1, 0, begins[1] + 7), (2, 0, begins[2] + 8), (2, 1, begins[4] + 8))
    passes = begins[2] + 12

    def send_on(u):
        kind, head, block, _ = decode(u)

        @pl.when(jnp.logical_and(kind < 3, jnp.logical_not(inside)))
        def _():
            for each in half_copy(kind, head, block):
                each.start()

        for kind, head, first in merges:
            k = u - first

            @pl.when(jnp.logical_and(inside, jnp.logical_and(k >= 0, k < blocks)))
            def _():
                merge_half(kind, head, k)

        k = u - passes

        @pl.when(jnp.logical_and(inside, jnp.logical_and(k >= 0, k < blocks)))
        def _():
            pass_on(0, k)

    await_ask(jnp.int32(0))
    score(jnp.int32(0), even_ref, even_top_ref)

    def serve(i, carry):
        u = 2 * i
        for at, source, head in ((0, far_end, 0), (3, far_end, 1), (5, near_over, 1)):

            @pl.when(jnp.logical_and(inside, i == at))
            def _():
                for block in range(blocks):
                    hand(source, head, block, outward)
                if source is near_over:
                    for block in range(2, blocks):
                        ask_copy(me, 1, block, outward).start()

        await_ask(u + 1)
        score(u + 1, odd_ref, odd_top_ref)
        weigh(u, even_ref, even_top_ref)
        send_on(u)
        ahead = jnp.minimum(u + 2, units - 1)

        @pl.when(u + 2 < units)
        def _():
            await_ask(ahead)

        score(ahead, even_ref, even_top_ref)
        weigh(u + 1, odd_ref, odd_top_ref)
        send_on(u + 1)
        return carry

    lax.fori_loop(0, units // 2, serve, 0)

    @pl.when(inside)
    def _():
        for block in range(blocks):
            pass_on(1, block)
            merge_half(1, 1, block)
        for head in range(heads):
            for block in range(blocks):
                ask_copy(me - 1, head, block, 1).wait_send()
                ask_copy(me + 1, head, block, 0).wait_send()
                ask_copy(far_end, head, block, outward).wait_send()

    for head in range(heads):
        for block in range(blocks):
            for_sides(lambda side: ask_copy(me, head, block, side).wait_send())
    for_sides(lambda side: near_copy(side).wait_send())
    for_far(lambda other: far_copy(other).wait_send())

    @pl.when(inside)
    def _():
        for head in range(heads):
            for block in range(blocks):
                settle(head, block)
        for head in range(heads):
            for block in range(blocks):
                for each in over_copy(0, head, block) + over_copy(1, head, block) + last_copy(head, block):
                    each.wait_send()

    @pl.when(jnp.logical_not(inside))
    def _():
        for kind in range(3):
            for head in range(heads):
                for block in range(blocks):
                    for each in half_copy(kind, head, block):
                        each.wait_send()
        for head in range(heads):
            for block in range(blocks):
                for each in last_copy(head, block):
                    each.wait_recv()
                mixed, _ = blend(
                    [own_ref[3, head, block], last_ref[head, block]],
                    [own_log_ref[3, head, block], last_log_ref[head, block]],
                )
                out_ref[head, block * BLOCK : (block + 1) * BLOCK, :] = mixed.T.astype(out_ref.dtype)


def hand_out(source_ref, out_ref):
    out_ref[...] = source_ref[...]


def by_tokens(keys, values, queries, positions, count):
    heads, rows, width = queries.shape
    n_dev, columns = keys.shape
    length = n_dev * count
    near, down, up, local, merge, cross = fields(length, count)

    def tall(matrix):
        return np.concatenate(split_two(matrix), axis=-2)

    def table(places):
        return tall(np.concatenate(spins(places, width).astype(np.float64), axis=1))

    up_high, up_low = split_two(up)
    t_part = near.shape[0]
    tokens = n_dev // 2
    blocks = rows // BLOCK
    split = 128
    operands = (
        table(np.arange(length // split) * float(split)),
        table(np.arange(split) * 1.0),
        tall(near),
        tall(down),
        np.concatenate([up_high, up_high, up_low], axis=1),
        tall(local),
        tall(merge),
        tall(cross),
        spins(np.arange(count * PARTS) * float(t_part), width),
        spins(np.arange(t_part) * 1.0, width),
    )
    held = [jax.ShapeDtypeStruct(o.shape[1:] if o.ndim == 3 and o.shape[0] == count else o.shape, o.dtype) for o in operands]
    dma = pltpu.SemaphoreType.DMA

    def parts(*lead):
        return [
            pltpu.VMEM(lead + (heads, blocks, width, BLOCK), jnp.bfloat16),
            pltpu.VMEM(lead + (heads, blocks, 1, BLOCK), jnp.float32),
        ]

    settled = pl.pallas_call(
        functools.partial(fused_kernel, count, math.log2(math.e) / math.sqrt(width)),
        in_specs=[pl.BlockSpec(memory_space=pl.ANY)] * 14,
        out_specs=pl.BlockSpec(memory_space=pltpu.VMEM),
        out_shape=jax.ShapeDtypeStruct(queries.shape, jnp.bfloat16),
        scratch_shapes=[
            pltpu.VMEM(keys.shape, keys.dtype),
            pltpu.VMEM(values.shape, values.dtype),
            pltpu.VMEM(queries.shape, queries.dtype),
            pltpu.VMEM((rows,), jnp.int32),
        ]
        + [pltpu.VMEM(h.shape, h.dtype) for h in held]
        + [
            pltpu.VMEM((PARTS * ORDER, 2 * columns), jnp.float32),
            pltpu.VMEM((2 * EDGE + FAR, 2 * columns), jnp.float32),
            pltpu.VMEM((cross.shape[2], 2 * columns), jnp.float32),
            pltpu.VMEM((PARTS, t_part, 2 * columns), jnp.float32),
            pltpu.VMEM((PARTS * ORDER, 2 * columns), jnp.float32),
            pltpu.VMEM((heads, tokens, width), jnp.bfloat16),
            pltpu.VMEM((heads, width, tokens), jnp.bfloat16),
            pltpu.VMEM((tokens, BLOCK), jnp.float32),
            pltpu.VMEM((tokens, BLOCK), jnp.float32),
            pltpu.VMEM((1, BLOCK), jnp.float32),
            pltpu.VMEM((1, BLOCK), jnp.float32),
            pltpu.VMEM((count, heads, rows, width), jnp.bfloat16),
        ]
        + parts(4)
        + parts(3)
        + parts(2)
        + parts(2)
        + parts()
        + parts()
        + [
            dma((12,)),
            dma((PARTS, 2)),
            pltpu.SemaphoreType.REGULAR((2,)),
            pltpu.SemaphoreType.REGULAR,
            dma((count,)),
            dma((count,)),
            dma((count, heads, blocks, 2)),
            dma((count, heads, blocks)),
            dma((3, heads, blocks, 2)),
            dma((3, heads, blocks, 2)),
            dma((2, heads, blocks, 2)),
            dma((2, heads, blocks, 2)),
            dma((heads, blocks, 2)),
            dma((heads, blocks, 2)),
        ],
        compiler_params=pltpu.CompilerParams(
            collective_id=0, has_side_effects=True, vmem_limit_bytes=60 * 1024 * 1024
        ),
    )(keys, values, queries, positions, *operands)
    return pl.pallas_call(
        hand_out,
        in_specs=[pl.BlockSpec(memory_space=pltpu.VMEM)],
        out_specs=pl.BlockSpec(memory_space=pltpu.VMEM),
        out_shape=jax.ShapeDtypeStruct(settled.shape, settled.dtype),
    )(settled)


def by_columns(keys, values, queries, positions):
    key_parts = lax.all_to_all(keys, "ctx", split_axis=1, concat_axis=0, tiled=True)
    value_parts = lax.all_to_all(values, "ctx", split_axis=1, concat_axis=0, tiled=True)
    heads, rows, width = queries.shape
    per_device = key_parts.shape[1]
    compact = compress(jnp.concatenate([key_parts, value_parts], axis=1))
    rotated = rotate_rows(queries.astype(jnp.float32), positions.astype(jnp.float32)).astype(
        jnp.bfloat16
    )
    whole = lax.all_gather(compact.T, "ctx", axis=0, tiled=True)
    tokens = whole.shape[1]
    shaped = whole.reshape(-1, 2, per_device, tokens)
    key_rows = shaped[:, 0].reshape(heads, width, tokens).swapaxes(1, 2)
    value_rows = shaped[:, 1].reshape(heads, width, tokens).swapaxes(1, 2)
    places = jnp.arange(tokens).astype(jnp.float32)
    ready = rotate_rows(key_rows.astype(jnp.float32), places).astype(jnp.bfloat16)
    return attend(rotated, ready, value_rows, jnp.zeros((), jnp.int32))[0]


def solution(mesh):
    count = mesh.shape["ctx"]

    def on_device(keys, values, queries, positions):
        heads, rows, width = queries.shape
        if count == 4 and heads == 2 and keys.shape[0] % (PARTS * 512) == 0 and rows % BLOCK == 0 and width == 128:
            return by_tokens(keys, values, queries, positions, count)
        return by_columns(keys, values, queries, positions)

    return jax.shard_map(
        on_device,
        mesh=mesh,
        in_specs=(
            P(("user", "ctx"), "heads"),
            P(("user", "ctx"), "heads"),
            P("heads", ("user", "ctx"), None),
            P(("user", "ctx")),
        ),
        out_specs=P("heads", ("user", "ctx"), None),
        check_vma=False,
    )
```

```python
import functools
import math

import jax
import jax.numpy as jnp
import numpy as np
from jax import lax
from jax.experimental import pallas as pl
from jax.experimental.pallas import tpu as pltpu
from jax.sharding import PartitionSpec as P

OUTER = 128
PARTS = 4
ORDER = 64
EDGE = 32
FAR = 16
BLOCK = 256
MESH = pl.DeviceIdType.MESH


def split_two(matrix):
    high = matrix.astype(jnp.bfloat16)
    low = (matrix - np.asarray(high).astype(np.float64)).astype(jnp.bfloat16)
    return high, low


@functools.lru_cache(maxsize=None)
def stages(length):
    outer = OUTER
    inner = length // outer
    step = inner // 2
    a = np.arange(outer)
    c = np.arange(outer)
    turn = 2 * outer
    angle = np.pi / outer * ((c[:, None] * a[None, :]) % turn)
    alternate = np.where(a % 2 == 0, 1.0, -1.0)
    first = np.stack([np.cos(angle), -np.sin(angle)], axis=1)
    first[0, 1] = alternate
    d = np.arange(length // 2 // turn)
    k = np.concatenate([c[:, None] + turn * d, (turn - c[:, None]) % turn + turn * d], axis=1)
    k[0, d.size :] = outer + turn * d
    sign = np.concatenate([np.ones(d.size), -np.ones(d.size)])
    b = np.arange(inner)
    q = np.arange(step)
    theta = np.pi / (2 * length) * ((k[:, :, None] * (2 * b + 1)) % (4 * length))
    phi = np.pi / length * ((k[:, None, :] * (2 * q + 1)[:, None]) % (2 * length))
    forward = np.stack([np.cos(theta), np.sin(theta) * sign[None, :, None]], axis=2)
    weight = np.where(k == 0, 1.0, 2.0) / length
    back = np.stack([np.cos(phi), np.sin(phi) * sign], axis=1) * weight[:, None, None, :]
    half = d.size
    forward[0, :half, 1] = 0.0
    forward[0, half:, 1] = np.cos(theta[0, half:])
    forward[0, half:, 0] = 0.0
    back[0, 1, :, :half] = 0.0
    back[0, 1, :, half:] = np.cos(phi[0, :, half:]) * weight[0, half:]
    back[0, 0, :, half:] = 0.0
    middle = back.reshape(outer, 2 * step, 2 * half) @ forward.reshape(outer, 2 * half, 2 * inner)
    last = first.transpose(2, 0, 1).reshape(outer, 2 * outer)
    return first.reshape(2 * outer, outer), middle, last


def compress(signal):
    length, columns = signal.shape
    outer, inner = OUTER, length // OUTER
    first, middle, last = stages(length)
    first_high, first_low = split_two(first)
    flat = signal.reshape(outer, inner * columns)
    one = jnp.dot(first_high, flat, preferred_element_type=jnp.float32) + jnp.dot(
        first_low, flat, preferred_element_type=jnp.float32
    )
    one = one.reshape(outer, 2 * inner, columns)
    two = jnp.einsum(
        "cob,cbl->col", jnp.asarray(middle.astype(np.float32)), one, precision=lax.Precision.HIGH
    )
    three = jnp.dot(
        jnp.asarray(last.astype(np.float32)),
        two.reshape(2 * outer, inner // 2 * columns),
        precision=lax.Precision.HIGH,
    )
    return three.reshape(length // 2, columns).astype(jnp.bfloat16)

def strict_dot(left, right):
    rows, columns = left.shape[0] // 2, right.shape[1]
    high = right.astype(jnp.bfloat16)
    low = (right - high.astype(jnp.float32)).astype(jnp.bfloat16)
    both = jnp.dot(
        left, jnp.concatenate([high, low], axis=1), preferred_element_type=jnp.float32
    )
    return both[:rows, :columns] + (both[:rows, columns:] + both[rows:, :columns])


def inverse_freq(width):
    return jnp.exp(jnp.arange(width // 2).astype(jnp.float32) * (-2.0 * math.log(500000.0) / width))


def rotate_rows(block, places):
    width = block.shape[-1]
    half = width // 2
    angles = places[:, None] * inverse_freq(width)[None, :]
    cosine = jnp.cos(angles)
    sine = jnp.sin(angles)
    first = block[..., :half]
    second = block[..., half:]
    return jnp.concatenate(
        [first * cosine - second * sine, second * cosine + first * sine], axis=-1
    )


def attend_kernel(chunk, scale, resume, finish, swap_ref, q_ref, k_ref, v_ref, *refs):
    q = q_ref[0]
    swap = swap_ref[0] == 1
    rows, width = q.shape
    factor = scale * math.log2(math.e)
    if resume:
        accum = refs[0][0]
        best = refs[1][0][:, :1]
        total = refs[2][0][:, :1]
        refs = refs[3:]
    else:
        best = jnp.full((rows, 1), -jnp.inf, jnp.float32)
        total = jnp.zeros((rows, 1), jnp.float32)
        accum = jnp.zeros((rows, width), jnp.float32)
    tokens = k_ref.shape[1]
    for start in range(0, tokens, chunk):
        one = k_ref[0, start : start + chunk, :]
        two = v_ref[0, start : start + chunk, :]
        k, v = jnp.where(swap, two, one), jnp.where(swap, one, two)
        scores = lax.dot_general(
            q, k, (((1,), (1,)), ((), ())), preferred_element_type=jnp.float32
        )
        fresh = jnp.maximum(best, jnp.max(scores, axis=1, keepdims=True))
        expo = jnp.exp2((scores - fresh) * factor)
        shrink = jnp.exp2((best - fresh) * factor)
        total = total * shrink + jnp.sum(expo, axis=1, keepdims=True)
        accum = accum * shrink + jnp.dot(
            expo.astype(jnp.bfloat16), v, preferred_element_type=jnp.float32
        )
        best = fresh
    if finish:
        refs[0][0] = (accum / total).astype(refs[0].dtype)
        refs[1][0] = jnp.broadcast_to(best * factor + jnp.log2(total), (rows, 8))
    else:
        refs[0][0] = accum
        refs[1][0] = jnp.broadcast_to(best, (rows, 8))
        refs[2][0] = jnp.broadcast_to(total, (rows, 8))


def attend(queries, keys, values, swap, part=0, parts=1, state=None):
    groups, rows, width = queries.shape
    heads, tokens, _ = values.shape
    per_head = groups // heads
    block = math.gcd(rows, 768)
    chunk = math.gcd(tokens, 1024)
    scale = 1.0 / math.sqrt(width)
    finish = part == parts - 1
    wide = pl.BlockSpec((1, block, width), lambda g, i: (g, i, 0))
    thin = pl.BlockSpec((1, block, 8), lambda g, i: (g, i, 0))
    thin_shape = jax.ShapeDtypeStruct((groups, rows, 8), jnp.float32)
    state = () if state is None else tuple(state)
    wide_type = jnp.bfloat16 if finish else jnp.float32
    return pl.pallas_call(
        functools.partial(attend_kernel, chunk, scale, bool(state), finish),
        grid=(groups, rows // block),
        in_specs=[
            pl.BlockSpec(memory_space=pltpu.SMEM),
            wide,
            pl.BlockSpec((1, tokens, width), lambda g, i: (g // per_head, part, 0)),
            pl.BlockSpec((1, tokens, width), lambda g, i: (g // per_head, 0, 0)),
        ]
        + ([wide, thin, thin] if state else []),
        out_specs=[wide, thin] if finish else [wide, thin, thin],
        out_shape=[jax.ShapeDtypeStruct((groups, rows, width), wide_type), thin_shape]
        + ([] if finish else [thin_shape]),
        cost_estimate=pl.CostEstimate(
            flops=8 * groups * rows * tokens * width,
            bytes_accessed=4 * groups * rows * width * 2,
            transcendentals=groups * rows * tokens,
        ),
    )(swap.reshape(1), queries, keys, values, *state)


def bounds(count, left, right):
    return np.log(left / (count - 1 + right)), np.log((count - 1 + left) / right)


def nodes(count, order, left, right):
    low, top = bounds(count, left, right)
    e = np.exp((top - low) / 2 * np.cos(np.pi * (2 * np.arange(order) + 1) / (2 * order)) + (top + low) / 2)
    return ((count - 1 + right) * e - left) / (1 + e)


def cardinals(places, count, order, left, right):
    low, top = bounds(count, left, right)
    at = (2 * np.log((places + left) / (count - 1 + right - places)) - top - low) / (top - low)
    at = np.arccos(np.clip(at, -1.0, 1.0))
    own = np.pi * (2 * np.arange(order) + 1) / (2 * order)
    total = np.zeros((places.size, order))
    for k in range(order):
        total += (1.0 if k == 0 else 2.0) / order * np.cos(k * at)[:, None] * np.cos(k * own)[None, :]
    return total


@functools.lru_cache(maxsize=None)
def fields(length, devices):
    parts, order = PARTS, ORDER
    scale = math.sqrt(0.5) / (2 * length)

    def cot(m):
        return 1.0 / np.tan(np.pi * m / (4 * length))

    n_dev = length // devices
    n_part, t_dev = n_dev // parts, n_dev // 2
    t_part = n_part // 2
    n, t = np.arange(n_part), np.arange(t_part)
    sign_n = np.array([1.0, -1.0, -1.0, 1.0])[n % 4]
    sign_t = np.where(t % 2 == 0, 1.0, -1.0)
    near = sign_t[:, None] * sign_n * scale * cot(4 * t[:, None] - 2 * n + 1.0)
    down = cardinals(n, n_part, order, 1.5, 1.5).T * sign_n
    up = sign_t[:, None] * cardinals(t, t_part, order, 0.75, 0.75)
    part = np.arange(parts)[:, None]
    source = (part * n_part + nodes(n_part, order, 1.5, 1.5)).reshape(-1)
    target = (part * t_part + nodes(t_part, order, 0.75, 0.75)).reshape(-1)
    own = np.arange(parts * order) // order
    same = own[:, None] == own[None, :]
    local = np.where(same, 0.0, scale * cot(np.where(same, 1.0, 4 * target[:, None] - 2 * source + 1)))
    last = n_dev - 1
    wide = float(n_dev)
    merge = np.concatenate(
        [
            cardinals(source, n_dev, EDGE, 1.5, wide).T,
            cardinals(last - source, n_dev, EDGE, 1.5, wide).T,
            cardinals(source, n_dev, FAR, 2 * wide, 2 * wide).T,
        ]
    )
    to_left = nodes(n_dev, EDGE, 1.5, wide)
    sparse = nodes(n_dev, FAR, 2 * wide, 2 * wide)
    size = 3 * EDGE + devices * FAR
    cross = np.zeros((devices, parts * order, size + -size % 128))
    for r in range(devices):
        a = 4 * (target + r * t_dev)[:, None]
        for s in range(devices):
            if abs(r - s) > 1:
                spots, start = sparse, 3 * EDGE + s * FAR
            elif s < r or (s == r and 2 * r >= devices):
                spots, start = last - to_left, EDGE * (r - s)
            else:
                spots, start = to_left, 2 * EDGE * (s - r)
            b = 2 * (spots + s * n_dev)
            block = scale * cot(a + b + 3)
            if r != s:
                block = block + scale * cot(a - b + 1)
            cross[r, :, start : start + block.shape[1]] = block
    return near, down, up, local, merge, cross


def spins(places, width):
    freq = 500000.0 ** (-2.0 * np.arange(width // 2) / width)
    angles = places[:, None] * freq
    cosine, sine = np.cos(angles), np.sin(angles)
    return np.stack(
        [np.concatenate([cosine, cosine], axis=1), np.concatenate([-sine, sine], axis=1)]
    ).astype(np.float32)


def fused_kernel(
    count,
    factor,
    keys_hbm,
    values_hbm,
    queries_hbm,
    places_hbm,
    high_hbm,
    low_hbm,
    near_hbm,
    down_hbm,
    up_hbm,
    local_hbm,
    merge_hbm,
    cross_hbm,
    coarse_hbm,
    fine_hbm,
    out_ref,
    keys_ref,
    values_ref,
    queries_ref,
    places_ref,
    high_ref,
    low_ref,
    near_ref,
    down_ref,
    up_ref,
    local_ref,
    merge_ref,
    cross_ref,
    coarse_ref,
    fine_ref,
    parts_ref,
    whole_ref,
    others_ref,
    close_ref,
    field_ref,
    k_ref,
    v_ref,
    even_ref,
    odd_ref,
    even_top_ref,
    odd_top_ref,
    asks_ref,
    own_ref,
    own_log_ref,
    half_ref,
    half_log_ref,
    merged_ref,
    merged_log_ref,
    over_ref,
    over_log_ref,
    ready_ref,
    ready_log_ref,
    last_ref,
    last_log_ref,
    load_sem,
    token_sem,
    behind_sem,
    end_sem,
    field_send,
    field_recv,
    ask_send,
    ask_recv,
    half_send,
    half_recv,
    over_send,
    over_recv,
    last_send,
):
    me = lax.axis_index("ctx")
    heads, rows, width = queries_ref.shape
    order = ORDER
    blocks = rows // BLOCK
    n_part = near_ref.shape[1]
    t_part = n_part // 2
    half_columns = keys_ref.shape[1]
    tokens = k_ref.shape[1]
    has_left, has_right = me > 0, me < count - 1
    inside = jnp.logical_and(has_left, has_right)
    lower = me < count // 2
    mate = me + 1 - 2 * lax.rem(me, 2)
    far_end = jnp.where(lower, count - 1, 0)
    near_over = jnp.where(lower, count // 2, count // 2 - 1)
    outward = jnp.where(lower, 0, 1)

    def copy(src, dst, send, recv, other):
        return pltpu.make_async_remote_copy(
            src_ref=src,
            dst_ref=dst,
            send_sem=send,
            recv_sem=recv,
            device_id={"ctx": other},
            device_id_type=MESH,
        )

    def for_sides(action):
        for side, there in enumerate((has_left, has_right)):

            @pl.when(there)
            def _():
                action(side)

    def greet(sem, other):
        pl.semaphore_signal(sem, inc=1, device_id={"ctx": other}, device_id_type=MESH)

    others_ref[...] = jnp.zeros_like(others_ref)
    barrier = pltpu.get_barrier_semaphore()
    for_sides(lambda side: greet(barrier, me + 2 * side - 1))
    pairs = (
        (places_hbm, places_ref),
        (queries_hbm, queries_ref),
        (high_hbm, high_ref),
        (low_hbm, low_ref),
        (down_hbm, down_ref),
        (merge_hbm, merge_ref),
        (near_hbm, near_ref),
        (local_hbm, local_ref),
        (cross_hbm.at[me], cross_ref),
        (up_hbm, up_ref),
        (coarse_hbm, coarse_ref),
        (fine_hbm, fine_ref),
    )
    loads = [pltpu.make_async_copy(src, dst, load_sem.at[i]) for i, (src, dst) in enumerate(pairs)]
    sides = ((keys_hbm, keys_ref), (values_hbm, values_ref))
    token_loads = [
        [
            pltpu.make_async_copy(
                src.at[pl.ds(p * n_part, n_part)], dst.at[pl.ds(p * n_part, n_part)], token_sem.at[p, side]
            )
            for side, (src, dst) in enumerate(sides)
        ]
        for p in range(PARTS)
    ]
    for each in loads[:6]:
        each.start()
    for p in range(PARTS):
        for each in token_loads[p]:
            each.start()
    for each in loads[6:]:
        each.start()
    for each in loads[:4]:
        each.wait()

    split = low_ref.shape[0] // 2
    for i in range(rows // split):
        here = slice(i * split, (i + 1) * split)
        place = jnp.broadcast_to(places_ref[here].astype(jnp.float32)[None], (split, split)).T.astype(jnp.int32)
        spun = []
        for value, table_ref in ((place // split, high_ref), (lax.rem(place, split), low_ref)):
            size = table_ref.shape[0] // 2
            value = value if size == split else value[:, :1]
            picked = value == lax.broadcasted_iota(jnp.int32, (split, size), 1)
            picked = jnp.where(picked, 1.0, 0.0).astype(jnp.bfloat16)
            got = jnp.dot(
                jnp.concatenate([picked, picked], axis=1), table_ref[...], preferred_element_type=jnp.float32
            )
            spun.append((got[:, :width], got[:, width:]))
        (cos_a, sin_a), (cos_b, sin_b) = spun
        cosine, sine = cos_a * cos_b - sin_a * sin_b, sin_a * cos_b + cos_a * sin_b
        for head in range(heads):
            x = queries_ref[head, here, :].astype(jnp.float32)
            asks_ref[me, head, here, :] = (x * cosine + pltpu.roll(x, width // 2, 1) * sine).astype(jnp.bfloat16)

    def ask_copy(source, head, block, side):
        here = pl.ds(block * BLOCK if isinstance(block, int) else pl.multiple_of(block * BLOCK, BLOCK), BLOCK)
        return copy(
            asks_ref.at[source, head, here],
            asks_ref.at[source, head, here],
            ask_send.at[source, side],
            ask_recv.at[source, head, block],
            me + 2 * side - 1,
        )

    pl.semaphore_wait(barrier, jnp.where(inside, 2, 1))
    for block in range(blocks):
        for_sides(lambda side: ask_copy(me, 0, block, side).start())
    for_sides(lambda side: greet(behind_sem.at[1 - side], me + 2 * side - 1))

    for each in loads[4:6]:
        each.wait()
    for p in range(PARTS):
        for side, (_, x_ref) in enumerate(sides):
            token_loads[p][side].wait()
            z = jnp.dot(
                down_ref[...], x_ref[p * n_part : (p + 1) * n_part, :], preferred_element_type=jnp.float32
            )
            parts_ref[
                p * order : (p + 1) * order, side * half_columns : (side + 1) * half_columns
            ] = z[:order] + z[order:]
        if p == 1:
            for_sides(lambda side: pl.semaphore_wait(behind_sem.at[side], 1))

            @pl.when(inside)
            def _():
                greet(end_sem, mate)

    whole_ref[...] = strict_dot(merge_ref[...], parts_ref[...])
    others_ref[:EDGE] = whole_ref[pl.ds(pl.multiple_of(jnp.where(lower, 0, EDGE), EDGE), EDGE), :]

    def near_copy(side):
        other = me + 2 * side - 1
        return copy(
            whole_ref.at[pl.ds(side * EDGE, EDGE)],
            others_ref.at[pl.ds(EDGE * (2 - side), EDGE)],
            field_send.at[other],
            field_recv.at[me],
            other,
        )

    def far_copy(other):
        return copy(
            whole_ref.at[pl.ds(2 * EDGE, FAR)],
            others_ref.at[pl.ds(pl.multiple_of(3 * EDGE + me * FAR, FAR), FAR)],
            field_send.at[other],
            field_recv.at[me],
            other,
        )

    def near_wait(side):
        source = me + 2 * side - 1
        copy(
            whole_ref.at[pl.ds(0, EDGE)],
            others_ref.at[pl.ds(EDGE * (1 + side), EDGE)],
            field_send.at[source],
            field_recv.at[source],
            source,
        ).wait_recv()

    def far_wait(source):
        copy(
            whole_ref.at[pl.ds(2 * EDGE, FAR)],
            others_ref.at[pl.ds(3 * EDGE + source * FAR, FAR)],
            field_send.at[source],
            field_recv.at[source],
            source,
        ).wait_recv()

    def ask_sent(source, side):
        copy(
            asks_ref.at[source],
            asks_ref.at[source],
            ask_send.at[source, side],
            ask_recv.at[source, 0, 0],
            me + 2 * side - 1,
        ).wait_send()

    def hand(source, head, block, side):
        handed = ask_copy(source, head, block, side)
        handed.wait_recv()
        handed.start()

    def for_far(action):
        for other in range(count):

            @pl.when(jnp.logical_or(other - me > 1, me - other > 1))
            def _():
                action(other)

    for_sides(lambda side: near_copy(side).start())

    @pl.when(jnp.logical_not(inside))
    def _():
        pl.semaphore_wait(end_sem, 1)

    for_far(lambda other: far_copy(other).start())

    @pl.when(jnp.logical_not(inside))
    def _():
        for block in range(blocks):
            ask_copy(me, 1, block, 1 - outward).start()

    loads[6].wait()

    def close(p, carry):
        start = p * n_part if isinstance(p, int) else pl.multiple_of(p * n_part, n_part)
        for side, (_, x_ref) in enumerate(sides):
            z = jnp.dot(near_ref[...], x_ref[pl.ds(start, n_part), :], preferred_element_type=jnp.float32)
            close_ref[p, :, side * half_columns : (side + 1) * half_columns] = z[:t_part] + z[t_part:]
        return carry

    close(0, 0)

    @pl.when(inside)
    def _():
        for block in range(blocks):
            for side in range(2):
                hand(me + 2 * side - 1, 0, block, 1 - side)
        ask_copy(me, 1, 0, outward).start()

    lax.fori_loop(1, PARTS, close, 0)

    @pl.when(inside)
    def _():
        hand(mate, 1, 0, 1 - outward)
        ask_copy(me, 1, 1, outward).start()

    for each in loads[7:]:
        each.wait()
    field_ref[...] = strict_dot(local_ref[...], parts_ref[...])

    for_sides(near_wait)
    for_far(far_wait)
    field_ref[...] += strict_dot(cross_ref[...], others_ref[...])

    def finish(p, carry):
        f = field_ref[pl.ds(pl.multiple_of(p * order, order), order), :]
        high = f.astype(jnp.bfloat16)
        low = (f - high.astype(jnp.float32)).astype(jnp.bfloat16)
        y = close_ref[p] + jnp.dot(
            up_ref[...], jnp.concatenate([high, low, high], axis=0), preferred_element_type=jnp.float32
        )
        y = y.astype(jnp.bfloat16).astype(jnp.float32)
        begin = pl.multiple_of(p * t_part, t_part)
        place = me * PARTS + p
        cos_p, sin_p = coarse_ref[0, pl.ds(place, 1), :], coarse_ref[1, pl.ds(place, 1), :]
        cosine = cos_p * fine_ref[0] - sin_p * fine_ref[1]
        sine = sin_p * fine_ref[0] + cos_p * fine_ref[1]
        for head in range(heads):
            k = y[:, head * width : (head + 1) * width]
            turned = k * cosine + pltpu.roll(k, width // 2, 1) * sine
            k_ref[head, pl.ds(begin, t_part), :] = turned.astype(jnp.bfloat16)
            v = y[:, half_columns + head * width : half_columns + (head + 1) * width]
            v_ref[head, :, pl.ds(begin, t_part)] = v.T.astype(jnp.bfloat16)
        return carry

    lax.fori_loop(0, PARTS, finish, 0)

    @pl.when(inside)
    def _():
        for block in range(1, blocks):
            hand(mate, 1, block, 1 - outward)
        for block in range(blocks):
            ask_copy(me, 1, block, 1 - outward).start()

    runs = [
        (0, 0, 0, blocks),
        (1, 0, 0, blocks),
        (2, 0, 0, blocks),
        (3, 0, 0, blocks - 1),
        (2, 1, 0, blocks),
        (3, 0, blocks - 1, 1),
        (3, 1, 0, 1),
        (1, 1, 0, blocks),
        (0, 1, 0, blocks),
        (3, 1, 1, blocks - 1),
    ]
    begins = [sum(run[3] for run in runs[:i]) for i in range(len(runs))]
    units = begins[-1] + runs[-1][3]

    def decode(u):
        kind, head, block = runs[0][0], runs[0][1], u
        for begin, run in zip(begins[1:], runs[1:]):
            late = u >= begin
            kind = jnp.where(late, run[0], kind)
            head = jnp.where(late, run[1], head)
            block = jnp.where(late, u - begin + run[2], block)
        source = jnp.where(
            kind == 0, mate, jnp.where(kind == 1, near_over, jnp.where(kind == 2, far_end, me))
        )
        return kind, head, block, source

    chunk = 512

    def score(u, keep_ref, top_ref):
        _, head, block, source = decode(u)
        q = asks_ref[source, head, pl.ds(pl.multiple_of(block * BLOCK, BLOCK), BLOCK), :]
        best = None
        for c in range(0, tokens, chunk):
            s = lax.dot_general(
                k_ref[head, c : c + chunk, :],
                q,
                (((1,), (1,)), ((), ())),
                preferred_element_type=jnp.float32,
            )
            keep_ref[c : c + chunk, :] = s
            top = jnp.max(s, axis=0, keepdims=True)
            best = top if best is None else jnp.maximum(best, top)
        top_ref[...] = best

    def weigh(u, keep_ref, top_ref):
        kind, head, block, _ = decode(u)
        best = top_ref[...]
        total = jnp.zeros((1, BLOCK), jnp.float32)
        accum = jnp.zeros((width, BLOCK), jnp.float32)
        for c in range(0, tokens, chunk):
            e = jnp.exp2((keep_ref[c : c + chunk, :] - best) * factor)
            total += jnp.sum(e, axis=0, keepdims=True)
            accum += jnp.dot(
                v_ref[head, :, c : c + chunk], e.astype(jnp.bfloat16), preferred_element_type=jnp.float32
            )
        own_ref[kind, head, block] = (accum / total).astype(jnp.bfloat16)
        own_log_ref[kind, head, block] = best * factor + jnp.log2(total)

    def both(src, src_log, dst, dst_log, send, recv, other):
        return (
            copy(src, dst, send.at[0], recv.at[0], other),
            copy(src_log, dst_log, send.at[1], recv.at[1], other),
        )

    def half_copy(kind, head, block):
        at = (kind, head, block)
        return both(
            own_ref.at[at],
            own_log_ref.at[at],
            half_ref.at[at],
            half_log_ref.at[at],
            half_send,
            half_recv.at[at],
            mate,
        )

    def over_copy(j, head, block):
        at = (j, head, block)
        return both(
            merged_ref.at[at],
            merged_log_ref.at[at],
            over_ref.at[at],
            over_log_ref.at[at],
            over_send,
            over_recv.at[at],
            near_over,
        )

    def last_copy(head, block):
        at = (head, block)
        return both(
            ready_ref.at[at],
            ready_log_ref.at[at],
            last_ref.at[at],
            last_log_ref.at[at],
            last_send,
            half_recv.at[(0,) + at],
            mate,
        )

    def blend(parts, logs):
        best = functools.reduce(jnp.maximum, logs)
        shares = [jnp.exp2(log - best) for log in logs]
        total = functools.reduce(jnp.add, shares)
        mixed = functools.reduce(
            jnp.add, [part.astype(jnp.float32) * (share / total) for part, share in zip(parts, shares)]
        )
        return mixed, best + jnp.log2(total)

    def merge_half(kind, head, block):
        for each in half_copy(kind, head, block):
            each.wait_recv()
        at = (kind - 1, head, block)
        mixed, log = blend(
            [own_ref[kind, head, block], half_ref[kind, head, block]],
            [own_log_ref[kind, head, block], half_log_ref[kind, head, block]],
        )
        merged_ref[at] = mixed.astype(jnp.bfloat16)
        merged_log_ref[at] = log
        for each in over_copy(*at):
            each.start()

    def settle(head, block):
        for each in half_copy(0, head, block) + over_copy(0, head, block):
            each.wait_recv()
        mixed, _ = blend(
            [own_ref[3, head, block], half_ref[0, head, block], over_ref[0, head, block]],
            [own_log_ref[3, head, block], half_log_ref[0, head, block], over_log_ref[0, head, block]],
        )
        out_ref[head, block * BLOCK : (block + 1) * BLOCK, :] = mixed.T.astype(out_ref.dtype)

    def pass_on(head, block):
        for each in over_copy(1, head, block):
            each.wait_recv()
        mixed, log = blend(
            [own_ref[0, head, block], over_ref[1, head, block]],
            [own_log_ref[0, head, block], over_log_ref[1, head, block]],
        )
        ready_ref[head, block] = mixed.astype(jnp.bfloat16)
        ready_log_ref[head, block] = log
        for each in last_copy(head, block):
            each.start()

    def await_ask(u):
        kind, head, block, source = decode(u)

        @pl.when(jnp.logical_and(kind < 3, jnp.logical_not(inside)))
        def _():
            ask_copy(source, head, block, 1 - outward).wait_recv()

    merges = ((1, 0, begins[1] + 9), (2, 0, begins[2] + 12))

    def send_on(u):
        kind, head, block, _ = decode(u)

        @pl.when(jnp.logical_and(kind < 3, jnp.logical_not(inside)))
        def _():
            for each in half_copy(kind, head, block):
                each.start()

        for kind, head, first in merges:
            k = u - first

            @pl.when(jnp.logical_and(inside, jnp.logical_and(k >= 0, k < blocks)))
            def _():
                merge_half(kind, head, k)

    await_ask(jnp.int32(0))
    score(jnp.int32(0), even_ref, even_top_ref)

    def serve(i, carry):
        u = 2 * i
        for at, source, head in ((0, far_end, 0), (3, far_end, 1), (5, near_over, 1)):

            @pl.when(jnp.logical_and(inside, i == at))
            def _():
                for block in range(blocks):
                    hand(source, head, block, outward)
                if source is near_over:
                    for block in range(2, blocks):
                        ask_copy(me, 1, block, outward).start()

        await_ask(u + 1)
        score(u + 1, odd_ref, odd_top_ref)
        weigh(u, even_ref, even_top_ref)
        send_on(u)
        ahead = jnp.minimum(u + 2, units - 1)

        @pl.when(u + 2 < units)
        def _():
            await_ask(ahead)

        score(ahead, even_ref, even_top_ref)
        weigh(u + 1, odd_ref, odd_top_ref)
        send_on(u + 1)
        return carry

    lax.fori_loop(0, units // 2, serve, 0)

    @pl.when(inside)
    def _():
        for block in range(blocks):
            pass_on(0, block)
            merge_half(2, 1, block)
        for block in range(blocks):
            pass_on(1, block)
            merge_half(1, 1, block)
        ask_sent(me - 1, 1)
        ask_sent(me + 1, 0)
        ask_sent(far_end, outward)

    for_sides(lambda side: ask_sent(me, side))
    for_sides(lambda side: near_copy(side).wait_send())
    for_far(lambda other: far_copy(other).wait_send())

    @pl.when(inside)
    def _():
        for head in range(heads):
            for block in range(blocks):
                settle(head, block)
        for each in both(
            merged_ref, merged_log_ref, over_ref, over_log_ref, over_send, over_recv.at[0, 0, 0], near_over
        ) + both(ready_ref, ready_log_ref, last_ref, last_log_ref, last_send, half_recv.at[0, 0, 0], mate):
            each.wait_send()

    @pl.when(jnp.logical_not(inside))
    def _():
        for head in range(heads):
            for block in range(blocks):
                for each in last_copy(head, block):
                    each.wait_recv()
                mixed, _ = blend(
                    [own_ref[3, head, block], last_ref[head, block]],
                    [own_log_ref[3, head, block], last_log_ref[head, block]],
                )
                out_ref[head, block * BLOCK : (block + 1) * BLOCK, :] = mixed.T.astype(out_ref.dtype)
        kinds = pl.ds(0, 3)
        for each in both(
            own_ref.at[kinds], own_log_ref.at[kinds], half_ref, half_log_ref, half_send, half_recv.at[0, 0, 0], mate
        ):
            each.wait_send()


def by_tokens(keys, values, queries, positions, count):
    heads, rows, width = queries.shape
    n_dev, columns = keys.shape
    length = n_dev * count
    near, down, up, local, merge, cross = fields(length, count)

    def tall(matrix):
        return np.concatenate(split_two(matrix), axis=-2)

    def table(places):
        return tall(np.concatenate(spins(places, width).astype(np.float64), axis=1))

    up_high, up_low = split_two(up)
    t_part = near.shape[0]
    tokens = n_dev // 2
    blocks = rows // BLOCK
    split = 128
    operands = (
        table(np.arange(length // split) * float(split)),
        table(np.arange(split) * 1.0),
        tall(near),
        tall(down),
        np.concatenate([up_high, up_high, up_low], axis=1),
        tall(local),
        tall(merge),
        tall(cross),
        spins(np.arange(count * PARTS) * float(t_part), width),
        spins(np.arange(t_part) * 1.0, width),
    )
    held = [jax.ShapeDtypeStruct(o.shape[1:] if o.ndim == 3 and o.shape[0] == count else o.shape, o.dtype) for o in operands]
    dma = pltpu.SemaphoreType.DMA

    def parts(*lead):
        return [
            pltpu.VMEM(lead + (heads, blocks, width, BLOCK), jnp.bfloat16),
            pltpu.VMEM(lead + (heads, blocks, 1, BLOCK), jnp.float32),
        ]

    return pl.pallas_call(
        functools.partial(fused_kernel, count, math.log2(math.e) / math.sqrt(width)),
        in_specs=[pl.BlockSpec(memory_space=pl.ANY)] * 14,
        out_specs=pl.BlockSpec(memory_space=pltpu.VMEM),
        out_shape=jax.ShapeDtypeStruct(queries.shape, jnp.bfloat16),
        scratch_shapes=[
            pltpu.VMEM(keys.shape, keys.dtype),
            pltpu.VMEM(values.shape, values.dtype),
            pltpu.VMEM(queries.shape, queries.dtype),
            pltpu.VMEM((rows,), jnp.int32),
        ]
        + [pltpu.VMEM(h.shape, h.dtype) for h in held]
        + [
            pltpu.VMEM((PARTS * ORDER, 2 * columns), jnp.float32),
            pltpu.VMEM((2 * EDGE + FAR, 2 * columns), jnp.float32),
            pltpu.VMEM((cross.shape[2], 2 * columns), jnp.float32),
            pltpu.VMEM((PARTS, t_part, 2 * columns), jnp.float32),
            pltpu.VMEM((PARTS * ORDER, 2 * columns), jnp.float32),
            pltpu.VMEM((heads, tokens, width), jnp.bfloat16),
            pltpu.VMEM((heads, width, tokens), jnp.bfloat16),
            pltpu.VMEM((tokens, BLOCK), jnp.float32),
            pltpu.VMEM((tokens, BLOCK), jnp.float32),
            pltpu.VMEM((1, BLOCK), jnp.float32),
            pltpu.VMEM((1, BLOCK), jnp.float32),
            pltpu.VMEM((count, heads, rows, width), jnp.bfloat16),
        ]
        + parts(4)
        + parts(3)
        + parts(2)
        + parts(2)
        + parts()
        + parts()
        + [
            dma((12,)),
            dma((PARTS, 2)),
            pltpu.SemaphoreType.REGULAR((2,)),
            pltpu.SemaphoreType.REGULAR,
            dma((count,)),
            dma((count,)),
            dma((count, 2)),
            dma((count, heads, blocks)),
            dma((2,)),
            dma((3, heads, blocks, 2)),
            dma((2,)),
            dma((2, heads, blocks, 2)),
            dma((2,)),
        ],
        compiler_params=pltpu.CompilerParams(
            collective_id=0, has_side_effects=True, vmem_limit_bytes=60 * 1024 * 1024
        ),
    )(keys, values, queries, positions, *operands)


def by_columns(keys, values, queries, positions):
    key_parts = lax.all_to_all(keys, "ctx", split_axis=1, concat_axis=0, tiled=True)
    value_parts = lax.all_to_all(values, "ctx", split_axis=1, concat_axis=0, tiled=True)
    heads, rows, width = queries.shape
    per_device = key_parts.shape[1]
    compact = compress(jnp.concatenate([key_parts, value_parts], axis=1))
    rotated = rotate_rows(queries.astype(jnp.float32), positions.astype(jnp.float32)).astype(
        jnp.bfloat16
    )
    whole = lax.all_gather(compact.T, "ctx", axis=0, tiled=True)
    tokens = whole.shape[1]
    shaped = whole.reshape(-1, 2, per_device, tokens)
    key_rows = shaped[:, 0].reshape(heads, width, tokens).swapaxes(1, 2)
    value_rows = shaped[:, 1].reshape(heads, width, tokens).swapaxes(1, 2)
    places = jnp.arange(tokens).astype(jnp.float32)
    ready = rotate_rows(key_rows.astype(jnp.float32), places).astype(jnp.bfloat16)
    return attend(rotated, ready, value_rows, jnp.zeros((), jnp.int32))[0]


def solution(mesh):
    count = mesh.shape["ctx"]

    def on_device(keys, values, queries, positions):
        heads, rows, width = queries.shape
        if count == 4 and heads == 2 and keys.shape[0] % (PARTS * 512) == 0 and rows % BLOCK == 0 and width == 128:
            return by_tokens(keys, values, queries, positions, count)
        return by_columns(keys, values, queries, positions)

    return jax.shard_map(
        on_device,
        mesh=mesh,
        in_specs=(
            P(("user", "ctx"), "heads"),
            P(("user", "ctx"), "heads"),
            P("heads", ("user", "ctx"), None),
            P(("user", "ctx")),
        ),
        out_specs=P("heads", ("user", "ctx"), None),
        check_vma=False,
    )
```

```python
import functools
import math

import jax
import jax.numpy as jnp
import numpy as np
from jax import lax
from jax.experimental import pallas as pl
from jax.experimental.pallas import tpu as pltpu
from jax.sharding import PartitionSpec as P

OUTER = 128
PARTS = 4
ORDER = 64
EDGE = 32
FAR = 8
BLOCK = 256
MESH = pl.DeviceIdType.MESH


def split_two(matrix):
    high = matrix.astype(jnp.bfloat16)
    low = (matrix - np.asarray(high).astype(np.float64)).astype(jnp.bfloat16)
    return high, low


@functools.lru_cache(maxsize=None)
def stages(length):
    outer = OUTER
    inner = length // outer
    step = inner // 2
    a = np.arange(outer)
    c = np.arange(outer)
    turn = 2 * outer
    angle = np.pi / outer * ((c[:, None] * a[None, :]) % turn)
    alternate = np.where(a % 2 == 0, 1.0, -1.0)
    first = np.stack([np.cos(angle), -np.sin(angle)], axis=1)
    first[0, 1] = alternate
    d = np.arange(length // 2 // turn)
    k = np.concatenate([c[:, None] + turn * d, (turn - c[:, None]) % turn + turn * d], axis=1)
    k[0, d.size :] = outer + turn * d
    sign = np.concatenate([np.ones(d.size), -np.ones(d.size)])
    b = np.arange(inner)
    q = np.arange(step)
    theta = np.pi / (2 * length) * ((k[:, :, None] * (2 * b + 1)) % (4 * length))
    phi = np.pi / length * ((k[:, None, :] * (2 * q + 1)[:, None]) % (2 * length))
    forward = np.stack([np.cos(theta), np.sin(theta) * sign[None, :, None]], axis=2)
    weight = np.where(k == 0, 1.0, 2.0) / length
    back = np.stack([np.cos(phi), np.sin(phi) * sign], axis=1) * weight[:, None, None, :]
    half = d.size
    forward[0, :half, 1] = 0.0
    forward[0, half:, 1] = np.cos(theta[0, half:])
    forward[0, half:, 0] = 0.0
    back[0, 1, :, :half] = 0.0
    back[0, 1, :, half:] = np.cos(phi[0, :, half:]) * weight[0, half:]
    back[0, 0, :, half:] = 0.0
    middle = back.reshape(outer, 2 * step, 2 * half) @ forward.reshape(outer, 2 * half, 2 * inner)
    last = first.transpose(2, 0, 1).reshape(outer, 2 * outer)
    return first.reshape(2 * outer, outer), middle, last


def compress(signal):
    length, columns = signal.shape
    outer, inner = OUTER, length // OUTER
    first, middle, last = stages(length)
    first_high, first_low = split_two(first)
    flat = signal.reshape(outer, inner * columns)
    one = jnp.dot(first_high, flat, preferred_element_type=jnp.float32) + jnp.dot(
        first_low, flat, preferred_element_type=jnp.float32
    )
    one = one.reshape(outer, 2 * inner, columns)
    two = jnp.einsum(
        "cob,cbl->col", jnp.asarray(middle.astype(np.float32)), one, precision=lax.Precision.HIGH
    )
    three = jnp.dot(
        jnp.asarray(last.astype(np.float32)),
        two.reshape(2 * outer, inner // 2 * columns),
        precision=lax.Precision.HIGH,
    )
    return three.reshape(length // 2, columns).astype(jnp.bfloat16)

def strict_dot(left, right):
    rows, columns = left.shape[0] // 2, right.shape[1]
    high = right.astype(jnp.bfloat16)
    low = (right - high.astype(jnp.float32)).astype(jnp.bfloat16)
    both = jnp.dot(
        left, jnp.concatenate([high, low], axis=1), preferred_element_type=jnp.float32
    )
    return both[:rows, :columns] + (both[:rows, columns:] + both[rows:, :columns])


def inverse_freq(width):
    return jnp.exp(jnp.arange(width // 2).astype(jnp.float32) * (-2.0 * math.log(500000.0) / width))


def rotate_rows(block, places):
    width = block.shape[-1]
    half = width // 2
    angles = places[:, None] * inverse_freq(width)[None, :]
    cosine = jnp.cos(angles)
    sine = jnp.sin(angles)
    first = block[..., :half]
    second = block[..., half:]
    return jnp.concatenate(
        [first * cosine - second * sine, second * cosine + first * sine], axis=-1
    )


def attend_kernel(chunk, scale, resume, finish, swap_ref, q_ref, k_ref, v_ref, *refs):
    q = q_ref[0]
    swap = swap_ref[0] == 1
    rows, width = q.shape
    factor = scale * math.log2(math.e)
    if resume:
        accum = refs[0][0]
        best = refs[1][0][:, :1]
        total = refs[2][0][:, :1]
        refs = refs[3:]
    else:
        best = jnp.full((rows, 1), -jnp.inf, jnp.float32)
        total = jnp.zeros((rows, 1), jnp.float32)
        accum = jnp.zeros((rows, width), jnp.float32)
    tokens = k_ref.shape[1]
    for start in range(0, tokens, chunk):
        one = k_ref[0, start : start + chunk, :]
        two = v_ref[0, start : start + chunk, :]
        k, v = jnp.where(swap, two, one), jnp.where(swap, one, two)
        scores = lax.dot_general(
            q, k, (((1,), (1,)), ((), ())), preferred_element_type=jnp.float32
        )
        fresh = jnp.maximum(best, jnp.max(scores, axis=1, keepdims=True))
        expo = jnp.exp2((scores - fresh) * factor)
        shrink = jnp.exp2((best - fresh) * factor)
        total = total * shrink + jnp.sum(expo, axis=1, keepdims=True)
        accum = accum * shrink + jnp.dot(
            expo.astype(jnp.bfloat16), v, preferred_element_type=jnp.float32
        )
        best = fresh
    if finish:
        refs[0][0] = (accum / total).astype(refs[0].dtype)
        refs[1][0] = jnp.broadcast_to(best * factor + jnp.log2(total), (rows, 8))
    else:
        refs[0][0] = accum
        refs[1][0] = jnp.broadcast_to(best, (rows, 8))
        refs[2][0] = jnp.broadcast_to(total, (rows, 8))


def attend(queries, keys, values, swap, part=0, parts=1, state=None):
    groups, rows, width = queries.shape
    heads, tokens, _ = values.shape
    per_head = groups // heads
    block = math.gcd(rows, 768)
    chunk = math.gcd(tokens, 1024)
    scale = 1.0 / math.sqrt(width)
    finish = part == parts - 1
    wide = pl.BlockSpec((1, block, width), lambda g, i: (g, i, 0))
    thin = pl.BlockSpec((1, block, 8), lambda g, i: (g, i, 0))
    thin_shape = jax.ShapeDtypeStruct((groups, rows, 8), jnp.float32)
    state = () if state is None else tuple(state)
    wide_type = jnp.bfloat16 if finish else jnp.float32
    return pl.pallas_call(
        functools.partial(attend_kernel, chunk, scale, bool(state), finish),
        grid=(groups, rows // block),
        in_specs=[
            pl.BlockSpec(memory_space=pltpu.SMEM),
            wide,
            pl.BlockSpec((1, tokens, width), lambda g, i: (g // per_head, part, 0)),
            pl.BlockSpec((1, tokens, width), lambda g, i: (g // per_head, 0, 0)),
        ]
        + ([wide, thin, thin] if state else []),
        out_specs=[wide, thin] if finish else [wide, thin, thin],
        out_shape=[jax.ShapeDtypeStruct((groups, rows, width), wide_type), thin_shape]
        + ([] if finish else [thin_shape]),
        cost_estimate=pl.CostEstimate(
            flops=8 * groups * rows * tokens * width,
            bytes_accessed=4 * groups * rows * width * 2,
            transcendentals=groups * rows * tokens,
        ),
    )(swap.reshape(1), queries, keys, values, *state)


def bounds(count, left, right):
    return np.log(left / (count - 1 + right)), np.log((count - 1 + left) / right)


def nodes(count, order, left, right):
    low, top = bounds(count, left, right)
    e = np.exp((top - low) / 2 * np.cos(np.pi * (2 * np.arange(order) + 1) / (2 * order)) + (top + low) / 2)
    return ((count - 1 + right) * e - left) / (1 + e)


def cardinals(places, count, order, left, right):
    low, top = bounds(count, left, right)
    at = (2 * np.log((places + left) / (count - 1 + right - places)) - top - low) / (top - low)
    at = np.arccos(np.clip(at, -1.0, 1.0))
    own = np.pi * (2 * np.arange(order) + 1) / (2 * order)
    total = np.zeros((places.size, order))
    for k in range(order):
        total += (1.0 if k == 0 else 2.0) / order * np.cos(k * at)[:, None] * np.cos(k * own)[None, :]
    return total


@functools.lru_cache(maxsize=None)
def fields(length, devices):
    parts, order = PARTS, ORDER
    scale = math.sqrt(0.5) / (2 * length)

    def cot(m):
        return 1.0 / np.tan(np.pi * m / (4 * length))

    n_dev = length // devices
    n_part, t_dev = n_dev // parts, n_dev // 2
    t_part = n_part // 2
    n, t = np.arange(n_part), np.arange(t_part)
    sign_n = np.array([1.0, -1.0, -1.0, 1.0])[n % 4]
    sign_t = np.where(t % 2 == 0, 1.0, -1.0)
    near = sign_t[:, None] * sign_n * scale * cot(4 * t[:, None] - 2 * n + 1.0)
    down = cardinals(n, n_part, order, 1.5, 1.5).T * sign_n
    up = sign_t[:, None] * cardinals(t, t_part, order, 0.75, 0.75)
    part = np.arange(parts)[:, None]
    source = (part * n_part + nodes(n_part, order, 1.5, 1.5)).reshape(-1)
    target = (part * t_part + nodes(t_part, order, 0.75, 0.75)).reshape(-1)
    own = np.arange(parts * order) // order
    same = own[:, None] == own[None, :]
    local = np.where(same, 0.0, scale * cot(np.where(same, 1.0, 4 * target[:, None] - 2 * source + 1)))
    last = n_dev - 1
    wide = float(n_dev)
    merge = np.concatenate(
        [
            cardinals(source, n_dev, EDGE, 1.5, wide).T,
            cardinals(last - source, n_dev, EDGE, 1.5, wide).T,
            cardinals(source, n_dev, FAR, 2 * wide, 2 * wide).T,
        ]
    )
    to_left = nodes(n_dev, EDGE, 1.5, wide)
    sparse = nodes(n_dev, FAR, 2 * wide, 2 * wide)
    size = 3 * EDGE + devices * FAR
    cross = np.zeros((devices, parts * order, size + -size % 128))
    for r in range(devices):
        a = 4 * (target + r * t_dev)[:, None]
        for s in range(devices):
            if abs(r - s) > 1:
                spots, start = sparse, 3 * EDGE + s * FAR
            elif s < r or (s == r and 2 * r >= devices):
                spots, start = last - to_left, EDGE * (r - s)
            else:
                spots, start = to_left, 2 * EDGE * (s - r)
            b = 2 * (spots + s * n_dev)
            block = scale * cot(a + b + 3)
            if r != s:
                block = block + scale * cot(a - b + 1)
            cross[r, :, start : start + block.shape[1]] = block
    return near, down, up, local, merge, cross


def spins(places, width):
    freq = 500000.0 ** (-2.0 * np.arange(width // 2) / width)
    angles = places[:, None] * freq
    cosine, sine = np.cos(angles), np.sin(angles)
    return np.stack(
        [np.concatenate([cosine, cosine], axis=1), np.concatenate([-sine, sine], axis=1)]
    ).astype(np.float32)


def fused_kernel(
    count,
    factor,
    keys_hbm,
    values_hbm,
    queries_hbm,
    places_hbm,
    high_hbm,
    low_hbm,
    near_hbm,
    down_hbm,
    up_hbm,
    local_hbm,
    merge_hbm,
    cross_hbm,
    coarse_hbm,
    fine_hbm,
    out_ref,
    keys_ref,
    values_ref,
    queries_ref,
    places_ref,
    high_ref,
    low_ref,
    near_ref,
    down_ref,
    up_ref,
    local_ref,
    merge_ref,
    cross_ref,
    coarse_ref,
    fine_ref,
    parts_ref,
    whole_ref,
    others_ref,
    close_ref,
    field_ref,
    k_ref,
    v_ref,
    even_ref,
    odd_ref,
    even_top_ref,
    odd_top_ref,
    asks_ref,
    own_ref,
    own_log_ref,
    half_ref,
    half_log_ref,
    merged_ref,
    merged_log_ref,
    over_ref,
    over_log_ref,
    ready_ref,
    ready_log_ref,
    last_ref,
    last_log_ref,
    load_sem,
    token_sem,
    behind_sem,
    end_sem,
    field_send,
    field_recv,
    ask_send,
    ask_recv,
    half_send,
    half_recv,
    over_send,
    over_recv,
    last_send,
):
    me = lax.axis_index("ctx")
    heads, rows, width = queries_ref.shape
    order = ORDER
    blocks = rows // BLOCK
    n_part = near_ref.shape[1]
    t_part = n_part // 2
    half_columns = keys_ref.shape[1]
    tokens = k_ref.shape[1]
    has_left, has_right = me > 0, me < count - 1
    inside = jnp.logical_and(has_left, has_right)
    lower = me < count // 2
    mate = me + 1 - 2 * lax.rem(me, 2)
    far_end = jnp.where(lower, count - 1, 0)
    near_over = jnp.where(lower, count // 2, count // 2 - 1)
    outward = jnp.where(lower, 0, 1)

    def copy(src, dst, send, recv, other):
        return pltpu.make_async_remote_copy(
            src_ref=src,
            dst_ref=dst,
            send_sem=send,
            recv_sem=recv,
            device_id={"ctx": other},
            device_id_type=MESH,
        )

    def for_sides(action):
        for side, there in enumerate((has_left, has_right)):

            @pl.when(there)
            def _():
                action(side)

    def greet(sem, other):
        pl.semaphore_signal(sem, inc=1, device_id={"ctx": other}, device_id_type=MESH)

    others_ref[...] = jnp.zeros_like(others_ref)
    barrier = pltpu.get_barrier_semaphore()
    for_sides(lambda side: greet(barrier, me + 2 * side - 1))
    pairs = (
        (places_hbm, places_ref),
        (queries_hbm, queries_ref),
        (high_hbm, high_ref),
        (low_hbm, low_ref),
        (down_hbm, down_ref),
        (merge_hbm, merge_ref),
        (near_hbm, near_ref),
        (local_hbm, local_ref),
        (cross_hbm.at[me], cross_ref),
        (up_hbm, up_ref),
        (coarse_hbm, coarse_ref),
        (fine_hbm, fine_ref),
    )
    loads = [pltpu.make_async_copy(src, dst, load_sem.at[i]) for i, (src, dst) in enumerate(pairs)]
    sides = ((keys_hbm, keys_ref), (values_hbm, values_ref))
    token_loads = [
        [
            pltpu.make_async_copy(
                src.at[pl.ds(p * n_part, n_part)], dst.at[pl.ds(p * n_part, n_part)], token_sem.at[p, side]
            )
            for side, (src, dst) in enumerate(sides)
        ]
        for p in range(PARTS)
    ]
    for each in loads[:6]:
        each.start()
    for p in range(PARTS):
        for each in token_loads[p]:
            each.start()
    for each in loads[6:]:
        each.start()
    for each in loads[:4]:
        each.wait()

    split = low_ref.shape[0] // 2
    for i in range(rows // split):
        here = slice(i * split, (i + 1) * split)
        place = jnp.broadcast_to(places_ref[here].astype(jnp.float32)[None], (split, split)).T.astype(jnp.int32)
        spun = []
        for value, table_ref in ((place // split, high_ref), (lax.rem(place, split), low_ref)):
            size = table_ref.shape[0] // 2
            value = value if size == split else value[:, :1]
            picked = value == lax.broadcasted_iota(jnp.int32, (split, size), 1)
            picked = jnp.where(picked, 1.0, 0.0).astype(jnp.bfloat16)
            got = jnp.dot(
                jnp.concatenate([picked, picked], axis=1), table_ref[...], preferred_element_type=jnp.float32
            )
            spun.append((got[:, :width], got[:, width:]))
        (cos_a, sin_a), (cos_b, sin_b) = spun
        cosine, sine = cos_a * cos_b - sin_a * sin_b, sin_a * cos_b + cos_a * sin_b
        for head in range(heads):
            x = queries_ref[head, here, :].astype(jnp.float32)
            asks_ref[me, head, here, :] = (x * cosine + pltpu.roll(x, width // 2, 1) * sine).astype(jnp.bfloat16)

    def ask_copy(source, head, block, side):
        here = pl.ds(block * BLOCK if isinstance(block, int) else pl.multiple_of(block * BLOCK, BLOCK), BLOCK)
        return copy(
            asks_ref.at[source, head, here],
            asks_ref.at[source, head, here],
            ask_send.at[source, side],
            ask_recv.at[source, head, block],
            me + 2 * side - 1,
        )

    pl.semaphore_wait(barrier, jnp.where(inside, 2, 1))
    for block in range(blocks - 1):
        for_sides(lambda side: ask_copy(me, 0, block, side).start())
    for_sides(lambda side: greet(behind_sem.at[1 - side], me + 2 * side - 1))

    for each in loads[4:6]:
        each.wait()
    for p in range(PARTS):
        for side, (_, x_ref) in enumerate(sides):
            token_loads[p][side].wait()
            z = jnp.dot(
                down_ref[...], x_ref[p * n_part : (p + 1) * n_part, :], preferred_element_type=jnp.float32
            )
            parts_ref[
                p * order : (p + 1) * order, side * half_columns : (side + 1) * half_columns
            ] = z[:order] + z[order:]
        if p == 1:
            for_sides(lambda side: pl.semaphore_wait(behind_sem.at[side], 1))

            @pl.when(inside)
            def _():
                greet(end_sem, mate)

    whole_ref[...] = strict_dot(merge_ref[...], parts_ref[...])
    others_ref[:EDGE] = whole_ref[pl.ds(pl.multiple_of(jnp.where(lower, 0, EDGE), EDGE), EDGE), :]

    def near_copy(side):
        other = me + 2 * side - 1
        return copy(
            whole_ref.at[pl.ds(side * EDGE, EDGE)],
            others_ref.at[pl.ds(EDGE * (2 - side), EDGE)],
            field_send.at[other],
            field_recv.at[me],
            other,
        )

    def far_copy(other):
        return copy(
            whole_ref.at[pl.ds(2 * EDGE, FAR)],
            others_ref.at[pl.ds(pl.multiple_of(3 * EDGE + me * FAR, FAR), FAR)],
            field_send.at[other],
            field_recv.at[me],
            other,
        )

    def near_wait(side):
        source = me + 2 * side - 1
        copy(
            whole_ref.at[pl.ds(0, EDGE)],
            others_ref.at[pl.ds(EDGE * (1 + side), EDGE)],
            field_send.at[source],
            field_recv.at[source],
            source,
        ).wait_recv()

    def far_wait(source):
        copy(
            whole_ref.at[pl.ds(2 * EDGE, FAR)],
            others_ref.at[pl.ds(3 * EDGE + source * FAR, FAR)],
            field_send.at[source],
            field_recv.at[source],
            source,
        ).wait_recv()

    def ask_sent(source, side):
        copy(
            asks_ref.at[source],
            asks_ref.at[source],
            ask_send.at[source, side],
            ask_recv.at[source, 0, 0],
            me + 2 * side - 1,
        ).wait_send()

    def hand(source, head, block, side):
        handed = ask_copy(source, head, block, side)
        handed.wait_recv()
        handed.start()

    def for_far(action):
        for other in range(count):

            @pl.when(jnp.logical_or(other - me > 1, me - other > 1))
            def _():
                action(other)

    @pl.when(jnp.logical_not(inside))
    def _():
        pl.semaphore_wait(end_sem, 1)

    for_far(lambda other: far_copy(other).start())
    for_sides(lambda side: near_copy(side).start())
    for_sides(lambda side: ask_copy(me, 0, blocks - 1, side).start())

    @pl.when(jnp.logical_not(inside))
    def _():
        for block in range(blocks):
            ask_copy(me, 1, block, 1 - outward).start()

    loads[6].wait()

    def close(p, carry):
        start = p * n_part if isinstance(p, int) else pl.multiple_of(p * n_part, n_part)
        for side, (_, x_ref) in enumerate(sides):
            z = jnp.dot(near_ref[...], x_ref[pl.ds(start, n_part), :], preferred_element_type=jnp.float32)
            close_ref[p, :, side * half_columns : (side + 1) * half_columns] = z[:t_part] + z[t_part:]
        return carry

    close(0, 0)

    @pl.when(inside)
    def _():
        for block in range(blocks):
            for side in range(2):
                hand(me + 2 * side - 1, 0, block, 1 - side)
        ask_copy(me, 1, 0, outward).start()

    lax.fori_loop(1, PARTS, close, 0)

    @pl.when(inside)
    def _():
        hand(mate, 1, 0, 1 - outward)
        ask_copy(me, 1, 1, outward).start()

    for each in loads[7:]:
        each.wait()
    field_ref[...] = strict_dot(local_ref[...], parts_ref[...])

    for_sides(near_wait)
    for_far(far_wait)
    field_ref[...] += strict_dot(cross_ref[...], others_ref[...])

    def finish(head):
        k_columns = slice(head * width, (head + 1) * width)
        v_columns = slice(half_columns + head * width, half_columns + (head + 1) * width)

        def one(p, carry):
            at = pl.ds(pl.multiple_of(p * order, order), order)
            f = jnp.concatenate([field_ref[at, k_columns], field_ref[at, v_columns]], axis=1)
            high = f.astype(jnp.bfloat16)
            low = (f - high.astype(jnp.float32)).astype(jnp.bfloat16)
            y = jnp.dot(
                up_ref[...], jnp.concatenate([high, low, high], axis=0), preferred_element_type=jnp.float32
            )
            k = (close_ref[p, :, k_columns] + y[:, :width]).astype(jnp.bfloat16).astype(jnp.float32)
            v = (close_ref[p, :, v_columns] + y[:, width:]).astype(jnp.bfloat16).astype(jnp.float32)
            begin = pl.multiple_of(p * t_part, t_part)
            place = me * PARTS + p
            cos_p, sin_p = coarse_ref[0, pl.ds(place, 1), :], coarse_ref[1, pl.ds(place, 1), :]
            cosine = cos_p * fine_ref[0] - sin_p * fine_ref[1]
            sine = sin_p * fine_ref[0] + cos_p * fine_ref[1]
            turned = k * cosine + pltpu.roll(k, width // 2, 1) * sine
            k_ref[head, pl.ds(begin, t_part), :] = turned.astype(jnp.bfloat16)
            v_ref[head, :, pl.ds(begin, t_part)] = v.T.astype(jnp.bfloat16)
            return carry

        lax.fori_loop(0, PARTS, one, 0)

    finish(0)

    @pl.when(inside)
    def _():
        for block in range(1, blocks):
            hand(mate, 1, block, 1 - outward)
        for block in range(blocks):
            ask_copy(me, 1, block, 1 - outward).start()

    runs = [
        (0, 0, 0, blocks),
        (1, 0, 0, blocks),
        (2, 0, 0, blocks),
        (3, 0, 0, blocks - 1),
        (2, 1, 0, blocks),
        (3, 0, blocks - 1, 1),
        (3, 1, 0, 1),
        (1, 1, 0, blocks),
        (0, 1, 0, blocks),
        (3, 1, 1, blocks - 1),
    ]
    begins = [sum(run[3] for run in runs[:i]) for i in range(len(runs))]
    units = begins[-1] + runs[-1][3]

    def decode(u):
        kind, head, block = runs[0][0], runs[0][1], u
        for begin, run in zip(begins[1:], runs[1:]):
            late = u >= begin
            kind = jnp.where(late, run[0], kind)
            head = jnp.where(late, run[1], head)
            block = jnp.where(late, u - begin + run[2], block)
        source = jnp.where(
            kind == 0, mate, jnp.where(kind == 1, near_over, jnp.where(kind == 2, far_end, me))
        )
        return kind, head, block, source

    chunk = 512

    def score(u, keep_ref, top_ref):
        _, head, block, source = decode(u)
        q = asks_ref[source, head, pl.ds(pl.multiple_of(block * BLOCK, BLOCK), BLOCK), :]
        best = None
        for c in range(0, tokens, chunk):
            s = lax.dot_general(
                k_ref[head, c : c + chunk, :],
                q,
                (((1,), (1,)), ((), ())),
                preferred_element_type=jnp.float32,
            )
            keep_ref[c : c + chunk, :] = s
            top = jnp.max(s, axis=0, keepdims=True)
            best = top if best is None else jnp.maximum(best, top)
        top_ref[...] = best

    def weigh(u, keep_ref, top_ref):
        kind, head, block, _ = decode(u)
        best = top_ref[...]
        total = jnp.zeros((1, BLOCK), jnp.float32)
        accum = jnp.zeros((width, BLOCK), jnp.float32)
        for c in range(0, tokens, chunk):
            e = jnp.exp2((keep_ref[c : c + chunk, :] - best) * factor)
            total += jnp.sum(e, axis=0, keepdims=True)
            accum += jnp.dot(
                v_ref[head, :, c : c + chunk], e.astype(jnp.bfloat16), preferred_element_type=jnp.float32
            )
        own_ref[kind, head, block] = (accum / total).astype(jnp.bfloat16)
        own_log_ref[kind, head, block] = best * factor + jnp.log2(total)

    def both(src, src_log, dst, dst_log, send, recv, other):
        return (
            copy(src, dst, send.at[0], recv.at[0], other),
            copy(src_log, dst_log, send.at[1], recv.at[1], other),
        )

    def half_copy(kind, head, block):
        at = (kind, head, block)
        return both(
            own_ref.at[at],
            own_log_ref.at[at],
            half_ref.at[at],
            half_log_ref.at[at],
            half_send,
            half_recv.at[at],
            mate,
        )

    def over_copy(j, head, block):
        at = (j, head, block)
        return both(
            merged_ref.at[at],
            merged_log_ref.at[at],
            over_ref.at[at],
            over_log_ref.at[at],
            over_send,
            over_recv.at[at],
            near_over,
        )

    def last_copy(head, block):
        at = (head, block)
        return both(
            ready_ref.at[at],
            ready_log_ref.at[at],
            last_ref.at[at],
            last_log_ref.at[at],
            last_send,
            half_recv.at[(0,) + at],
            mate,
        )

    def blend(parts, logs):
        best = functools.reduce(jnp.maximum, logs)
        shares = [jnp.exp2(log - best) for log in logs]
        total = functools.reduce(jnp.add, shares)
        mixed = functools.reduce(
            jnp.add, [part.astype(jnp.float32) * (share / total) for part, share in zip(parts, shares)]
        )
        return mixed, best + jnp.log2(total)

    def merge_half(kind, head, block):
        for each in half_copy(kind, head, block):
            each.wait_recv()
        at = (kind - 1, head, block)
        mixed, log = blend(
            [own_ref[kind, head, block], half_ref[kind, head, block]],
            [own_log_ref[kind, head, block], half_log_ref[kind, head, block]],
        )
        merged_ref[at] = mixed.astype(jnp.bfloat16)
        merged_log_ref[at] = log
        for each in over_copy(*at):
            each.start()

    def settle(head, block):
        for each in half_copy(0, head, block) + over_copy(0, head, block):
            each.wait_recv()
        mixed, _ = blend(
            [own_ref[3, head, block], half_ref[0, head, block], over_ref[0, head, block]],
            [own_log_ref[3, head, block], half_log_ref[0, head, block], over_log_ref[0, head, block]],
        )
        out_ref[head, block * BLOCK : (block + 1) * BLOCK, :] = mixed.T.astype(out_ref.dtype)

    def pass_on(head, block):
        for each in over_copy(1, head, block):
            each.wait_recv()
        mixed, log = blend(
            [own_ref[0, head, block], over_ref[1, head, block]],
            [own_log_ref[0, head, block], over_log_ref[1, head, block]],
        )
        ready_ref[head, block] = mixed.astype(jnp.bfloat16)
        ready_log_ref[head, block] = log
        for each in last_copy(head, block):
            each.start()

    def await_ask(u):
        kind, head, block, source = decode(u)

        @pl.when(jnp.logical_and(kind < 3, jnp.logical_not(inside)))
        def _():
            ask_copy(source, head, block, 1 - outward).wait_recv()

    merges = ((1, 0, begins[1] + 9), (2, 0, begins[2] + 12))

    def send_on(u):
        kind, head, block, _ = decode(u)

        @pl.when(jnp.logical_and(kind < 3, jnp.logical_not(inside)))
        def _():
            for each in half_copy(kind, head, block):
                each.start()

        for kind, head, first in merges:
            k = u - first

            @pl.when(jnp.logical_and(inside, jnp.logical_and(k >= 0, k < blocks)))
            def _():
                merge_half(kind, head, k)

    await_ask(jnp.int32(0))
    score(jnp.int32(0), even_ref, even_top_ref)

    def serve(i, carry):
        u = 2 * i
        for at, source, head in ((0, far_end, 0), (3, far_end, 1), (5, near_over, 1)):

            @pl.when(jnp.logical_and(inside, i == at))
            def _():
                for block in range(blocks):
                    hand(source, head, block, outward)
                if source is near_over:
                    for block in range(2, blocks):
                        ask_copy(me, 1, block, outward).start()

        @pl.when(i == 2)
        def _():
            finish(1)

        await_ask(u + 1)
        score(u + 1, odd_ref, odd_top_ref)
        weigh(u, even_ref, even_top_ref)
        send_on(u)
        ahead = jnp.minimum(u + 2, units - 1)

        @pl.when(u + 2 < units)
        def _():
            await_ask(ahead)

        score(ahead, even_ref, even_top_ref)
        weigh(u + 1, odd_ref, odd_top_ref)
        send_on(u + 1)
        return carry

    lax.fori_loop(0, units // 2, serve, 0)

    @pl.when(inside)
    def _():
        for block in range(blocks):
            pass_on(0, block)
            merge_half(2, 1, block)
        for block in range(blocks):
            pass_on(1, block)
            merge_half(1, 1, block)
        ask_sent(me - 1, 1)
        ask_sent(me + 1, 0)
        ask_sent(far_end, outward)

    for_sides(lambda side: ask_sent(me, side))
    for_sides(lambda side: near_copy(side).wait_send())
    for_far(lambda other: far_copy(other).wait_send())

    @pl.when(inside)
    def _():
        for head in range(heads):
            for block in range(blocks):
                settle(head, block)
        for each in both(
            merged_ref, merged_log_ref, over_ref, over_log_ref, over_send, over_recv.at[0, 0, 0], near_over
        ) + both(ready_ref, ready_log_ref, last_ref, last_log_ref, last_send, half_recv.at[0, 0, 0], mate):
            each.wait_send()

    @pl.when(jnp.logical_not(inside))
    def _():
        for head in range(heads):
            for block in range(blocks):
                for each in last_copy(head, block):
                    each.wait_recv()
                mixed, _ = blend(
                    [own_ref[3, head, block], last_ref[head, block]],
                    [own_log_ref[3, head, block], last_log_ref[head, block]],
                )
                out_ref[head, block * BLOCK : (block + 1) * BLOCK, :] = mixed.T.astype(out_ref.dtype)
        kinds = pl.ds(0, 3)
        for each in both(
            own_ref.at[kinds], own_log_ref.at[kinds], half_ref, half_log_ref, half_send, half_recv.at[0, 0, 0], mate
        ):
            each.wait_send()


def by_tokens(keys, values, queries, positions, count):
    heads, rows, width = queries.shape
    n_dev, columns = keys.shape
    length = n_dev * count
    near, down, up, local, merge, cross = fields(length, count)

    def tall(matrix):
        return np.concatenate(split_two(matrix), axis=-2)

    def table(places):
        return tall(np.concatenate(spins(places, width).astype(np.float64), axis=1))

    up_high, up_low = split_two(up)
    t_part = near.shape[0]
    tokens = n_dev // 2
    blocks = rows // BLOCK
    split = 128
    operands = (
        table(np.arange(length // split) * float(split)),
        table(np.arange(split) * 1.0),
        tall(near),
        tall(down),
        np.concatenate([up_high, up_high, up_low], axis=1),
        tall(local),
        tall(merge),
        tall(cross),
        spins(np.arange(count * PARTS) * float(t_part), width),
        spins(np.arange(t_part) * 1.0, width),
    )
    held = [jax.ShapeDtypeStruct(o.shape[1:] if o.ndim == 3 and o.shape[0] == count else o.shape, o.dtype) for o in operands]
    dma = pltpu.SemaphoreType.DMA

    def parts(*lead):
        return [
            pltpu.VMEM(lead + (heads, blocks, width, BLOCK), jnp.bfloat16),
            pltpu.VMEM(lead + (heads, blocks, 1, BLOCK), jnp.float32),
        ]

    return pl.pallas_call(
        functools.partial(fused_kernel, count, math.log2(math.e) / math.sqrt(width)),
        in_specs=[pl.BlockSpec(memory_space=pl.ANY)] * 14,
        out_specs=pl.BlockSpec(memory_space=pltpu.VMEM),
        out_shape=jax.ShapeDtypeStruct(queries.shape, jnp.bfloat16),
        scratch_shapes=[
            pltpu.VMEM(keys.shape, keys.dtype),
            pltpu.VMEM(values.shape, values.dtype),
            pltpu.VMEM(queries.shape, queries.dtype),
            pltpu.VMEM((rows,), jnp.int32),
        ]
        + [pltpu.VMEM(h.shape, h.dtype) for h in held]
        + [
            pltpu.VMEM((PARTS * ORDER, 2 * columns), jnp.float32),
            pltpu.VMEM((2 * EDGE + FAR, 2 * columns), jnp.float32),
            pltpu.VMEM((cross.shape[2], 2 * columns), jnp.float32),
            pltpu.VMEM((PARTS, t_part, 2 * columns), jnp.float32),
            pltpu.VMEM((PARTS * ORDER, 2 * columns), jnp.float32),
            pltpu.VMEM((heads, tokens, width), jnp.bfloat16),
            pltpu.VMEM((heads, width, tokens), jnp.bfloat16),
            pltpu.VMEM((tokens, BLOCK), jnp.float32),
            pltpu.VMEM((tokens, BLOCK), jnp.float32),
            pltpu.VMEM((1, BLOCK), jnp.float32),
            pltpu.VMEM((1, BLOCK), jnp.float32),
            pltpu.VMEM((count, heads, rows, width), jnp.bfloat16),
        ]
        + parts(4)
        + parts(3)
        + parts(2)
        + parts(2)
        + parts()
        + parts()
        + [
            dma((12,)),
            dma((PARTS, 2)),
            pltpu.SemaphoreType.REGULAR((2,)),
            pltpu.SemaphoreType.REGULAR,
            dma((count,)),
            dma((count,)),
            dma((count, 2)),
            dma((count, heads, blocks)),
            dma((2,)),
            dma((3, heads, blocks, 2)),
            dma((2,)),
            dma((2, heads, blocks, 2)),
            dma((2,)),
        ],
        compiler_params=pltpu.CompilerParams(
            collective_id=0, has_side_effects=True, vmem_limit_bytes=60 * 1024 * 1024
        ),
    )(keys, values, queries, positions, *operands)


def by_columns(keys, values, queries, positions):
    key_parts = lax.all_to_all(keys, "ctx", split_axis=1, concat_axis=0, tiled=True)
    value_parts = lax.all_to_all(values, "ctx", split_axis=1, concat_axis=0, tiled=True)
    heads, rows, width = queries.shape
    per_device = key_parts.shape[1]
    compact = compress(jnp.concatenate([key_parts, value_parts], axis=1))
    rotated = rotate_rows(queries.astype(jnp.float32), positions.astype(jnp.float32)).astype(
        jnp.bfloat16
    )
    whole = lax.all_gather(compact.T, "ctx", axis=0, tiled=True)
    tokens = whole.shape[1]
    shaped = whole.reshape(-1, 2, per_device, tokens)
    key_rows = shaped[:, 0].reshape(heads, width, tokens).swapaxes(1, 2)
    value_rows = shaped[:, 1].reshape(heads, width, tokens).swapaxes(1, 2)
    places = jnp.arange(tokens).astype(jnp.float32)
    ready = rotate_rows(key_rows.astype(jnp.float32), places).astype(jnp.bfloat16)
    return attend(rotated, ready, value_rows, jnp.zeros((), jnp.int32))[0]


def solution(mesh):
    count = mesh.shape["ctx"]

    def on_device(keys, values, queries, positions):
        heads, rows, width = queries.shape
        if count == 4 and heads == 2 and keys.shape[0] % (PARTS * 512) == 0 and rows % BLOCK == 0 and width == 128:
            return by_tokens(keys, values, queries, positions, count)
        return by_columns(keys, values, queries, positions)

    return jax.shard_map(
        on_device,
        mesh=mesh,
        in_specs=(
            P(("user", "ctx"), "heads"),
            P(("user", "ctx"), "heads"),
            P("heads", ("user", "ctx"), None),
            P(("user", "ctx")),
        ),
        out_specs=P("heads", ("user", "ctx"), None),
        check_vma=False,
    )
```

```python
import functools
import math

import jax
import jax.numpy as jnp
import numpy as np
from jax import lax
from jax.experimental import pallas as pl
from jax.experimental.pallas import tpu as pltpu
from jax.sharding import PartitionSpec as P

OUTER = 128
PARTS = 4
ORDER = 64
EDGE = 32
FAR = 8
BLOCK = 256
MESH = pl.DeviceIdType.MESH


def split_two(matrix):
    high = matrix.astype(jnp.bfloat16)
    low = (matrix - np.asarray(high).astype(np.float64)).astype(jnp.bfloat16)
    return high, low


@functools.lru_cache(maxsize=None)
def stages(length):
    outer = OUTER
    inner = length // outer
    step = inner // 2
    a = np.arange(outer)
    c = np.arange(outer)
    turn = 2 * outer
    angle = np.pi / outer * ((c[:, None] * a[None, :]) % turn)
    alternate = np.where(a % 2 == 0, 1.0, -1.0)
    first = np.stack([np.cos(angle), -np.sin(angle)], axis=1)
    first[0, 1] = alternate
    d = np.arange(length // 2 // turn)
    k = np.concatenate([c[:, None] + turn * d, (turn - c[:, None]) % turn + turn * d], axis=1)
    k[0, d.size :] = outer + turn * d
    sign = np.concatenate([np.ones(d.size), -np.ones(d.size)])
    b = np.arange(inner)
    q = np.arange(step)
    theta = np.pi / (2 * length) * ((k[:, :, None] * (2 * b + 1)) % (4 * length))
    phi = np.pi / length * ((k[:, None, :] * (2 * q + 1)[:, None]) % (2 * length))
    forward = np.stack([np.cos(theta), np.sin(theta) * sign[None, :, None]], axis=2)
    weight = np.where(k == 0, 1.0, 2.0) / length
    back = np.stack([np.cos(phi), np.sin(phi) * sign], axis=1) * weight[:, None, None, :]
    half = d.size
    forward[0, :half, 1] = 0.0
    forward[0, half:, 1] = np.cos(theta[0, half:])
    forward[0, half:, 0] = 0.0
    back[0, 1, :, :half] = 0.0
    back[0, 1, :, half:] = np.cos(phi[0, :, half:]) * weight[0, half:]
    back[0, 0, :, half:] = 0.0
    middle = back.reshape(outer, 2 * step, 2 * half) @ forward.reshape(outer, 2 * half, 2 * inner)
    last = first.transpose(2, 0, 1).reshape(outer, 2 * outer)
    return first.reshape(2 * outer, outer), middle, last


def compress(signal):
    length, columns = signal.shape
    outer, inner = OUTER, length // OUTER
    first, middle, last = stages(length)
    first_high, first_low = split_two(first)
    flat = signal.reshape(outer, inner * columns)
    one = jnp.dot(first_high, flat, preferred_element_type=jnp.float32) + jnp.dot(
        first_low, flat, preferred_element_type=jnp.float32
    )
    one = one.reshape(outer, 2 * inner, columns)
    two = jnp.einsum(
        "cob,cbl->col", jnp.asarray(middle.astype(np.float32)), one, precision=lax.Precision.HIGH
    )
    three = jnp.dot(
        jnp.asarray(last.astype(np.float32)),
        two.reshape(2 * outer, inner // 2 * columns),
        precision=lax.Precision.HIGH,
    )
    return three.reshape(length // 2, columns).astype(jnp.bfloat16)

def strict_dot(left, right):
    rows, columns = left.shape[0] // 2, right.shape[1]
    high = right.astype(jnp.bfloat16)
    low = (right - high.astype(jnp.float32)).astype(jnp.bfloat16)
    both = jnp.dot(
        left, jnp.concatenate([high, low], axis=1), preferred_element_type=jnp.float32
    )
    return both[:rows, :columns] + (both[:rows, columns:] + both[rows:, :columns])


def inverse_freq(width):
    return jnp.exp(jnp.arange(width // 2).astype(jnp.float32) * (-2.0 * math.log(500000.0) / width))


def rotate_rows(block, places):
    width = block.shape[-1]
    half = width // 2
    angles = places[:, None] * inverse_freq(width)[None, :]
    cosine = jnp.cos(angles)
    sine = jnp.sin(angles)
    first = block[..., :half]
    second = block[..., half:]
    return jnp.concatenate(
        [first * cosine - second * sine, second * cosine + first * sine], axis=-1
    )


def attend_kernel(chunk, scale, resume, finish, swap_ref, q_ref, k_ref, v_ref, *refs):
    q = q_ref[0]
    swap = swap_ref[0] == 1
    rows, width = q.shape
    factor = scale * math.log2(math.e)
    if resume:
        accum = refs[0][0]
        best = refs[1][0][:, :1]
        total = refs[2][0][:, :1]
        refs = refs[3:]
    else:
        best = jnp.full((rows, 1), -jnp.inf, jnp.float32)
        total = jnp.zeros((rows, 1), jnp.float32)
        accum = jnp.zeros((rows, width), jnp.float32)
    tokens = k_ref.shape[1]
    for start in range(0, tokens, chunk):
        one = k_ref[0, start : start + chunk, :]
        two = v_ref[0, start : start + chunk, :]
        k, v = jnp.where(swap, two, one), jnp.where(swap, one, two)
        scores = lax.dot_general(
            q, k, (((1,), (1,)), ((), ())), preferred_element_type=jnp.float32
        )
        fresh = jnp.maximum(best, jnp.max(scores, axis=1, keepdims=True))
        expo = jnp.exp2((scores - fresh) * factor)
        shrink = jnp.exp2((best - fresh) * factor)
        total = total * shrink + jnp.sum(expo, axis=1, keepdims=True)
        accum = accum * shrink + jnp.dot(
            expo.astype(jnp.bfloat16), v, preferred_element_type=jnp.float32
        )
        best = fresh
    if finish:
        refs[0][0] = (accum / total).astype(refs[0].dtype)
        refs[1][0] = jnp.broadcast_to(best * factor + jnp.log2(total), (rows, 8))
    else:
        refs[0][0] = accum
        refs[1][0] = jnp.broadcast_to(best, (rows, 8))
        refs[2][0] = jnp.broadcast_to(total, (rows, 8))


def attend(queries, keys, values, swap, part=0, parts=1, state=None):
    groups, rows, width = queries.shape
    heads, tokens, _ = values.shape
    per_head = groups // heads
    block = math.gcd(rows, 768)
    chunk = math.gcd(tokens, 1024)
    scale = 1.0 / math.sqrt(width)
    finish = part == parts - 1
    wide = pl.BlockSpec((1, block, width), lambda g, i: (g, i, 0))
    thin = pl.BlockSpec((1, block, 8), lambda g, i: (g, i, 0))
    thin_shape = jax.ShapeDtypeStruct((groups, rows, 8), jnp.float32)
    state = () if state is None else tuple(state)
    wide_type = jnp.bfloat16 if finish else jnp.float32
    return pl.pallas_call(
        functools.partial(attend_kernel, chunk, scale, bool(state), finish),
        grid=(groups, rows // block),
        in_specs=[
            pl.BlockSpec(memory_space=pltpu.SMEM),
            wide,
            pl.BlockSpec((1, tokens, width), lambda g, i: (g // per_head, part, 0)),
            pl.BlockSpec((1, tokens, width), lambda g, i: (g // per_head, 0, 0)),
        ]
        + ([wide, thin, thin] if state else []),
        out_specs=[wide, thin] if finish else [wide, thin, thin],
        out_shape=[jax.ShapeDtypeStruct((groups, rows, width), wide_type), thin_shape]
        + ([] if finish else [thin_shape]),
        cost_estimate=pl.CostEstimate(
            flops=8 * groups * rows * tokens * width,
            bytes_accessed=4 * groups * rows * width * 2,
            transcendentals=groups * rows * tokens,
        ),
    )(swap.reshape(1), queries, keys, values, *state)


def bounds(count, left, right):
    return np.log(left / (count - 1 + right)), np.log((count - 1 + left) / right)


def nodes(count, order, left, right):
    low, top = bounds(count, left, right)
    e = np.exp((top - low) / 2 * np.cos(np.pi * (2 * np.arange(order) + 1) / (2 * order)) + (top + low) / 2)
    return ((count - 1 + right) * e - left) / (1 + e)


def cardinals(places, count, order, left, right):
    low, top = bounds(count, left, right)
    at = (2 * np.log((places + left) / (count - 1 + right - places)) - top - low) / (top - low)
    at = np.arccos(np.clip(at, -1.0, 1.0))
    own = np.pi * (2 * np.arange(order) + 1) / (2 * order)
    total = np.zeros((places.size, order))
    for k in range(order):
        total += (1.0 if k == 0 else 2.0) / order * np.cos(k * at)[:, None] * np.cos(k * own)[None, :]
    return total


@functools.lru_cache(maxsize=None)
def fields(length, devices):
    parts, order = PARTS, ORDER
    scale = math.sqrt(0.5) / (2 * length)

    def cot(m):
        return 1.0 / np.tan(np.pi * m / (4 * length))

    n_dev = length // devices
    n_part, t_dev = n_dev // parts, n_dev // 2
    t_part = n_part // 2
    n, t = np.arange(n_part), np.arange(t_part)
    sign_n = np.array([1.0, -1.0, -1.0, 1.0])[n % 4]
    sign_t = np.where(t % 2 == 0, 1.0, -1.0)
    near = sign_t[:, None] * sign_n * scale * cot(4 * t[:, None] - 2 * n + 1.0)
    down = cardinals(n, n_part, order, 1.5, 1.5).T * sign_n
    up = sign_t[:, None] * cardinals(t, t_part, order, 0.75, 0.75)
    part = np.arange(parts)[:, None]
    source = (part * n_part + nodes(n_part, order, 1.5, 1.5)).reshape(-1)
    target = (part * t_part + nodes(t_part, order, 0.75, 0.75)).reshape(-1)
    own = np.arange(parts * order) // order
    same = own[:, None] == own[None, :]
    local = np.where(same, 0.0, scale * cot(np.where(same, 1.0, 4 * target[:, None] - 2 * source + 1)))
    last = n_dev - 1
    wide = float(n_dev)
    merge = np.concatenate(
        [
            cardinals(source, n_dev, EDGE, 1.5, wide).T,
            cardinals(last - source, n_dev, EDGE, 1.5, wide).T,
            cardinals(source, n_dev, FAR, 2 * wide, 2 * wide).T,
        ]
    )
    to_left = nodes(n_dev, EDGE, 1.5, wide)
    sparse = nodes(n_dev, FAR, 2 * wide, 2 * wide)
    size = 3 * EDGE + devices * FAR
    cross = np.zeros((devices, parts * order, size + -size % 128))
    for r in range(devices):
        a = 4 * (target + r * t_dev)[:, None]
        for s in range(devices):
            if abs(r - s) > 1:
                spots, start = sparse, 3 * EDGE + s * FAR
            elif s < r or (s == r and 2 * r >= devices):
                spots, start = last - to_left, EDGE * (r - s)
            else:
                spots, start = to_left, 2 * EDGE * (s - r)
            b = 2 * (spots + s * n_dev)
            block = scale * cot(a + b + 3)
            if r != s:
                block = block + scale * cot(a - b + 1)
            cross[r, :, start : start + block.shape[1]] = block
    return near, down, up, local, merge, cross


def spins(places, width):
    freq = 500000.0 ** (-2.0 * np.arange(width // 2) / width)
    angles = places[:, None] * freq
    cosine, sine = np.cos(angles), np.sin(angles)
    return np.stack(
        [np.concatenate([cosine, cosine], axis=1), np.concatenate([-sine, sine], axis=1)]
    ).astype(np.float32)


def fused_kernel(
    count,
    factor,
    keys_hbm,
    values_hbm,
    queries_hbm,
    places_hbm,
    high_hbm,
    low_hbm,
    near_hbm,
    down_hbm,
    up_hbm,
    local_hbm,
    merge_hbm,
    cross_hbm,
    coarse_hbm,
    fine_hbm,
    out_ref,
    keys_ref,
    values_ref,
    queries_ref,
    places_ref,
    high_ref,
    low_ref,
    near_ref,
    down_ref,
    up_ref,
    local_ref,
    merge_ref,
    cross_ref,
    coarse_ref,
    fine_ref,
    parts_ref,
    whole_ref,
    others_ref,
    close_ref,
    field_ref,
    k_ref,
    v_ref,
    even_ref,
    odd_ref,
    even_top_ref,
    odd_top_ref,
    asks_ref,
    own_ref,
    own_log_ref,
    half_ref,
    half_log_ref,
    merged_ref,
    merged_log_ref,
    over_ref,
    over_log_ref,
    ready_ref,
    ready_log_ref,
    last_ref,
    last_log_ref,
    load_sem,
    token_sem,
    behind_sem,
    end_sem,
    field_send,
    field_recv,
    ask_send,
    ask_recv,
    half_send,
    half_recv,
    over_send,
    over_recv,
    last_send,
):
    me = lax.axis_index("ctx")
    heads, rows, width = queries_ref.shape
    order = ORDER
    blocks = rows // BLOCK
    n_part = near_ref.shape[1]
    t_part = n_part // 2
    half_columns = keys_ref.shape[1]
    tokens = k_ref.shape[1]
    has_left, has_right = me > 0, me < count - 1
    inside = jnp.logical_and(has_left, has_right)
    lower = me < count // 2
    mate = me + 1 - 2 * lax.rem(me, 2)
    far_end = jnp.where(lower, count - 1, 0)
    near_over = jnp.where(lower, count // 2, count // 2 - 1)
    outward = jnp.where(lower, 0, 1)

    def copy(src, dst, send, recv, other):
        return pltpu.make_async_remote_copy(
            src_ref=src,
            dst_ref=dst,
            send_sem=send,
            recv_sem=recv,
            device_id={"ctx": other},
            device_id_type=MESH,
        )

    def for_sides(action):
        for side, there in enumerate((has_left, has_right)):

            @pl.when(there)
            def _():
                action(side)

    def greet(sem, other):
        pl.semaphore_signal(sem, inc=1, device_id={"ctx": other}, device_id_type=MESH)

    others_ref[...] = jnp.zeros_like(others_ref)
    barrier = pltpu.get_barrier_semaphore()
    for_sides(lambda side: greet(barrier, me + 2 * side - 1))
    pairs = (
        (places_hbm, places_ref),
        (queries_hbm, queries_ref),
        (high_hbm, high_ref),
        (low_hbm, low_ref),
        (down_hbm, down_ref),
        (merge_hbm, merge_ref),
        (near_hbm, near_ref),
        (local_hbm, local_ref),
        (cross_hbm.at[me], cross_ref),
        (up_hbm, up_ref),
        (coarse_hbm, coarse_ref),
        (fine_hbm, fine_ref),
    )
    loads = [pltpu.make_async_copy(src, dst, load_sem.at[i]) for i, (src, dst) in enumerate(pairs)]
    sides = ((keys_hbm, keys_ref), (values_hbm, values_ref))
    token_loads = [
        [
            pltpu.make_async_copy(
                src.at[pl.ds(p * n_part, n_part)], dst.at[pl.ds(p * n_part, n_part)], token_sem.at[p, side]
            )
            for side, (src, dst) in enumerate(sides)
        ]
        for p in range(PARTS)
    ]
    for each in loads[:6]:
        each.start()
    for p in range(PARTS):
        for each in token_loads[p]:
            each.start()
    for each in loads[6:]:
        each.start()
    for each in loads[:4]:
        each.wait()

    split = low_ref.shape[0] // 2
    for i in range(rows // split):
        here = slice(i * split, (i + 1) * split)
        place = jnp.broadcast_to(places_ref[here].astype(jnp.float32)[None], (split, split)).T.astype(jnp.int32)
        spun = []
        for value, table_ref in ((place // split, high_ref), (lax.rem(place, split), low_ref)):
            size = table_ref.shape[0] // 2
            value = value if size == split else value[:, :1]
            picked = value == lax.broadcasted_iota(jnp.int32, (split, size), 1)
            picked = jnp.where(picked, 1.0, 0.0).astype(jnp.bfloat16)
            got = jnp.dot(
                jnp.concatenate([picked, picked], axis=1), table_ref[...], preferred_element_type=jnp.float32
            )
            spun.append((got[:, :width], got[:, width:]))
        (cos_a, sin_a), (cos_b, sin_b) = spun
        cosine, sine = cos_a * cos_b - sin_a * sin_b, sin_a * cos_b + cos_a * sin_b
        for head in range(heads):
            x = queries_ref[head, here, :].astype(jnp.float32)
            asks_ref[me, head, here, :] = (x * cosine + pltpu.roll(x, width // 2, 1) * sine).astype(jnp.bfloat16)

    def ask_copy(source, head, block, side):
        here = pl.ds(block * BLOCK if isinstance(block, int) else pl.multiple_of(block * BLOCK, BLOCK), BLOCK)
        return copy(
            asks_ref.at[source, head, here],
            asks_ref.at[source, head, here],
            ask_send.at[source, side],
            ask_recv.at[source, head, block],
            me + 2 * side - 1,
        )

    pl.semaphore_wait(barrier, jnp.where(inside, 2, 1))
    for block in range(blocks - 1):
        for_sides(lambda side: ask_copy(me, 0, block, side).start())
    for_sides(lambda side: greet(behind_sem.at[1 - side], me + 2 * side - 1))

    for each in loads[4:6]:
        each.wait()
    for p in range(PARTS):
        for side, (_, x_ref) in enumerate(sides):
            token_loads[p][side].wait()
            z = jnp.dot(
                down_ref[...], x_ref[p * n_part : (p + 1) * n_part, :], preferred_element_type=jnp.float32
            )
            parts_ref[
                p * order : (p + 1) * order, side * half_columns : (side + 1) * half_columns
            ] = z[:order] + z[order:]
        if p == 1:
            for_sides(lambda side: pl.semaphore_wait(behind_sem.at[side], 1))

            @pl.when(inside)
            def _():
                greet(end_sem, mate)

    whole_ref[...] = strict_dot(merge_ref[...], parts_ref[...])
    others_ref[:EDGE] = whole_ref[pl.ds(pl.multiple_of(jnp.where(lower, 0, EDGE), EDGE), EDGE), :]

    def near_copy(side):
        other = me + 2 * side - 1
        return copy(
            whole_ref.at[pl.ds(side * EDGE, EDGE)],
            others_ref.at[pl.ds(EDGE * (2 - side), EDGE)],
            field_send.at[other],
            field_recv.at[me],
            other,
        )

    def far_copy(other):
        return copy(
            whole_ref.at[pl.ds(2 * EDGE, FAR)],
            others_ref.at[pl.ds(pl.multiple_of(3 * EDGE + me * FAR, FAR), FAR)],
            field_send.at[other],
            field_recv.at[me],
            other,
        )

    def near_wait(side):
        source = me + 2 * side - 1
        copy(
            whole_ref.at[pl.ds(0, EDGE)],
            others_ref.at[pl.ds(EDGE * (1 + side), EDGE)],
            field_send.at[source],
            field_recv.at[source],
            source,
        ).wait_recv()

    def far_wait(source):
        copy(
            whole_ref.at[pl.ds(2 * EDGE, FAR)],
            others_ref.at[pl.ds(3 * EDGE + source * FAR, FAR)],
            field_send.at[source],
            field_recv.at[source],
            source,
        ).wait_recv()

    def ask_sent(source, side):
        copy(
            asks_ref.at[source],
            asks_ref.at[source],
            ask_send.at[source, side],
            ask_recv.at[source, 0, 0],
            me + 2 * side - 1,
        ).wait_send()

    def hand(source, head, block, side):
        handed = ask_copy(source, head, block, side)
        handed.wait_recv()
        handed.start()

    def for_far(action):
        for other in range(count):

            @pl.when(jnp.logical_or(other - me > 1, me - other > 1))
            def _():
                action(other)

    @pl.when(jnp.logical_not(inside))
    def _():
        pl.semaphore_wait(end_sem, 1)

    for_far(lambda other: far_copy(other).start())
    for_sides(lambda side: near_copy(side).start())
    for_sides(lambda side: ask_copy(me, 0, blocks - 1, side).start())

    @pl.when(jnp.logical_not(inside))
    def _():
        for block in range(blocks):
            ask_copy(me, 1, block, 1 - outward).start()

    loads[6].wait()

    def close(p, carry):
        start = p * n_part if isinstance(p, int) else pl.multiple_of(p * n_part, n_part)
        for side, (_, x_ref) in enumerate(sides):
            z = jnp.dot(near_ref[...], x_ref[pl.ds(start, n_part), :], preferred_element_type=jnp.float32)
            close_ref[p, :, side * half_columns : (side + 1) * half_columns] = z[:t_part] + z[t_part:]
        return carry

    close(0, 0)

    @pl.when(inside)
    def _():
        for block in range(blocks - 1):
            for side in range(2):
                hand(me + 2 * side - 1, 0, block, 1 - side)
        ask_copy(me, 1, 0, outward).start()

    lax.fori_loop(1, PARTS, close, 0)

    @pl.when(inside)
    def _():
        for side in range(2):
            hand(me + 2 * side - 1, 0, blocks - 1, 1 - side)
        hand(mate, 1, 0, 1 - outward)
        ask_copy(me, 1, 1, outward).start()

    for each in loads[7:]:
        each.wait()
    field_ref[...] = strict_dot(local_ref[...], parts_ref[...])

    for_sides(near_wait)
    for_far(far_wait)
    field_ref[...] += strict_dot(cross_ref[...], others_ref[...])

    def finish(head):
        k_columns = slice(head * width, (head + 1) * width)
        v_columns = slice(half_columns + head * width, half_columns + (head + 1) * width)

        def one(p, carry):
            at = pl.ds(pl.multiple_of(p * order, order), order)
            f = jnp.concatenate([field_ref[at, k_columns], field_ref[at, v_columns]], axis=1)
            high = f.astype(jnp.bfloat16)
            low = (f - high.astype(jnp.float32)).astype(jnp.bfloat16)
            y = jnp.dot(
                up_ref[...], jnp.concatenate([high, low, high], axis=0), preferred_element_type=jnp.float32
            )
            k = (close_ref[p, :, k_columns] + y[:, :width]).astype(jnp.bfloat16).astype(jnp.float32)
            v = (close_ref[p, :, v_columns] + y[:, width:]).astype(jnp.bfloat16).astype(jnp.float32)
            begin = pl.multiple_of(p * t_part, t_part)
            place = me * PARTS + p
            cos_p, sin_p = coarse_ref[0, pl.ds(place, 1), :], coarse_ref[1, pl.ds(place, 1), :]
            cosine = cos_p * fine_ref[0] - sin_p * fine_ref[1]
            sine = sin_p * fine_ref[0] + cos_p * fine_ref[1]
            turned = k * cosine + pltpu.roll(k, width // 2, 1) * sine
            k_ref[head, pl.ds(begin, t_part), :] = turned.astype(jnp.bfloat16)
            v_ref[head, :, pl.ds(begin, t_part)] = v.T.astype(jnp.bfloat16)
            return carry

        lax.fori_loop(0, PARTS, one, 0)

    finish(0)

    @pl.when(inside)
    def _():
        for block in range(1, blocks):
            hand(mate, 1, block, 1 - outward)
        for block in range(blocks):
            ask_copy(me, 1, block, 1 - outward).start()

    runs = [
        (0, 0, 0, blocks),
        (1, 0, 0, blocks),
        (2, 0, 0, blocks),
        (3, 0, 0, blocks - 1),
        (2, 1, 0, blocks),
        (3, 0, blocks - 1, 1),
        (3, 1, 0, 1),
        (1, 1, 0, blocks),
        (0, 1, 0, blocks),
        (3, 1, 1, blocks - 1),
    ]
    begins = [sum(run[3] for run in runs[:i]) for i in range(len(runs))]
    units = begins[-1] + runs[-1][3]

    def decode(u):
        kind, head, block = runs[0][0], runs[0][1], u
        for begin, run in zip(begins[1:], runs[1:]):
            late = u >= begin
            kind = jnp.where(late, run[0], kind)
            head = jnp.where(late, run[1], head)
            block = jnp.where(late, u - begin + run[2], block)
        source = jnp.where(
            kind == 0, mate, jnp.where(kind == 1, near_over, jnp.where(kind == 2, far_end, me))
        )
        return kind, head, block, source

    chunk = 512

    def score(u, keep_ref, top_ref):
        _, head, block, source = decode(u)
        q = asks_ref[source, head, pl.ds(pl.multiple_of(block * BLOCK, BLOCK), BLOCK), :]
        best = None
        for c in range(0, tokens, chunk):
            s = lax.dot_general(
                k_ref[head, c : c + chunk, :],
                q,
                (((1,), (1,)), ((), ())),
                preferred_element_type=jnp.float32,
            )
            keep_ref[c : c + chunk, :] = s
            top = jnp.max(s, axis=0, keepdims=True)
            best = top if best is None else jnp.maximum(best, top)
        top_ref[...] = best

    def weigh(u, keep_ref, top_ref):
        kind, head, block, _ = decode(u)
        best = top_ref[...]
        total = jnp.zeros((1, BLOCK), jnp.float32)
        accum = jnp.zeros((width, BLOCK), jnp.float32)
        for c in range(0, tokens, chunk):
            e = jnp.exp2((keep_ref[c : c + chunk, :] - best) * factor)
            total += jnp.sum(e, axis=0, keepdims=True)
            accum += jnp.dot(
                v_ref[head, :, c : c + chunk], e.astype(jnp.bfloat16), preferred_element_type=jnp.float32
            )
        own_ref[kind, head, block] = (accum / total).astype(jnp.bfloat16)
        own_log_ref[kind, head, block] = best * factor + jnp.log2(total)

    def both(src, src_log, dst, dst_log, send, recv, other):
        return (
            copy(src, dst, send.at[0], recv.at[0], other),
            copy(src_log, dst_log, send.at[1], recv.at[1], other),
        )

    def half_copy(kind, head, block):
        at = (kind, head, block)
        return both(
            own_ref.at[at],
            own_log_ref.at[at],
            half_ref.at[at],
            half_log_ref.at[at],
            half_send,
            half_recv.at[at],
            mate,
        )

    def over_copy(j, head, block):
        at = (j, head, block)
        return both(
            merged_ref.at[at],
            merged_log_ref.at[at],
            over_ref.at[at],
            over_log_ref.at[at],
            over_send,
            over_recv.at[at],
            near_over,
        )

    def last_copy(head, block):
        at = (head, block)
        return both(
            ready_ref.at[at],
            ready_log_ref.at[at],
            last_ref.at[at],
            last_log_ref.at[at],
            last_send,
            half_recv.at[(0,) + at],
            mate,
        )

    def blend(parts, logs):
        best = functools.reduce(jnp.maximum, logs)
        shares = [jnp.exp2(log - best) for log in logs]
        total = functools.reduce(jnp.add, shares)
        mixed = functools.reduce(
            jnp.add, [part.astype(jnp.float32) * (share / total) for part, share in zip(parts, shares)]
        )
        return mixed, best + jnp.log2(total)

    def merge_half(kind, head, block):
        for each in half_copy(kind, head, block):
            each.wait_recv()
        at = (kind - 1, head, block)
        mixed, log = blend(
            [own_ref[kind, head, block], half_ref[kind, head, block]],
            [own_log_ref[kind, head, block], half_log_ref[kind, head, block]],
        )
        merged_ref[at] = mixed.astype(jnp.bfloat16)
        merged_log_ref[at] = log
        for each in over_copy(*at):
            each.start()

    def settle(head, block):
        for each in half_copy(0, head, block) + over_copy(0, head, block):
            each.wait_recv()
        mixed, _ = blend(
            [own_ref[3, head, block], half_ref[0, head, block], over_ref[0, head, block]],
            [own_log_ref[3, head, block], half_log_ref[0, head, block], over_log_ref[0, head, block]],
        )
        out_ref[head, block * BLOCK : (block + 1) * BLOCK, :] = mixed.T.astype(out_ref.dtype)

    def pass_on(head, block):
        for each in over_copy(1, head, block):
            each.wait_recv()
        mixed, log = blend(
            [own_ref[0, head, block], over_ref[1, head, block]],
            [own_log_ref[0, head, block], over_log_ref[1, head, block]],
        )
        ready_ref[head, block] = mixed.astype(jnp.bfloat16)
        ready_log_ref[head, block] = log
        for each in last_copy(head, block):
            each.start()

    def await_ask(u):
        kind, head, block, source = decode(u)

        @pl.when(jnp.logical_and(kind < 3, jnp.logical_not(inside)))
        def _():
            ask_copy(source, head, block, 1 - outward).wait_recv()

    merges = ((1, 0, begins[1] + 9), (2, 0, begins[2] + 12))

    def send_on(u):
        kind, head, block, _ = decode(u)

        @pl.when(jnp.logical_and(kind < 3, jnp.logical_not(inside)))
        def _():
            for each in half_copy(kind, head, block):
                each.start()

        for kind, head, first in merges:
            k = u - first

            @pl.when(jnp.logical_and(inside, jnp.logical_and(k >= 0, k < blocks)))
            def _():
                merge_half(kind, head, k)

    await_ask(jnp.int32(0))
    score(jnp.int32(0), even_ref, even_top_ref)

    def serve(i, carry):
        u = 2 * i
        for at, source, head in ((0, far_end, 0), (3, far_end, 1), (5, near_over, 1)):

            @pl.when(jnp.logical_and(inside, i == at))
            def _():
                for block in range(blocks):
                    hand(source, head, block, outward)
                if source is near_over:
                    for block in range(2, blocks):
                        ask_copy(me, 1, block, outward).start()

        @pl.when(i == 2)
        def _():
            finish(1)

        await_ask(u + 1)
        score(u + 1, odd_ref, odd_top_ref)
        weigh(u, even_ref, even_top_ref)
        send_on(u)
        ahead = jnp.minimum(u + 2, units - 1)

        @pl.when(u + 2 < units)
        def _():
            await_ask(ahead)

        score(ahead, even_ref, even_top_ref)
        weigh(u + 1, odd_ref, odd_top_ref)
        send_on(u + 1)
        return carry

    lax.fori_loop(0, units // 2, serve, 0)

    @pl.when(inside)
    def _():
        for block in range(blocks):
            pass_on(0, block)
            merge_half(2, 1, block)
        for block in range(blocks):
            pass_on(1, block)
            merge_half(1, 1, block)
        ask_sent(me - 1, 1)
        ask_sent(me + 1, 0)
        ask_sent(far_end, outward)

    for_sides(lambda side: ask_sent(me, side))
    for_sides(lambda side: near_copy(side).wait_send())
    for_far(lambda other: far_copy(other).wait_send())

    @pl.when(inside)
    def _():
        for head in range(heads):
            for block in range(blocks):
                settle(head, block)
        for each in both(
            merged_ref, merged_log_ref, over_ref, over_log_ref, over_send, over_recv.at[0, 0, 0], near_over
        ) + both(ready_ref, ready_log_ref, last_ref, last_log_ref, last_send, half_recv.at[0, 0, 0], mate):
            each.wait_send()

    @pl.when(jnp.logical_not(inside))
    def _():
        for head in range(heads):
            for block in range(blocks):
                for each in last_copy(head, block):
                    each.wait_recv()
                mixed, _ = blend(
                    [own_ref[3, head, block], last_ref[head, block]],
                    [own_log_ref[3, head, block], last_log_ref[head, block]],
                )
                out_ref[head, block * BLOCK : (block + 1) * BLOCK, :] = mixed.T.astype(out_ref.dtype)
        kinds = pl.ds(0, 3)
        for each in both(
            own_ref.at[kinds], own_log_ref.at[kinds], half_ref, half_log_ref, half_send, half_recv.at[0, 0, 0], mate
        ):
            each.wait_send()


def by_tokens(keys, values, queries, positions, count):
    heads, rows, width = queries.shape
    n_dev, columns = keys.shape
    length = n_dev * count
    near, down, up, local, merge, cross = fields(length, count)

    def tall(matrix):
        return np.concatenate(split_two(matrix), axis=-2)

    def table(places):
        return tall(np.concatenate(spins(places, width).astype(np.float64), axis=1))

    up_high, up_low = split_two(up)
    t_part = near.shape[0]
    tokens = n_dev // 2
    blocks = rows // BLOCK
    split = 128
    operands = (
        table(np.arange(length // split) * float(split)),
        table(np.arange(split) * 1.0),
        tall(near),
        tall(down),
        np.concatenate([up_high, up_high, up_low], axis=1),
        tall(local),
        tall(merge),
        tall(cross),
        spins(np.arange(count * PARTS) * float(t_part), width),
        spins(np.arange(t_part) * 1.0, width),
    )
    held = [jax.ShapeDtypeStruct(o.shape[1:] if o.ndim == 3 and o.shape[0] == count else o.shape, o.dtype) for o in operands]
    dma = pltpu.SemaphoreType.DMA

    def parts(*lead):
        return [
            pltpu.VMEM(lead + (heads, blocks, width, BLOCK), jnp.bfloat16),
            pltpu.VMEM(lead + (heads, blocks, 1, BLOCK), jnp.float32),
        ]

    return pl.pallas_call(
        functools.partial(fused_kernel, count, math.log2(math.e) / math.sqrt(width)),
        in_specs=[pl.BlockSpec(memory_space=pl.ANY)] * 14,
        out_specs=pl.BlockSpec(memory_space=pltpu.VMEM),
        out_shape=jax.ShapeDtypeStruct(queries.shape, jnp.bfloat16),
        scratch_shapes=[
            pltpu.VMEM(keys.shape, keys.dtype),
            pltpu.VMEM(values.shape, values.dtype),
            pltpu.VMEM(queries.shape, queries.dtype),
            pltpu.VMEM((rows,), jnp.int32),
        ]
        + [pltpu.VMEM(h.shape, h.dtype) for h in held]
        + [
            pltpu.VMEM((PARTS * ORDER, 2 * columns), jnp.float32),
            pltpu.VMEM((2 * EDGE + FAR, 2 * columns), jnp.float32),
            pltpu.VMEM((cross.shape[2], 2 * columns), jnp.float32),
            pltpu.VMEM((PARTS, t_part, 2 * columns), jnp.float32),
            pltpu.VMEM((PARTS * ORDER, 2 * columns), jnp.float32),
            pltpu.VMEM((heads, tokens, width), jnp.bfloat16),
            pltpu.VMEM((heads, width, tokens), jnp.bfloat16),
            pltpu.VMEM((tokens, BLOCK), jnp.float32),
            pltpu.VMEM((tokens, BLOCK), jnp.float32),
            pltpu.VMEM((1, BLOCK), jnp.float32),
            pltpu.VMEM((1, BLOCK), jnp.float32),
            pltpu.VMEM((count, heads, rows, width), jnp.bfloat16),
        ]
        + parts(4)
        + parts(3)
        + parts(2)
        + parts(2)
        + parts()
        + parts()
        + [
            dma((12,)),
            dma((PARTS, 2)),
            pltpu.SemaphoreType.REGULAR((2,)),
            pltpu.SemaphoreType.REGULAR,
            dma((count,)),
            dma((count,)),
            dma((count, 2)),
            dma((count, heads, blocks)),
            dma((2,)),
            dma((3, heads, blocks, 2)),
            dma((2,)),
            dma((2, heads, blocks, 2)),
            dma((2,)),
        ],
        compiler_params=pltpu.CompilerParams(
            collective_id=0, has_side_effects=True, vmem_limit_bytes=60 * 1024 * 1024
        ),
    )(keys, values, queries, positions, *operands)


def by_columns(keys, values, queries, positions):
    key_parts = lax.all_to_all(keys, "ctx", split_axis=1, concat_axis=0, tiled=True)
    value_parts = lax.all_to_all(values, "ctx", split_axis=1, concat_axis=0, tiled=True)
    heads, rows, width = queries.shape
    per_device = key_parts.shape[1]
    compact = compress(jnp.concatenate([key_parts, value_parts], axis=1))
    rotated = rotate_rows(queries.astype(jnp.float32), positions.astype(jnp.float32)).astype(
        jnp.bfloat16
    )
    whole = lax.all_gather(compact.T, "ctx", axis=0, tiled=True)
    tokens = whole.shape[1]
    shaped = whole.reshape(-1, 2, per_device, tokens)
    key_rows = shaped[:, 0].reshape(heads, width, tokens).swapaxes(1, 2)
    value_rows = shaped[:, 1].reshape(heads, width, tokens).swapaxes(1, 2)
    places = jnp.arange(tokens).astype(jnp.float32)
    ready = rotate_rows(key_rows.astype(jnp.float32), places).astype(jnp.bfloat16)
    return attend(rotated, ready, value_rows, jnp.zeros((), jnp.int32))[0]


def solution(mesh):
    count = mesh.shape["ctx"]

    def on_device(keys, values, queries, positions):
        heads, rows, width = queries.shape
        if count == 4 and heads == 2 and keys.shape[0] % (PARTS * 512) == 0 and rows % BLOCK == 0 and width == 128:
            return by_tokens(keys, values, queries, positions, count)
        return by_columns(keys, values, queries, positions)

    return jax.shard_map(
        on_device,
        mesh=mesh,
        in_specs=(
            P(("user", "ctx"), "heads"),
            P(("user", "ctx"), "heads"),
            P("heads", ("user", "ctx"), None),
            P(("user", "ctx")),
        ),
        out_specs=P("heads", ("user", "ctx"), None),
        check_vma=False,
    )
```

```python
import functools
import math

import jax
import jax.numpy as jnp
import numpy as np
from jax import lax
from jax.experimental import pallas as pl
from jax.experimental.pallas import tpu as pltpu
from jax.sharding import PartitionSpec as P

OUTER = 128
PARTS = 4
ORDER = 64
EDGE = 32
FAR = 8
BLOCK = 256
MESH = pl.DeviceIdType.MESH


def split_two(matrix):
    high = matrix.astype(jnp.bfloat16)
    low = (matrix - np.asarray(high).astype(np.float64)).astype(jnp.bfloat16)
    return high, low


@functools.lru_cache(maxsize=None)
def stages(length):
    outer = OUTER
    inner = length // outer
    step = inner // 2
    a = np.arange(outer)
    c = np.arange(outer)
    turn = 2 * outer
    angle = np.pi / outer * ((c[:, None] * a[None, :]) % turn)
    alternate = np.where(a % 2 == 0, 1.0, -1.0)
    first = np.stack([np.cos(angle), -np.sin(angle)], axis=1)
    first[0, 1] = alternate
    d = np.arange(length // 2 // turn)
    k = np.concatenate([c[:, None] + turn * d, (turn - c[:, None]) % turn + turn * d], axis=1)
    k[0, d.size :] = outer + turn * d
    sign = np.concatenate([np.ones(d.size), -np.ones(d.size)])
    b = np.arange(inner)
    q = np.arange(step)
    theta = np.pi / (2 * length) * ((k[:, :, None] * (2 * b + 1)) % (4 * length))
    phi = np.pi / length * ((k[:, None, :] * (2 * q + 1)[:, None]) % (2 * length))
    forward = np.stack([np.cos(theta), np.sin(theta) * sign[None, :, None]], axis=2)
    weight = np.where(k == 0, 1.0, 2.0) / length
    back = np.stack([np.cos(phi), np.sin(phi) * sign], axis=1) * weight[:, None, None, :]
    half = d.size
    forward[0, :half, 1] = 0.0
    forward[0, half:, 1] = np.cos(theta[0, half:])
    forward[0, half:, 0] = 0.0
    back[0, 1, :, :half] = 0.0
    back[0, 1, :, half:] = np.cos(phi[0, :, half:]) * weight[0, half:]
    back[0, 0, :, half:] = 0.0
    middle = back.reshape(outer, 2 * step, 2 * half) @ forward.reshape(outer, 2 * half, 2 * inner)
    last = first.transpose(2, 0, 1).reshape(outer, 2 * outer)
    return first.reshape(2 * outer, outer), middle, last


def compress(signal):
    length, columns = signal.shape
    outer, inner = OUTER, length // OUTER
    first, middle, last = stages(length)
    first_high, first_low = split_two(first)
    flat = signal.reshape(outer, inner * columns)
    one = jnp.dot(first_high, flat, preferred_element_type=jnp.float32) + jnp.dot(
        first_low, flat, preferred_element_type=jnp.float32
    )
    one = one.reshape(outer, 2 * inner, columns)
    two = jnp.einsum(
        "cob,cbl->col", jnp.asarray(middle.astype(np.float32)), one, precision=lax.Precision.HIGH
    )
    three = jnp.dot(
        jnp.asarray(last.astype(np.float32)),
        two.reshape(2 * outer, inner // 2 * columns),
        precision=lax.Precision.HIGH,
    )
    return three.reshape(length // 2, columns).astype(jnp.bfloat16)

def strict_dot(left, right):
    rows, columns = left.shape[0] // 2, right.shape[1]
    high = right.astype(jnp.bfloat16)
    low = (right - high.astype(jnp.float32)).astype(jnp.bfloat16)
    both = jnp.dot(
        left, jnp.concatenate([high, low], axis=1), preferred_element_type=jnp.float32
    )
    return both[:rows, :columns] + (both[:rows, columns:] + both[rows:, :columns])


def inverse_freq(width):
    return jnp.exp(jnp.arange(width // 2).astype(jnp.float32) * (-2.0 * math.log(500000.0) / width))


def rotate_rows(block, places):
    width = block.shape[-1]
    half = width // 2
    angles = places[:, None] * inverse_freq(width)[None, :]
    cosine = jnp.cos(angles)
    sine = jnp.sin(angles)
    first = block[..., :half]
    second = block[..., half:]
    return jnp.concatenate(
        [first * cosine - second * sine, second * cosine + first * sine], axis=-1
    )


def attend_kernel(chunk, scale, resume, finish, swap_ref, q_ref, k_ref, v_ref, *refs):
    q = q_ref[0]
    swap = swap_ref[0] == 1
    rows, width = q.shape
    factor = scale * math.log2(math.e)
    if resume:
        accum = refs[0][0]
        best = refs[1][0][:, :1]
        total = refs[2][0][:, :1]
        refs = refs[3:]
    else:
        best = jnp.full((rows, 1), -jnp.inf, jnp.float32)
        total = jnp.zeros((rows, 1), jnp.float32)
        accum = jnp.zeros((rows, width), jnp.float32)
    tokens = k_ref.shape[1]
    for start in range(0, tokens, chunk):
        one = k_ref[0, start : start + chunk, :]
        two = v_ref[0, start : start + chunk, :]
        k, v = jnp.where(swap, two, one), jnp.where(swap, one, two)
        scores = lax.dot_general(
            q, k, (((1,), (1,)), ((), ())), preferred_element_type=jnp.float32
        )
        fresh = jnp.maximum(best, jnp.max(scores, axis=1, keepdims=True))
        expo = jnp.exp2((scores - fresh) * factor)
        shrink = jnp.exp2((best - fresh) * factor)
        total = total * shrink + jnp.sum(expo, axis=1, keepdims=True)
        accum = accum * shrink + jnp.dot(
            expo.astype(jnp.bfloat16), v, preferred_element_type=jnp.float32
        )
        best = fresh
    if finish:
        refs[0][0] = (accum / total).astype(refs[0].dtype)
        refs[1][0] = jnp.broadcast_to(best * factor + jnp.log2(total), (rows, 8))
    else:
        refs[0][0] = accum
        refs[1][0] = jnp.broadcast_to(best, (rows, 8))
        refs[2][0] = jnp.broadcast_to(total, (rows, 8))


def attend(queries, keys, values, swap, part=0, parts=1, state=None):
    groups, rows, width = queries.shape
    heads, tokens, _ = values.shape
    per_head = groups // heads
    block = math.gcd(rows, 768)
    chunk = math.gcd(tokens, 1024)
    scale = 1.0 / math.sqrt(width)
    finish = part == parts - 1
    wide = pl.BlockSpec((1, block, width), lambda g, i: (g, i, 0))
    thin = pl.BlockSpec((1, block, 8), lambda g, i: (g, i, 0))
    thin_shape = jax.ShapeDtypeStruct((groups, rows, 8), jnp.float32)
    state = () if state is None else tuple(state)
    wide_type = jnp.bfloat16 if finish else jnp.float32
    return pl.pallas_call(
        functools.partial(attend_kernel, chunk, scale, bool(state), finish),
        grid=(groups, rows // block),
        in_specs=[
            pl.BlockSpec(memory_space=pltpu.SMEM),
            wide,
            pl.BlockSpec((1, tokens, width), lambda g, i: (g // per_head, part, 0)),
            pl.BlockSpec((1, tokens, width), lambda g, i: (g // per_head, 0, 0)),
        ]
        + ([wide, thin, thin] if state else []),
        out_specs=[wide, thin] if finish else [wide, thin, thin],
        out_shape=[jax.ShapeDtypeStruct((groups, rows, width), wide_type), thin_shape]
        + ([] if finish else [thin_shape]),
        cost_estimate=pl.CostEstimate(
            flops=8 * groups * rows * tokens * width,
            bytes_accessed=4 * groups * rows * width * 2,
            transcendentals=groups * rows * tokens,
        ),
    )(swap.reshape(1), queries, keys, values, *state)


def bounds(count, left, right):
    return np.log(left / (count - 1 + right)), np.log((count - 1 + left) / right)


def nodes(count, order, left, right):
    low, top = bounds(count, left, right)
    e = np.exp((top - low) / 2 * np.cos(np.pi * (2 * np.arange(order) + 1) / (2 * order)) + (top + low) / 2)
    return ((count - 1 + right) * e - left) / (1 + e)


def cardinals(places, count, order, left, right):
    low, top = bounds(count, left, right)
    at = (2 * np.log((places + left) / (count - 1 + right - places)) - top - low) / (top - low)
    at = np.arccos(np.clip(at, -1.0, 1.0))
    own = np.pi * (2 * np.arange(order) + 1) / (2 * order)
    total = np.zeros((places.size, order))
    for k in range(order):
        total += (1.0 if k == 0 else 2.0) / order * np.cos(k * at)[:, None] * np.cos(k * own)[None, :]
    return total


@functools.lru_cache(maxsize=None)
def fields(length, devices):
    parts, order = PARTS, ORDER
    scale = math.sqrt(0.5) / (2 * length)

    def cot(m):
        return 1.0 / np.tan(np.pi * m / (4 * length))

    n_dev = length // devices
    n_part, t_dev = n_dev // parts, n_dev // 2
    t_part = n_part // 2
    n, t = np.arange(n_part), np.arange(t_part)
    sign_n = np.array([1.0, -1.0, -1.0, 1.0])[n % 4]
    sign_t = np.where(t % 2 == 0, 1.0, -1.0)
    near = sign_t[:, None] * sign_n * scale * cot(4 * t[:, None] - 2 * n + 1.0)
    down = cardinals(n, n_part, order, 1.5, 1.5).T * sign_n
    up = sign_t[:, None] * cardinals(t, t_part, order, 0.75, 0.75)
    part = np.arange(parts)[:, None]
    source = (part * n_part + nodes(n_part, order, 1.5, 1.5)).reshape(-1)
    target = (part * t_part + nodes(t_part, order, 0.75, 0.75)).reshape(-1)
    own = np.arange(parts * order) // order
    same = own[:, None] == own[None, :]
    local = np.where(same, 0.0, scale * cot(np.where(same, 1.0, 4 * target[:, None] - 2 * source + 1)))
    last = n_dev - 1
    wide = float(n_dev)
    merge = np.concatenate(
        [
            cardinals(source, n_dev, EDGE, 1.5, wide).T,
            cardinals(last - source, n_dev, EDGE, 1.5, wide).T,
            cardinals(source, n_dev, FAR, 2 * wide, 2 * wide).T,
        ]
    )
    to_left = nodes(n_dev, EDGE, 1.5, wide)
    sparse = nodes(n_dev, FAR, 2 * wide, 2 * wide)
    size = 3 * EDGE + devices * FAR
    cross = np.zeros((devices, parts * order, size + -size % 128))
    for r in range(devices):
        a = 4 * (target + r * t_dev)[:, None]
        for s in range(devices):
            if abs(r - s) > 1:
                spots, start = sparse, 3 * EDGE + s * FAR
            elif s < r or (s == r and 2 * r >= devices):
                spots, start = last - to_left, EDGE * (r - s)
            else:
                spots, start = to_left, 2 * EDGE * (s - r)
            b = 2 * (spots + s * n_dev)
            block = scale * cot(a + b + 3)
            if r != s:
                block = block + scale * cot(a - b + 1)
            cross[r, :, start : start + block.shape[1]] = block
    return near, down, up, local, merge, cross


def spins(places, width):
    freq = 500000.0 ** (-2.0 * np.arange(width // 2) / width)
    angles = places[:, None] * freq
    cosine, sine = np.cos(angles), np.sin(angles)
    return np.stack(
        [np.concatenate([cosine, cosine], axis=1), np.concatenate([-sine, sine], axis=1)]
    ).astype(np.float32)


def fused_kernel(
    count,
    factor,
    keys_hbm,
    values_hbm,
    queries_hbm,
    places_hbm,
    high_hbm,
    low_hbm,
    near_hbm,
    down_hbm,
    up_hbm,
    local_hbm,
    merge_hbm,
    cross_hbm,
    coarse_hbm,
    fine_hbm,
    out_ref,
    keys_ref,
    values_ref,
    queries_ref,
    places_ref,
    high_ref,
    low_ref,
    near_ref,
    down_ref,
    up_ref,
    local_ref,
    merge_ref,
    cross_ref,
    coarse_ref,
    fine_ref,
    parts_ref,
    whole_ref,
    others_ref,
    close_ref,
    field_ref,
    k_ref,
    v_ref,
    even_ref,
    odd_ref,
    even_top_ref,
    odd_top_ref,
    asks_ref,
    own_ref,
    own_log_ref,
    half_ref,
    half_log_ref,
    merged_ref,
    merged_log_ref,
    over_ref,
    over_log_ref,
    ready_ref,
    ready_log_ref,
    last_ref,
    last_log_ref,
    load_sem,
    token_sem,
    behind_sem,
    end_sem,
    field_send,
    field_recv,
    ask_send,
    ask_recv,
    half_send,
    half_recv,
    over_send,
    over_recv,
    last_send,
):
    me = lax.axis_index("ctx")
    heads, rows, width = queries_ref.shape
    order = ORDER
    blocks = rows // BLOCK
    n_part = near_ref.shape[1]
    t_part = n_part // 2
    half_columns = keys_ref.shape[1]
    tokens = k_ref.shape[1]
    has_left, has_right = me > 0, me < count - 1
    inside = jnp.logical_and(has_left, has_right)
    lower = me < count // 2
    mate = me + 1 - 2 * lax.rem(me, 2)
    far_end = jnp.where(lower, count - 1, 0)
    near_over = jnp.where(lower, count // 2, count // 2 - 1)
    outward = jnp.where(lower, 0, 1)

    def copy(src, dst, send, recv, other):
        return pltpu.make_async_remote_copy(
            src_ref=src,
            dst_ref=dst,
            send_sem=send,
            recv_sem=recv,
            device_id={"ctx": other},
            device_id_type=MESH,
        )

    def for_sides(action):
        for side, there in enumerate((has_left, has_right)):

            @pl.when(there)
            def _():
                action(side)

    def greet(sem, other):
        pl.semaphore_signal(sem, inc=1, device_id={"ctx": other}, device_id_type=MESH)

    others_ref[...] = jnp.zeros_like(others_ref)
    barrier = pltpu.get_barrier_semaphore()
    for_sides(lambda side: greet(barrier, me + 2 * side - 1))
    pairs = (
        (places_hbm, places_ref),
        (queries_hbm, queries_ref),
        (high_hbm, high_ref),
        (low_hbm, low_ref),
        (down_hbm, down_ref),
        (merge_hbm, merge_ref),
        (near_hbm, near_ref),
        (local_hbm, local_ref),
        (cross_hbm.at[me], cross_ref),
        (up_hbm, up_ref),
        (coarse_hbm, coarse_ref),
        (fine_hbm, fine_ref),
    )
    loads = [pltpu.make_async_copy(src, dst, load_sem.at[i]) for i, (src, dst) in enumerate(pairs)]
    sides = ((keys_hbm, keys_ref), (values_hbm, values_ref))
    token_loads = [
        [
            pltpu.make_async_copy(
                src.at[pl.ds(p * n_part, n_part)], dst.at[pl.ds(p * n_part, n_part)], token_sem.at[p, side]
            )
            for side, (src, dst) in enumerate(sides)
        ]
        for p in range(PARTS)
    ]
    for each in loads[:6]:
        each.start()
    for p in range(PARTS):
        for each in token_loads[p]:
            each.start()
    for each in loads[6:]:
        each.start()
    for each in loads[:4]:
        each.wait()

    split = low_ref.shape[0] // 2
    for i in range(rows // split):
        here = slice(i * split, (i + 1) * split)
        place = jnp.broadcast_to(places_ref[here].astype(jnp.float32)[None], (split, split)).T.astype(jnp.int32)
        spun = []
        for value, table_ref in ((place // split, high_ref), (lax.rem(place, split), low_ref)):
            size = table_ref.shape[0] // 2
            value = value if size == split else value[:, :1]
            picked = value == lax.broadcasted_iota(jnp.int32, (split, size), 1)
            picked = jnp.where(picked, 1.0, 0.0).astype(jnp.bfloat16)
            got = jnp.dot(
                jnp.concatenate([picked, picked], axis=1), table_ref[...], preferred_element_type=jnp.float32
            )
            spun.append((got[:, :width], got[:, width:]))
        (cos_a, sin_a), (cos_b, sin_b) = spun
        cosine, sine = cos_a * cos_b - sin_a * sin_b, sin_a * cos_b + cos_a * sin_b
        for head in range(heads):
            x = queries_ref[head, here, :].astype(jnp.float32)
            asks_ref[me, head, here, :] = (x * cosine + pltpu.roll(x, width // 2, 1) * sine).astype(jnp.bfloat16)

    def ask_copy(source, head, block, side):
        here = pl.ds(block * BLOCK if isinstance(block, int) else pl.multiple_of(block * BLOCK, BLOCK), BLOCK)
        return copy(
            asks_ref.at[source, head, here],
            asks_ref.at[source, head, here],
            ask_send.at[source, side],
            ask_recv.at[source, head, block],
            me + 2 * side - 1,
        )

    pl.semaphore_wait(barrier, jnp.where(inside, 2, 1))
    for block in range(blocks - 1):
        for_sides(lambda side: ask_copy(me, 0, block, side).start())
    for_sides(lambda side: greet(behind_sem.at[1 - side], me + 2 * side - 1))

    for each in loads[4:6]:
        each.wait()
    for p in range(PARTS):
        for side, (_, x_ref) in enumerate(sides):
            token_loads[p][side].wait()
            z = jnp.dot(
                down_ref[...], x_ref[p * n_part : (p + 1) * n_part, :], preferred_element_type=jnp.float32
            )
            parts_ref[
                p * order : (p + 1) * order, side * half_columns : (side + 1) * half_columns
            ] = z[:order] + z[order:]
        if p == 1:
            for_sides(lambda side: pl.semaphore_wait(behind_sem.at[side], 1))

            @pl.when(inside)
            def _():
                greet(end_sem, mate)

    whole_ref[...] = strict_dot(merge_ref[...], parts_ref[...])
    others_ref[:EDGE] = whole_ref[pl.ds(pl.multiple_of(jnp.where(lower, 0, EDGE), EDGE), EDGE), :]

    def near_copy(side):
        other = me + 2 * side - 1
        return copy(
            whole_ref.at[pl.ds(side * EDGE, EDGE)],
            others_ref.at[pl.ds(EDGE * (2 - side), EDGE)],
            field_send.at[other],
            field_recv.at[me],
            other,
        )

    def far_copy(other):
        return copy(
            whole_ref.at[pl.ds(2 * EDGE, FAR)],
            others_ref.at[pl.ds(pl.multiple_of(3 * EDGE + me * FAR, FAR), FAR)],
            field_send.at[other],
            field_recv.at[me],
            other,
        )

    def near_wait(side):
        source = me + 2 * side - 1
        copy(
            whole_ref.at[pl.ds(0, EDGE)],
            others_ref.at[pl.ds(EDGE * (1 + side), EDGE)],
            field_send.at[source],
            field_recv.at[source],
            source,
        ).wait_recv()

    def far_wait(source):
        copy(
            whole_ref.at[pl.ds(2 * EDGE, FAR)],
            others_ref.at[pl.ds(3 * EDGE + source * FAR, FAR)],
            field_send.at[source],
            field_recv.at[source],
            source,
        ).wait_recv()

    def ask_sent(source, side):
        copy(
            asks_ref.at[source],
            asks_ref.at[source],
            ask_send.at[source, side],
            ask_recv.at[source, 0, 0],
            me + 2 * side - 1,
        ).wait_send()

    def hand(source, head, block, side):
        handed = ask_copy(source, head, block, side)
        handed.wait_recv()
        handed.start()

    def for_far(action):
        for other in range(count):

            @pl.when(jnp.logical_or(other - me > 1, me - other > 1))
            def _():
                action(other)

    @pl.when(jnp.logical_not(inside))
    def _():
        pl.semaphore_wait(end_sem, 1)

    for_far(lambda other: far_copy(other).start())
    for_sides(lambda side: near_copy(side).start())
    for_sides(lambda side: ask_copy(me, 0, blocks - 1, side).start())

    @pl.when(jnp.logical_not(inside))
    def _():
        for block in range(blocks):
            ask_copy(me, 1, block, 1 - outward).start()

    loads[6].wait()

    def close(p, carry):
        start = p * n_part if isinstance(p, int) else pl.multiple_of(p * n_part, n_part)
        for side, (_, x_ref) in enumerate(sides):
            z = jnp.dot(near_ref[...], x_ref[pl.ds(start, n_part), :], preferred_element_type=jnp.float32)
            close_ref[p, :, side * half_columns : (side + 1) * half_columns] = z[:t_part] + z[t_part:]
        return carry

    close(0, 0)

    @pl.when(inside)
    def _():
        for block in range(blocks - 1):
            for side in range(2):
                hand(me + 2 * side - 1, 0, block, 1 - side)
        ask_copy(me, 1, 0, outward).start()

    lax.fori_loop(1, PARTS, close, 0)

    @pl.when(inside)
    def _():
        for side in range(2):
            hand(me + 2 * side - 1, 0, blocks - 1, 1 - side)
        hand(mate, 1, 0, 1 - outward)
        ask_copy(me, 1, 1, outward).start()

    for each in loads[7:]:
        each.wait()
    field_ref[...] = strict_dot(local_ref[...], parts_ref[...])

    for_sides(near_wait)
    for_far(far_wait)
    field_ref[...] += strict_dot(cross_ref[...], others_ref[...])

    def finish(head):
        k_columns = slice(head * width, (head + 1) * width)
        v_columns = slice(half_columns + head * width, half_columns + (head + 1) * width)

        def one(p, carry):
            at = pl.ds(pl.multiple_of(p * order, order), order)
            f = jnp.concatenate([field_ref[at, k_columns], field_ref[at, v_columns]], axis=1)
            high = f.astype(jnp.bfloat16)
            low = (f - high.astype(jnp.float32)).astype(jnp.bfloat16)
            y = jnp.dot(
                up_ref[...], jnp.concatenate([high, low, high], axis=0), preferred_element_type=jnp.float32
            )
            k = (close_ref[p, :, k_columns] + y[:, :width]).astype(jnp.bfloat16).astype(jnp.float32)
            v = (close_ref[p, :, v_columns] + y[:, width:]).astype(jnp.bfloat16).astype(jnp.float32)
            begin = pl.multiple_of(p * t_part, t_part)
            place = me * PARTS + p
            cos_p, sin_p = coarse_ref[0, pl.ds(place, 1), :], coarse_ref[1, pl.ds(place, 1), :]
            cosine = cos_p * fine_ref[0] - sin_p * fine_ref[1]
            sine = sin_p * fine_ref[0] + cos_p * fine_ref[1]
            turned = k * cosine + pltpu.roll(k, width // 2, 1) * sine
            k_ref[head, pl.ds(begin, t_part), :] = turned.astype(jnp.bfloat16)
            v_ref[head, :, pl.ds(begin, t_part)] = v.T.astype(jnp.bfloat16)
            return carry

        lax.fori_loop(0, PARTS, one, 0)

    finish(0)

    @pl.when(inside)
    def _():
        for block in range(1, blocks):
            hand(mate, 1, block, 1 - outward)
        for block in range(blocks):
            ask_copy(me, 1, block, 1 - outward).start()

    runs = [
        (0, 0, 0, blocks),
        (1, 0, 0, blocks),
        (2, 0, 0, blocks),
        (3, 0, 0, blocks - 1),
        (2, 1, 0, blocks),
        (3, 0, blocks - 1, 1),
        (3, 1, 0, 1),
        (1, 1, 0, blocks),
        (0, 1, 0, blocks),
        (3, 1, 1, blocks - 1),
    ]
    begins = [sum(run[3] for run in runs[:i]) for i in range(len(runs))]
    units = begins[-1] + runs[-1][3]

    def decode(u):
        kind, head, block = runs[0][0], runs[0][1], u
        for begin, run in zip(begins[1:], runs[1:]):
            late = u >= begin
            kind = jnp.where(late, run[0], kind)
            head = jnp.where(late, run[1], head)
            block = jnp.where(late, u - begin + run[2], block)
        source = jnp.where(
            kind == 0, mate, jnp.where(kind == 1, near_over, jnp.where(kind == 2, far_end, me))
        )
        return kind, head, block, source

    chunk = 512

    def score(u, keep_ref, top_ref):
        _, head, block, source = decode(u)
        q = asks_ref[source, head, pl.ds(pl.multiple_of(block * BLOCK, BLOCK), BLOCK), :]
        best = None
        for c in range(0, tokens, chunk):
            s = lax.dot_general(
                k_ref[head, c : c + chunk, :],
                q,
                (((1,), (1,)), ((), ())),
                preferred_element_type=jnp.float32,
            )
            keep_ref[c : c + chunk, :] = s
            top = jnp.max(s, axis=0, keepdims=True)
            best = top if best is None else jnp.maximum(best, top)
        top_ref[...] = best

    def weigh(u, keep_ref, top_ref):
        kind, head, block, _ = decode(u)
        best = top_ref[...]
        total = jnp.zeros((1, BLOCK), jnp.float32)
        accum = jnp.zeros((width, BLOCK), jnp.float32)
        for c in range(0, tokens, chunk):
            e = jnp.exp2((keep_ref[c : c + chunk, :] - best) * factor)
            total += jnp.sum(e, axis=0, keepdims=True)
            accum += jnp.dot(
                v_ref[head, :, c : c + chunk], e.astype(jnp.bfloat16), preferred_element_type=jnp.float32
            )
        own_ref[kind, head, block] = (accum / total).astype(jnp.bfloat16)
        own_log_ref[kind, head, block] = best * factor + jnp.log2(total)

    def both(src, src_log, dst, dst_log, send, recv, other):
        return (
            copy(src, dst, send.at[0], recv.at[0], other),
            copy(src_log, dst_log, send.at[1], recv.at[1], other),
        )

    def half_copy(kind, head, block):
        at = (kind, head, block)
        return both(
            own_ref.at[at],
            own_log_ref.at[at],
            half_ref.at[at],
            half_log_ref.at[at],
            half_send,
            half_recv.at[at],
            mate,
        )

    def over_copy(j, head, block):
        at = (j, head, block)
        return both(
            merged_ref.at[at],
            merged_log_ref.at[at],
            over_ref.at[at],
            over_log_ref.at[at],
            over_send,
            over_recv.at[at],
            near_over,
        )

    def last_copy(head, block):
        at = (head, block)
        return both(
            ready_ref.at[at],
            ready_log_ref.at[at],
            last_ref.at[at],
            last_log_ref.at[at],
            last_send,
            half_recv.at[(0,) + at],
            mate,
        )

    def blend(parts, logs):
        best = functools.reduce(jnp.maximum, logs)
        shares = [jnp.exp2(log - best) for log in logs]
        total = functools.reduce(jnp.add, shares)
        mixed = functools.reduce(
            jnp.add, [part.astype(jnp.float32) * (share / total) for part, share in zip(parts, shares)]
        )
        return mixed, best + jnp.log2(total)

    def merge_half(kind, head, block):
        for each in half_copy(kind, head, block):
            each.wait_recv()
        at = (kind - 1, head, block)
        mixed, log = blend(
            [own_ref[kind, head, block], half_ref[kind, head, block]],
            [own_log_ref[kind, head, block], half_log_ref[kind, head, block]],
        )
        merged_ref[at] = mixed.astype(jnp.bfloat16)
        merged_log_ref[at] = log
        for each in over_copy(*at):
            each.start()

    def settle(head, block):
        for each in half_copy(0, head, block) + over_copy(0, head, block):
            each.wait_recv()
        mixed, _ = blend(
            [own_ref[3, head, block], half_ref[0, head, block], over_ref[0, head, block]],
            [own_log_ref[3, head, block], half_log_ref[0, head, block], over_log_ref[0, head, block]],
        )
        out_ref[head, block * BLOCK : (block + 1) * BLOCK, :] = mixed.T.astype(out_ref.dtype)

    def pass_on(head, block):
        for each in over_copy(1, head, block):
            each.wait_recv()
        mixed, log = blend(
            [own_ref[0, head, block], over_ref[1, head, block]],
            [own_log_ref[0, head, block], over_log_ref[1, head, block]],
        )
        ready_ref[head, block] = mixed.astype(jnp.bfloat16)
        ready_log_ref[head, block] = log
        for each in last_copy(head, block):
            each.start()

    def await_ask(u):
        kind, head, block, source = decode(u)

        @pl.when(jnp.logical_and(kind < 3, jnp.logical_not(inside)))
        def _():
            ask_copy(source, head, block, 1 - outward).wait_recv()

    merges = ((1, 0, begins[1] + 5), (2, 0, begins[2] + 7), (2, 1, begins[4] + 8))
    passes = begins[4] + 8

    def send_on(u):
        kind, head, block, _ = decode(u)

        @pl.when(jnp.logical_and(kind < 3, jnp.logical_not(inside)))
        def _():
            for each in half_copy(kind, head, block):
                each.start()

        k_pass = u - passes

        @pl.when(jnp.logical_and(inside, jnp.logical_and(k_pass >= 0, k_pass < blocks)))
        def _():
            pass_on(0, k_pass)

        for kind, head, first in merges:
            k = u - first

            @pl.when(jnp.logical_and(inside, jnp.logical_and(k >= 0, k < blocks)))
            def _():
                merge_half(kind, head, k)

    await_ask(jnp.int32(0))
    score(jnp.int32(0), even_ref, even_top_ref)

    def serve(i, carry):
        u = 2 * i
        for at, source, head in ((0, far_end, 0), (3, far_end, 1), (5, near_over, 1)):

            @pl.when(jnp.logical_and(inside, i == at))
            def _():
                for block in range(blocks):
                    hand(source, head, block, outward)
                if source is near_over:
                    for block in range(2, blocks):
                        ask_copy(me, 1, block, outward).start()

        @pl.when(i == 2)
        def _():
            finish(1)

        await_ask(u + 1)
        score(u + 1, odd_ref, odd_top_ref)
        weigh(u, even_ref, even_top_ref)
        send_on(u)
        ahead = jnp.minimum(u + 2, units - 1)

        @pl.when(u + 2 < units)
        def _():
            await_ask(ahead)

        score(ahead, even_ref, even_top_ref)
        weigh(u + 1, odd_ref, odd_top_ref)
        send_on(u + 1)
        return carry

    lax.fori_loop(0, units // 2, serve, 0)

    @pl.when(inside)
    def _():
        for block in range(blocks):
            pass_on(1, block)
            merge_half(1, 1, block)
        ask_sent(me - 1, 1)
        ask_sent(me + 1, 0)
        ask_sent(far_end, outward)

    for_sides(lambda side: ask_sent(me, side))
    for_sides(lambda side: near_copy(side).wait_send())
    for_far(lambda other: far_copy(other).wait_send())

    @pl.when(inside)
    def _():
        for head in range(heads):
            for block in range(blocks):
                settle(head, block)
        for each in both(
            merged_ref, merged_log_ref, over_ref, over_log_ref, over_send, over_recv.at[0, 0, 0], near_over
        ) + both(ready_ref, ready_log_ref, last_ref, last_log_ref, last_send, half_recv.at[0, 0, 0], mate):
            each.wait_send()

    @pl.when(jnp.logical_not(inside))
    def _():
        for head in range(heads):
            for block in range(blocks):
                for each in last_copy(head, block):
                    each.wait_recv()
                mixed, _ = blend(
                    [own_ref[3, head, block], last_ref[head, block]],
                    [own_log_ref[3, head, block], last_log_ref[head, block]],
                )
                out_ref[head, block * BLOCK : (block + 1) * BLOCK, :] = mixed.T.astype(out_ref.dtype)
        kinds = pl.ds(0, 3)
        for each in both(
            own_ref.at[kinds], own_log_ref.at[kinds], half_ref, half_log_ref, half_send, half_recv.at[0, 0, 0], mate
        ):
            each.wait_send()


def by_tokens(keys, values, queries, positions, count):
    heads, rows, width = queries.shape
    n_dev, columns = keys.shape
    length = n_dev * count
    near, down, up, local, merge, cross = fields(length, count)

    def tall(matrix):
        return np.concatenate(split_two(matrix), axis=-2)

    def table(places):
        return tall(np.concatenate(spins(places, width).astype(np.float64), axis=1))

    up_high, up_low = split_two(up)
    t_part = near.shape[0]
    tokens = n_dev // 2
    blocks = rows // BLOCK
    split = 128
    operands = (
        table(np.arange(length // split) * float(split)),
        table(np.arange(split) * 1.0),
        tall(near),
        tall(down),
        np.concatenate([up_high, up_high, up_low], axis=1),
        tall(local),
        tall(merge),
        tall(cross),
        spins(np.arange(count * PARTS) * float(t_part), width),
        spins(np.arange(t_part) * 1.0, width),
    )
    held = [jax.ShapeDtypeStruct(o.shape[1:] if o.ndim == 3 and o.shape[0] == count else o.shape, o.dtype) for o in operands]
    dma = pltpu.SemaphoreType.DMA

    def parts(*lead):
        return [
            pltpu.VMEM(lead + (heads, blocks, width, BLOCK), jnp.bfloat16),
            pltpu.VMEM(lead + (heads, blocks, 1, BLOCK), jnp.float32),
        ]

    return pl.pallas_call(
        functools.partial(fused_kernel, count, math.log2(math.e) / math.sqrt(width)),
        in_specs=[pl.BlockSpec(memory_space=pl.ANY)] * 14,
        out_specs=pl.BlockSpec(memory_space=pltpu.VMEM),
        out_shape=jax.ShapeDtypeStruct(queries.shape, jnp.bfloat16),
        scratch_shapes=[
            pltpu.VMEM(keys.shape, keys.dtype),
            pltpu.VMEM(values.shape, values.dtype),
            pltpu.VMEM(queries.shape, queries.dtype),
            pltpu.VMEM((rows,), jnp.int32),
        ]
        + [pltpu.VMEM(h.shape, h.dtype) for h in held]
        + [
            pltpu.VMEM((PARTS * ORDER, 2 * columns), jnp.float32),
            pltpu.VMEM((2 * EDGE + FAR, 2 * columns), jnp.float32),
            pltpu.VMEM((cross.shape[2], 2 * columns), jnp.float32),
            pltpu.VMEM((PARTS, t_part, 2 * columns), jnp.float32),
            pltpu.VMEM((PARTS * ORDER, 2 * columns), jnp.float32),
            pltpu.VMEM((heads, tokens, width), jnp.bfloat16),
            pltpu.VMEM((heads, width, tokens), jnp.bfloat16),
            pltpu.VMEM((tokens, BLOCK), jnp.float32),
            pltpu.VMEM((tokens, BLOCK), jnp.float32),
            pltpu.VMEM((1, BLOCK), jnp.float32),
            pltpu.VMEM((1, BLOCK), jnp.float32),
            pltpu.VMEM((count, heads, rows, width), jnp.bfloat16),
        ]
        + parts(4)
        + parts(3)
        + parts(2)
        + parts(2)
        + parts()
        + parts()
        + [
            dma((12,)),
            dma((PARTS, 2)),
            pltpu.SemaphoreType.REGULAR((2,)),
            pltpu.SemaphoreType.REGULAR,
            dma((count,)),
            dma((count,)),
            dma((count, 2)),
            dma((count, heads, blocks)),
            dma((2,)),
            dma((3, heads, blocks, 2)),
            dma((2,)),
            dma((2, heads, blocks, 2)),
            dma((2,)),
        ],
        compiler_params=pltpu.CompilerParams(
            collective_id=0, has_side_effects=True, vmem_limit_bytes=60 * 1024 * 1024
        ),
    )(keys, values, queries, positions, *operands)


def by_columns(keys, values, queries, positions):
    key_parts = lax.all_to_all(keys, "ctx", split_axis=1, concat_axis=0, tiled=True)
    value_parts = lax.all_to_all(values, "ctx", split_axis=1, concat_axis=0, tiled=True)
    heads, rows, width = queries.shape
    per_device = key_parts.shape[1]
    compact = compress(jnp.concatenate([key_parts, value_parts], axis=1))
    rotated = rotate_rows(queries.astype(jnp.float32), positions.astype(jnp.float32)).astype(
        jnp.bfloat16
    )
    whole = lax.all_gather(compact.T, "ctx", axis=0, tiled=True)
    tokens = whole.shape[1]
    shaped = whole.reshape(-1, 2, per_device, tokens)
    key_rows = shaped[:, 0].reshape(heads, width, tokens).swapaxes(1, 2)
    value_rows = shaped[:, 1].reshape(heads, width, tokens).swapaxes(1, 2)
    places = jnp.arange(tokens).astype(jnp.float32)
    ready = rotate_rows(key_rows.astype(jnp.float32), places).astype(jnp.bfloat16)
    return attend(rotated, ready, value_rows, jnp.zeros((), jnp.int32))[0]


def solution(mesh):
    count = mesh.shape["ctx"]

    def on_device(keys, values, queries, positions):
        heads, rows, width = queries.shape
        if count == 4 and heads == 2 and keys.shape[0] % (PARTS * 512) == 0 and rows % BLOCK == 0 and width == 128:
            return by_tokens(keys, values, queries, positions, count)
        return by_columns(keys, values, queries, positions)

    return jax.shard_map(
        on_device,
        mesh=mesh,
        in_specs=(
            P(("user", "ctx"), "heads"),
            P(("user", "ctx"), "heads"),
            P("heads", ("user", "ctx"), None),
            P(("user", "ctx")),
        ),
        out_specs=P("heads", ("user", "ctx"), None),
        check_vma=False,
    )
```

```python
import functools
import math

import jax
import jax.numpy as jnp
import numpy as np
from jax import lax
from jax.experimental import pallas as pl
from jax.experimental.pallas import tpu as pltpu
from jax.sharding import PartitionSpec as P

OUTER = 128
PARTS = 4
ORDER = 64
EDGE = 32
FAR = 8
BLOCK = 256
MESH = pl.DeviceIdType.MESH


def split_two(matrix):
    high = matrix.astype(jnp.bfloat16)
    low = (matrix - np.asarray(high).astype(np.float64)).astype(jnp.bfloat16)
    return high, low


@functools.lru_cache(maxsize=None)
def stages(length):
    outer = OUTER
    inner = length // outer
    step = inner // 2
    a = np.arange(outer)
    c = np.arange(outer)
    turn = 2 * outer
    angle = np.pi / outer * ((c[:, None] * a[None, :]) % turn)
    alternate = np.where(a % 2 == 0, 1.0, -1.0)
    first = np.stack([np.cos(angle), -np.sin(angle)], axis=1)
    first[0, 1] = alternate
    d = np.arange(length // 2 // turn)
    k = np.concatenate([c[:, None] + turn * d, (turn - c[:, None]) % turn + turn * d], axis=1)
    k[0, d.size :] = outer + turn * d
    sign = np.concatenate([np.ones(d.size), -np.ones(d.size)])
    b = np.arange(inner)
    q = np.arange(step)
    theta = np.pi / (2 * length) * ((k[:, :, None] * (2 * b + 1)) % (4 * length))
    phi = np.pi / length * ((k[:, None, :] * (2 * q + 1)[:, None]) % (2 * length))
    forward = np.stack([np.cos(theta), np.sin(theta) * sign[None, :, None]], axis=2)
    weight = np.where(k == 0, 1.0, 2.0) / length
    back = np.stack([np.cos(phi), np.sin(phi) * sign], axis=1) * weight[:, None, None, :]
    half = d.size
    forward[0, :half, 1] = 0.0
    forward[0, half:, 1] = np.cos(theta[0, half:])
    forward[0, half:, 0] = 0.0
    back[0, 1, :, :half] = 0.0
    back[0, 1, :, half:] = np.cos(phi[0, :, half:]) * weight[0, half:]
    back[0, 0, :, half:] = 0.0
    middle = back.reshape(outer, 2 * step, 2 * half) @ forward.reshape(outer, 2 * half, 2 * inner)
    last = first.transpose(2, 0, 1).reshape(outer, 2 * outer)
    return first.reshape(2 * outer, outer), middle, last


def compress(signal):
    length, columns = signal.shape
    outer, inner = OUTER, length // OUTER
    first, middle, last = stages(length)
    first_high, first_low = split_two(first)
    flat = signal.reshape(outer, inner * columns)
    one = jnp.dot(first_high, flat, preferred_element_type=jnp.float32) + jnp.dot(
        first_low, flat, preferred_element_type=jnp.float32
    )
    one = one.reshape(outer, 2 * inner, columns)
    two = jnp.einsum(
        "cob,cbl->col", jnp.asarray(middle.astype(np.float32)), one, precision=lax.Precision.HIGH
    )
    three = jnp.dot(
        jnp.asarray(last.astype(np.float32)),
        two.reshape(2 * outer, inner // 2 * columns),
        precision=lax.Precision.HIGH,
    )
    return three.reshape(length // 2, columns).astype(jnp.bfloat16)

def strict_dot(left, right):
    rows, columns = left.shape[0] // 2, right.shape[1]
    high = right.astype(jnp.bfloat16)
    low = (right - high.astype(jnp.float32)).astype(jnp.bfloat16)
    both = jnp.dot(
        left, jnp.concatenate([high, low], axis=1), preferred_element_type=jnp.float32
    )
    return both[:rows, :columns] + (both[:rows, columns:] + both[rows:, :columns])


def inverse_freq(width):
    return jnp.exp(jnp.arange(width // 2).astype(jnp.float32) * (-2.0 * math.log(500000.0) / width))


def rotate_rows(block, places):
    width = block.shape[-1]
    half = width // 2
    angles = places[:, None] * inverse_freq(width)[None, :]
    cosine = jnp.cos(angles)
    sine = jnp.sin(angles)
    first = block[..., :half]
    second = block[..., half:]
    return jnp.concatenate(
        [first * cosine - second * sine, second * cosine + first * sine], axis=-1
    )


def attend_kernel(chunk, scale, resume, finish, swap_ref, q_ref, k_ref, v_ref, *refs):
    q = q_ref[0]
    swap = swap_ref[0] == 1
    rows, width = q.shape
    factor = scale * math.log2(math.e)
    if resume:
        accum = refs[0][0]
        best = refs[1][0][:, :1]
        total = refs[2][0][:, :1]
        refs = refs[3:]
    else:
        best = jnp.full((rows, 1), -jnp.inf, jnp.float32)
        total = jnp.zeros((rows, 1), jnp.float32)
        accum = jnp.zeros((rows, width), jnp.float32)
    tokens = k_ref.shape[1]
    for start in range(0, tokens, chunk):
        one = k_ref[0, start : start + chunk, :]
        two = v_ref[0, start : start + chunk, :]
        k, v = jnp.where(swap, two, one), jnp.where(swap, one, two)
        scores = lax.dot_general(
            q, k, (((1,), (1,)), ((), ())), preferred_element_type=jnp.float32
        )
        fresh = jnp.maximum(best, jnp.max(scores, axis=1, keepdims=True))
        expo = jnp.exp2((scores - fresh) * factor)
        shrink = jnp.exp2((best - fresh) * factor)
        total = total * shrink + jnp.sum(expo, axis=1, keepdims=True)
        accum = accum * shrink + jnp.dot(
            expo.astype(jnp.bfloat16), v, preferred_element_type=jnp.float32
        )
        best = fresh
    if finish:
        refs[0][0] = (accum / total).astype(refs[0].dtype)
        refs[1][0] = jnp.broadcast_to(best * factor + jnp.log2(total), (rows, 8))
    else:
        refs[0][0] = accum
        refs[1][0] = jnp.broadcast_to(best, (rows, 8))
        refs[2][0] = jnp.broadcast_to(total, (rows, 8))


def attend(queries, keys, values, swap, part=0, parts=1, state=None):
    groups, rows, width = queries.shape
    heads, tokens, _ = values.shape
    per_head = groups // heads
    block = math.gcd(rows, 768)
    chunk = math.gcd(tokens, 1024)
    scale = 1.0 / math.sqrt(width)
    finish = part == parts - 1
    wide = pl.BlockSpec((1, block, width), lambda g, i: (g, i, 0))
    thin = pl.BlockSpec((1, block, 8), lambda g, i: (g, i, 0))
    thin_shape = jax.ShapeDtypeStruct((groups, rows, 8), jnp.float32)
    state = () if state is None else tuple(state)
    wide_type = jnp.bfloat16 if finish else jnp.float32
    return pl.pallas_call(
        functools.partial(attend_kernel, chunk, scale, bool(state), finish),
        grid=(groups, rows // block),
        in_specs=[
            pl.BlockSpec(memory_space=pltpu.SMEM),
            wide,
            pl.BlockSpec((1, tokens, width), lambda g, i: (g // per_head, part, 0)),
            pl.BlockSpec((1, tokens, width), lambda g, i: (g // per_head, 0, 0)),
        ]
        + ([wide, thin, thin] if state else []),
        out_specs=[wide, thin] if finish else [wide, thin, thin],
        out_shape=[jax.ShapeDtypeStruct((groups, rows, width), wide_type), thin_shape]
        + ([] if finish else [thin_shape]),
        cost_estimate=pl.CostEstimate(
            flops=8 * groups * rows * tokens * width,
            bytes_accessed=4 * groups * rows * width * 2,
            transcendentals=groups * rows * tokens,
        ),
    )(swap.reshape(1), queries, keys, values, *state)


def bounds(count, left, right):
    return np.log(left / (count - 1 + right)), np.log((count - 1 + left) / right)


def nodes(count, order, left, right):
    low, top = bounds(count, left, right)
    e = np.exp((top - low) / 2 * np.cos(np.pi * (2 * np.arange(order) + 1) / (2 * order)) + (top + low) / 2)
    return ((count - 1 + right) * e - left) / (1 + e)


def cardinals(places, count, order, left, right):
    low, top = bounds(count, left, right)
    at = (2 * np.log((places + left) / (count - 1 + right - places)) - top - low) / (top - low)
    at = np.arccos(np.clip(at, -1.0, 1.0))
    own = np.pi * (2 * np.arange(order) + 1) / (2 * order)
    total = np.zeros((places.size, order))
    for k in range(order):
        total += (1.0 if k == 0 else 2.0) / order * np.cos(k * at)[:, None] * np.cos(k * own)[None, :]
    return total


@functools.lru_cache(maxsize=None)
def fields(length, devices):
    parts, order = PARTS, ORDER
    scale = math.sqrt(0.5) / (2 * length)

    def cot(m):
        return 1.0 / np.tan(np.pi * m / (4 * length))

    n_dev = length // devices
    n_part, t_dev = n_dev // parts, n_dev // 2
    t_part = n_part // 2
    n, t = np.arange(n_part), np.arange(t_part)
    sign_n = np.array([1.0, -1.0, -1.0, 1.0])[n % 4]
    sign_t = np.where(t % 2 == 0, 1.0, -1.0)
    near = sign_t[:, None] * sign_n * scale * cot(4 * t[:, None] - 2 * n + 1.0)
    down = cardinals(n, n_part, order, 1.5, 1.5).T * sign_n
    up = sign_t[:, None] * cardinals(t, t_part, order, 0.75, 0.75)
    part = np.arange(parts)[:, None]
    source = (part * n_part + nodes(n_part, order, 1.5, 1.5)).reshape(-1)
    target = (part * t_part + nodes(t_part, order, 0.75, 0.75)).reshape(-1)
    own = np.arange(parts * order) // order
    same = own[:, None] == own[None, :]
    local = np.where(same, 0.0, scale * cot(np.where(same, 1.0, 4 * target[:, None] - 2 * source + 1)))
    last = n_dev - 1
    wide = float(n_dev)
    merge = np.concatenate(
        [
            cardinals(source, n_dev, EDGE, 1.5, wide).T,
            cardinals(last - source, n_dev, EDGE, 1.5, wide).T,
            cardinals(source, n_dev, FAR, 2 * wide, 2 * wide).T,
        ]
    )
    to_left = nodes(n_dev, EDGE, 1.5, wide)
    sparse = nodes(n_dev, FAR, 2 * wide, 2 * wide)
    size = 3 * EDGE + devices * FAR
    cross = np.zeros((devices, parts * order, size + -size % 128))
    for r in range(devices):
        a = 4 * (target + r * t_dev)[:, None]
        for s in range(devices):
            if abs(r - s) > 1:
                spots, start = sparse, 3 * EDGE + s * FAR
            elif s < r or (s == r and 2 * r >= devices):
                spots, start = last - to_left, EDGE * (r - s)
            else:
                spots, start = to_left, 2 * EDGE * (s - r)
            b = 2 * (spots + s * n_dev)
            block = scale * cot(a + b + 3)
            if r != s:
                block = block + scale * cot(a - b + 1)
            cross[r, :, start : start + block.shape[1]] = block
    return near, down, up, local, merge, cross


def spins(places, width):
    freq = 500000.0 ** (-2.0 * np.arange(width // 2) / width)
    angles = places[:, None] * freq
    cosine, sine = np.cos(angles), np.sin(angles)
    return np.stack(
        [np.concatenate([cosine, cosine], axis=1), np.concatenate([-sine, sine], axis=1)]
    ).astype(np.float32)


def fused_kernel(
    count,
    factor,
    keys_hbm,
    values_hbm,
    queries_hbm,
    places_hbm,
    high_hbm,
    low_hbm,
    near_hbm,
    down_hbm,
    up_hbm,
    local_hbm,
    merge_hbm,
    cross_hbm,
    coarse_hbm,
    fine_hbm,
    out_ref,
    keys_ref,
    values_ref,
    queries_ref,
    places_ref,
    high_ref,
    low_ref,
    near_ref,
    down_ref,
    up_ref,
    local_ref,
    merge_ref,
    cross_ref,
    coarse_ref,
    fine_ref,
    parts_ref,
    whole_ref,
    others_ref,
    close_ref,
    field_ref,
    k_ref,
    v_ref,
    even_ref,
    odd_ref,
    even_top_ref,
    odd_top_ref,
    asks_ref,
    own_ref,
    own_log_ref,
    half_ref,
    half_log_ref,
    merged_ref,
    merged_log_ref,
    over_ref,
    over_log_ref,
    ready_ref,
    ready_log_ref,
    last_ref,
    last_log_ref,
    load_sem,
    token_sem,
    behind_sem,
    end_sem,
    field_send,
    field_recv,
    ask_send,
    ask_recv,
    half_send,
    half_recv,
    over_send,
    over_recv,
    last_send,
):
    me = lax.axis_index("ctx")
    heads, rows, width = queries_ref.shape
    order = ORDER
    blocks = rows // BLOCK
    n_part = near_ref.shape[1]
    t_part = n_part // 2
    half_columns = keys_ref.shape[1]
    tokens = k_ref.shape[1]
    has_left, has_right = me > 0, me < count - 1
    inside = jnp.logical_and(has_left, has_right)
    lower = me < count // 2
    mate = me + 1 - 2 * lax.rem(me, 2)
    far_end = jnp.where(lower, count - 1, 0)
    near_over = jnp.where(lower, count // 2, count // 2 - 1)
    outward = jnp.where(lower, 0, 1)

    def copy(src, dst, send, recv, other):
        return pltpu.make_async_remote_copy(
            src_ref=src,
            dst_ref=dst,
            send_sem=send,
            recv_sem=recv,
            device_id={"ctx": other},
            device_id_type=MESH,
        )

    def for_sides(action):
        for side, there in enumerate((has_left, has_right)):

            @pl.when(there)
            def _():
                action(side)

    def greet(sem, other):
        pl.semaphore_signal(sem, inc=1, device_id={"ctx": other}, device_id_type=MESH)

    others_ref[...] = jnp.zeros_like(others_ref)
    barrier = pltpu.get_barrier_semaphore()
    for_sides(lambda side: greet(barrier, me + 2 * side - 1))
    pairs = (
        (places_hbm, places_ref),
        (queries_hbm, queries_ref),
        (high_hbm, high_ref),
        (low_hbm, low_ref),
        (down_hbm, down_ref),
        (merge_hbm, merge_ref),
        (near_hbm, near_ref),
        (local_hbm, local_ref),
        (cross_hbm.at[me], cross_ref),
        (up_hbm, up_ref),
        (coarse_hbm, coarse_ref),
        (fine_hbm, fine_ref),
    )
    loads = [pltpu.make_async_copy(src, dst, load_sem.at[i]) for i, (src, dst) in enumerate(pairs)]
    sides = ((keys_hbm, keys_ref), (values_hbm, values_ref))
    token_loads = [
        [
            pltpu.make_async_copy(
                src.at[pl.ds(p * n_part, n_part)], dst.at[pl.ds(p * n_part, n_part)], token_sem.at[p, side]
            )
            for side, (src, dst) in enumerate(sides)
        ]
        for p in range(PARTS)
    ]
    for each in loads[:6]:
        each.start()
    for p in range(PARTS):
        for each in token_loads[p]:
            each.start()
    for each in loads[6:]:
        each.start()
    for each in loads[:4]:
        each.wait()

    split = low_ref.shape[0] // 2
    for i in range(rows // split):
        here = slice(i * split, (i + 1) * split)
        place = jnp.broadcast_to(places_ref[here].astype(jnp.float32)[None], (split, split)).T.astype(jnp.int32)
        spun = []
        for value, table_ref in ((place // split, high_ref), (lax.rem(place, split), low_ref)):
            size = table_ref.shape[0] // 2
            value = value if size == split else value[:, :1]
            picked = value == lax.broadcasted_iota(jnp.int32, (split, size), 1)
            picked = jnp.where(picked, 1.0, 0.0).astype(jnp.bfloat16)
            got = jnp.dot(
                jnp.concatenate([picked, picked], axis=1), table_ref[...], preferred_element_type=jnp.float32
            )
            spun.append((got[:, :width], got[:, width:]))
        (cos_a, sin_a), (cos_b, sin_b) = spun
        cosine, sine = cos_a * cos_b - sin_a * sin_b, sin_a * cos_b + cos_a * sin_b
        for head in range(heads):
            x = queries_ref[head, here, :].astype(jnp.float32)
            asks_ref[me, head, here, :] = (x * cosine + pltpu.roll(x, width // 2, 1) * sine).astype(jnp.bfloat16)

    def ask_copy(source, head, block, side):
        here = pl.ds(block * BLOCK if isinstance(block, int) else pl.multiple_of(block * BLOCK, BLOCK), BLOCK)
        return copy(
            asks_ref.at[source, head, here],
            asks_ref.at[source, head, here],
            ask_send.at[source, side],
            ask_recv.at[source, head, block],
            me + 2 * side - 1,
        )

    pl.semaphore_wait(barrier, jnp.where(inside, 2, 1))
    for block in range(blocks - 1):
        for_sides(lambda side: ask_copy(me, 0, block, side).start())
    for_sides(lambda side: greet(behind_sem.at[1 - side], me + 2 * side - 1))

    for each in loads[4:6]:
        each.wait()
    for p in range(PARTS):
        for side, (_, x_ref) in enumerate(sides):
            token_loads[p][side].wait()
            z = jnp.dot(
                down_ref[...], x_ref[p * n_part : (p + 1) * n_part, :], preferred_element_type=jnp.float32
            )
            parts_ref[
                p * order : (p + 1) * order, side * half_columns : (side + 1) * half_columns
            ] = z[:order] + z[order:]
        if p == 1:
            for_sides(lambda side: pl.semaphore_wait(behind_sem.at[side], 1))

            @pl.when(inside)
            def _():
                greet(end_sem, mate)

    whole_ref[...] = strict_dot(merge_ref[...], parts_ref[...])
    others_ref[:EDGE] = whole_ref[pl.ds(pl.multiple_of(jnp.where(lower, 0, EDGE), EDGE), EDGE), :]

    def near_copy(side):
        other = me + 2 * side - 1
        return copy(
            whole_ref.at[pl.ds(side * EDGE, EDGE)],
            others_ref.at[pl.ds(EDGE * (2 - side), EDGE)],
            field_send.at[other],
            field_recv.at[me],
            other,
        )

    def far_copy(other):
        return copy(
            whole_ref.at[pl.ds(2 * EDGE, FAR)],
            others_ref.at[pl.ds(pl.multiple_of(3 * EDGE + me * FAR, FAR), FAR)],
            field_send.at[other],
            field_recv.at[me],
            other,
        )

    def near_wait(side):
        source = me + 2 * side - 1
        copy(
            whole_ref.at[pl.ds(0, EDGE)],
            others_ref.at[pl.ds(EDGE * (1 + side), EDGE)],
            field_send.at[source],
            field_recv.at[source],
            source,
        ).wait_recv()

    def far_wait(source):
        copy(
            whole_ref.at[pl.ds(2 * EDGE, FAR)],
            others_ref.at[pl.ds(3 * EDGE + source * FAR, FAR)],
            field_send.at[source],
            field_recv.at[source],
            source,
        ).wait_recv()

    def ask_sent(source, side):
        copy(
            asks_ref.at[source],
            asks_ref.at[source],
            ask_send.at[source, side],
            ask_recv.at[source, 0, 0],
            me + 2 * side - 1,
        ).wait_send()

    def hand(source, head, block, side):
        handed = ask_copy(source, head, block, side)
        handed.wait_recv()
        handed.start()

    def for_far(action):
        for other in range(count):

            @pl.when(jnp.logical_or(other - me > 1, me - other > 1))
            def _():
                action(other)

    @pl.when(jnp.logical_not(inside))
    def _():
        pl.semaphore_wait(end_sem, 1)

    for_far(lambda other: far_copy(other).start())
    for_sides(lambda side: near_copy(side).start())
    for_sides(lambda side: ask_copy(me, 0, blocks - 1, side).start())

    @pl.when(jnp.logical_not(inside))
    def _():
        for block in range(blocks):
            ask_copy(me, 1, block, 1 - outward).start()

    loads[6].wait()

    def close(p, carry):
        start = p * n_part if isinstance(p, int) else pl.multiple_of(p * n_part, n_part)
        for side, (_, x_ref) in enumerate(sides):
            z = jnp.dot(near_ref[...], x_ref[pl.ds(start, n_part), :], preferred_element_type=jnp.float32)
            close_ref[p, :, side * half_columns : (side + 1) * half_columns] = z[:t_part] + z[t_part:]
        return carry

    close(0, 0)

    @pl.when(inside)
    def _():
        for block in range(blocks - 1):
            for side in range(2):
                hand(me + 2 * side - 1, 0, block, 1 - side)
        ask_copy(me, 1, 0, outward).start()

    lax.fori_loop(1, PARTS, close, 0)

    @pl.when(inside)
    def _():
        for side in range(2):
            hand(me + 2 * side - 1, 0, blocks - 1, 1 - side)
        hand(mate, 1, 0, 1 - outward)
        ask_copy(me, 1, 1, outward).start()

    for each in loads[7:]:
        each.wait()
    field_ref[...] = strict_dot(local_ref[...], parts_ref[...])

    for_sides(near_wait)
    for_far(far_wait)
    field_ref[...] += strict_dot(cross_ref[...], others_ref[...])

    def finish(head):
        k_columns = slice(head * width, (head + 1) * width)
        v_columns = slice(half_columns + head * width, half_columns + (head + 1) * width)

        def one(p, carry):
            at = pl.ds(pl.multiple_of(p * order, order), order)
            f = jnp.concatenate([field_ref[at, k_columns], field_ref[at, v_columns]], axis=1)
            high = f.astype(jnp.bfloat16)
            low = (f - high.astype(jnp.float32)).astype(jnp.bfloat16)
            y = jnp.dot(
                up_ref[...], jnp.concatenate([high, low, high], axis=0), preferred_element_type=jnp.float32
            )
            k = (close_ref[p, :, k_columns] + y[:, :width]).astype(jnp.bfloat16).astype(jnp.float32)
            v = (close_ref[p, :, v_columns] + y[:, width:]).astype(jnp.bfloat16).astype(jnp.float32)
            begin = pl.multiple_of(p * t_part, t_part)
            place = me * PARTS + p
            cos_p, sin_p = coarse_ref[0, pl.ds(place, 1), :], coarse_ref[1, pl.ds(place, 1), :]
            cosine = cos_p * fine_ref[0] - sin_p * fine_ref[1]
            sine = sin_p * fine_ref[0] + cos_p * fine_ref[1]
            turned = k * cosine + pltpu.roll(k, width // 2, 1) * sine
            k_ref[head, pl.ds(begin, t_part), :] = turned.astype(jnp.bfloat16)
            v_ref[head, :, pl.ds(begin, t_part)] = v.T.astype(jnp.bfloat16)
            return carry

        lax.fori_loop(0, PARTS, one, 0)

    finish(0)

    @pl.when(inside)
    def _():
        for block in range(1, blocks):
            hand(mate, 1, block, 1 - outward)
        for block in range(blocks):
            ask_copy(me, 1, block, 1 - outward).start()

    runs = [
        (0, 0, 0, blocks),
        (1, 0, 0, blocks),
        (2, 0, 0, blocks),
        (3, 0, 0, blocks - 1),
        (2, 1, 0, blocks),
        (3, 0, blocks - 1, 1),
        (3, 1, 0, 1),
        (1, 1, 0, blocks),
        (0, 1, 0, blocks),
        (3, 1, 1, blocks - 1),
    ]
    begins = [sum(run[3] for run in runs[:i]) for i in range(len(runs))]
    units = begins[-1] + runs[-1][3]

    def decode(u):
        kind, head, block = runs[0][0], runs[0][1], u
        for begin, run in zip(begins[1:], runs[1:]):
            late = u >= begin
            kind = jnp.where(late, run[0], kind)
            head = jnp.where(late, run[1], head)
            block = jnp.where(late, u - begin + run[2], block)
        source = jnp.where(
            kind == 0, mate, jnp.where(kind == 1, near_over, jnp.where(kind == 2, far_end, me))
        )
        return kind, head, block, source

    chunk = 512

    def score(u, keep_ref, top_ref):
        _, head, block, source = decode(u)
        q = asks_ref[source, head, pl.ds(pl.multiple_of(block * BLOCK, BLOCK), BLOCK), :]
        best = None
        for c in range(0, tokens, chunk):
            s = lax.dot_general(
                k_ref[head, c : c + chunk, :],
                q,
                (((1,), (1,)), ((), ())),
                preferred_element_type=jnp.float32,
            )
            keep_ref[c : c + chunk, :] = s
            top = jnp.max(s, axis=0, keepdims=True)
            best = top if best is None else jnp.maximum(best, top)
        top_ref[...] = best

    def weigh(u, keep_ref, top_ref):
        kind, head, block, _ = decode(u)
        best = top_ref[...]
        total = jnp.zeros((1, BLOCK), jnp.float32)
        accum = jnp.zeros((width, BLOCK), jnp.float32)
        for c in range(0, tokens, chunk):
            e = jnp.exp2((keep_ref[c : c + chunk, :] - best) * factor)
            total += jnp.sum(e, axis=0, keepdims=True)
            accum += jnp.dot(
                v_ref[head, :, c : c + chunk], e.astype(jnp.bfloat16), preferred_element_type=jnp.float32
            )
        own_ref[kind, head, block] = (accum / total).astype(jnp.bfloat16)
        own_log_ref[kind, head, block] = best * factor + jnp.log2(total)

    def both(src, src_log, dst, dst_log, send, recv, other):
        return (
            copy(src, dst, send.at[0], recv.at[0], other),
            copy(src_log, dst_log, send.at[1], recv.at[1], other),
        )

    def half_copy(kind, head, block):
        at = (kind, head, block)
        return both(
            own_ref.at[at],
            own_log_ref.at[at],
            half_ref.at[at],
            half_log_ref.at[at],
            half_send,
            half_recv.at[at],
            mate,
        )

    def over_copy(j, head, block):
        at = (j, head, block)
        return both(
            merged_ref.at[at],
            merged_log_ref.at[at],
            over_ref.at[at],
            over_log_ref.at[at],
            over_send,
            over_recv.at[at],
            near_over,
        )

    def last_copy(head, block):
        at = (head, block)
        return both(
            ready_ref.at[at],
            ready_log_ref.at[at],
            last_ref.at[at],
            last_log_ref.at[at],
            last_send,
            half_recv.at[(0,) + at],
            mate,
        )

    def blend(parts, logs):
        best = functools.reduce(jnp.maximum, logs)
        shares = [jnp.exp2(log - best) for log in logs]
        total = functools.reduce(jnp.add, shares)
        mixed = functools.reduce(
            jnp.add, [part.astype(jnp.float32) * (share / total) for part, share in zip(parts, shares)]
        )
        return mixed, best + jnp.log2(total)

    def merge_half(kind, head, block):
        for each in half_copy(kind, head, block):
            each.wait_recv()
        at = (kind - 1, head, block)
        mixed, log = blend(
            [own_ref[kind, head, block], half_ref[kind, head, block]],
            [own_log_ref[kind, head, block], half_log_ref[kind, head, block]],
        )
        merged_ref[at] = mixed.astype(jnp.bfloat16)
        merged_log_ref[at] = log
        for each in over_copy(*at):
            each.start()

    def settle(head, block):
        for each in half_copy(0, head, block) + over_copy(0, head, block):
            each.wait_recv()
        mixed, _ = blend(
            [own_ref[3, head, block], half_ref[0, head, block], over_ref[0, head, block]],
            [own_log_ref[3, head, block], half_log_ref[0, head, block], over_log_ref[0, head, block]],
        )
        out_ref[head, block * BLOCK : (block + 1) * BLOCK, :] = mixed.T.astype(out_ref.dtype)

    def pass_on(head, block):
        for each in over_copy(1, head, block):
            each.wait_recv()
        mixed, log = blend(
            [own_ref[0, head, block], over_ref[1, head, block]],
            [own_log_ref[0, head, block], over_log_ref[1, head, block]],
        )
        ready_ref[head, block] = mixed.astype(jnp.bfloat16)
        ready_log_ref[head, block] = log
        for each in last_copy(head, block):
            each.start()

    def await_ask(u):
        kind, head, block, source = decode(u)

        @pl.when(jnp.logical_and(kind < 3, jnp.logical_not(inside)))
        def _():
            ask_copy(source, head, block, 1 - outward).wait_recv()

    merges = ((1, 0, begins[1] + 3), (2, 0, begins[2] + 5), (2, 1, begins[4] + 6))
    passes = begins[4] + 7

    def send_on(u):
        kind, head, block, _ = decode(u)

        @pl.when(jnp.logical_and(kind < 3, jnp.logical_not(inside)))
        def _():
            for each in half_copy(kind, head, block):
                each.start()

        k_pass = u - passes

        @pl.when(jnp.logical_and(inside, jnp.logical_and(k_pass >= 0, k_pass < blocks)))
        def _():
            pass_on(0, k_pass)

        for kind, head, first in merges:
            k = u - first

            @pl.when(jnp.logical_and(inside, jnp.logical_and(k >= 0, k < blocks)))
            def _():
                merge_half(kind, head, k)

    await_ask(jnp.int32(0))
    score(jnp.int32(0), even_ref, even_top_ref)

    def serve(i, carry):
        u = 2 * i
        for at, source, head in ((0, far_end, 0), (3, far_end, 1), (5, near_over, 1)):

            @pl.when(jnp.logical_and(inside, i == at))
            def _():
                for block in range(blocks):
                    hand(source, head, block, outward)
                if source is near_over:
                    for block in range(2, blocks):
                        ask_copy(me, 1, block, outward).start()

        @pl.when(i == 2)
        def _():
            finish(1)

        await_ask(u + 1)
        score(u + 1, odd_ref, odd_top_ref)
        weigh(u, even_ref, even_top_ref)
        send_on(u)
        ahead = jnp.minimum(u + 2, units - 1)

        @pl.when(u + 2 < units)
        def _():
            await_ask(ahead)

        score(ahead, even_ref, even_top_ref)
        weigh(u + 1, odd_ref, odd_top_ref)
        send_on(u + 1)
        return carry

    lax.fori_loop(0, units // 2, serve, 0)

    @pl.when(inside)
    def _():
        for block in range(blocks):
            pass_on(1, block)
            merge_half(1, 1, block)
        ask_sent(me - 1, 1)
        ask_sent(me + 1, 0)
        ask_sent(far_end, outward)

    for_sides(lambda side: ask_sent(me, side))
    for_sides(lambda side: near_copy(side).wait_send())
    for_far(lambda other: far_copy(other).wait_send())

    @pl.when(inside)
    def _():
        for head in range(heads):
            for block in range(blocks):
                settle(head, block)
        for each in both(
            merged_ref, merged_log_ref, over_ref, over_log_ref, over_send, over_recv.at[0, 0, 0], near_over
        ) + both(ready_ref, ready_log_ref, last_ref, last_log_ref, last_send, half_recv.at[0, 0, 0], mate):
            each.wait_send()

    @pl.when(jnp.logical_not(inside))
    def _():
        for head in range(heads):
            for block in range(blocks):
                for each in last_copy(head, block):
                    each.wait_recv()
                mixed, _ = blend(
                    [own_ref[3, head, block], last_ref[head, block]],
                    [own_log_ref[3, head, block], last_log_ref[head, block]],
                )
                out_ref[head, block * BLOCK : (block + 1) * BLOCK, :] = mixed.T.astype(out_ref.dtype)
        kinds = pl.ds(0, 3)
        for each in both(
            own_ref.at[kinds], own_log_ref.at[kinds], half_ref, half_log_ref, half_send, half_recv.at[0, 0, 0], mate
        ):
            each.wait_send()


def by_tokens(keys, values, queries, positions, count):
    heads, rows, width = queries.shape
    n_dev, columns = keys.shape
    length = n_dev * count
    near, down, up, local, merge, cross = fields(length, count)

    def tall(matrix):
        return np.concatenate(split_two(matrix), axis=-2)

    def table(places):
        return tall(np.concatenate(spins(places, width).astype(np.float64), axis=1))

    up_high, up_low = split_two(up)
    t_part = near.shape[0]
    tokens = n_dev // 2
    blocks = rows // BLOCK
    split = 128
    operands = (
        table(np.arange(length // split) * float(split)),
        table(np.arange(split) * 1.0),
        tall(near),
        tall(down),
        np.concatenate([up_high, up_high, up_low], axis=1),
        tall(local),
        tall(merge),
        tall(cross),
        spins(np.arange(count * PARTS) * float(t_part), width),
        spins(np.arange(t_part) * 1.0, width),
    )
    held = [jax.ShapeDtypeStruct(o.shape[1:] if o.ndim == 3 and o.shape[0] == count else o.shape, o.dtype) for o in operands]
    dma = pltpu.SemaphoreType.DMA

    def parts(*lead):
        return [
            pltpu.VMEM(lead + (heads, blocks, width, BLOCK), jnp.bfloat16),
            pltpu.VMEM(lead + (heads, blocks, 1, BLOCK), jnp.float32),
        ]

    return pl.pallas_call(
        functools.partial(fused_kernel, count, math.log2(math.e) / math.sqrt(width)),
        in_specs=[pl.BlockSpec(memory_space=pl.ANY)] * 14,
        out_specs=pl.BlockSpec(memory_space=pltpu.VMEM),
        out_shape=jax.ShapeDtypeStruct(queries.shape, jnp.bfloat16),
        scratch_shapes=[
            pltpu.VMEM(keys.shape, keys.dtype),
            pltpu.VMEM(values.shape, values.dtype),
            pltpu.VMEM(queries.shape, queries.dtype),
            pltpu.VMEM((rows,), jnp.int32),
        ]
        + [pltpu.VMEM(h.shape, h.dtype) for h in held]
        + [
            pltpu.VMEM((PARTS * ORDER, 2 * columns), jnp.float32),
            pltpu.VMEM((2 * EDGE + FAR, 2 * columns), jnp.float32),
            pltpu.VMEM((cross.shape[2], 2 * columns), jnp.float32),
            pltpu.VMEM((PARTS, t_part, 2 * columns), jnp.float32),
            pltpu.VMEM((PARTS * ORDER, 2 * columns), jnp.float32),
            pltpu.VMEM((heads, tokens, width), jnp.bfloat16),
            pltpu.VMEM((heads, width, tokens), jnp.bfloat16),
            pltpu.VMEM((tokens, BLOCK), jnp.float32),
            pltpu.VMEM((tokens, BLOCK), jnp.float32),
            pltpu.VMEM((1, BLOCK), jnp.float32),
            pltpu.VMEM((1, BLOCK), jnp.float32),
            pltpu.VMEM((count, heads, rows, width), jnp.bfloat16),
        ]
        + parts(4)
        + parts(3)
        + parts(2)
        + parts(2)
        + parts()
        + parts()
        + [
            dma((12,)),
            dma((PARTS, 2)),
            pltpu.SemaphoreType.REGULAR((2,)),
            pltpu.SemaphoreType.REGULAR,
            dma((count,)),
            dma((count,)),
            dma((count, 2)),
            dma((count, heads, blocks)),
            dma((2,)),
            dma((3, heads, blocks, 2)),
            dma((2,)),
            dma((2, heads, blocks, 2)),
            dma((2,)),
        ],
        compiler_params=pltpu.CompilerParams(
            collective_id=0, has_side_effects=True, vmem_limit_bytes=60 * 1024 * 1024
        ),
    )(keys, values, queries, positions, *operands)


def by_columns(keys, values, queries, positions):
    key_parts = lax.all_to_all(keys, "ctx", split_axis=1, concat_axis=0, tiled=True)
    value_parts = lax.all_to_all(values, "ctx", split_axis=1, concat_axis=0, tiled=True)
    heads, rows, width = queries.shape
    per_device = key_parts.shape[1]
    compact = compress(jnp.concatenate([key_parts, value_parts], axis=1))
    rotated = rotate_rows(queries.astype(jnp.float32), positions.astype(jnp.float32)).astype(
        jnp.bfloat16
    )
    whole = lax.all_gather(compact.T, "ctx", axis=0, tiled=True)
    tokens = whole.shape[1]
    shaped = whole.reshape(-1, 2, per_device, tokens)
    key_rows = shaped[:, 0].reshape(heads, width, tokens).swapaxes(1, 2)
    value_rows = shaped[:, 1].reshape(heads, width, tokens).swapaxes(1, 2)
    places = jnp.arange(tokens).astype(jnp.float32)
    ready = rotate_rows(key_rows.astype(jnp.float32), places).astype(jnp.bfloat16)
    return attend(rotated, ready, value_rows, jnp.zeros((), jnp.int32))[0]


def solution(mesh):
    count = mesh.shape["ctx"]

    def on_device(keys, values, queries, positions):
        heads, rows, width = queries.shape
        if count == 4 and heads == 2 and keys.shape[0] % (PARTS * 512) == 0 and rows % BLOCK == 0 and width == 128:
            return by_tokens(keys, values, queries, positions, count)
        return by_columns(keys, values, queries, positions)

    return jax.shard_map(
        on_device,
        mesh=mesh,
        in_specs=(
            P(("user", "ctx"), "heads"),
            P(("user", "ctx"), "heads"),
            P("heads", ("user", "ctx"), None),
            P(("user", "ctx")),
        ),
        out_specs=P("heads", ("user", "ctx"), None),
        check_vma=False,
    )
```

```python
import functools
import math

import jax
import jax.numpy as jnp
import numpy as np
from jax import lax
from jax.experimental import pallas as pl
from jax.experimental.pallas import tpu as pltpu
from jax.sharding import PartitionSpec as P

OUTER = 128
PARTS = 4
ORDER = 64
EDGE = 32
FAR = 8
BLOCK = 256
MESH = pl.DeviceIdType.MESH


def split_two(matrix):
    high = matrix.astype(jnp.bfloat16)
    low = (matrix - np.asarray(high).astype(np.float64)).astype(jnp.bfloat16)
    return high, low


@functools.lru_cache(maxsize=None)
def stages(length):
    outer = OUTER
    inner = length // outer
    step = inner // 2
    a = np.arange(outer)
    c = np.arange(outer)
    turn = 2 * outer
    angle = np.pi / outer * ((c[:, None] * a[None, :]) % turn)
    alternate = np.where(a % 2 == 0, 1.0, -1.0)
    first = np.stack([np.cos(angle), -np.sin(angle)], axis=1)
    first[0, 1] = alternate
    d = np.arange(length // 2 // turn)
    k = np.concatenate([c[:, None] + turn * d, (turn - c[:, None]) % turn + turn * d], axis=1)
    k[0, d.size :] = outer + turn * d
    sign = np.concatenate([np.ones(d.size), -np.ones(d.size)])
    b = np.arange(inner)
    q = np.arange(step)
    theta = np.pi / (2 * length) * ((k[:, :, None] * (2 * b + 1)) % (4 * length))
    phi = np.pi / length * ((k[:, None, :] * (2 * q + 1)[:, None]) % (2 * length))
    forward = np.stack([np.cos(theta), np.sin(theta) * sign[None, :, None]], axis=2)
    weight = np.where(k == 0, 1.0, 2.0) / length
    back = np.stack([np.cos(phi), np.sin(phi) * sign], axis=1) * weight[:, None, None, :]
    half = d.size
    forward[0, :half, 1] = 0.0
    forward[0, half:, 1] = np.cos(theta[0, half:])
    forward[0, half:, 0] = 0.0
    back[0, 1, :, :half] = 0.0
    back[0, 1, :, half:] = np.cos(phi[0, :, half:]) * weight[0, half:]
    back[0, 0, :, half:] = 0.0
    middle = back.reshape(outer, 2 * step, 2 * half) @ forward.reshape(outer, 2 * half, 2 * inner)
    last = first.transpose(2, 0, 1).reshape(outer, 2 * outer)
    return first.reshape(2 * outer, outer), middle, last


def compress(signal):
    length, columns = signal.shape
    outer, inner = OUTER, length // OUTER
    first, middle, last = stages(length)
    first_high, first_low = split_two(first)
    flat = signal.reshape(outer, inner * columns)
    one = jnp.dot(first_high, flat, preferred_element_type=jnp.float32) + jnp.dot(
        first_low, flat, preferred_element_type=jnp.float32
    )
    one = one.reshape(outer, 2 * inner, columns)
    two = jnp.einsum(
        "cob,cbl->col", jnp.asarray(middle.astype(np.float32)), one, precision=lax.Precision.HIGH
    )
    three = jnp.dot(
        jnp.asarray(last.astype(np.float32)),
        two.reshape(2 * outer, inner // 2 * columns),
        precision=lax.Precision.HIGH,
    )
    return three.reshape(length // 2, columns).astype(jnp.bfloat16)

def strict_dot(left, right):
    rows, columns = left.shape[0] // 2, right.shape[1]
    high = right.astype(jnp.bfloat16)
    low = (right - high.astype(jnp.float32)).astype(jnp.bfloat16)
    both = jnp.dot(
        left, jnp.concatenate([high, low], axis=1), preferred_element_type=jnp.float32
    )
    return both[:rows, :columns] + (both[:rows, columns:] + both[rows:, :columns])


def inverse_freq(width):
    return jnp.exp(jnp.arange(width // 2).astype(jnp.float32) * (-2.0 * math.log(500000.0) / width))


def rotate_rows(block, places):
    width = block.shape[-1]
    half = width // 2
    angles = places[:, None] * inverse_freq(width)[None, :]
    cosine = jnp.cos(angles)
    sine = jnp.sin(angles)
    first = block[..., :half]
    second = block[..., half:]
    return jnp.concatenate(
        [first * cosine - second * sine, second * cosine + first * sine], axis=-1
    )


def attend_kernel(chunk, scale, resume, finish, swap_ref, q_ref, k_ref, v_ref, *refs):
    q = q_ref[0]
    swap = swap_ref[0] == 1
    rows, width = q.shape
    factor = scale * math.log2(math.e)
    if resume:
        accum = refs[0][0]
        best = refs[1][0][:, :1]
        total = refs[2][0][:, :1]
        refs = refs[3:]
    else:
        best = jnp.full((rows, 1), -jnp.inf, jnp.float32)
        total = jnp.zeros((rows, 1), jnp.float32)
        accum = jnp.zeros((rows, width), jnp.float32)
    tokens = k_ref.shape[1]
    for start in range(0, tokens, chunk):
        one = k_ref[0, start : start + chunk, :]
        two = v_ref[0, start : start + chunk, :]
        k, v = jnp.where(swap, two, one), jnp.where(swap, one, two)
        scores = lax.dot_general(
            q, k, (((1,), (1,)), ((), ())), preferred_element_type=jnp.float32
        )
        fresh = jnp.maximum(best, jnp.max(scores, axis=1, keepdims=True))
        expo = jnp.exp2((scores - fresh) * factor)
        shrink = jnp.exp2((best - fresh) * factor)
        total = total * shrink + jnp.sum(expo, axis=1, keepdims=True)
        accum = accum * shrink + jnp.dot(
            expo.astype(jnp.bfloat16), v, preferred_element_type=jnp.float32
        )
        best = fresh
    if finish:
        refs[0][0] = (accum / total).astype(refs[0].dtype)
        refs[1][0] = jnp.broadcast_to(best * factor + jnp.log2(total), (rows, 8))
    else:
        refs[0][0] = accum
        refs[1][0] = jnp.broadcast_to(best, (rows, 8))
        refs[2][0] = jnp.broadcast_to(total, (rows, 8))


def attend(queries, keys, values, swap, part=0, parts=1, state=None):
    groups, rows, width = queries.shape
    heads, tokens, _ = values.shape
    per_head = groups // heads
    block = math.gcd(rows, 768)
    chunk = math.gcd(tokens, 1024)
    scale = 1.0 / math.sqrt(width)
    finish = part == parts - 1
    wide = pl.BlockSpec((1, block, width), lambda g, i: (g, i, 0))
    thin = pl.BlockSpec((1, block, 8), lambda g, i: (g, i, 0))
    thin_shape = jax.ShapeDtypeStruct((groups, rows, 8), jnp.float32)
    state = () if state is None else tuple(state)
    wide_type = jnp.bfloat16 if finish else jnp.float32
    return pl.pallas_call(
        functools.partial(attend_kernel, chunk, scale, bool(state), finish),
        grid=(groups, rows // block),
        in_specs=[
            pl.BlockSpec(memory_space=pltpu.SMEM),
            wide,
            pl.BlockSpec((1, tokens, width), lambda g, i: (g // per_head, part, 0)),
            pl.BlockSpec((1, tokens, width), lambda g, i: (g // per_head, 0, 0)),
        ]
        + ([wide, thin, thin] if state else []),
        out_specs=[wide, thin] if finish else [wide, thin, thin],
        out_shape=[jax.ShapeDtypeStruct((groups, rows, width), wide_type), thin_shape]
        + ([] if finish else [thin_shape]),
        cost_estimate=pl.CostEstimate(
            flops=8 * groups * rows * tokens * width,
            bytes_accessed=4 * groups * rows * width * 2,
            transcendentals=groups * rows * tokens,
        ),
    )(swap.reshape(1), queries, keys, values, *state)


def bounds(count, left, right):
    return np.log(left / (count - 1 + right)), np.log((count - 1 + left) / right)


def nodes(count, order, left, right):
    low, top = bounds(count, left, right)
    e = np.exp((top - low) / 2 * np.cos(np.pi * (2 * np.arange(order) + 1) / (2 * order)) + (top + low) / 2)
    return ((count - 1 + right) * e - left) / (1 + e)


def cardinals(places, count, order, left, right):
    low, top = bounds(count, left, right)
    at = (2 * np.log((places + left) / (count - 1 + right - places)) - top - low) / (top - low)
    at = np.arccos(np.clip(at, -1.0, 1.0))
    own = np.pi * (2 * np.arange(order) + 1) / (2 * order)
    total = np.zeros((places.size, order))
    for k in range(order):
        total += (1.0 if k == 0 else 2.0) / order * np.cos(k * at)[:, None] * np.cos(k * own)[None, :]
    return total


@functools.lru_cache(maxsize=None)
def fields(length, devices):
    parts, order = PARTS, ORDER
    scale = math.sqrt(0.5) / (2 * length)

    def cot(m):
        return 1.0 / np.tan(np.pi * m / (4 * length))

    n_dev = length // devices
    n_part, t_dev = n_dev // parts, n_dev // 2
    t_part = n_part // 2
    n, t = np.arange(n_part), np.arange(t_part)
    sign_n = np.array([1.0, -1.0, -1.0, 1.0])[n % 4]
    sign_t = np.where(t % 2 == 0, 1.0, -1.0)
    near = sign_t[:, None] * sign_n * scale * cot(4 * t[:, None] - 2 * n + 1.0)
    down = cardinals(n, n_part, order, 1.5, 1.5).T * sign_n
    up = sign_t[:, None] * cardinals(t, t_part, order, 0.75, 0.75)
    part = np.arange(parts)[:, None]
    source = (part * n_part + nodes(n_part, order, 1.5, 1.5)).reshape(-1)
    target = (part * t_part + nodes(t_part, order, 0.75, 0.75)).reshape(-1)
    own = np.arange(parts * order) // order
    same = own[:, None] == own[None, :]
    local = np.where(same, 0.0, scale * cot(np.where(same, 1.0, 4 * target[:, None] - 2 * source + 1)))
    last = n_dev - 1
    wide = float(n_dev)
    merge = np.concatenate(
        [
            cardinals(source, n_dev, EDGE, 1.5, wide).T,
            cardinals(last - source, n_dev, EDGE, 1.5, wide).T,
            cardinals(source, n_dev, FAR, 2 * wide, 2 * wide).T,
        ]
    )
    to_left = nodes(n_dev, EDGE, 1.5, wide)
    sparse = nodes(n_dev, FAR, 2 * wide, 2 * wide)
    size = 3 * EDGE + devices * FAR
    cross = np.zeros((devices, parts * order, size + -size % 128))
    for r in range(devices):
        a = 4 * (target + r * t_dev)[:, None]
        for s in range(devices):
            if abs(r - s) > 1:
                spots, start = sparse, 3 * EDGE + s * FAR
            elif s < r or (s == r and 2 * r >= devices):
                spots, start = last - to_left, EDGE * (r - s)
            else:
                spots, start = to_left, 2 * EDGE * (s - r)
            b = 2 * (spots + s * n_dev)
            block = scale * cot(a + b + 3)
            if r != s:
                block = block + scale * cot(a - b + 1)
            cross[r, :, start : start + block.shape[1]] = block
    return near, down, up, local, merge, cross


def spins(places, width):
    freq = 500000.0 ** (-2.0 * np.arange(width // 2) / width)
    angles = places[:, None] * freq
    cosine, sine = np.cos(angles), np.sin(angles)
    return np.stack(
        [np.concatenate([cosine, cosine], axis=1), np.concatenate([-sine, sine], axis=1)]
    ).astype(np.float32)


def fused_kernel(
    count,
    factor,
    keys_hbm,
    values_hbm,
    queries_hbm,
    places_hbm,
    high_hbm,
    low_hbm,
    near_hbm,
    down_hbm,
    up_hbm,
    local_hbm,
    merge_hbm,
    cross_hbm,
    coarse_hbm,
    fine_hbm,
    out_ref,
    keys_ref,
    values_ref,
    queries_ref,
    places_ref,
    high_ref,
    low_ref,
    near_ref,
    down_ref,
    up_ref,
    local_ref,
    merge_ref,
    cross_ref,
    coarse_ref,
    fine_ref,
    parts_ref,
    whole_ref,
    others_ref,
    close_ref,
    field_ref,
    k_ref,
    v_ref,
    even_ref,
    odd_ref,
    even_top_ref,
    odd_top_ref,
    asks_ref,
    own_ref,
    own_log_ref,
    half_ref,
    half_log_ref,
    merged_ref,
    merged_log_ref,
    over_ref,
    over_log_ref,
    ready_ref,
    ready_log_ref,
    last_ref,
    last_log_ref,
    load_sem,
    token_sem,
    behind_sem,
    end_sem,
    field_send,
    field_recv,
    ask_send,
    ask_recv,
    half_send,
    half_recv,
    over_send,
    over_recv,
    last_send,
):
    me = lax.axis_index("ctx")
    heads, rows, width = queries_ref.shape
    order = ORDER
    blocks = rows // BLOCK
    n_part = near_ref.shape[1]
    t_part = n_part // 2
    half_columns = keys_ref.shape[1]
    tokens = k_ref.shape[1]
    has_left, has_right = me > 0, me < count - 1
    inside = jnp.logical_and(has_left, has_right)
    lower = me < count // 2
    mate = me + 1 - 2 * lax.rem(me, 2)
    far_end = jnp.where(lower, count - 1, 0)
    near_over = jnp.where(lower, count // 2, count // 2 - 1)
    outward = jnp.where(lower, 0, 1)

    def copy(src, dst, send, recv, other):
        return pltpu.make_async_remote_copy(
            src_ref=src,
            dst_ref=dst,
            send_sem=send,
            recv_sem=recv,
            device_id={"ctx": other},
            device_id_type=MESH,
        )

    def for_sides(action):
        for side, there in enumerate((has_left, has_right)):

            @pl.when(there)
            def _():
                action(side)

    def greet(sem, other):
        pl.semaphore_signal(sem, inc=1, device_id={"ctx": other}, device_id_type=MESH)

    others_ref[...] = jnp.zeros_like(others_ref)
    barrier = pltpu.get_barrier_semaphore()
    for_sides(lambda side: greet(barrier, me + 2 * side - 1))
    pairs = (
        (places_hbm, places_ref),
        (queries_hbm, queries_ref),
        (high_hbm, high_ref),
        (low_hbm, low_ref),
        (down_hbm, down_ref),
        (merge_hbm, merge_ref),
        (near_hbm, near_ref),
        (local_hbm, local_ref),
        (cross_hbm.at[me], cross_ref),
        (up_hbm, up_ref),
        (coarse_hbm, coarse_ref),
        (fine_hbm, fine_ref),
    )
    loads = [pltpu.make_async_copy(src, dst, load_sem.at[i]) for i, (src, dst) in enumerate(pairs)]
    sides = ((keys_hbm, keys_ref), (values_hbm, values_ref))
    token_loads = [
        [
            pltpu.make_async_copy(
                src.at[pl.ds(p * n_part, n_part)], dst.at[pl.ds(p * n_part, n_part)], token_sem.at[p, side]
            )
            for side, (src, dst) in enumerate(sides)
        ]
        for p in range(PARTS)
    ]
    for each in loads[:6]:
        each.start()
    for p in range(PARTS):
        for each in token_loads[p]:
            each.start()
    for each in loads[6:]:
        each.start()
    for each in loads[:4]:
        each.wait()

    split = low_ref.shape[0] // 2
    for i in range(rows // split):
        here = slice(i * split, (i + 1) * split)
        place = jnp.broadcast_to(places_ref[here].astype(jnp.float32)[None], (split, split)).T.astype(jnp.int32)
        spun = []
        for value, table_ref in ((place // split, high_ref), (lax.rem(place, split), low_ref)):
            size = table_ref.shape[0] // 2
            value = value if size == split else value[:, :1]
            picked = value == lax.broadcasted_iota(jnp.int32, (split, size), 1)
            picked = jnp.where(picked, 1.0, 0.0).astype(jnp.bfloat16)
            got = jnp.dot(
                jnp.concatenate([picked, picked], axis=1), table_ref[...], preferred_element_type=jnp.float32
            )
            spun.append((got[:, :width], got[:, width:]))
        (cos_a, sin_a), (cos_b, sin_b) = spun
        cosine, sine = cos_a * cos_b - sin_a * sin_b, sin_a * cos_b + cos_a * sin_b
        for head in range(heads):
            x = queries_ref[head, here, :].astype(jnp.float32)
            asks_ref[me, head, here, :] = (x * cosine + pltpu.roll(x, width // 2, 1) * sine).astype(jnp.bfloat16)

    def ask_copy(source, head, block, side):
        here = pl.ds(block * BLOCK if isinstance(block, int) else pl.multiple_of(block * BLOCK, BLOCK), BLOCK)
        return copy(
            asks_ref.at[source, head, here],
            asks_ref.at[source, head, here],
            ask_send.at[source, side],
            ask_recv.at[source, head, block],
            me + 2 * side - 1,
        )

    pl.semaphore_wait(barrier, jnp.where(inside, 2, 1))
    for block in range(blocks - 1):
        for_sides(lambda side: ask_copy(me, 0, block, side).start())
    for_sides(lambda side: greet(behind_sem.at[1 - side], me + 2 * side - 1))

    for each in loads[4:6]:
        each.wait()
    for p in range(PARTS):
        for side, (_, x_ref) in enumerate(sides):
            token_loads[p][side].wait()
            z = jnp.dot(
                down_ref[...], x_ref[p * n_part : (p + 1) * n_part, :], preferred_element_type=jnp.float32
            )
            parts_ref[
                p * order : (p + 1) * order, side * half_columns : (side + 1) * half_columns
            ] = z[:order] + z[order:]
        if p == 1:
            for_sides(lambda side: pl.semaphore_wait(behind_sem.at[side], 1))

            @pl.when(inside)
            def _():
                greet(end_sem, mate)

    whole_ref[...] = strict_dot(merge_ref[...], parts_ref[...])
    others_ref[:EDGE] = whole_ref[pl.ds(pl.multiple_of(jnp.where(lower, 0, EDGE), EDGE), EDGE), :]

    def near_copy(side):
        other = me + 2 * side - 1
        return copy(
            whole_ref.at[pl.ds(side * EDGE, EDGE)],
            others_ref.at[pl.ds(EDGE * (2 - side), EDGE)],
            field_send.at[other],
            field_recv.at[me],
            other,
        )

    def far_copy(other):
        return copy(
            whole_ref.at[pl.ds(2 * EDGE, FAR)],
            others_ref.at[pl.ds(pl.multiple_of(3 * EDGE + me * FAR, FAR), FAR)],
            field_send.at[other],
            field_recv.at[me],
            other,
        )

    def near_wait(side):
        source = me + 2 * side - 1
        copy(
            whole_ref.at[pl.ds(0, EDGE)],
            others_ref.at[pl.ds(EDGE * (1 + side), EDGE)],
            field_send.at[source],
            field_recv.at[source],
            source,
        ).wait_recv()

    def far_wait(source):
        copy(
            whole_ref.at[pl.ds(2 * EDGE, FAR)],
            others_ref.at[pl.ds(3 * EDGE + source * FAR, FAR)],
            field_send.at[source],
            field_recv.at[source],
            source,
        ).wait_recv()

    def ask_sent(source, side):
        copy(
            asks_ref.at[source],
            asks_ref.at[source],
            ask_send.at[source, side],
            ask_recv.at[source, 0, 0],
            me + 2 * side - 1,
        ).wait_send()

    def hand(source, head, block, side):
        handed = ask_copy(source, head, block, side)
        handed.wait_recv()
        handed.start()

    def for_far(action):
        for other in range(count):

            @pl.when(jnp.logical_or(other - me > 1, me - other > 1))
            def _():
                action(other)

    @pl.when(jnp.logical_not(inside))
    def _():
        pl.semaphore_wait(end_sem, 1)

    for_far(lambda other: far_copy(other).start())
    for_sides(lambda side: near_copy(side).start())
    for_sides(lambda side: ask_copy(me, 0, blocks - 1, side).start())

    @pl.when(jnp.logical_not(inside))
    def _():
        for block in range(blocks):
            ask_copy(me, 1, block, 1 - outward).start()

    loads[6].wait()

    def close(p, carry):
        start = p * n_part if isinstance(p, int) else pl.multiple_of(p * n_part, n_part)
        for side, (_, x_ref) in enumerate(sides):
            z = jnp.dot(near_ref[...], x_ref[pl.ds(start, n_part), :], preferred_element_type=jnp.float32)
            close_ref[p, :, side * half_columns : (side + 1) * half_columns] = z[:t_part] + z[t_part:]
        return carry

    close(0, 0)

    @pl.when(inside)
    def _():
        for block in range(blocks - 1):
            for side in range(2):
                hand(me + 2 * side - 1, 0, block, 1 - side)
        ask_copy(me, 1, 0, outward).start()

    lax.fori_loop(1, PARTS, close, 0)

    @pl.when(inside)
    def _():
        for side in range(2):
            hand(me + 2 * side - 1, 0, blocks - 1, 1 - side)
        hand(mate, 1, 0, 1 - outward)
        ask_copy(me, 1, 1, outward).start()

    for each in loads[7:]:
        each.wait()
    field_ref[...] = strict_dot(local_ref[...], parts_ref[...])

    for_sides(near_wait)
    for_far(far_wait)
    field_ref[...] += strict_dot(cross_ref[...], others_ref[...])

    def finish(head):
        k_columns = slice(head * width, (head + 1) * width)
        v_columns = slice(half_columns + head * width, half_columns + (head + 1) * width)

        def one(p, carry):
            at = pl.ds(pl.multiple_of(p * order, order), order)
            f = jnp.concatenate([field_ref[at, k_columns], field_ref[at, v_columns]], axis=1)
            high = f.astype(jnp.bfloat16)
            low = (f - high.astype(jnp.float32)).astype(jnp.bfloat16)
            y = jnp.dot(
                up_ref[...], jnp.concatenate([high, low, high], axis=0), preferred_element_type=jnp.float32
            )
            k = (close_ref[p, :, k_columns] + y[:, :width]).astype(jnp.bfloat16).astype(jnp.float32)
            v = (close_ref[p, :, v_columns] + y[:, width:]).astype(jnp.bfloat16).astype(jnp.float32)
            begin = pl.multiple_of(p * t_part, t_part)
            place = me * PARTS + p
            cos_p, sin_p = coarse_ref[0, pl.ds(place, 1), :], coarse_ref[1, pl.ds(place, 1), :]
            cosine = cos_p * fine_ref[0] - sin_p * fine_ref[1]
            sine = sin_p * fine_ref[0] + cos_p * fine_ref[1]
            turned = k * cosine + pltpu.roll(k, width // 2, 1) * sine
            k_ref[head, pl.ds(begin, t_part), :] = turned.astype(jnp.bfloat16)
            v_ref[head, :, pl.ds(begin, t_part)] = v.T.astype(jnp.bfloat16)
            return carry

        lax.fori_loop(0, PARTS, one, 0)

    finish(0)

    @pl.when(inside)
    def _():
        for block in range(1, blocks):
            hand(mate, 1, block, 1 - outward)
        for block in range(blocks):
            ask_copy(me, 1, block, 1 - outward).start()

    runs = [
        (0, 0, 0, blocks),
        (1, 0, 0, blocks),
        (2, 0, 0, blocks),
        (3, 0, 0, blocks - 1),
        (2, 1, 0, blocks),
        (3, 0, blocks - 1, 1),
        (3, 1, 0, 1),
        (1, 1, 0, blocks),
        (0, 1, 0, blocks),
        (3, 1, 1, blocks - 1),
    ]
    begins = [sum(run[3] for run in runs[:i]) for i in range(len(runs))]
    units = begins[-1] + runs[-1][3]

    def decode(u):
        kind, head, block = runs[0][0], runs[0][1], u
        for begin, run in zip(begins[1:], runs[1:]):
            late = u >= begin
            kind = jnp.where(late, run[0], kind)
            head = jnp.where(late, run[1], head)
            block = jnp.where(late, u - begin + run[2], block)
        source = jnp.where(
            kind == 0, mate, jnp.where(kind == 1, near_over, jnp.where(kind == 2, far_end, me))
        )
        return kind, head, block, source

    chunk = 512

    def score(u, keep_ref, top_ref):
        _, head, block, source = decode(u)
        q = asks_ref[source, head, pl.ds(pl.multiple_of(block * BLOCK, BLOCK), BLOCK), :]
        best = None
        for c in range(0, tokens, chunk):
            s = lax.dot_general(
                k_ref[head, c : c + chunk, :],
                q,
                (((1,), (1,)), ((), ())),
                preferred_element_type=jnp.float32,
            )
            keep_ref[c : c + chunk, :] = s
            top = jnp.max(s, axis=0, keepdims=True)
            best = top if best is None else jnp.maximum(best, top)
        top_ref[...] = best

    def weigh(u, keep_ref, top_ref):
        kind, head, block, _ = decode(u)
        best = top_ref[...]
        total = jnp.zeros((1, BLOCK), jnp.float32)
        accum = jnp.zeros((width, BLOCK), jnp.float32)
        for c in range(0, tokens, chunk):
            e = jnp.exp2((keep_ref[c : c + chunk, :] - best) * factor)
            total += jnp.sum(e, axis=0, keepdims=True)
            accum += jnp.dot(
                v_ref[head, :, c : c + chunk], e.astype(jnp.bfloat16), preferred_element_type=jnp.float32
            )
        own_ref[kind, head, block] = (accum / total).astype(jnp.bfloat16)
        own_log_ref[kind, head, block] = best * factor + jnp.log2(total)

    def both(src, src_log, dst, dst_log, send, recv, other):
        return (
            copy(src, dst, send.at[0], recv.at[0], other),
            copy(src_log, dst_log, send.at[1], recv.at[1], other),
        )

    def half_copy(kind, head, block):
        at = (kind, head, block)
        return both(
            own_ref.at[at],
            own_log_ref.at[at],
            half_ref.at[at],
            half_log_ref.at[at],
            half_send,
            half_recv.at[at],
            mate,
        )

    def over_copy(j, head, block):
        at = (j, head, block)
        return both(
            merged_ref.at[at],
            merged_log_ref.at[at],
            over_ref.at[at],
            over_log_ref.at[at],
            over_send,
            over_recv.at[at],
            near_over,
        )

    def last_copy(head, block):
        at = (head, block)
        return both(
            ready_ref.at[at],
            ready_log_ref.at[at],
            last_ref.at[at],
            last_log_ref.at[at],
            last_send,
            half_recv.at[(0,) + at],
            mate,
        )

    def blend(parts, logs):
        best = functools.reduce(jnp.maximum, logs)
        shares = [jnp.exp2(log - best) for log in logs]
        total = functools.reduce(jnp.add, shares)
        mixed = functools.reduce(
            jnp.add, [part.astype(jnp.float32) * (share / total) for part, share in zip(parts, shares)]
        )
        return mixed, best + jnp.log2(total)

    def merge_half(kind, head, block):
        for each in half_copy(kind, head, block):
            each.wait_recv()
        at = (kind - 1, head, block)
        mixed, log = blend(
            [own_ref[kind, head, block], half_ref[kind, head, block]],
            [own_log_ref[kind, head, block], half_log_ref[kind, head, block]],
        )
        merged_ref[at] = mixed.astype(jnp.bfloat16)
        merged_log_ref[at] = log
        for each in over_copy(*at):
            each.start()

    def settle(head, block):
        for each in half_copy(0, head, block) + over_copy(0, head, block):
            each.wait_recv()
        mixed, _ = blend(
            [own_ref[3, head, block], half_ref[0, head, block], over_ref[0, head, block]],
            [own_log_ref[3, head, block], half_log_ref[0, head, block], over_log_ref[0, head, block]],
        )
        out_ref[head, block * BLOCK : (block + 1) * BLOCK, :] = mixed.T.astype(out_ref.dtype)

    def pass_on(head, block):
        for each in over_copy(1, head, block):
            each.wait_recv()
        mixed, log = blend(
            [own_ref[0, head, block], over_ref[1, head, block]],
            [own_log_ref[0, head, block], over_log_ref[1, head, block]],
        )
        ready_ref[head, block] = mixed.astype(jnp.bfloat16)
        ready_log_ref[head, block] = log
        for each in last_copy(head, block):
            each.start()

    def await_ask(u):
        kind, head, block, source = decode(u)

        @pl.when(jnp.logical_and(kind < 3, jnp.logical_not(inside)))
        def _():
            ask_copy(source, head, block, 1 - outward).wait_recv()

    merges = ((1, 0, begins[1] + 3), (2, 0, begins[2] + 4), (2, 1, begins[4] + 5))
    passes = begins[4] + 6

    def send_on(u):
        kind, head, block, _ = decode(u)

        @pl.when(jnp.logical_and(kind < 3, jnp.logical_not(inside)))
        def _():
            for each in half_copy(kind, head, block):
                each.start()

        k_pass = u - passes

        @pl.when(jnp.logical_and(inside, jnp.logical_and(k_pass >= 0, k_pass < blocks)))
        def _():
            pass_on(0, k_pass)

        for kind, head, first in merges:
            k = u - first

            @pl.when(jnp.logical_and(inside, jnp.logical_and(k >= 0, k < blocks)))
            def _():
                merge_half(kind, head, k)

    await_ask(jnp.int32(0))
    score(jnp.int32(0), even_ref, even_top_ref)

    def serve(i, carry):
        u = 2 * i
        for at, source, head in ((0, far_end, 0), (3, far_end, 1), (5, near_over, 1)):

            @pl.when(jnp.logical_and(inside, i == at))
            def _():
                for block in range(blocks):
                    hand(source, head, block, outward)
                if source is near_over:
                    for block in range(2, blocks):
                        ask_copy(me, 1, block, outward).start()

        @pl.when(i == 2)
        def _():
            finish(1)

        await_ask(u + 1)
        score(u + 1, odd_ref, odd_top_ref)
        weigh(u, even_ref, even_top_ref)
        send_on(u)
        ahead = jnp.minimum(u + 2, units - 1)

        @pl.when(u + 2 < units)
        def _():
            await_ask(ahead)

        score(ahead, even_ref, even_top_ref)
        weigh(u + 1, odd_ref, odd_top_ref)
        send_on(u + 1)
        return carry

    lax.fori_loop(0, units // 2, serve, 0)

    @pl.when(inside)
    def _():
        for block in range(blocks):
            pass_on(1, block)
            merge_half(1, 1, block)
        ask_sent(me - 1, 1)
        ask_sent(me + 1, 0)
        ask_sent(far_end, outward)

    for_sides(lambda side: ask_sent(me, side))
    for_sides(lambda side: near_copy(side).wait_send())
    for_far(lambda other: far_copy(other).wait_send())

    @pl.when(inside)
    def _():
        for head in range(heads):
            for block in range(blocks):
                settle(head, block)
        for each in both(
            merged_ref, merged_log_ref, over_ref, over_log_ref, over_send, over_recv.at[0, 0, 0], near_over
        ) + both(ready_ref, ready_log_ref, last_ref, last_log_ref, last_send, half_recv.at[0, 0, 0], mate):
            each.wait_send()

    @pl.when(jnp.logical_not(inside))
    def _():
        for head in range(heads):
            for block in range(blocks):
                for each in last_copy(head, block):
                    each.wait_recv()
                mixed, _ = blend(
                    [own_ref[3, head, block], last_ref[head, block]],
                    [own_log_ref[3, head, block], last_log_ref[head, block]],
                )
                out_ref[head, block * BLOCK : (block + 1) * BLOCK, :] = mixed.T.astype(out_ref.dtype)
        kinds = pl.ds(0, 3)
        for each in both(
            own_ref.at[kinds], own_log_ref.at[kinds], half_ref, half_log_ref, half_send, half_recv.at[0, 0, 0], mate
        ):
            each.wait_send()


def by_tokens(keys, values, queries, positions, count):
    heads, rows, width = queries.shape
    n_dev, columns = keys.shape
    length = n_dev * count
    near, down, up, local, merge, cross = fields(length, count)

    def tall(matrix):
        return np.concatenate(split_two(matrix), axis=-2)

    def table(places):
        return tall(np.concatenate(spins(places, width).astype(np.float64), axis=1))

    up_high, up_low = split_two(up)
    t_part = near.shape[0]
    tokens = n_dev // 2
    blocks = rows // BLOCK
    split = 128
    operands = (
        table(np.arange(length // split) * float(split)),
        table(np.arange(split) * 1.0),
        tall(near),
        tall(down),
        np.concatenate([up_high, up_high, up_low], axis=1),
        tall(local),
        tall(merge),
        tall(cross),
        spins(np.arange(count * PARTS) * float(t_part), width),
        spins(np.arange(t_part) * 1.0, width),
    )
    held = [jax.ShapeDtypeStruct(o.shape[1:] if o.ndim == 3 and o.shape[0] == count else o.shape, o.dtype) for o in operands]
    dma = pltpu.SemaphoreType.DMA

    def parts(*lead):
        return [
            pltpu.VMEM(lead + (heads, blocks, width, BLOCK), jnp.bfloat16),
            pltpu.VMEM(lead + (heads, blocks, 1, BLOCK), jnp.float32),
        ]

    return pl.pallas_call(
        functools.partial(fused_kernel, count, math.log2(math.e) / math.sqrt(width)),
        in_specs=[pl.BlockSpec(memory_space=pl.ANY)] * 14,
        out_specs=pl.BlockSpec(memory_space=pltpu.VMEM),
        out_shape=jax.ShapeDtypeStruct(queries.shape, jnp.bfloat16),
        scratch_shapes=[
            pltpu.VMEM(keys.shape, keys.dtype),
            pltpu.VMEM(values.shape, values.dtype),
            pltpu.VMEM(queries.shape, queries.dtype),
            pltpu.VMEM((rows,), jnp.int32),
        ]
        + [pltpu.VMEM(h.shape, h.dtype) for h in held]
        + [
            pltpu.VMEM((PARTS * ORDER, 2 * columns), jnp.float32),
            pltpu.VMEM((2 * EDGE + FAR, 2 * columns), jnp.float32),
            pltpu.VMEM((cross.shape[2], 2 * columns), jnp.float32),
            pltpu.VMEM((PARTS, t_part, 2 * columns), jnp.float32),
            pltpu.VMEM((PARTS * ORDER, 2 * columns), jnp.float32),
            pltpu.VMEM((heads, tokens, width), jnp.bfloat16),
            pltpu.VMEM((heads, width, tokens), jnp.bfloat16),
            pltpu.VMEM((tokens, BLOCK), jnp.float32),
            pltpu.VMEM((tokens, BLOCK), jnp.float32),
            pltpu.VMEM((1, BLOCK), jnp.float32),
            pltpu.VMEM((1, BLOCK), jnp.float32),
            pltpu.VMEM((count, heads, rows, width), jnp.bfloat16),
        ]
        + parts(4)
        + parts(3)
        + parts(2)
        + parts(2)
        + parts()
        + parts()
        + [
            dma((12,)),
            dma((PARTS, 2)),
            pltpu.SemaphoreType.REGULAR((2,)),
            pltpu.SemaphoreType.REGULAR,
            dma((count,)),
            dma((count,)),
            dma((count, 2)),
            dma((count, heads, blocks)),
            dma((2,)),
            dma((3, heads, blocks, 2)),
            dma((2,)),
            dma((2, heads, blocks, 2)),
            dma((2,)),
        ],
        compiler_params=pltpu.CompilerParams(
            collective_id=0, has_side_effects=True, vmem_limit_bytes=60 * 1024 * 1024
        ),
    )(keys, values, queries, positions, *operands)


def by_columns(keys, values, queries, positions):
    key_parts = lax.all_to_all(keys, "ctx", split_axis=1, concat_axis=0, tiled=True)
    value_parts = lax.all_to_all(values, "ctx", split_axis=1, concat_axis=0, tiled=True)
    heads, rows, width = queries.shape
    per_device = key_parts.shape[1]
    compact = compress(jnp.concatenate([key_parts, value_parts], axis=1))
    rotated = rotate_rows(queries.astype(jnp.float32), positions.astype(jnp.float32)).astype(
        jnp.bfloat16
    )
    whole = lax.all_gather(compact.T, "ctx", axis=0, tiled=True)
    tokens = whole.shape[1]
    shaped = whole.reshape(-1, 2, per_device, tokens)
    key_rows = shaped[:, 0].reshape(heads, width, tokens).swapaxes(1, 2)
    value_rows = shaped[:, 1].reshape(heads, width, tokens).swapaxes(1, 2)
    places = jnp.arange(tokens).astype(jnp.float32)
    ready = rotate_rows(key_rows.astype(jnp.float32), places).astype(jnp.bfloat16)
    return attend(rotated, ready, value_rows, jnp.zeros((), jnp.int32))[0]


def solution(mesh):
    count = mesh.shape["ctx"]

    def on_device(keys, values, queries, positions):
        heads, rows, width = queries.shape
        if count == 4 and heads == 2 and keys.shape[0] % (PARTS * 512) == 0 and rows % BLOCK == 0 and width == 128:
            return by_tokens(keys, values, queries, positions, count)
        return by_columns(keys, values, queries, positions)

    return jax.shard_map(
        on_device,
        mesh=mesh,
        in_specs=(
            P(("user", "ctx"), "heads"),
            P(("user", "ctx"), "heads"),
            P("heads", ("user", "ctx"), None),
            P(("user", "ctx")),
        ),
        out_specs=P("heads", ("user", "ctx"), None),
        check_vma=False,
    )
```
